32 devices in a mesh: section: 4 (over x, core), dp: 8 (over z, y).
Axes of the slice: x: 2, y: 2, z: 4, core: 2. Of those that a mesh axis runs over, the one named last changes fastest.
Arguments:
- section_rows: bfloat16 [4, 12288, 768], P('section', 'dp'), may hold values from -6 to 6
- span_lengths: int32 [24, 6], P('dp'), may hold values from 1 to 256, 512 in all within a row
- first_weights: bfloat16 [4, 768, 3072], P('section'), may hold values from -3 to 3, as said below
- second_weights: bfloat16 [4, 768, 1536], P('section'), may hold values from -0.109375 to 0.109375
- norm_gain: float32 [4, 768], P('section'), may hold values from 0.25 to 1.75
- norm_shift: float32 [4, 768], P('section'), may hold values from -1.5 to 1.5
Outputs:
- section_out: float32 [4, 12288, 768], P('section', 'dp')
- grad_first: float32 [4, 768, 3072], P('section')
- grad_second: float32 [4, 768, 1536], P('section')
- grad_gain: float32 [4, 768], P('section')
- grad_shift: float32 [4, 768], P('section')
The draws below stay inside these ranges and needn't reach their ends.
Inputs may be any that keep to these rules, and one draw needn't show every extreme that they name: `span_lengths`: each row's 6 entries sum to 512; the last entry is the row's padding; every row has an entry equal to 256. `first_weights`: independent entries.
All inputs are finite; a program needn't handle non-finite values.
Results may differ from the reference program's by a relative error of at most 0.014.
Values may be sent and summed in bfloat16 or wider, within the bound.
A program may use at most 192 MiB of HBM per device.

```python
import math
import jax
import jax.numpy as jnp
import numpy as np
from jax import lax

D = 768
HEADS = 12
HEAD_DIM = 64
FF = 3072
SEQ = 512
SPANS = 6
ROWS = 24
TOKENS = 12288
N_SECTION = 4


def draw_first_weights(key, part):
    values = jax.random.truncated_normal(key, -4.0, 4.0, (N_SECTION, D, FF), jnp.float32)
    section_ids = jnp.arange(N_SECTION)[:, None, None]
    column = jnp.arange(FF)[None, None, :]
    boost = jnp.where((section_ids % 2 == 0) & (column >= 3 * D), 6.0, 1.0)
    return (values * boost * D ** (-0.5)).astype(jnp.bfloat16)


def block_levels(key, shape, split, least, high):
    gain, own = 1.0, jax.random.fold_in(key, 6)
    for dim, parts in split:
        heights = jnp.exp(jax.random.uniform(jax.random.fold_in(own, dim), (parts,), jnp.float32, least / len(split), high / len(split)))
        gain = gain * jnp.repeat(heights, shape[dim] // parts).reshape([-1 if axis == dim else 1 for axis in range(len(shape))])
    return gain


def split_up(count, total, most, slope):
    weights = [(1 << 20) // math.isqrt(grade ** slope) + 1 for grade in range(2, count + 1)]
    rest, holding = total - most - (count - 1), [1] * (count - 1)
    while rest > 0:
        free = [i for i in range(count - 1) if holding[i] < most]
        mass, left = sum([weights[i] for i in free]), rest
        for i in free:
            extra = min(most - holding[i], max(1, left * weights[i] // mass), rest)
            holding[i] = holding[i] + extra
            rest = rest - extra
    return np.array([most] + holding)


def ragged_sizes(own_key, amount, total, limit, lean):
    if amount == 2:
        one = jax.random.randint(own_key, (), max(1, total - limit), min(limit, total - 1) + 1)
        return jnp.stack([one, total - one])
    sizes = jnp.asarray(split_up(amount, total, limit, lean), jnp.int32)
    twos = (amount - 1) // 2
    giver, taker = sizes[1:1 + 2 * twos:2], sizes[2:2 + 2 * twos:2]
    room = jnp.minimum(giver - 1, limit - taker)
    shifted = jax.random.randint(jax.random.fold_in(own_key, 1), (twos,), 0, 1 << 20) % (room + 1)
    sizes = sizes.at[1:1 + 2 * twos:2].set(giver - shifted).at[2:2 + 2 * twos:2].set(taker + shifted)
    return sizes[jax.random.permutation(jax.random.fold_in(own_key, 2), amount)]


def noise(rng, shape, width, bound, pieces=(), kind=jnp.bfloat16):
    loudness = block_levels(rng, shape, pieces, -0.22, 0.18) if pieces else 1.0
    result = jax.random.normal(rng, shape, jnp.float32) * width * loudness
    return jnp.minimum(jnp.maximum(result, -bound), bound).astype(kind)


def setup_inputs(seed: int = 0) -> dict:
    key_of = jax.random.split(jax.random.key(seed), 7)
    return {
        "section_rows": noise(key_of[0], (N_SECTION, TOKENS, D), 1.0, 6.0, ((0, 4), (1, 8))),
        "span_lengths": jax.vmap(lambda own: ragged_sizes(own, SPANS, SEQ, SEQ // 2, 1))(jax.random.split(key_of[1], ROWS)).reshape((ROWS, SPANS)).astype(jnp.int32),
        "first_weights": draw_first_weights(jax.random.fold_in(key_of[6], 71), 0),
        "second_weights": noise(key_of[3], (N_SECTION, D, FF // 2), FF ** -0.5, 0.109375, ((0, 4),)),
        "norm_gain": jnp.clip(1.0 + 0.15 * jax.random.normal(key_of[4], (N_SECTION, D), jnp.float32), 0.25, 1.75),
        "norm_shift": noise(key_of[5], (N_SECTION, D), 0.3, 1.5, ((0, 4),), jnp.float32),
    }


@jax.custom_vjp
def low(v):
    return lax.optimization_barrier(v.astype(jnp.bfloat16)).astype(jnp.float32)

@jax.custom_vjp
def low_back(v):
    return v

def low_keep(v):
    return (low(v), None)

def low_pass(kept, grad):
    return (grad,)

def back_keep(v):
    return (v, None)

def back_low(kept, grad):
    return (low(grad),)
low.defvjp(low_keep, low_pass)
low_back.defvjp(back_keep, back_low)
highest = lax.Precision.HIGHEST
epsilon = 1e-12

def layer_norm(summed, gain_row, shift_row):
    centered = summed - lax.optimization_barrier(jnp.mean(summed, axis=-1, keepdims=True))
    factor = lax.rsqrt(lax.optimization_barrier(jnp.mean(centered * centered, axis=-1, keepdims=True)) + epsilon)
    return centered * factor * gain_row + shift_row

def span_tables(lengths):
    span_ends = jnp.cumsum(lengths, axis=-1).astype(jnp.int32)
    span_starts = (span_ends - lengths).astype(jnp.int32)
    positions = jnp.arange(SEQ, dtype=jnp.int32)
    segment = lax.optimization_barrier(jnp.sum((positions[None, :, None] >= span_ends[:, None, :]).astype(jnp.int32), axis=-1))
    leading = jnp.any(positions[None, :, None] == span_starts[:, None, :SPANS - 1], axis=-1)
    allowed = segment[:, :, None] == segment[:, None, :]
    return (leading, allowed)

def attention(inputs, weights, gain_row, shift_row, allowed):
    row_count = inputs.shape[0]

    def project(columns_in):
        return jnp.einsum('gtd,de->gte', inputs, columns_in, precision=highest)
    queries = low_back(low(project(weights[:, :D]))).reshape(row_count, SEQ, HEADS, HEAD_DIM)
    keys_h = low_back(low(project(weights[:, D:2 * D]))).reshape(row_count, SEQ, HEADS, HEAD_DIM)
    values_h = low_back(low(project(weights[:, 2 * D:3 * D]))).reshape(row_count, SEQ, HEADS, HEAD_DIM)
    scores = jnp.einsum('gqhd,gkhd->ghqk', queries, keys_h, precision=highest) * HEAD_DIM ** (-0.5)
    scores = low_back(jnp.where(allowed[:, None], scores, -1e+30))
    row_max = lax.optimization_barrier(jnp.max(scores, axis=-1, keepdims=True))
    exponent = jnp.exp(scores - row_max)
    soft_probs = exponent / lax.optimization_barrier(jnp.sum(exponent, axis=-1, keepdims=True))
    context = jnp.einsum('ghqk,gkhd->gqhd', low(soft_probs), values_h, precision=highest)
    context = low_back(low(context.reshape(row_count, SEQ, D)))
    branch = low_back(jnp.einsum('gtd,de->gte', context, weights[:, 3 * D:], precision=highest))
    return layer_norm(inputs + branch, gain_row, shift_row)

def feed_forward(inputs, weights, second_t, gain_row, shift_row):
    hidden = low_back(jnp.einsum('gtd,df->gtf', inputs, weights, precision=highest))
    active = low(jax.nn.gelu(hidden, approximate=False))
    branch = low_back(jnp.einsum('gtf,df->gtd', active, second_t, precision=highest))
    return layer_norm(inputs + branch, gain_row, shift_row)

def forward(params, base_rows, skipped, leading, allowed):
    first_w, second_w, gains, shifts = params
    start_out = attention(base_rows, first_w[0], gains[0], shifts[0], allowed)
    lower_down = jnp.concatenate([second_w[0], second_w[1]], axis=1)
    middle = feed_forward(low_back(low(start_out)), first_w[1], lower_down, gains[1], shifts[1])
    backbone = low_back(low(middle))
    head_in = jnp.where(leading[..., None], backbone, low_back(skipped))
    head_mid = attention(head_in, first_w[2], gains[2], shifts[2], allowed)
    upper_down = jnp.concatenate([second_w[2], second_w[3]], axis=1)
    final_out = feed_forward(low_back(low(head_mid)), first_w[3], upper_down, gains[3], shifts[3])
    return (final_out, backbone)

def reference(section_rows, span_lengths, first_weights, second_weights, norm_gain, norm_shift):
    rows_all = section_rows.astype(jnp.float32).reshape(N_SECTION, -1, SEQ, D)
    row_count = rows_all.shape[1]
    group_rows = 8
    blocks = rows_all.reshape(N_SECTION, row_count // group_rows, group_rows, SEQ, D)
    blocks = jnp.transpose(blocks, (1, 0, 2, 3, 4))
    lengths = span_lengths.reshape(row_count // group_rows, group_rows, SPANS)
    params = (first_weights.astype(jnp.float32), second_weights.astype(jnp.float32), norm_gain.astype(jnp.float32), norm_shift.astype(jnp.float32))

    def one_group(totals, inputs):
        rows_in, length_rows = inputs
        leading, allowed = span_tables(length_rows)

        def run_forward(params_in, base_rows, skipped):
            return forward(params_in, base_rows, skipped, leading, allowed)
        (final_out, backbone), pullback = jax.vjp(run_forward, params, rows_in[0], rows_in[1])
        grads, base_grad, skip_grad = pullback((rows_in[3], rows_in[2]))
        totals = jax.tree.map(lambda a, b: a + b, totals, grads)
        return (totals, jnp.stack([base_grad, skip_grad, backbone, final_out]))
    zero_grads = jax.tree.map(jnp.zeros_like, params)
    totals, stacked = lax.scan(one_group, zero_grads, (blocks, lengths))
    section_out = jnp.transpose(stacked, (1, 0, 2, 3, 4)).reshape(N_SECTION, -1, D)
    return (section_out, totals[0], totals[1], totals[2], totals[3])
```

```python
import jax
import jax.numpy as jnp
from jax import lax
from jax.sharding import PartitionSpec as P

HEAD_DIM = 64
SEQ = 512
BLOCK = 256
LEADS = 16

epsilon = 1e-12
f32 = jnp.float32
bf16 = jnp.bfloat16
rows_rows = (((0,), (0,)), ((), ()))
cols_cols = (((1,), (1,)), ((), ()))


def normalize(summed):
    centered = summed - jnp.mean(summed, axis=-1, keepdims=True)
    rstd = lax.rsqrt(jnp.mean(centered * centered, axis=-1, keepdims=True) + epsilon)
    return centered * rstd, rstd


def normalize_back(zh, rstd, gain, upstream):
    g = upstream * gain
    mean_g = jnp.mean(g, axis=-1, keepdims=True)
    mean_gz = jnp.mean(g * zh, axis=-1, keepdims=True)
    d_gain = jnp.sum(upstream * zh, axis=0)
    d_shift = jnp.sum(upstream, axis=0)
    return rstd * (g - mean_g - zh * mean_gz), d_gain, d_shift


def attend(inputs, weights, gain, shift, allowed):
    tokens, features = inputs.shape
    heads = features // HEAD_DIM
    blocks = tokens // BLOCK
    qkv = jnp.dot(inputs, weights[:, : 3 * features], preferred_element_type=f32).astype(bf16)
    split = qkv.reshape(blocks, BLOCK, 3, heads, HEAD_DIM)
    q, k, v = split[:, :, 0], split[:, :, 1], split[:, :, 2]
    scores = jnp.einsum("bqhd,bkhd->bhqk", q, k, preferred_element_type=f32) * HEAD_DIM**-0.5
    scores = jnp.where(allowed[:, None], scores, -1e30)
    exponent = jnp.exp(scores - jnp.max(scores, axis=-1, keepdims=True))
    probs = exponent / jnp.sum(exponent, axis=-1, keepdims=True)
    low_probs = probs.astype(bf16)
    ctx = jnp.einsum("bhqk,bkhd->bqhd", low_probs, v, preferred_element_type=f32)
    ctx = ctx.reshape(tokens, features).astype(bf16)
    branch = jnp.dot(ctx, weights[:, 3 * features :], preferred_element_type=f32)
    zh, rstd = normalize(inputs.astype(f32) + branch)
    return zh * gain + shift, (q, k, v, low_probs, ctx, zh, rstd)


def attend_back(saved, weights, gain, upstream):
    q, k, v, low_probs, ctx, zh, rstd = saved
    tokens, features = ctx.shape
    blocks, _, heads, _ = q.shape
    scale = HEAD_DIM**-0.5
    dz, d_gain, d_shift = normalize_back(zh, rstd, gain, upstream)
    d_out = dz.astype(bf16)
    d_ctx = lax.dot_general(
        d_out, weights[:, 3 * features :], cols_cols, preferred_element_type=f32
    ).astype(bf16)
    d_ctx = d_ctx.reshape(blocks, BLOCK, heads, HEAD_DIM)
    probs = low_probs.astype(f32)
    d_probs = jnp.einsum("bqhd,bkhd->bhqk", d_ctx, v, preferred_element_type=f32)
    ds = probs * (d_probs - jnp.sum(d_probs * probs, axis=-1, keepdims=True))
    ds = ds.astype(bf16)
    dv = jnp.einsum("bhqk,bqhd->bkhd", low_probs, d_ctx, preferred_element_type=f32)
    dq = jnp.einsum("bhqk,bkhd->bqhd", ds, k, preferred_element_type=f32) * scale
    dk = jnp.einsum("bhqk,bqhd->bkhd", ds, q, preferred_element_type=f32) * scale
    dqkv = jnp.concatenate(
        [t.reshape(tokens, features).astype(bf16) for t in (dq, dk, dv)], axis=1
    )
    dx = dz + lax.dot_general(
        dqkv, weights[:, : 3 * features], cols_cols, preferred_element_type=f32
    )
    return dx, d_out, dqkv, d_gain, d_shift


def expand(inputs, w_up, w_down, gain, shift):
    u = jnp.dot(inputs, w_up, preferred_element_type=f32)
    cdf = 0.5 * (1.0 + lax.erf(u * (0.5**0.5)))
    pdf = jnp.exp(-0.5 * u * u) * 0.3989422804014327
    a = (u * cdf).astype(bf16)
    slope = (cdf + u * pdf).astype(bf16)
    branch = lax.dot_general(a, w_down, cols_cols, preferred_element_type=f32)
    zh, rstd = normalize(inputs.astype(f32) + branch)
    return zh * gain + shift, (a, slope, zh, rstd)


def expand_back(saved, w_up, w_down, gain, upstream):
    a, slope, zh, rstd = saved
    dz, d_gain, d_shift = normalize_back(zh, rstd, gain, upstream)
    df = dz.astype(bf16)
    da = jnp.dot(df, w_down, preferred_element_type=f32)
    du = (da * slope.astype(f32)).astype(bf16)
    dx = dz + lax.dot_general(du, w_up, cols_cols, preferred_element_type=f32)
    return dx, df, du, d_gain, d_shift


def row_tables(lengths, core):
    rows, spans = lengths.shape
    order = jnp.arange(spans)
    ends = jnp.sum(jnp.where(order[:, None] <= order[None, :], lengths[:, :, None], 0), axis=1)
    starts = ends - lengths
    first = jnp.sum(jnp.where(lengths == BLOCK, starts, 0), axis=1)
    place = jnp.arange(SEQ)
    origin = (place[None, :] + first[:, None]) % SEQ
    roll = (origin[:, :, None] == place[None, None, :]).astype(bf16)
    mine = lax.dynamic_slice_in_dim(origin, core * BLOCK, BLOCK, 1)
    segment = jnp.sum((mine[:, :, None] >= ends[:, None, :]).astype(jnp.int32), axis=2)
    allowed = segment[:, :, None] == segment[:, None, :]
    lead = (starts[:, : spans - 1] - first[:, None]) % SEQ
    spot = jnp.where(lead // BLOCK == core, jnp.arange(rows)[:, None] * BLOCK + lead % BLOCK, -1)
    spot = jnp.concatenate([spot.reshape(-1), jnp.full((LEADS,), -1)])[:LEADS]
    pick = spot[:, None] == jnp.arange(rows * BLOCK)[None, :]
    return roll, allowed, pick.astype(bf16)


def per_device(section_rows, span_lengths, first_weights, second_weights, norm_gain, norm_shift):
    sec = lax.axis_index("section")
    core = sec % 2
    at_head = sec // 2 == 1
    own_rows = section_rows[0]
    tokens, features = own_rows.shape
    rows = tokens // SEQ
    half_tokens = rows * BLOCK
    pairs = [[0, 1], [2, 3]]
    swap = [(0, 1), (1, 0), (2, 3), (3, 2)]
    roll, allowed, pick = row_tables(span_lengths, core)

    rolled = jnp.einsum(
        "rij,rjd->rid", roll, own_rows.reshape(rows, SEQ, features), preferred_element_type=f32
    ).astype(bf16)
    rolled = rolled.reshape(rows, 2, BLOCK, features)
    half0 = rolled[:, 0].reshape(half_tokens, features)
    half1 = rolled[:, 1].reshape(half_tokens, features)
    inner = lax.ppermute(jnp.where(at_head, half0, half1), "section", [(0, 1), (3, 2)])
    aux0 = lax.ppermute(half0, "section", [(1, 2), (2, 0)])
    aux1 = lax.ppermute(half1, "section", [(1, 3), (2, 1)])
    main = jnp.where(sec == 0, half0, jnp.where(sec == 3, half1, inner))
    aux = jnp.where(core == 0, aux0, aux1)

    def both(block):
        return lax.all_gather(block, "section", axis_index_groups=pairs)

    first2 = both(first_weights[0])
    second2 = both(second_weights[0])
    norm2 = both(jnp.concatenate([norm_gain, norm_shift], axis=0))
    w_att, w_up = first2[0], first2[1]
    w_down = jnp.concatenate([second2[0], second2[1]], axis=1)

    def forward(inputs):
        y_att, saved_att = attend(inputs, w_att, norm2[0, 0], norm2[0, 1], allowed)
        middle = y_att.astype(bf16)
        y_ffn, saved_ffn = expand(middle, w_up, w_down, norm2[1, 0], norm2[1, 1])
        return y_ffn, middle, saved_att, saved_ffn

    def backward(upstream, saved_att, saved_ffn):
        d_mid, df, du, dg1, ds1 = expand_back(saved_ffn, w_up, w_down, norm2[1, 0], upstream)
        d_mid = d_mid.astype(bf16).astype(f32)
        dx, d_out, dqkv, dg0, ds0 = attend_back(saved_att, w_att, norm2[0, 0], d_mid)
        return dx, df, du, d_out, dqkv, jnp.stack([jnp.stack([dg0, ds0]), jnp.stack([dg1, ds1])])

    def at_leads(values):
        return jnp.dot(pick, values, precision=lax.Precision.HIGHEST, preferred_element_type=f32)

    def from_leads(values):
        return lax.dot_general(
            pick.astype(values.dtype), values, rows_rows, precision=lax.Precision.HIGHEST,
            preferred_element_type=f32,
        )

    leading = jnp.sum(pick.astype(f32), axis=0)[:, None] > 0
    y_first = forward(main)[0]
    lead_rows = lax.ppermute(at_leads(y_first.astype(bf16)).astype(bf16), "section", [(0, 2), (1, 3)])
    head_in = jnp.where(leading, from_leads(lead_rows).astype(bf16), aux)
    inputs = jnp.where(at_head, head_in, main)
    y_ffn, middle, saved_att, saved_ffn = forward(inputs)
    dx_first = backward(main.astype(f32), saved_att, saved_ffn)[0]
    lead_grads = lax.ppermute(at_leads(dx_first), "section", [(2, 0), (3, 1)])
    d_twelve = (from_leads(lead_grads) + aux.astype(f32)).astype(bf16)
    upstream = jnp.where(at_head, main, d_twelve).astype(f32)
    dx, df, du, d_out, dqkv, d_norm = backward(upstream, saved_att, saved_ffn)

    a, ctx = saved_ffn[0], saved_att[4]

    def outer(left, right):
        return lax.dot_general(left, right, rows_rows, preferred_element_type=f32).astype(bf16)

    d_down = outer(df, a)
    half_ff = d_down.shape[1] // 2
    for_even = jnp.concatenate([outer(inputs, dqkv), outer(ctx, d_out), d_down[:, :half_ff]], axis=1)
    for_odd = jnp.concatenate([outer(middle, du), d_down[:, half_ff:]], axis=1)
    kept = jnp.where(core == 0, for_even, for_odd)
    given = lax.ppermute(jnp.where(core == 0, for_odd, for_even), "section", swap)
    total = (kept.astype(f32) + given.astype(f32)).astype(bf16)
    total = lax.psum(total, "dp").astype(f32)
    ff = first_weights.shape[2]
    d_norm_kept = jnp.where(core == 0, d_norm[0], d_norm[1])
    d_norm_given = lax.ppermute(jnp.where(core == 0, d_norm[1], d_norm[0]), "section", swap)
    norm_total = lax.psum(d_norm_kept + d_norm_given, "dp")

    dskip = jnp.where(leading, 0.0, dx).astype(bf16)
    across = jnp.where(at_head, dskip, y_ffn.astype(bf16))
    out0 = lax.ppermute(across, "section", [(0, 2), (2, 1)])
    out1 = lax.ppermute(across, "section", [(1, 2), (3, 1)])
    own_out = jnp.where(at_head, y_ffn, dx).astype(bf16)
    inner_out = lax.ppermute(own_out, "section", [(1, 0), (2, 3)])
    out0 = jnp.where(sec == 0, own_out, jnp.where(sec == 3, inner_out, out0))
    out1 = jnp.where(sec == 0, inner_out, jnp.where(sec == 3, own_out, out1))
    out = jnp.stack([t.reshape(rows, BLOCK, features) for t in (out0, out1)], axis=1)
    out = jnp.einsum(
        "rij,rid->rjd", roll, out.reshape(rows, SEQ, features), preferred_element_type=f32
    ).reshape(tokens, features)
    return (
        out[None], total[None, :, :ff], total[None, :, ff:], norm_total[None, 0], norm_total[None, 1]
    )


def solution(mesh):
    in_specs = (
        P("section", "dp", None),
        P("dp", None),
        P("section", None, None),
        P("section", None, None),
        P("section", None),
        P("section", None),
    )
    out_specs = (
        P("section", "dp", None),
        P("section", None, None),
        P("section", None, None),
        P("section", None),
        P("section", None),
    )
    return jax.shard_map(
        per_device, mesh=mesh, in_specs=in_specs, out_specs=out_specs, check_vma=False
    )
```

```python
import jax
import jax.numpy as jnp
from jax import lax
from jax.experimental import pallas as pl
from jax.experimental.pallas import tpu as pltpu
from jax.sharding import PartitionSpec as P

HEAD_DIM = 64
PAIR = 2 * HEAD_DIM
BLOCK = 256
SEQ = 512
LEADS = 16
CHUNK = 512
f32 = jnp.float32
bf16 = jnp.bfloat16
epsilon = 1e-12
NN = (((1,), (0,)), ((), ()))
NT = (((1,), (1,)), ((), ()))
TN = (((0,), (0,)), ((), ()))
LOG2E = 1.4426950408889634


def mm(a, b, dims=NN):
    return lax.dot_general(a, b, dims, preferred_element_type=f32)


def gelu_and_slope(u):
    x = jnp.abs(u)
    bell = jnp.exp2(u * u * (-0.5 * LOG2E))
    t = 1.0 / (1.0 + (0.3275911 * 0.5**0.5) * x)
    poly = t * (0.127414796 + t * (-0.142248368 + t * (0.7107068705 + t * (-0.7265760135 + t * 0.5307027145))))
    tail = poly * bell
    cdf = jnp.where(u < 0, tail, 1.0 - tail)
    return u * cdf, cdf + u * bell * 0.3989422804014327


def normalize(z):
    centered = z - jnp.mean(z, axis=-1, keepdims=True)
    rstd = lax.rsqrt(jnp.mean(centered * centered, axis=-1, keepdims=True) + epsilon)
    return centered * rstd, rstd


def lane_masks(rows):
    lane = lax.broadcasted_iota(jnp.int32, (rows, PAIR), 1)
    return lane < HEAD_DIM


def forward_kernel(
    x, seg_rows, seg_cols, norms, pick, first_h, second_h,
    y_h, lead, qkv_h, p_h, ctx_h, zh0_h, rstd0, mid_h, a_h, slope_h, zh1_h, rstd1,
    wa, wu, wd, qkv, p, ctx, zh0, mid, a, slope, zh1, y, acc, sems, out_sems,
):
    tokens, features = x.shape
    ff = wu.shape[1]
    blocks = tokens // BLOCK
    pairs = features // PAIR
    half = ff // 2
    n3 = 3 * features
    loads = [
        pltpu.make_async_copy(first_h.at[0], wa, sems.at[0]),
        pltpu.make_async_copy(first_h.at[1], wu, sems.at[1]),
        pltpu.make_async_copy(second_h.at[0], wd.at[:, pl.ds(0, half)], sems.at[2]),
        pltpu.make_async_copy(second_h.at[1], wd.at[:, pl.ds(half, half)], sems.at[3]),
    ]
    for c in loads:
        c.start()
    stores = []

    def keep(src, dst):
        c = pltpu.make_async_copy(src, dst, out_sems.at[len(stores)])
        c.start()
        stores.append(c)

    loads[0].wait()
    for c in range(n3 // features):
        cols = pl.ds(c * features, features)
        qkv[:, cols] = mm(x[...], wa[:, cols]).astype(bf16)
    keep(qkv, qkv_h)
    first = lane_masks(BLOCK)
    zero = jnp.zeros((BLOCK, PAIR), bf16)

    def block_step(b, carry):
        rows = pl.ds(pl.multiple_of(b * BLOCK, BLOCK), BLOCK)
        bias = jnp.where(seg_rows[rows, :] == seg_cols[b], 0.0, -1e30)
        for h in range(pairs):
            q = qkv[rows, pl.ds(h * PAIR, PAIR)]
            k = qkv[rows, pl.ds(features + h * PAIR, PAIR)]
            v = qkv[rows, pl.ds(2 * features + h * PAIR, PAIR)]
            total = None
            for side in range(2):
                own = first if side == 0 else ~first
                s = mm(q, jnp.where(own, k, zero), NT) * (HEAD_DIM**-0.5) + bias
                e = jnp.exp(s - jnp.max(s, axis=-1, keepdims=True))
                pr = (e * (1.0 / jnp.sum(e, axis=-1, keepdims=True))).astype(bf16)
                p[b, h, :, pl.ds(side * BLOCK, BLOCK)] = pr
                part = mm(pr, jnp.where(own, v, zero))
                total = part if total is None else total + part
            ctx[rows, pl.ds(h * PAIR, PAIR)] = total.astype(bf16)
        return carry

    lax.fori_loop(0, blocks, block_step, 0)
    keep(p, p_h)
    keep(ctx, ctx_h)
    z = x[...].astype(f32) + mm(ctx[...], wa[:, pl.ds(n3, features)])
    zn, r = normalize(z)
    rstd0[...] = r
    zh0[...] = zn.astype(bf16)
    mid[...] = (zn * norms[0:1, :] + norms[1:2, :]).astype(bf16)
    keep(zh0, zh0_h)
    keep(mid, mid_h)
    for c in loads[1:]:
        c.wait()
    acc[...] = mid[...].astype(f32)

    for c in range(ff // CHUNK):
        cols = pl.ds(c * CHUNK, CHUNK)
        u = mm(mid[...], wu[:, cols])
        act, sl = gelu_and_slope(u)
        act = act.astype(bf16)
        a[:, cols] = act
        slope[:, cols] = sl.astype(bf16)
        acc[...] += mm(act, wd[:, cols], NT)
    keep(a, a_h)
    keep(slope, slope_h)
    zn, r = normalize(acc[...])
    rstd1[...] = r
    zh1[...] = zn.astype(bf16)
    y[...] = (zn * norms[2:3, :] + norms[3:4, :]).astype(bf16)
    keep(zh1, zh1_h)
    keep(y, y_h)
    lead[...] = mm(pick[...], y[...]).astype(bf16)
    for c in stores:
        c.wait()


def forward(x, seg_rows, seg_cols, norms, pick, firsts, seconds):
    tokens, features = x.shape
    ff = firsts.shape[2]
    blocks, pairs = tokens // BLOCK, features // PAIR
    S = jax.ShapeDtypeStruct
    any_ = pl.BlockSpec(memory_space=pl.ANY)
    vm = pl.BlockSpec(memory_space=pltpu.VMEM)
    shapes = dict(
        y=S((tokens, features), bf16), lead=S((pick.shape[0], features), bf16),
        qkv=S((tokens, 3 * features), bf16), p=S((blocks, pairs, BLOCK, 2 * BLOCK), bf16),
        ctx=S((tokens, features), bf16), zh0=S((tokens, features), bf16), rstd0=S((tokens, 1), f32),
        mid=S((tokens, features), bf16), a=S((tokens, ff), bf16), slope=S((tokens, ff), bf16),
        zh1=S((tokens, features), bf16), rstd1=S((tokens, 1), f32),
    )
    V = lambda k: pltpu.VMEM(shapes[k].shape, shapes[k].dtype)
    outs = pl.pallas_call(
        forward_kernel,
        out_shape=list(shapes.values()),
        in_specs=[vm] * 5 + [any_] * 2,
        out_specs=[vm if k in ("lead", "rstd0", "rstd1") else any_ for k in shapes],
        scratch_shapes=[
            pltpu.VMEM(firsts.shape[1:], bf16), pltpu.VMEM(firsts.shape[1:], bf16), pltpu.VMEM((features, ff), bf16),
            V("qkv"), V("p"), V("ctx"), V("zh0"), V("mid"), V("a"), V("slope"), V("zh1"), V("y"),
            pltpu.VMEM((tokens, features), f32),
            pltpu.SemaphoreType.DMA((4,)), pltpu.SemaphoreType.DMA((9,)),
        ],
        compiler_params=pltpu.CompilerParams(vmem_limit_bytes=60 << 20),
        name="layer_forward",
    )(x, seg_rows, seg_cols, norms, pick, firsts, seconds)
    return dict(zip(shapes, outs))


def normalize_back(zh, rstd, gain, dy):
    g = dy * gain
    mean_g = jnp.mean(g, axis=-1, keepdims=True)
    mean_gz = jnp.mean(g * zh, axis=-1, keepdims=True)
    dz = rstd * (g - mean_g - zh * mean_gz)
    return dz, jnp.sum(dy * zh, axis=0, keepdims=True), jnp.sum(dy, axis=0, keepdims=True)


def backward_kernel(
    dy, norms, pick, rstd0, rstd1, first_h, second_h,
    qkv_h, p_h, zh0_h, slope_h, zh1_h,
    dx_h, lead, df_h, du_h, do_h, dqkv_h, dnorm,
    wa, wu, wd, qkv, p, zh0, slope, zh1, dx, df, du, do, dqkv, dctx, acc, sems, out_sems,
):
    tokens, features = dy.shape
    ff = wu.shape[1]
    blocks = tokens // BLOCK
    pairs = features // PAIR
    half = ff // 2
    n3 = 3 * features
    C = pltpu.make_async_copy
    ld = [
        C(zh1_h, zh1, sems.at[0]),
        C(second_h.at[0], wd.at[:, pl.ds(0, half)], sems.at[1]),
        C(first_h.at[1], wu, sems.at[2]),
        C(slope_h, slope, sems.at[3]),
        C(second_h.at[1], wd.at[:, pl.ds(half, half)], sems.at[4]),
        C(zh0_h, zh0, sems.at[5]),
        C(first_h.at[0], wa, sems.at[6]),
        C(qkv_h, qkv, sems.at[7]),
        C(p_h, p, sems.at[8]),
    ]
    for c in ld:
        c.start()
    stores = []

    def keep(src, dst):
        c = C(src, dst, out_sems.at[len(stores)])
        c.start()
        stores.append(c)

    ld[0].wait()
    dz, dg, ds_ = normalize_back(zh1[...].astype(f32), rstd1[...], norms[2:3, :], dy[...].astype(f32))
    dnorm[2:3, :] = dg
    dnorm[3:4, :] = ds_
    df[...] = dz.astype(bf16)
    acc[...] = dz
    keep(df, df_h)
    for i in (1, 2, 3):
        ld[i].wait()
    for c in range(ff // CHUNK):
        if c == ff // CHUNK // 2:
            ld[4].wait()
        cols = pl.ds(c * CHUNK, CHUNK)
        da = mm(df[...], wd[:, cols])
        g = (da * slope[:, cols].astype(f32)).astype(bf16)
        du[:, cols] = g
        acc[...] += mm(g, wu[:, cols], NT)
    keep(du, du_h)
    ld[5].wait()
    d_mid = acc[...].astype(bf16).astype(f32)
    dz, dg, ds_ = normalize_back(zh0[...].astype(f32), rstd0[...], norms[0:1, :], d_mid)
    dnorm[0:1, :] = dg
    dnorm[1:2, :] = ds_
    do[...] = dz.astype(bf16)
    acc[...] = dz
    keep(do, do_h)
    ld[6].wait()
    dctx[...] = mm(do[...], wa[:, pl.ds(n3, features)], NT).astype(bf16)
    ld[7].wait()
    ld[8].wait()
    first = lane_masks(BLOCK)
    zero = jnp.zeros((BLOCK, PAIR), bf16)
    scale = HEAD_DIM**-0.5

    def block_step(b, carry):
        rows = pl.ds(pl.multiple_of(b * BLOCK, BLOCK), BLOCK)
        for h in range(pairs):
            q = qkv[rows, pl.ds(h * PAIR, PAIR)]
            k = qkv[rows, pl.ds(features + h * PAIR, PAIR)]
            v = qkv[rows, pl.ds(2 * features + h * PAIR, PAIR)]
            dc = dctx[rows, pl.ds(h * PAIR, PAIR)]
            dq = dk = dv = None
            for side in range(2):
                own = first if side == 0 else ~first
                pr = p[b, h, :, pl.ds(side * BLOCK, BLOCK)]
                prf = pr.astype(f32)
                dp = mm(dc, jnp.where(own, v, zero), NT)
                r = jnp.sum(dp * prf, axis=-1, keepdims=True)
                ds = (prf * (dp - r)).astype(bf16)
                parts = (
                    mm(ds, jnp.where(own, k, zero)),
                    mm(ds, jnp.where(own, q, zero), TN),
                    mm(pr, jnp.where(own, dc, zero), TN),
                )
                if dq is None:
                    dq, dk, dv = parts
                else:
                    dq, dk, dv = dq + parts[0], dk + parts[1], dv + parts[2]
            dqkv[rows, pl.ds(h * PAIR, PAIR)] = (dq * scale).astype(bf16)
            dqkv[rows, pl.ds(features + h * PAIR, PAIR)] = (dk * scale).astype(bf16)
            dqkv[rows, pl.ds(2 * features + h * PAIR, PAIR)] = dv.astype(bf16)
        return carry

    lax.fori_loop(0, blocks, block_step, 0)
    keep(dqkv, dqkv_h)
    for c in range(3):
        cols = pl.ds(c * features, features)
        acc[...] += mm(dqkv[:, cols], wa[:, cols], NT)
    dx[...] = acc[...].astype(bf16)
    keep(dx, dx_h)
    hi = acc[...].astype(bf16)
    lo = (acc[...] - hi.astype(f32)).astype(bf16)
    lead[...] = mm(pick[...], hi) + mm(pick[...], lo)
    for c in stores:
        c.wait()


def backward(dy, norms, pick, sv, firsts, seconds):
    tokens, features = dy.shape
    ff = firsts.shape[2]
    blocks, pairs = tokens // BLOCK, features // PAIR
    S = jax.ShapeDtypeStruct
    any_ = pl.BlockSpec(memory_space=pl.ANY)
    vm = pl.BlockSpec(memory_space=pltpu.VMEM)
    shapes = dict(
        dx=S((tokens, features), bf16), lead=S((pick.shape[0], features), f32),
        df=S((tokens, features), bf16), du=S((tokens, ff), bf16), do=S((tokens, features), bf16),
        dqkv=S((tokens, 3 * features), bf16), dnorm=S((4, features), f32),
    )
    V = lambda k: pltpu.VMEM(shapes[k].shape, shapes[k].dtype)
    L = lambda k: pltpu.VMEM(sv[k].shape, sv[k].dtype)
    outs = pl.pallas_call(
        backward_kernel,
        out_shape=list(shapes.values()),
        in_specs=[vm] * 5 + [any_] * 7,
        out_specs=[vm if k in ("lead", "dnorm") else any_ for k in shapes],
        scratch_shapes=[
            pltpu.VMEM(firsts.shape[1:], bf16), pltpu.VMEM(firsts.shape[1:], bf16), pltpu.VMEM((features, ff), bf16),
            L("qkv"), L("p"), L("zh0"), L("slope"), L("zh1"),
            V("dx"), V("df"), V("du"), V("do"), V("dqkv"), pltpu.VMEM((tokens, features), bf16),
            pltpu.VMEM((tokens, features), f32),
            pltpu.SemaphoreType.DMA((9,)), pltpu.SemaphoreType.DMA((5,)),
        ],
        compiler_params=pltpu.CompilerParams(vmem_limit_bytes=60 << 20),
        name="layer_backward",
    )(dy, norms, pick, sv["rstd0"], sv["rstd1"], firsts, seconds, sv["qkv"], sv["p"], sv["zh0"], sv["slope"], sv["zh1"])
    return dict(zip(shapes, outs))


def row_tables(lengths, core):
    rows, spans = lengths.shape
    order = jnp.arange(spans)
    ends = jnp.sum(jnp.where(order[:, None] <= order[None, :], lengths[:, :, None], 0), axis=1)
    starts = ends - lengths
    first = jnp.sum(jnp.where(lengths == BLOCK, starts, 0), axis=1)
    place = jnp.arange(SEQ)
    origin = (place[None, :] + first[:, None]) % SEQ
    roll = (origin[:, :, None] == place[None, None, :]).astype(bf16)
    mine = lax.dynamic_slice_in_dim(origin, core * BLOCK, BLOCK, 1)
    segment = jnp.sum((mine[:, :, None] >= ends[:, None, :]).astype(jnp.int32), axis=2)
    lead = (starts[:, : spans - 1] - first[:, None]) % SEQ
    spot = jnp.where(lead // BLOCK == core, jnp.arange(rows)[:, None] * BLOCK + lead % BLOCK, -1)
    spot = jnp.concatenate([spot.reshape(-1), jnp.full((LEADS,), -1)])[:LEADS]
    pick = spot[:, None] == jnp.arange(rows * BLOCK)[None, :]
    return roll, segment, pick.astype(bf16)


def per_device(section_rows, span_lengths, first_weights, second_weights, norm_gain, norm_shift):
    sec = lax.axis_index("section")
    core = sec % 2
    at_head = sec // 2 == 1
    own_rows = section_rows[0]
    tokens, features = own_rows.shape
    rows = tokens // SEQ
    half_tokens = rows * BLOCK
    pairs = [[0, 1], [2, 3]]
    swap = [(0, 1), (1, 0), (2, 3), (3, 2)]
    roll, segment, pick = row_tables(span_lengths, core)

    rolled = jnp.einsum(
        "rij,rjd->rid", roll, own_rows.reshape(rows, SEQ, features), preferred_element_type=f32
    ).astype(bf16)
    rolled = rolled.reshape(rows, 2, BLOCK, features)
    half0 = rolled[:, 0].reshape(half_tokens, features)
    half1 = rolled[:, 1].reshape(half_tokens, features)
    inner = lax.ppermute(jnp.where(at_head, half0, half1), "section", [(0, 1), (3, 2)])
    aux0 = lax.ppermute(half0, "section", [(1, 2), (2, 0)])
    aux1 = lax.ppermute(half1, "section", [(1, 3), (2, 1)])
    main = jnp.where(sec == 0, half0, jnp.where(sec == 3, half1, inner))
    aux = jnp.where(core == 0, aux0, aux1)

    def both(block):
        return lax.all_gather(block, "section", axis_index_groups=pairs)

    first2 = both(first_weights[0])
    second2 = both(second_weights[0])
    norm2 = both(jnp.concatenate([norm_gain, norm_shift], axis=0))
    norms = norm2.reshape(4, features)
    seg_rows = segment.reshape(half_tokens, 1)
    seg_cols = segment.reshape(rows, 1, BLOCK)

    def from_leads(values):
        return lax.dot_general(
            pick.astype(values.dtype), values, TN, precision=lax.Precision.HIGHEST,
            preferred_element_type=f32,
        )

    leading = jnp.sum(pick.astype(f32), axis=0)[:, None] > 0
    lead_rows = forward(main, seg_rows, seg_cols, norms, pick, first2, second2)["lead"]
    lead_rows = lax.ppermute(lead_rows, "section", [(0, 2), (1, 3)])
    head_in = jnp.where(leading, from_leads(lead_rows).astype(bf16), aux)
    inputs = jnp.where(at_head, head_in, main)
    saved = forward(inputs, seg_rows, seg_cols, norms, pick, first2, second2)
    lead_grads = backward(main, norms, pick, saved, first2, second2)["lead"]
    lead_grads = lax.ppermute(lead_grads, "section", [(2, 0), (3, 1)])
    d_twelve = (from_leads(lead_grads) + aux.astype(f32)).astype(bf16)
    upstream = jnp.where(at_head, main, d_twelve)
    grads = backward(upstream, norms, pick, saved, first2, second2)
    dx, df, du, d_out, dqkv = (grads[k] for k in ("dx", "df", "du", "do", "dqkv"))
    d_norm = grads["dnorm"].reshape(2, 2, features)
    y_ffn, middle, a, ctx = (saved[k] for k in ("y", "mid", "a", "ctx"))

    def outer(left, right):
        return lax.dot_general(left, right, TN, preferred_element_type=f32).astype(bf16)

    d_down = outer(df, a)
    half_ff = d_down.shape[1] // 2
    for_even = jnp.concatenate([outer(inputs, dqkv), outer(ctx, d_out), d_down[:, :half_ff]], axis=1)
    for_odd = jnp.concatenate([outer(middle, du), d_down[:, half_ff:]], axis=1)
    kept = jnp.where(core == 0, for_even, for_odd)
    given = lax.ppermute(jnp.where(core == 0, for_odd, for_even), "section", swap)
    total = (kept.astype(f32) + given.astype(f32)).astype(bf16)
    total = lax.psum(total, "dp").astype(f32)
    ff = first_weights.shape[2]
    d_norm_kept = jnp.where(core == 0, d_norm[0], d_norm[1])
    d_norm_given = lax.ppermute(jnp.where(core == 0, d_norm[1], d_norm[0]), "section", swap)
    norm_total = lax.psum(d_norm_kept + d_norm_given, "dp")

    dskip = jnp.where(leading, jnp.zeros_like(dx), dx)
    across = jnp.where(at_head, dskip, y_ffn)
    out0 = lax.ppermute(across, "section", [(0, 2), (2, 1)])
    out1 = lax.ppermute(across, "section", [(1, 2), (3, 1)])
    own_out = jnp.where(at_head, y_ffn, dx)
    inner_out = lax.ppermute(own_out, "section", [(1, 0), (2, 3)])
    out0 = jnp.where(sec == 0, own_out, jnp.where(sec == 3, inner_out, out0))
    out1 = jnp.where(sec == 0, inner_out, jnp.where(sec == 3, own_out, out1))
    out = jnp.stack([t.reshape(rows, BLOCK, features) for t in (out0, out1)], axis=1)
    out = jnp.einsum(
        "rij,rid->rjd", roll, out.reshape(rows, SEQ, features), preferred_element_type=f32
    ).reshape(tokens, features)
    return (
        out[None], total[None, :, :ff], total[None, :, ff:], norm_total[None, 0], norm_total[None, 1]
    )


def solution(mesh):
    in_specs = (
        P("section", "dp", None),
        P("dp", None),
        P("section", None, None),
        P("section", None, None),
        P("section", None),
        P("section", None),
    )
    out_specs = (
        P("section", "dp", None),
        P("section", None, None),
        P("section", None, None),
        P("section", None),
        P("section", None),
    )
    return jax.shard_map(
        per_device, mesh=mesh, in_specs=in_specs, out_specs=out_specs, check_vma=False
    )
```

```python
import functools

import jax
import jax.numpy as jnp
from jax import lax
from jax.experimental import pallas as pl
from jax.experimental.pallas import tpu as pltpu
from jax.sharding import PartitionSpec as P

HEAD_DIM = 64
PAIR = 2 * HEAD_DIM
BLOCK = 256
SEQ = 512
LEADS = 16
CHUNK = 512
f32 = jnp.float32
bf16 = jnp.bfloat16
epsilon = 1e-12
NN = (((1,), (0,)), ((), ()))
NT = (((1,), (1,)), ((), ()))
TN = (((0,), (0,)), ((), ()))
LOG2E = 1.4426950408889634


def mm(a, b, dims=NN):
    return lax.dot_general(a, b, dims, preferred_element_type=f32)


def gelu_and_slope(u):
    x = jnp.abs(u)
    bell = jnp.exp2(u * u * (-0.5 * LOG2E))
    t = 1.0 / (1.0 + (0.3275911 * 0.5**0.5) * x)
    poly = t * (0.127414796 + t * (-0.142248368 + t * (0.7107068705 + t * (-0.7265760135 + t * 0.5307027145))))
    tail = poly * bell
    cdf = jnp.where(u < 0, tail, 1.0 - tail)
    return u * cdf, cdf + u * bell * 0.3989422804014327


def normalize(z):
    centered = z - jnp.mean(z, axis=-1, keepdims=True)
    rstd = lax.rsqrt(jnp.mean(centered * centered, axis=-1, keepdims=True) + epsilon)
    return centered * rstd, rstd


def lane_masks(rows):
    lane = lax.broadcasted_iota(jnp.int32, (rows, PAIR), 1)
    return lane < HEAD_DIM


def forward_kernel(
    x, seg_rows, seg_cols, norms, pick, first_h, second_h,
    y_h, lead, qkv_h, p_h, ctx_h, zh0_h, rstd0, mid_h, a_h, slope_h, zh1_h, rstd1,
    wa, wu, wd, qkv, p, ctx, zh0, mid, a, slope, zh1, y, acc, sems, out_sems,
):
    tokens, features = x.shape
    ff = wu.shape[1]
    blocks = tokens // BLOCK
    pairs = features // PAIR
    half = ff // 2
    n3 = 3 * features
    loads = [
        pltpu.make_async_copy(first_h.at[0], wa, sems.at[0]),
        pltpu.make_async_copy(first_h.at[1], wu, sems.at[1]),
        pltpu.make_async_copy(second_h.at[0], wd.at[:, pl.ds(0, half)], sems.at[2]),
        pltpu.make_async_copy(second_h.at[1], wd.at[:, pl.ds(half, half)], sems.at[3]),
    ]
    for c in loads:
        c.start()
    stores = []

    def keep(src, dst):
        c = pltpu.make_async_copy(src, dst, out_sems.at[len(stores)])
        c.start()
        stores.append(c)

    loads[0].wait()
    for c in range(n3 // features):
        cols = pl.ds(c * features, features)
        qkv[:, cols] = mm(x[...], wa[:, cols]).astype(bf16)
    keep(qkv, qkv_h)
    first = lane_masks(BLOCK)
    zero = jnp.zeros((BLOCK, PAIR), bf16)

    def block_step(b, carry):
        rows = pl.ds(pl.multiple_of(b * BLOCK, BLOCK), BLOCK)
        bias = jnp.where(seg_rows[rows, :] == seg_cols[b], 0.0, -1e30)
        for h in range(pairs):
            q = qkv[rows, pl.ds(h * PAIR, PAIR)]
            k = qkv[rows, pl.ds(features + h * PAIR, PAIR)]
            v = qkv[rows, pl.ds(2 * features + h * PAIR, PAIR)]
            total = None
            for side in range(2):
                own = first if side == 0 else ~first
                s = mm(q, jnp.where(own, k, zero), NT) * (HEAD_DIM**-0.5) + bias
                e = jnp.exp(s - jnp.max(s, axis=-1, keepdims=True))
                pr = (e * (1.0 / jnp.sum(e, axis=-1, keepdims=True))).astype(bf16)
                p[b, h, :, pl.ds(side * BLOCK, BLOCK)] = pr
                part = mm(pr, jnp.where(own, v, zero))
                total = part if total is None else total + part
            ctx[rows, pl.ds(h * PAIR, PAIR)] = total.astype(bf16)
        return carry

    lax.fori_loop(0, blocks, block_step, 0)
    keep(p, p_h)
    keep(ctx, ctx_h)
    z = x[...].astype(f32) + mm(ctx[...], wa[:, pl.ds(n3, features)])
    zn, r = normalize(z)
    rstd0[...] = r
    zh0[...] = zn.astype(bf16)
    mid[...] = (zn * norms[0:1, :] + norms[1:2, :]).astype(bf16)
    keep(zh0, zh0_h)
    keep(mid, mid_h)
    for c in loads[1:]:
        c.wait()
    acc[...] = mid[...].astype(f32)

    for c in range(ff // CHUNK):
        cols = pl.ds(c * CHUNK, CHUNK)
        u = mm(mid[...], wu[:, cols])
        act, sl = gelu_and_slope(u)
        act = act.astype(bf16)
        a[:, cols] = act
        slope[:, cols] = sl.astype(bf16)
        acc[...] += mm(act, wd[:, cols], NT)
    keep(a, a_h)
    keep(slope, slope_h)
    zn, r = normalize(acc[...])
    rstd1[...] = r
    zh1[...] = zn.astype(bf16)
    y[...] = (zn * norms[2:3, :] + norms[3:4, :]).astype(bf16)
    keep(zh1, zh1_h)
    keep(y, y_h)
    lead[...] = mm(pick[...], y[...]).astype(bf16)
    for c in stores:
        c.wait()


def forward(x, seg_rows, seg_cols, norms, pick, firsts, seconds):
    tokens, features = x.shape
    ff = firsts.shape[2]
    blocks, pairs = tokens // BLOCK, features // PAIR
    S = jax.ShapeDtypeStruct
    any_ = pl.BlockSpec(memory_space=pl.ANY)
    vm = pl.BlockSpec(memory_space=pltpu.VMEM)
    shapes = dict(
        y=S((tokens, features), bf16), lead=S((pick.shape[0], features), bf16),
        qkv=S((tokens, 3 * features), bf16), p=S((blocks, pairs, BLOCK, 2 * BLOCK), bf16),
        ctx=S((tokens, features), bf16), zh0=S((tokens, features), bf16), rstd0=S((tokens, 1), f32),
        mid=S((tokens, features), bf16), a=S((tokens, ff), bf16), slope=S((tokens, ff), bf16),
        zh1=S((tokens, features), bf16), rstd1=S((tokens, 1), f32),
    )
    V = lambda k: pltpu.VMEM(shapes[k].shape, shapes[k].dtype)
    outs = pl.pallas_call(
        forward_kernel,
        out_shape=list(shapes.values()),
        in_specs=[vm] * 5 + [any_] * 2,
        out_specs=[vm if k in ("lead", "rstd0", "rstd1") else any_ for k in shapes],
        scratch_shapes=[
            pltpu.VMEM(firsts.shape[1:], bf16), pltpu.VMEM(firsts.shape[1:], bf16), pltpu.VMEM((features, ff), bf16),
            V("qkv"), V("p"), V("ctx"), V("zh0"), V("mid"), V("a"), V("slope"), V("zh1"), V("y"),
            pltpu.VMEM((tokens, features), f32),
            pltpu.SemaphoreType.DMA((4,)), pltpu.SemaphoreType.DMA((9,)),
        ],
        compiler_params=pltpu.CompilerParams(vmem_limit_bytes=60 << 20),
        name="layer_forward",
    )(x, seg_rows, seg_cols, norms, pick, firsts, seconds)
    return dict(zip(shapes, outs))


def normalize_back(zh, rstd, gain, dy):
    g = dy * gain
    mean_g = jnp.mean(g, axis=-1, keepdims=True)
    mean_gz = jnp.mean(g * zh, axis=-1, keepdims=True)
    dz = rstd * (g - mean_g - zh * mean_gz)
    return dz, jnp.sum(dy * zh, axis=0, keepdims=True), jnp.sum(dy, axis=0, keepdims=True)


def backward_kernel(
    dy, norms, pick, rstd0, rstd1, first_h, second_h,
    qkv_h, p_h, zh0_h, slope_h, zh1_h, a_h,
    dx_h, lead, df_h, rights, dnorm,
    wa, wu, wd, qkv, p, zh0, slope, zh1, dx, df, du, do, dqkv, dctx, acc, sems, out_sems,
):
    tokens, features = dy.shape
    ff = wu.shape[1]
    blocks = tokens // BLOCK
    pairs = features // PAIR
    half = ff // 2
    n3 = 3 * features
    C = pltpu.make_async_copy
    ld = [
        C(zh1_h, zh1, sems.at[0]),
        C(second_h.at[0], wd.at[:, pl.ds(0, half)], sems.at[1]),
        C(first_h.at[1], wu, sems.at[2]),
        C(slope_h, slope, sems.at[3]),
        C(second_h.at[1], wd.at[:, pl.ds(half, half)], sems.at[4]),
        C(zh0_h, zh0, sems.at[5]),
        C(first_h.at[0], wa, sems.at[6]),
        C(qkv_h, qkv, sems.at[7]),
        C(p_h, p, sems.at[8]),
    ]
    for c in ld:
        c.start()
    stores = []

    def keep(src, dst):
        c = C(src, dst, out_sems.at[len(stores)])
        c.start()
        stores.append(c)

    keep(a_h.at[:, pl.ds(0, half)], rights.at[0, :, pl.ds(ff, half)])
    keep(a_h.at[:, pl.ds(half, half)], rights.at[1, :, pl.ds(ff, half)])
    ld[0].wait()
    dz, dg, ds_ = normalize_back(zh1[...].astype(f32), rstd1[...], norms[2:3, :], dy[...].astype(f32))
    dnorm[2:3, :] = dg
    dnorm[3:4, :] = ds_
    df[...] = dz.astype(bf16)
    acc[...] = dz
    keep(df, df_h)
    for i in (1, 2, 3):
        ld[i].wait()
    for c in range(ff // CHUNK):
        if c == ff // CHUNK // 2:
            ld[4].wait()
        cols = pl.ds(c * CHUNK, CHUNK)
        da = mm(df[...], wd[:, cols])
        g = (da * slope[:, cols].astype(f32)).astype(bf16)
        du[:, cols] = g
        acc[...] += mm(g, wu[:, cols], NT)
    keep(du, rights.at[1, :, pl.ds(0, ff)])
    ld[5].wait()
    d_mid = acc[...].astype(bf16).astype(f32)
    dz, dg, ds_ = normalize_back(zh0[...].astype(f32), rstd0[...], norms[0:1, :], d_mid)
    dnorm[0:1, :] = dg
    dnorm[1:2, :] = ds_
    do[...] = dz.astype(bf16)
    acc[...] = dz
    keep(do, rights.at[0, :, pl.ds(n3, features)])
    ld[6].wait()
    dctx[...] = mm(do[...], wa[:, pl.ds(n3, features)], NT).astype(bf16)
    ld[7].wait()
    ld[8].wait()
    first = lane_masks(BLOCK)
    zero = jnp.zeros((BLOCK, PAIR), bf16)
    scale = HEAD_DIM**-0.5

    def block_step(b, carry):
        rows = pl.ds(pl.multiple_of(b * BLOCK, BLOCK), BLOCK)
        for h in range(pairs):
            q = qkv[rows, pl.ds(h * PAIR, PAIR)]
            k = qkv[rows, pl.ds(features + h * PAIR, PAIR)]
            v = qkv[rows, pl.ds(2 * features + h * PAIR, PAIR)]
            dc = dctx[rows, pl.ds(h * PAIR, PAIR)]
            dq = dk = dv = None
            for side in range(2):
                own = first if side == 0 else ~first
                pr = p[b, h, :, pl.ds(side * BLOCK, BLOCK)]
                prf = pr.astype(f32)
                dp = mm(dc, jnp.where(own, v, zero), NT)
                r = jnp.sum(dp * prf, axis=-1, keepdims=True)
                ds = (prf * (dp - r)).astype(bf16)
                parts = (
                    mm(ds, jnp.where(own, k, zero)),
                    mm(ds, jnp.where(own, q, zero), TN),
                    mm(pr, jnp.where(own, dc, zero), TN),
                )
                if dq is None:
                    dq, dk, dv = parts
                else:
                    dq, dk, dv = dq + parts[0], dk + parts[1], dv + parts[2]
            dqkv[rows, pl.ds(h * PAIR, PAIR)] = (dq * scale).astype(bf16)
            dqkv[rows, pl.ds(features + h * PAIR, PAIR)] = (dk * scale).astype(bf16)
            dqkv[rows, pl.ds(2 * features + h * PAIR, PAIR)] = dv.astype(bf16)
        return carry

    lax.fori_loop(0, blocks, block_step, 0)
    keep(dqkv, rights.at[0, :, pl.ds(0, n3)])
    for c in range(3):
        cols = pl.ds(c * features, features)
        acc[...] += mm(dqkv[:, cols], wa[:, cols], NT)
    dx[...] = acc[...].astype(bf16)
    keep(dx, dx_h)
    hi = acc[...].astype(bf16)
    lo = (acc[...] - hi.astype(f32)).astype(bf16)
    lead[...] = mm(pick[...], hi) + mm(pick[...], lo)
    for c in stores:
        c.wait()


def backward(dy, norms, pick, sv, firsts, seconds):
    tokens, features = dy.shape
    ff = firsts.shape[2]
    blocks, pairs = tokens // BLOCK, features // PAIR
    S = jax.ShapeDtypeStruct
    any_ = pl.BlockSpec(memory_space=pl.ANY)
    vm = pl.BlockSpec(memory_space=pltpu.VMEM)
    shapes = dict(
        dx=S((tokens, features), bf16), lead=S((pick.shape[0], features), f32),
        df=S((tokens, features), bf16), rights=S((2, tokens, ff + ff // 2), bf16), dnorm=S((4, features), f32),
    )
    V = lambda k: pltpu.VMEM(shapes[k].shape, shapes[k].dtype)
    L = lambda k: pltpu.VMEM(sv[k].shape, sv[k].dtype)
    outs = pl.pallas_call(
        backward_kernel,
        out_shape=list(shapes.values()),
        in_specs=[vm] * 5 + [any_] * 8,
        out_specs=[vm if k in ("lead", "dnorm") else any_ for k in shapes],
        scratch_shapes=[
            pltpu.VMEM(firsts.shape[1:], bf16), pltpu.VMEM(firsts.shape[1:], bf16), pltpu.VMEM((features, ff), bf16),
            L("qkv"), L("p"), L("zh0"), L("slope"), L("zh1"),
            V("dx"), V("df"), pltpu.VMEM((tokens, ff), bf16), pltpu.VMEM((tokens, features), bf16),
            pltpu.VMEM((tokens, 3 * features), bf16), pltpu.VMEM((tokens, features), bf16),
            pltpu.VMEM((tokens, features), f32),
            pltpu.SemaphoreType.DMA((9,)), pltpu.SemaphoreType.DMA((7,)),
        ],
        compiler_params=pltpu.CompilerParams(vmem_limit_bytes=60 << 20),
        name="layer_backward",
    )(dy, norms, pick, sv["rstd0"], sv["rstd1"], firsts, seconds, sv["qkv"], sv["p"], sv["zh0"], sv["slope"], sv["zh1"], sv["a"])
    return dict(zip(shapes, outs))


PANEL = 128
RING = 4
MESH = pl.DeviceIdType.MESH


def reduce_kernel(
    chain, x_h, ctx_h, df_h, mid_h, rights, dnorm, out_h, norm_out,
    left, left_t, own_ring, sib_ring, sib_send, sib_recv, part, y1, c1, zin1, mid1, zin2, mid2, d2, y2, final,
    left_sem, own_sem, ring_sem, out_sem, sib_ss, sib_rs, y1_ss, y1_rs, z1_ss, z1_rs, m1_ss, m1_rs,
    z2_ss, z2_rs, m2_ss, m2_rs, y2_ss, y2_rs, f_ss, f_rs,
):
    sec = lax.axis_index("section")
    dp = lax.axis_index("dp")
    core = sec % 2
    panels, rows, _ = final.shape
    half = rows // 2
    features = rows
    spot = dp // 2
    side = spot // (chain // 2)
    depth = chain // 2 - 1
    dist = side * (spot - chain // 2) + (1 - side) * (chain // 2 - 1 - spot)
    inner = dist == 0
    y = dp % 2
    sibling = {"section": sec + 1 - 2 * core}
    across_y = {"dp": dp + 1 - 2 * y}
    inward = {"dp": dp + 2 - 4 * side}
    outward = {"dp": dp - 2 + 4 * side}
    has_out = dist < depth

    barrier = pltpu.get_barrier_semaphore()
    for target in (sibling, across_y, inward):
        pl.semaphore_signal(barrier, inc=1, device_id=target, device_id_type=MESH)

    @pl.when(has_out)
    def _():
        pl.semaphore_signal(barrier, inc=1, device_id=outward, device_id_type=MESH)

    def rows_at(which):
        return pl.ds(pl.multiple_of(which * half, half), half)

    mine, theirs = rows_at(y), rows_at(1 - y)
    kept, rest = rows_at(side), rows_at(1 - side)

    def remote(src, dst, ss, rs, target):
        return pltpu.make_async_remote_copy(
            src_ref=src, dst_ref=dst, send_sem=ss, recv_sem=rs, device_id=target, device_id_type=MESH
        )

    def to_sibling(j):
        return remote(sib_send.at[j % RING], sib_recv.at[j], sib_ss.at[j % RING], sib_rs.at[j], sibling)

    def one_y(j):
        i = j // 2
        return remote(part.at[j, theirs], y1.at[i], y1_ss.at[i], y1_rs.at[i], across_y)

    def one_in(j):
        i = j // 2
        return remote(c1.at[i], zin1.at[i], z1_ss.at[i], z1_rs.at[i], inward)

    def one_mid(j):
        i = j // 2
        return remote(c1.at[i], mid1.at[i], m1_ss.at[i], m1_rs.at[i], inward)

    def one_out(j):
        return remote(final.at[j, mine], final.at[j, mine], f_ss.at[0, j], f_rs.at[0, j], outward)

    def one_back(j):
        return remote(final.at[j, mine], final.at[j, mine], f_ss.at[1, j], f_rs.at[1, j], across_y)

    def one_back_in(j):
        return remote(final.at[j, theirs], final.at[j, theirs], f_ss.at[1, j], f_rs.at[1, j], across_y)

    def two_in(j):
        i = j // 2
        return remote(part.at[j], zin2.at[i], z2_ss.at[i], z2_rs.at[i], inward)

    def two_mid(j):
        i = j // 2
        return remote(part.at[j, rest], mid2.at[i], m2_ss.at[i], m2_rs.at[i], inward)

    def two_y(j):
        i = j // 2
        return remote(d2.at[i], y2.at[i], y2_ss.at[i], y2_rs.at[i], across_y)

    def two_swap(j):
        return remote(final.at[j, kept], final.at[j, kept], f_ss.at[2, j], f_rs.at[1, j], inward)

    def two_swap_in(j):
        return remote(final.at[j, rest], final.at[j, rest], f_ss.at[2, j], f_rs.at[1, j], inward)

    def two_out_kept(j):
        return remote(final.at[j, kept], final.at[j, kept], f_ss.at[0, j], f_rs.at[0, j], outward)

    def two_out_rest(j):
        return remote(final.at[j, rest], final.at[j, rest], f_ss.at[1, j], f_rs.at[1, j], outward)

    def left_of(who, j):
        p = j - 1
        even = p // (3 * features // PANEL) + p // (4 * features // PANEL)
        odd = 3 - p // (4 * features // PANEL)
        return who * odd + (1 - who) * even

    def fetch(who, j, ring, sem):
        cols = pl.ds(pl.multiple_of((j - 1) * PANEL, PANEL), PANEL)
        return pltpu.make_async_copy(rights.at[who, :, cols], ring.at[j % RING], sem.at[j % RING])

    def to_out(j):
        cols = pl.ds(pl.multiple_of((j - 1) * PANEL, PANEL), PANEL)
        return pltpu.make_async_copy(final.at[j], out_h.at[:, cols], out_sem.at[j])

    lefts = [pltpu.make_async_copy(h, left.at[i], left_sem.at[i]) for i, h in enumerate((x_h, ctx_h, df_h, mid_h))]
    for i in (0, 3, 1, 2):
        lefts[i].start()
    for j in range(1, RING):
        fetch(core, j, own_ring, own_sem).start()
        fetch(1 - core, j, sib_ring, ring_sem).start()

    def turn(i):
        grid = (rows, rows)
        eye = lax.broadcasted_iota(jnp.int32, grid, 0) == lax.broadcasted_iota(jnp.int32, grid, 1)
        left_t[i] = mm(eye.astype(bf16), left[i], NT).astype(bf16)

    def norm_panel(other):
        chosen = jnp.where(core == other, dnorm[2:4, :], dnorm[0:2, :])
        strips = [
            chosen[r : r + 1, c * PANEL : (c + 1) * PANEL]
            for r in range(2)
            for c in range(features // PANEL)
        ]
        return jnp.concatenate(strips + [jnp.zeros((16 - len(strips), PANEL), f32)], axis=0)

    pl.semaphore_wait(barrier, 3 + has_out.astype(jnp.int32))

    def when(cond, step, *args):
        @pl.when(cond)
        def _():
            step(*args)

    def stage_send(j):
        when(j >= RING, lambda: to_sibling(j - RING).wait_send())

        @pl.when(j == 0)
        def _():
            sib_send[0] = jnp.zeros((rows, PANEL), bf16)
            sib_send[0, 0:16, :] = norm_panel(0).astype(bf16)

        @pl.when(j > 0)
        def _():
            fetch(1 - core, j, sib_ring, ring_sem).wait()
            sib_send[j % RING] = mm(left_t[left_of(1 - core, j)], sib_ring[j % RING]).astype(bf16)

        to_sibling(j).start()
        nxt = j + RING
        when(
            (j >= 0) & (nxt < panels),
            lambda: fetch(1 - core, nxt, sib_ring, ring_sem).start(),
        )

    def stage_part(j):
        to_sibling(j).wait_recv()

        @pl.when(j == 0)
        def _():
            part[0] = jnp.zeros((rows, PANEL), bf16)
            part[0, 0:16, :] = (norm_panel(1) + sib_recv[0, 0:16, :].astype(f32)).astype(bf16)

        @pl.when(j > 0)
        def _():
            fetch(core, j, own_ring, own_sem).wait()
            own = mm(left_t[left_of(core, j)], own_ring[j % RING])
            part[j] = (own + sib_recv[j].astype(f32)).astype(bf16)

        nxt = j + RING
        when((nxt < panels), lambda: fetch(core, nxt, own_ring, own_sem).start())
        when(j % 2 == 0, lambda: one_y(j).start())
        when((j % 2 == 1) & (dist == depth) & (depth > 0), lambda: two_in(j).start())
        when((j % 2 == 1) & (dist == depth) & (depth == 0), lambda: two_mid(j).start())

    def one_halves(j):
        one_y(j).wait_recv()
        c1[j // 2] = (part[j, mine, :].astype(f32) + y1[j // 2].astype(f32)).astype(bf16)
        when((dist == depth) & (dist > 0), lambda: one_in(j).start())
        when((dist == depth) & inner, lambda: one_mid(j).start())

    def one_chain(j):
        one_in(j).wait_recv()
        c1[j // 2] = (c1[j // 2].astype(f32) + zin1[j // 2].astype(f32)).astype(bf16)
        when(dist > 0, lambda: one_in(j).start())
        when(inner, lambda: one_mid(j).start())

    def one_total(j):
        one_mid(j).wait_recv()
        final[j, mine, :] = (c1[j // 2].astype(f32) + mid1[j // 2].astype(f32)).astype(bf16)
        when(has_out, lambda: one_out(j).start())
        one_back(j).start()

    def one_spread(j):
        one_out(j).wait_recv()
        when(has_out, lambda: one_out(j).start())
        one_back(j).start()

    def two_chain(j):
        two_in(j).wait_recv()
        part[j] = (part[j].astype(f32) + zin2[j // 2].astype(f32)).astype(bf16)
        when(dist > 0, lambda: two_in(j).start())
        when(inner, lambda: two_mid(j).start())

    def two_halves(j):
        two_mid(j).wait_recv()
        d2[j // 2] = (part[j, kept, :].astype(f32) + mid2[j // 2].astype(f32)).astype(bf16)
        two_y(j).start()

    def two_total(j):
        two_y(j).wait_recv()
        final[j, kept, :] = (d2[j // 2].astype(f32) + y2[j // 2].astype(f32)).astype(bf16)
        two_swap(j).start()
        when(has_out, lambda: two_out_kept(j).start())

    def two_swapped(j):
        two_swap_in(j).wait_recv()
        when(has_out, lambda: two_out_rest(j).start())

    def two_spread_kept(j):
        two_out_kept(j).wait_recv()
        when(has_out, lambda: two_out_kept(j).start())

    def two_spread_rest(j):
        two_out_rest(j).wait_recv()
        when(has_out, lambda: two_out_rest(j).start())

    def finish(j):
        when(j % 2 == 0, lambda: one_back_in(j).wait_recv())

        @pl.when(j == 0)
        def _():
            norm_out[...] = final[0, 0:16, :].astype(f32)

        when(j > 0, lambda: to_out(j).start())

    last_lag = 4 + 2 * depth

    def step(t, carry):
        def at(lag, kind, cond, run):
            j = t - lag
            ok = (j >= 0) & (j < panels)
            if kind is not None:
                ok = ok & (j % 2 == kind)
            if cond is not None:
                ok = ok & cond
            when(ok, run, j)

        at(4 + depth + dist, 1, dist > 0, two_spread_rest)
        at(3 + depth + dist, 1, dist > 0, two_spread_kept)
        at(3 + depth + dist, 0, dist > 0, one_spread)
        at(4 + depth, 1, inner, two_swapped)
        at(3 + depth, 1, inner, two_total)
        at(3 + depth, 0, inner, one_total)
        at(2 + depth, 1, inner, two_halves)
        at(2 + depth - dist, 0, dist < depth, one_chain)
        at(1 + depth - dist, 1, dist < depth, two_chain)
        at(2, 0, None, one_halves)
        at(1, None, None, stage_part)
        at(0, None, None, stage_send)
        at(last_lag, None, None, finish)
        when(t == 0, lambda: [lefts[0].wait(), turn(0), lefts[3].wait(), turn(3)])
        when(t == 4, lambda: [lefts[1].wait(), turn(1), lefts[2].wait(), turn(2)])
        return carry

    lax.fori_loop(0, panels + last_lag, step, 0)

    def drain(j, carry):
        when(j >= panels - RING, lambda: to_sibling(j).wait_send())
        when(j > 0, lambda: to_out(j).wait())

        @pl.when(j % 2 == 0)
        def _():
            one_y(j).wait_send()
            when(dist > 0, lambda: one_in(j).wait_send())
            when(inner, lambda: one_mid(j).wait_send())
            when(has_out, lambda: one_out(j).wait_send())
            one_back(j).wait_send()

        @pl.when(j % 2 == 1)
        def _():
            when(dist > 0, lambda: two_in(j).wait_send())

            @pl.when(inner)
            def _():
                two_mid(j).wait_send()
                two_y(j).wait_send()
                two_swap(j).wait_send()

            @pl.when(has_out)
            def _():
                two_out_kept(j).wait_send()
                two_out_rest(j).wait_send()

        return carry

    lax.fori_loop(0, panels, drain, 0)


def reduce_gradients(lefts, rights, dnorm, chain):
    rows = lefts[0].shape[0]
    features = lefts[0].shape[1]
    panels = rights.shape[2] // PANEL + 1
    evens, odds = (panels + 1) // 2, panels // 2
    any_ = pl.BlockSpec(memory_space=pl.ANY)
    vm = pl.BlockSpec(memory_space=pltpu.VMEM)
    V = lambda *s: pltpu.VMEM(s, bf16)
    D = lambda *s: pltpu.SemaphoreType.DMA(s)
    h = features // 2
    return pl.pallas_call(
        functools.partial(reduce_kernel, chain),
        out_shape=[
            jax.ShapeDtypeStruct((features, rights.shape[2]), bf16),
            jax.ShapeDtypeStruct((16, PANEL), f32),
        ],
        in_specs=[any_] * 5 + [vm],
        out_specs=[any_, vm],
        scratch_shapes=[
            V(4, rows, features), V(4, features, rows), V(RING, rows, PANEL), V(RING, rows, PANEL),
            V(RING, features, PANEL), V(panels, features, PANEL), V(panels, features, PANEL),
            V(evens, h, PANEL), V(evens, h, PANEL), V(evens, h, PANEL), V(evens, h, PANEL),
            V(odds, features, PANEL), V(odds, h, PANEL), V(odds, h, PANEL), V(odds, h, PANEL),
            V(panels, features, PANEL),
            D(4), D(RING), D(RING), D(panels), D(RING), D(panels), D(evens), D(evens), D(evens), D(evens), D(evens), D(evens),
            D(odds), D(odds), D(odds), D(odds), D(odds), D(odds), D(3, panels), D(2, panels),
        ],
        compiler_params=pltpu.CompilerParams(
            vmem_limit_bytes=60 << 20, collective_id=1, has_side_effects=True
        ),
        name="reduce_gradients",
    )(*lefts, rights, dnorm)


def row_tables(lengths, core):
    rows, spans = lengths.shape
    order = jnp.arange(spans)
    ends = jnp.sum(jnp.where(order[:, None] <= order[None, :], lengths[:, :, None], 0), axis=1)
    starts = ends - lengths
    first = jnp.sum(jnp.where(lengths == BLOCK, starts, 0), axis=1)
    place = jnp.arange(SEQ)
    origin = (place[None, :] + first[:, None]) % SEQ
    roll = (origin[:, :, None] == place[None, None, :]).astype(bf16)
    mine = lax.dynamic_slice_in_dim(origin, core * BLOCK, BLOCK, 1)
    segment = jnp.sum((mine[:, :, None] >= ends[:, None, :]).astype(jnp.int32), axis=2)
    lead = (starts[:, : spans - 1] - first[:, None]) % SEQ
    spot = jnp.where(lead // BLOCK == core, jnp.arange(rows)[:, None] * BLOCK + lead % BLOCK, -1)
    spot = jnp.concatenate([spot.reshape(-1), jnp.full((LEADS,), -1)])[:LEADS]
    pick = spot[:, None] == jnp.arange(rows * BLOCK)[None, :]
    return roll, segment, pick.astype(bf16)


def per_device(section_rows, span_lengths, first_weights, second_weights, norm_gain, norm_shift):
    sec = lax.axis_index("section")
    core = sec % 2
    at_head = sec // 2 == 1
    own_rows = section_rows[0]
    tokens, features = own_rows.shape
    rows = tokens // SEQ
    half_tokens = rows * BLOCK
    pairs = [[0, 1], [2, 3]]
    roll, segment, pick = row_tables(span_lengths, core)

    rolled = jnp.einsum(
        "rij,rjd->rid", roll, own_rows.reshape(rows, SEQ, features), preferred_element_type=f32
    ).astype(bf16)
    rolled = rolled.reshape(rows, 2, BLOCK, features)
    half0 = rolled[:, 0].reshape(half_tokens, features)
    half1 = rolled[:, 1].reshape(half_tokens, features)
    inner = lax.ppermute(jnp.where(at_head, half0, half1), "section", [(0, 1), (3, 2)])
    aux0 = lax.ppermute(half0, "section", [(1, 2), (2, 0)])
    aux1 = lax.ppermute(half1, "section", [(1, 3), (2, 1)])
    main = jnp.where(sec == 0, half0, jnp.where(sec == 3, half1, inner))
    aux = jnp.where(core == 0, aux0, aux1)

    def both(block):
        return lax.all_gather(block, "section", axis_index_groups=pairs)

    first2 = both(first_weights[0])
    second2 = both(second_weights[0])
    norm2 = both(jnp.concatenate([norm_gain, norm_shift], axis=0))
    norms = norm2.reshape(4, features)
    seg_rows = segment.reshape(half_tokens, 1)
    seg_cols = segment.reshape(rows, 1, BLOCK)

    def from_leads(values):
        return lax.dot_general(
            pick.astype(values.dtype), values, TN, precision=lax.Precision.HIGHEST,
            preferred_element_type=f32,
        )

    leading = jnp.sum(pick.astype(f32), axis=0)[:, None] > 0
    lead_rows = forward(main, seg_rows, seg_cols, norms, pick, first2, second2)["lead"]
    lead_rows = lax.ppermute(lead_rows, "section", [(0, 2), (1, 3)])
    head_in = jnp.where(leading, from_leads(lead_rows).astype(bf16), aux)
    inputs = jnp.where(at_head, head_in, main)
    saved = forward(inputs, seg_rows, seg_cols, norms, pick, first2, second2)
    lead_grads = backward(main, norms, pick, saved, first2, second2)["lead"]
    lead_grads = lax.ppermute(lead_grads, "section", [(2, 0), (3, 1)])
    d_twelve = (from_leads(lead_grads) + aux.astype(f32)).astype(bf16)
    upstream = jnp.where(at_head, main, d_twelve)
    grads = backward(upstream, norms, pick, saved, first2, second2)
    dx, y_ffn = grads["dx"], saved["y"]
    lefts = (inputs, saved["ctx"], grads["df"], saved["mid"])
    total, norm_total = reduce_gradients(lefts, grads["rights"], grads["dnorm"], lax.axis_size("dp") // 2)
    ff = first_weights.shape[2]
    norm_total = norm_total.reshape(-1)[: 2 * features].reshape(2, features)

    dskip = jnp.where(leading, jnp.zeros_like(dx), dx)
    across = jnp.where(at_head, dskip, y_ffn)
    out0 = lax.ppermute(across, "section", [(0, 2), (2, 1)])
    out1 = lax.ppermute(across, "section", [(1, 2), (3, 1)])
    own_out = jnp.where(at_head, y_ffn, dx)
    inner_out = lax.ppermute(own_out, "section", [(1, 0), (2, 3)])
    out0 = jnp.where(sec == 0, own_out, jnp.where(sec == 3, inner_out, out0))
    out1 = jnp.where(sec == 0, inner_out, jnp.where(sec == 3, own_out, out1))
    out = jnp.stack([t.reshape(rows, BLOCK, features) for t in (out0, out1)], axis=1)
    out = jnp.einsum(
        "rij,rid->rjd", roll, out.reshape(rows, SEQ, features), preferred_element_type=f32
    ).reshape(tokens, features)
    return (
        out[None], total[None, :, :ff].astype(f32), total[None, :, ff:].astype(f32), norm_total[None, 0], norm_total[None, 1]
    )


def solution(mesh):
    in_specs = (
        P("section", "dp", None),
        P("dp", None),
        P("section", None, None),
        P("section", None, None),
        P("section", None),
        P("section", None),
    )
    out_specs = (
        P("section", "dp", None),
        P("section", None, None),
        P("section", None, None),
        P("section", None),
        P("section", None),
    )
    return jax.shard_map(
        per_device, mesh=mesh, in_specs=in_specs, out_specs=out_specs, check_vma=False
    )
```

```python
import functools

import jax
import jax.numpy as jnp
from jax import lax
from jax.experimental import pallas as pl
from jax.experimental.pallas import tpu as pltpu
from jax.sharding import PartitionSpec as P

HEAD_DIM = 64
PAIR = 2 * HEAD_DIM
BLOCK = 256
SEQ = 512
LEADS = 16
CHUNK = 512
f32 = jnp.float32
bf16 = jnp.bfloat16
epsilon = 1e-12
NN = (((1,), (0,)), ((), ()))
NT = (((1,), (1,)), ((), ()))
TN = (((0,), (0,)), ((), ()))
LOG2E = 1.4426950408889634


def mm(a, b, dims=NN):
    return lax.dot_general(a, b, dims, preferred_element_type=f32)


def gelu_and_slope(u):
    x = jnp.abs(u)
    bell = jnp.exp2(u * u * (-0.5 * LOG2E))
    t = 1.0 / (1.0 + (0.3275911 * 0.5**0.5) * x)
    poly = t * (0.127414796 + t * (-0.142248368 + t * (0.7107068705 + t * (-0.7265760135 + t * 0.5307027145))))
    tail = poly * bell
    cdf = jnp.where(u < 0, tail, 1.0 - tail)
    return u * cdf, cdf + u * bell * 0.3989422804014327


def normalize(z):
    centered = z - jnp.mean(z, axis=-1, keepdims=True)
    rstd = lax.rsqrt(jnp.mean(centered * centered, axis=-1, keepdims=True) + epsilon)
    return centered * rstd, rstd


def lane_masks(rows):
    lane = lax.broadcasted_iota(jnp.int32, (rows, PAIR), 1)
    return lane < HEAD_DIM


def forward_kernel(
    x, seg_rows, seg_cols, norms, pick, first_h, second_h,
    y_h, lead, qkv_h, p_h, ctx_h, zh0_h, rstd0, mid_h, a_h, slope_h, zh1_h, rstd1,
    wa, wu, wd, qkv, p, ctx, zh0, mid, a, slope, zh1, y, acc, sems, out_sems,
):
    tokens, features = x.shape
    ff = wu.shape[1]
    blocks = tokens // BLOCK
    pairs = features // PAIR
    half = ff // 2
    n3 = 3 * features
    loads = [
        pltpu.make_async_copy(first_h.at[0], wa, sems.at[0]),
        pltpu.make_async_copy(first_h.at[1], wu, sems.at[1]),
        pltpu.make_async_copy(second_h.at[0], wd.at[:, pl.ds(0, half)], sems.at[2]),
        pltpu.make_async_copy(second_h.at[1], wd.at[:, pl.ds(half, half)], sems.at[3]),
    ]
    for c in loads:
        c.start()
    stores = []

    def keep(src, dst):
        c = pltpu.make_async_copy(src, dst, out_sems.at[len(stores)])
        c.start()
        stores.append(c)

    loads[0].wait()
    for c in range(n3 // features):
        cols = pl.ds(c * features, features)
        qkv[:, cols] = mm(x[...], wa[:, cols]).astype(bf16)
    keep(qkv, qkv_h)
    first = lane_masks(BLOCK)
    zero = jnp.zeros((BLOCK, PAIR), bf16)

    def block_step(b, carry):
        rows = pl.ds(pl.multiple_of(b * BLOCK, BLOCK), BLOCK)
        bias = jnp.where(seg_rows[rows, :] == seg_cols[b], 0.0, -1e30)
        for h in range(pairs):
            q = qkv[rows, pl.ds(h * PAIR, PAIR)]
            k = qkv[rows, pl.ds(features + h * PAIR, PAIR)]
            v = qkv[rows, pl.ds(2 * features + h * PAIR, PAIR)]
            total = None
            for side in range(2):
                own = first if side == 0 else ~first
                s = mm(q, jnp.where(own, k, zero), NT) * (HEAD_DIM**-0.5) + bias
                e = jnp.exp(s - jnp.max(s, axis=-1, keepdims=True))
                pr = (e * (1.0 / jnp.sum(e, axis=-1, keepdims=True))).astype(bf16)
                p[b, h, :, pl.ds(side * BLOCK, BLOCK)] = pr
                part = mm(pr, jnp.where(own, v, zero))
                total = part if total is None else total + part
            ctx[rows, pl.ds(h * PAIR, PAIR)] = total.astype(bf16)
        return carry

    lax.fori_loop(0, blocks, block_step, 0)
    keep(p, p_h)
    keep(ctx, ctx_h)
    z = x[...].astype(f32) + mm(ctx[...], wa[:, pl.ds(n3, features)])
    zn, r = normalize(z)
    rstd0[...] = r
    zh0[...] = zn.astype(bf16)
    mid[...] = (zn * norms[0:1, :] + norms[1:2, :]).astype(bf16)
    keep(zh0, zh0_h)
    keep(mid, mid_h)
    for c in loads[1:]:
        c.wait()
    acc[...] = mid[...].astype(f32)

    for c in range(ff // CHUNK):
        cols = pl.ds(c * CHUNK, CHUNK)
        u = mm(mid[...], wu[:, cols])
        act, sl = gelu_and_slope(u)
        act = act.astype(bf16)
        a[:, cols] = act
        slope[:, cols] = sl.astype(bf16)
        acc[...] += mm(act, wd[:, cols], NT)
    keep(a, a_h)
    keep(slope, slope_h)
    zn, r = normalize(acc[...])
    rstd1[...] = r
    zh1[...] = zn.astype(bf16)
    y[...] = (zn * norms[2:3, :] + norms[3:4, :]).astype(bf16)
    keep(zh1, zh1_h)
    keep(y, y_h)
    lead[...] = mm(pick[...], y[...]).astype(bf16)
    for c in stores:
        c.wait()


def forward(x, seg_rows, seg_cols, norms, pick, firsts, seconds):
    tokens, features = x.shape
    ff = firsts.shape[2]
    blocks, pairs = tokens // BLOCK, features // PAIR
    S = jax.ShapeDtypeStruct
    any_ = pl.BlockSpec(memory_space=pl.ANY)
    vm = pl.BlockSpec(memory_space=pltpu.VMEM)
    shapes = dict(
        y=S((tokens, features), bf16), lead=S((pick.shape[0], features), bf16),
        qkv=S((tokens, 3 * features), bf16), p=S((blocks, pairs, BLOCK, 2 * BLOCK), bf16),
        ctx=S((tokens, features), bf16), zh0=S((tokens, features), bf16), rstd0=S((tokens, 1), f32),
        mid=S((tokens, features), bf16), a=S((tokens, ff), bf16), slope=S((tokens, ff), bf16),
        zh1=S((tokens, features), bf16), rstd1=S((tokens, 1), f32),
    )
    V = lambda k: pltpu.VMEM(shapes[k].shape, shapes[k].dtype)
    outs = pl.pallas_call(
        forward_kernel,
        out_shape=list(shapes.values()),
        in_specs=[vm] * 5 + [any_] * 2,
        out_specs=[vm if k in ("lead", "rstd0", "rstd1") else any_ for k in shapes],
        scratch_shapes=[
            pltpu.VMEM(firsts.shape[1:], bf16), pltpu.VMEM(firsts.shape[1:], bf16), pltpu.VMEM((features, ff), bf16),
            V("qkv"), V("p"), V("ctx"), V("zh0"), V("mid"), V("a"), V("slope"), V("zh1"), V("y"),
            pltpu.VMEM((tokens, features), f32),
            pltpu.SemaphoreType.DMA((4,)), pltpu.SemaphoreType.DMA((9,)),
        ],
        compiler_params=pltpu.CompilerParams(vmem_limit_bytes=60 << 20),
        name="layer_forward",
    )(x, seg_rows, seg_cols, norms, pick, firsts, seconds)
    return dict(zip(shapes, outs))


def normalize_back(zh, rstd, gain, dy):
    g = dy * gain
    mean_g = jnp.mean(g, axis=-1, keepdims=True)
    mean_gz = jnp.mean(g * zh, axis=-1, keepdims=True)
    dz = rstd * (g - mean_g - zh * mean_gz)
    return dz, jnp.sum(dy * zh, axis=0, keepdims=True), jnp.sum(dy, axis=0, keepdims=True)


def backward_kernel(
    dy, norms, pick, rstd0, rstd1, first_h, second_h,
    qkv_h, p_h, zh0_h, slope_h, zh1_h,
    dx_h, lead, df_h, rights, dnorm,
    wa, wu, wd, qkv, p, zh0, slope, zh1, dx, df, du, do, dqkv, dctx, acc, sems, out_sems,
):
    tokens, features = dy.shape
    ff = wu.shape[1]
    blocks = tokens // BLOCK
    pairs = features // PAIR
    half = ff // 2
    n3 = 3 * features
    C = pltpu.make_async_copy
    ld = [
        C(zh1_h, zh1, sems.at[0]),
        C(second_h.at[0], wd.at[:, pl.ds(0, half)], sems.at[1]),
        C(first_h.at[1], wu, sems.at[2]),
        C(slope_h, slope, sems.at[3]),
        C(second_h.at[1], wd.at[:, pl.ds(half, half)], sems.at[4]),
        C(zh0_h, zh0, sems.at[5]),
        C(first_h.at[0], wa, sems.at[6]),
        C(qkv_h, qkv, sems.at[7]),
        C(p_h, p, sems.at[8]),
    ]
    for c in ld:
        c.start()
    stores = []

    def keep(src, dst):
        c = C(src, dst, out_sems.at[len(stores)])
        c.start()
        stores.append(c)

    ld[0].wait()
    dz, dg, ds_ = normalize_back(zh1[...].astype(f32), rstd1[...], norms[2:3, :], dy[...].astype(f32))
    dnorm[2:3, :] = dg
    dnorm[3:4, :] = ds_
    df[...] = dz.astype(bf16)
    acc[...] = dz
    keep(df, df_h)
    for i in (1, 2, 3):
        ld[i].wait()
    for c in range(ff // CHUNK):
        if c == ff // CHUNK // 2:
            ld[4].wait()
        cols = pl.ds(c * CHUNK, CHUNK)
        da = mm(df[...], wd[:, cols])
        g = (da * slope[:, cols].astype(f32)).astype(bf16)
        du[:, cols] = g
        acc[...] += mm(g, wu[:, cols], NT)
    keep(du, rights.at[1, :, pl.ds(0, ff)])
    ld[5].wait()
    d_mid = acc[...].astype(bf16).astype(f32)
    dz, dg, ds_ = normalize_back(zh0[...].astype(f32), rstd0[...], norms[0:1, :], d_mid)
    dnorm[0:1, :] = dg
    dnorm[1:2, :] = ds_
    do[...] = dz.astype(bf16)
    acc[...] = dz
    keep(do, rights.at[0, :, pl.ds(n3, features)])
    ld[6].wait()
    dctx[...] = mm(do[...], wa[:, pl.ds(n3, features)], NT).astype(bf16)
    ld[7].wait()
    ld[8].wait()
    first = lane_masks(BLOCK)
    zero = jnp.zeros((BLOCK, PAIR), bf16)
    scale = HEAD_DIM**-0.5

    def block_step(b, carry):
        rows = pl.ds(pl.multiple_of(b * BLOCK, BLOCK), BLOCK)
        for h in range(pairs):
            q = qkv[rows, pl.ds(h * PAIR, PAIR)]
            k = qkv[rows, pl.ds(features + h * PAIR, PAIR)]
            v = qkv[rows, pl.ds(2 * features + h * PAIR, PAIR)]
            dc = dctx[rows, pl.ds(h * PAIR, PAIR)]
            dq = dk = dv = None
            for side in range(2):
                own = first if side == 0 else ~first
                pr = p[b, h, :, pl.ds(side * BLOCK, BLOCK)]
                prf = pr.astype(f32)
                dp = mm(dc, jnp.where(own, v, zero), NT)
                r = jnp.sum(dp * prf, axis=-1, keepdims=True)
                ds = (prf * (dp - r)).astype(bf16)
                parts = (
                    mm(ds, jnp.where(own, k, zero)),
                    mm(ds, jnp.where(own, q, zero), TN),
                    mm(pr, jnp.where(own, dc, zero), TN),
                )
                if dq is None:
                    dq, dk, dv = parts
                else:
                    dq, dk, dv = dq + parts[0], dk + parts[1], dv + parts[2]
            dqkv[rows, pl.ds(h * PAIR, PAIR)] = (dq * scale).astype(bf16)
            dqkv[rows, pl.ds(features + h * PAIR, PAIR)] = (dk * scale).astype(bf16)
            dqkv[rows, pl.ds(2 * features + h * PAIR, PAIR)] = dv.astype(bf16)
        return carry

    lax.fori_loop(0, blocks, block_step, 0)
    keep(dqkv, rights.at[0, :, pl.ds(0, n3)])
    for c in range(3):
        cols = pl.ds(c * features, features)
        acc[...] += mm(dqkv[:, cols], wa[:, cols], NT)
    dx[...] = acc[...].astype(bf16)
    keep(dx, dx_h)
    hi = acc[...].astype(bf16)
    lo = (acc[...] - hi.astype(f32)).astype(bf16)
    lead[...] = mm(pick[...], hi) + mm(pick[...], lo)
    for c in stores:
        c.wait()


def backward(dy, norms, pick, sv, firsts, seconds):
    tokens, features = dy.shape
    ff = firsts.shape[2]
    blocks, pairs = tokens // BLOCK, features // PAIR
    S = jax.ShapeDtypeStruct
    any_ = pl.BlockSpec(memory_space=pl.ANY)
    vm = pl.BlockSpec(memory_space=pltpu.VMEM)
    shapes = dict(
        dx=S((tokens, features), bf16), lead=S((pick.shape[0], features), f32),
        df=S((tokens, features), bf16), rights=S((2, tokens, ff), bf16), dnorm=S((4, features), f32),
    )
    V = lambda k: pltpu.VMEM(shapes[k].shape, shapes[k].dtype)
    L = lambda k: pltpu.VMEM(sv[k].shape, sv[k].dtype)
    outs = pl.pallas_call(
        backward_kernel,
        out_shape=list(shapes.values()),
        in_specs=[vm] * 5 + [any_] * 7,
        out_specs=[vm if k in ("lead", "dnorm") else any_ for k in shapes],
        scratch_shapes=[
            pltpu.VMEM(firsts.shape[1:], bf16), pltpu.VMEM(firsts.shape[1:], bf16), pltpu.VMEM((features, ff), bf16),
            L("qkv"), L("p"), L("zh0"), L("slope"), L("zh1"),
            V("dx"), V("df"), pltpu.VMEM((tokens, ff), bf16), pltpu.VMEM((tokens, features), bf16),
            pltpu.VMEM((tokens, 3 * features), bf16), pltpu.VMEM((tokens, features), bf16),
            pltpu.VMEM((tokens, features), f32),
            pltpu.SemaphoreType.DMA((9,)), pltpu.SemaphoreType.DMA((5,)),
        ],
        compiler_params=pltpu.CompilerParams(vmem_limit_bytes=60 << 20),
        name="layer_backward",
    )(dy, norms, pick, sv["rstd0"], sv["rstd1"], firsts, seconds, sv["qkv"], sv["p"], sv["zh0"], sv["slope"], sv["zh1"])
    return dict(zip(shapes, outs))


PANEL = 128
SPLIT = 1
RING = 4
MESH = pl.DeviceIdType.MESH


def reduce_kernel(
    chain, x_h, ctx_h, df_h, mid_h, rights, a_h, dnorm, out_h, norm_out,
    left, left_t, own_ring, sib_ring, sib_send, sib_recv, part, y1, c1, zin1, mid1, zin2, mid2, d2, y2, final,
    left_sem, own_sem, ring_sem, out_sem, sib_ss, sib_rs, y1_ss, y1_rs, z1_ss, z1_rs, m1_ss, m1_rs,
    z2_ss, z2_rs, m2_ss, m2_rs, y2_ss, y2_rs, f_ss, f_rs,
):
    sec = lax.axis_index("section")
    dp = lax.axis_index("dp")
    core = sec % 2
    panels, rows, _ = final.shape
    half = rows // 2
    features = rows * SPLIT
    spot = dp // 2
    side = spot // (chain // 2)
    depth = chain // 2 - 1
    dist = side * (spot - chain // 2) + (1 - side) * (chain // 2 - 1 - spot)
    inner = dist == 0
    y = dp % 2
    sibling = {"section": sec + 1 - 2 * core}
    across_y = {"dp": dp + 1 - 2 * y}
    inward = {"dp": dp + 2 - 4 * side}
    outward = {"dp": dp - 2 + 4 * side}
    has_out = dist < depth

    barrier = pltpu.get_barrier_semaphore()
    for target in (sibling, across_y, inward):
        pl.semaphore_signal(barrier, inc=1, device_id=target, device_id_type=MESH)

    @pl.when(has_out)
    def _():
        pl.semaphore_signal(barrier, inc=1, device_id=outward, device_id_type=MESH)

    def when(cond, step, *args):
        @pl.when(cond)
        def _():
            step(*args)

    def rows_at(which):
        return pl.ds(pl.multiple_of(which * half, half), half)

    mine, theirs = rows_at(y), rows_at(1 - y)
    kept, rest = rows_at(side), rows_at(1 - side)

    def remote(src, dst, ss, rs, target):
        return pltpu.make_async_remote_copy(
            src_ref=src, dst_ref=dst, send_sem=ss, recv_sem=rs, device_id=target, device_id_type=MESH
        )

    def to_sibling(j):
        return remote(sib_send.at[j % RING], sib_recv.at[j], sib_ss.at[j % RING], sib_rs.at[j], sibling)

    def one_y(j):
        i = j // 2
        return remote(part.at[j, theirs], y1.at[i], y1_ss.at[i], y1_rs.at[i], across_y)

    def one_in(j):
        i = j // 2
        return remote(c1.at[i], zin1.at[i], z1_ss.at[i], z1_rs.at[i], inward)

    def one_mid(j):
        i = j // 2
        return remote(c1.at[i], mid1.at[i], m1_ss.at[i], m1_rs.at[i], inward)

    def one_out(j):
        return remote(final.at[j, mine], final.at[j, mine], f_ss.at[0, j], f_rs.at[0, j], outward)

    def one_back(j):
        return remote(final.at[j, mine], final.at[j, mine], f_ss.at[1, j], f_rs.at[1, j], across_y)

    def one_back_in(j):
        return remote(final.at[j, theirs], final.at[j, theirs], f_ss.at[1, j], f_rs.at[1, j], across_y)

    def two_in(j):
        i = j // 2
        return remote(part.at[j], zin2.at[i], z2_ss.at[i], z2_rs.at[i], inward)

    def two_mid(j):
        i = j // 2
        return remote(part.at[j, rest], mid2.at[i], m2_ss.at[i], m2_rs.at[i], inward)

    def two_y(j):
        i = j // 2
        return remote(d2.at[i], y2.at[i], y2_ss.at[i], y2_rs.at[i], across_y)

    def two_swap(j):
        return remote(final.at[j, kept], final.at[j, kept], f_ss.at[2, j], f_rs.at[1, j], inward)

    def two_swap_in(j):
        return remote(final.at[j, rest], final.at[j, rest], f_ss.at[2, j], f_rs.at[1, j], inward)

    def two_out_kept(j):
        return remote(final.at[j, kept], final.at[j, kept], f_ss.at[0, j], f_rs.at[0, j], outward)

    def two_out_rest(j):
        return remote(final.at[j, rest], final.at[j, rest], f_ss.at[1, j], f_rs.at[1, j], outward)

    def left_of(who, j):
        p = (j - 1) // SPLIT
        even = p // (3 * features // PANEL) + p // (4 * features // PANEL)
        odd = 3 - p // (4 * features // PANEL)
        return who * odd + (1 - who) * even

    wide = rights.shape[2] // PANEL

    def strip(j):
        return pl.ds(pl.multiple_of((j - 1) % SPLIT * rows, rows), rows)

    class Fetch:
        def __init__(self, who, j, ring, sem):
            self.who, self.p, self.slot, self.sem = who, (j - 1) // SPLIT, ring.at[j % RING], sem.at[j % RING]

        def upper(self):
            cols = pl.ds(pl.multiple_of(self.p * PANEL, PANEL), PANEL)
            return pltpu.make_async_copy(rights.at[self.who, :, cols], self.slot, self.sem)

        def lower(self):
            col = self.p - wide + self.who * (wide // 2)
            cols = pl.ds(pl.multiple_of(col * PANEL, PANEL), PANEL)
            return pltpu.make_async_copy(a_h.at[:, cols], self.slot, self.sem)

        def start(self):
            when(self.p < wide, lambda: self.upper().start())
            when(self.p >= wide, lambda: self.lower().start())

        def wait(self):
            when(self.p < wide, lambda: self.upper().wait())
            when(self.p >= wide, lambda: self.lower().wait())

    fetch = Fetch

    def to_out(j):
        cols = pl.ds(pl.multiple_of((j - 1) // SPLIT * PANEL, PANEL), PANEL)
        return pltpu.make_async_copy(final.at[j], out_h.at[strip(j), cols], out_sem.at[j])

    lefts = [pltpu.make_async_copy(h, left.at[i], left_sem.at[i]) for i, h in enumerate((x_h, ctx_h, df_h, mid_h))]
    for i in (0, 3, 1, 2):
        lefts[i].start()
    for j in range(1, RING):
        fetch(core, j, own_ring, own_sem).upper().start()
        fetch(1 - core, j, sib_ring, ring_sem).upper().start()

    def turn(i):
        grid = (features, features)
        eye = lax.broadcasted_iota(jnp.int32, grid, 0) == lax.broadcasted_iota(jnp.int32, grid, 1)
        left_t[i] = mm(eye.astype(bf16), left[i], NT).astype(bf16)

    def norm_panel(other):
        chosen = jnp.where(core == other, dnorm[2:4, :], dnorm[0:2, :])
        strips = [
            chosen[r : r + 1, c * PANEL : (c + 1) * PANEL]
            for r in range(2)
            for c in range(features // PANEL)
        ]
        return jnp.concatenate(strips + [jnp.zeros((16 - len(strips), PANEL), f32)], axis=0)

    pl.semaphore_wait(barrier, 3 + has_out.astype(jnp.int32))

    def stage_send(j):
        when(j >= RING, lambda: to_sibling(j - RING).wait_send())

        @pl.when(j == 0)
        def _():
            sib_send[0] = jnp.zeros((rows, PANEL), bf16)
            sib_send[0, 0:16, :] = norm_panel(0).astype(bf16)

        @pl.when(j > 0)
        def _():
            fetch(1 - core, j, sib_ring, ring_sem).wait()
            sib_send[j % RING] = mm(left_t[left_of(1 - core, j), strip(j), :], sib_ring[j % RING]).astype(bf16)

        to_sibling(j).start()
        nxt = j + RING
        when(
            (j >= 0) & (nxt < panels),
            lambda: fetch(1 - core, nxt, sib_ring, ring_sem).start(),
        )

    def stage_part(j):
        to_sibling(j).wait_recv()

        @pl.when(j == 0)
        def _():
            part[0] = jnp.zeros((rows, PANEL), bf16)
            part[0, 0:16, :] = (norm_panel(1) + sib_recv[0, 0:16, :].astype(f32)).astype(bf16)

        @pl.when(j > 0)
        def _():
            fetch(core, j, own_ring, own_sem).wait()
            own = mm(left_t[left_of(core, j), strip(j), :], own_ring[j % RING])
            part[j] = (own + sib_recv[j].astype(f32)).astype(bf16)

        nxt = j + RING
        when((nxt < panels), lambda: fetch(core, nxt, own_ring, own_sem).start())
        when(j % 2 == 0, lambda: one_y(j).start())
        when((j % 2 == 1) & (dist == depth) & (depth > 0), lambda: two_in(j).start())
        when((j % 2 == 1) & (dist == depth) & (depth == 0), lambda: two_mid(j).start())

    def one_halves(j):
        one_y(j).wait_recv()
        c1[j // 2] = (part[j, mine, :].astype(f32) + y1[j // 2].astype(f32)).astype(bf16)
        when((dist == depth) & (dist > 0), lambda: one_in(j).start())
        when((dist == depth) & inner, lambda: one_mid(j).start())

    def one_chain(j):
        one_in(j).wait_recv()
        c1[j // 2] = (c1[j // 2].astype(f32) + zin1[j // 2].astype(f32)).astype(bf16)
        when(dist > 0, lambda: one_in(j).start())
        when(inner, lambda: one_mid(j).start())

    def one_total(j):
        one_mid(j).wait_recv()
        final[j, mine, :] = (c1[j // 2].astype(f32) + mid1[j // 2].astype(f32)).astype(bf16)
        when(has_out, lambda: one_out(j).start())
        one_back(j).start()

    def one_spread(j):
        one_out(j).wait_recv()
        when(has_out, lambda: one_out(j).start())
        one_back(j).start()

    def two_chain(j):
        two_in(j).wait_recv()
        part[j] = (part[j].astype(f32) + zin2[j // 2].astype(f32)).astype(bf16)
        when(dist > 0, lambda: two_in(j).start())
        when(inner, lambda: two_mid(j).start())

    def two_halves(j):
        two_mid(j).wait_recv()
        d2[j // 2] = (part[j, kept, :].astype(f32) + mid2[j // 2].astype(f32)).astype(bf16)
        two_y(j).start()

    def two_total(j):
        two_y(j).wait_recv()
        final[j, kept, :] = (d2[j // 2].astype(f32) + y2[j // 2].astype(f32)).astype(bf16)
        two_swap(j).start()
        when(has_out, lambda: two_out_kept(j).start())

    def two_swapped(j):
        two_swap_in(j).wait_recv()
        when(has_out, lambda: two_out_rest(j).start())

    def two_spread_kept(j):
        two_out_kept(j).wait_recv()
        when(has_out, lambda: two_out_kept(j).start())

    def two_spread_rest(j):
        two_out_rest(j).wait_recv()
        when(has_out, lambda: two_out_rest(j).start())

    def finish(j):
        when(j % 2 == 0, lambda: one_back_in(j).wait_recv())

        @pl.when(j == 0)
        def _():
            norm_out[...] = final[0, 0:16, :].astype(f32)

        when(j > 0, lambda: to_out(j).start())

    last_lag = 7 + 4 * depth

    def step(t, carry):
        def at(lag, kind, cond, run):
            j = t - lag
            ok = (j >= 0) & (j < panels)
            if kind is not None:
                ok = ok & (j % 2 == kind)
            if cond is not None:
                ok = ok & cond
            when(ok, run, j)

        at(last_lag, 1, dist > 0, two_spread_rest) if depth == 0 else at(7 + 2 * (depth + dist), 1, dist > 0, two_spread_rest)
        at(5 + 2 * (depth + dist), 1, dist > 0, two_spread_kept)
        at(5 + 2 * (depth + dist), 0, dist > 0, one_spread)
        at(7 + 2 * depth, 1, inner, two_swapped)
        at(5 + 2 * depth, 1, inner, two_total)
        at(5 + 2 * depth, 0, inner, one_total)
        at(3 + 2 * depth, 1, inner, two_halves)
        at(3 + 2 * (depth - dist), 0, dist < depth, one_chain)
        at(1 + 2 * (depth - dist), 1, dist < depth, two_chain)
        at(3, 0, None, one_halves)
        at(1, None, None, stage_part)
        at(0, None, None, stage_send)
        at(last_lag, None, None, finish)
        when(t == 0, lambda: [lefts[0].wait(), turn(0), lefts[3].wait(), turn(3)])
        when(t == 4 * SPLIT, lambda: [lefts[1].wait(), turn(1), lefts[2].wait(), turn(2)])
        return carry

    lax.fori_loop(0, panels + last_lag, step, 0)

    def drain(j, carry):
        when(j >= panels - RING, lambda: to_sibling(j).wait_send())
        when(j > 0, lambda: to_out(j).wait())

        @pl.when(j % 2 == 0)
        def _():
            one_y(j).wait_send()
            when(dist > 0, lambda: one_in(j).wait_send())
            when(inner, lambda: one_mid(j).wait_send())
            when(has_out, lambda: one_out(j).wait_send())
            one_back(j).wait_send()

        @pl.when(j % 2 == 1)
        def _():
            when(dist > 0, lambda: two_in(j).wait_send())

            @pl.when(inner)
            def _():
                two_mid(j).wait_send()
                two_y(j).wait_send()
                two_swap(j).wait_send()

            @pl.when(has_out)
            def _():
                two_out_kept(j).wait_send()
                two_out_rest(j).wait_send()

        return carry

    lax.fori_loop(0, panels, drain, 0)


def reduce_gradients(lefts, rights, acts, dnorm, chain):
    rows = lefts[0].shape[0]
    features = lefts[0].shape[1]
    width = rights.shape[2] + acts.shape[1] // 2
    panels = SPLIT * width // PANEL + 1
    unit = features // SPLIT
    evens, odds = (panels + 1) // 2, panels // 2
    any_ = pl.BlockSpec(memory_space=pl.ANY)
    vm = pl.BlockSpec(memory_space=pltpu.VMEM)
    V = lambda *s: pltpu.VMEM(s, bf16)
    D = lambda *s: pltpu.SemaphoreType.DMA(s)
    h = unit // 2
    return pl.pallas_call(
        functools.partial(reduce_kernel, chain),
        out_shape=[
            jax.ShapeDtypeStruct((features, width), bf16),
            jax.ShapeDtypeStruct((16, PANEL), f32),
        ],
        in_specs=[any_] * 6 + [vm],
        out_specs=[any_, vm],
        scratch_shapes=[
            V(4, rows, features), V(4, features, rows), V(RING, rows, PANEL), V(RING, rows, PANEL),
            V(RING, unit, PANEL), V(panels, unit, PANEL), V(panels, unit, PANEL),
            V(evens, h, PANEL), V(evens, h, PANEL), V(evens, h, PANEL), V(evens, h, PANEL),
            V(odds, unit, PANEL), V(odds, h, PANEL), V(odds, h, PANEL), V(odds, h, PANEL),
            V(panels, unit, PANEL),
            D(4), D(RING), D(RING), D(panels), D(RING), D(panels), D(evens), D(evens), D(evens), D(evens), D(evens), D(evens),
            D(odds), D(odds), D(odds), D(odds), D(odds), D(odds), D(3, panels), D(2, panels),
        ],
        compiler_params=pltpu.CompilerParams(
            vmem_limit_bytes=60 << 20, collective_id=1, has_side_effects=True
        ),
        name="reduce_gradients",
    )(*lefts, rights, acts, dnorm)


def row_tables(lengths, core):
    rows, spans = lengths.shape
    order = jnp.arange(spans)
    ends = jnp.sum(jnp.where(order[:, None] <= order[None, :], lengths[:, :, None], 0), axis=1)
    starts = ends - lengths
    first = jnp.sum(jnp.where(lengths == BLOCK, starts, 0), axis=1)
    place = jnp.arange(SEQ)
    origin = (place[None, :] + first[:, None]) % SEQ
    roll = (origin[:, :, None] == place[None, None, :]).astype(bf16)
    mine = lax.dynamic_slice_in_dim(origin, core * BLOCK, BLOCK, 1)
    segment = jnp.sum((mine[:, :, None] >= ends[:, None, :]).astype(jnp.int32), axis=2)
    lead = (starts[:, : spans - 1] - first[:, None]) % SEQ
    spot = jnp.where(lead // BLOCK == core, jnp.arange(rows)[:, None] * BLOCK + lead % BLOCK, -1)
    spot = jnp.concatenate([spot.reshape(-1), jnp.full((LEADS,), -1)])[:LEADS]
    pick = spot[:, None] == jnp.arange(rows * BLOCK)[None, :]
    return roll, segment, pick.astype(bf16)


def per_device(section_rows, span_lengths, first_weights, second_weights, norm_gain, norm_shift):
    sec = lax.axis_index("section")
    core = sec % 2
    at_head = sec // 2 == 1
    own_rows = section_rows[0]
    tokens, features = own_rows.shape
    rows = tokens // SEQ
    half_tokens = rows * BLOCK
    pairs = [[0, 1], [2, 3]]
    roll, segment, pick = row_tables(span_lengths, core)

    rolled = jnp.einsum(
        "rij,rjd->rid", roll, own_rows.reshape(rows, SEQ, features), preferred_element_type=f32
    ).astype(bf16)
    rolled = rolled.reshape(rows, 2, BLOCK, features)
    half0 = rolled[:, 0].reshape(half_tokens, features)
    half1 = rolled[:, 1].reshape(half_tokens, features)
    inner = lax.ppermute(jnp.where(at_head, half0, half1), "section", [(0, 1), (3, 2)])
    aux0 = lax.ppermute(half0, "section", [(1, 2), (2, 0)])
    aux1 = lax.ppermute(half1, "section", [(1, 3), (2, 1)])
    main = jnp.where(sec == 0, half0, jnp.where(sec == 3, half1, inner))
    aux = jnp.where(core == 0, aux0, aux1)

    def both(block):
        return lax.all_gather(block, "section", axis_index_groups=pairs)

    first2 = both(first_weights[0])
    second2 = both(second_weights[0])
    norm2 = both(jnp.concatenate([norm_gain, norm_shift], axis=0))
    norms = norm2.reshape(4, features)
    seg_rows = segment.reshape(half_tokens, 1)
    seg_cols = segment.reshape(rows, 1, BLOCK)

    def from_leads(values):
        return lax.dot_general(
            pick.astype(values.dtype), values, TN, precision=lax.Precision.HIGHEST,
            preferred_element_type=f32,
        )

    leading = jnp.sum(pick.astype(f32), axis=0)[:, None] > 0
    lead_rows = forward(main, seg_rows, seg_cols, norms, pick, first2, second2)["lead"]
    lead_rows = lax.ppermute(lead_rows, "section", [(0, 2), (1, 3)])
    head_in = jnp.where(leading, from_leads(lead_rows).astype(bf16), aux)
    inputs = jnp.where(at_head, head_in, main)
    saved = forward(inputs, seg_rows, seg_cols, norms, pick, first2, second2)
    lead_grads = backward(main, norms, pick, saved, first2, second2)["lead"]
    lead_grads = lax.ppermute(lead_grads, "section", [(2, 0), (3, 1)])
    d_twelve = (from_leads(lead_grads) + aux.astype(f32)).astype(bf16)
    upstream = jnp.where(at_head, main, d_twelve)
    grads = backward(upstream, norms, pick, saved, first2, second2)
    dx, y_ffn = grads["dx"], saved["y"]
    lefts = (inputs, saved["ctx"], grads["df"], saved["mid"])
    total, norm_total = reduce_gradients(lefts, grads["rights"], saved["a"], grads["dnorm"], lax.axis_size("dp") // 2)
    ff = first_weights.shape[2]
    norm_total = norm_total.reshape(-1)[: 2 * features].reshape(2, features)

    dskip = jnp.where(leading, jnp.zeros_like(dx), dx)
    across = jnp.where(at_head, dskip, y_ffn)
    out0 = lax.ppermute(across, "section", [(0, 2), (2, 1)])
    out1 = lax.ppermute(across, "section", [(1, 2), (3, 1)])
    own_out = jnp.where(at_head, y_ffn, dx)
    inner_out = lax.ppermute(own_out, "section", [(1, 0), (2, 3)])
    out0 = jnp.where(sec == 0, own_out, jnp.where(sec == 3, inner_out, out0))
    out1 = jnp.where(sec == 0, inner_out, jnp.where(sec == 3, own_out, out1))
    out = jnp.stack([t.reshape(rows, BLOCK, features) for t in (out0, out1)], axis=1)
    out = jnp.einsum(
        "rij,rid->rjd", roll, out.reshape(rows, SEQ, features), preferred_element_type=f32
    ).reshape(tokens, features)
    return (
        out[None], total[None, :, :ff].astype(f32), total[None, :, ff:].astype(f32), norm_total[None, 0], norm_total[None, 1]
    )


def solution(mesh):
    in_specs = (
        P("section", "dp", None),
        P("dp", None),
        P("section", None, None),
        P("section", None, None),
        P("section", None),
        P("section", None),
    )
    out_specs = (
        P("section", "dp", None),
        P("section", None, None),
        P("section", None, None),
        P("section", None),
        P("section", None),
    )
    return jax.shard_map(
        per_device, mesh=mesh, in_specs=in_specs, out_specs=out_specs, check_vma=False
    )
```

```python
import functools

import jax
import jax.numpy as jnp
from jax import lax
from jax.experimental import pallas as pl
from jax.experimental.pallas import tpu as pltpu
from jax.sharding import PartitionSpec as P

HEAD_DIM = 64
PAIR = 2 * HEAD_DIM
BLOCK = 256
SEQ = 512
LEADS = 16
VMEM_LIMIT = 60 << 20
MESH = pl.DeviceIdType.MESH
f32 = jnp.float32
bf16 = jnp.bfloat16
epsilon = 1e-12
NN = (((1,), (0,)), ((), ()))
NT = (((1,), (1,)), ((), ()))
TN = (((0,), (0,)), ((), ()))
LOG2E = 1.4426950408889634


def mm(a, b, dims=NN):
    return lax.dot_general(a, b, dims, preferred_element_type=f32)


def when(cond, step, *args):
    @pl.when(cond)
    def _():
        step(*args)


def remote(src, dst, ss, rs, target):
    return pltpu.make_async_remote_copy(
        src_ref=src, dst_ref=dst, send_sem=ss, recv_sem=rs, device_id=target, device_id_type=MESH
    )


def gelu_and_slope(u):
    bell = jnp.exp2(u * u * (-0.5 * LOG2E))
    t = 1.0 / (1.0 + (0.3275911 * 0.5**0.5) * jnp.abs(u))
    poly = t * (0.127414796 + t * (-0.142248368 + t * (0.7107068705 + t * (-0.7265760135 + t * 0.5307027145))))
    tail = poly * bell
    cdf = jnp.where(u < 0, tail, 1.0 - tail)
    return u * cdf, cdf + u * bell * 0.3989422804014327


def normalize(z):
    centered = z - jnp.mean(z, axis=-1, keepdims=True)
    rstd = lax.rsqrt(jnp.mean(centered * centered, axis=-1, keepdims=True) + epsilon)
    return centered * rstd, rstd


def normalize_back(zh, rstd, gain, dy):
    g = dy * gain
    mean_g = jnp.mean(g, axis=-1, keepdims=True)
    mean_gz = jnp.mean(g * zh, axis=-1, keepdims=True)
    dz = rstd * (g - mean_g - zh * mean_gz)
    return dz, jnp.sum(dy * zh, axis=0, keepdims=True), jnp.sum(dy, axis=0, keepdims=True)


def span_scalars(lengths, row):
    ends, starts, first, total = [], [], 0, 0
    for j in range(lengths.shape[1]):
        size = lengths[row, j]
        starts.append(total)
        first = first + jnp.where(size == BLOCK, total, 0)
        total = total + size
        ends.append(total)
    return ends, starts, first


def places(first, core, shape, axis):
    at = lax.broadcasted_iota(jnp.int32, shape, axis) + (first + core * BLOCK)
    return jnp.where(at >= SEQ, at - SEQ, at)


def mask_bias(lengths, row, core):
    ends, _, first = span_scalars(lengths, row)

    def segment(at):
        return sum((at >= end).astype(jnp.int32) for end in ends)

    rows = segment(places(first, core, (BLOCK, BLOCK), 0))
    cols = segment(places(first, core, (BLOCK, BLOCK), 1))
    return jnp.where(rows == cols, 0.0, -1e30)


def lead_picks(lengths, core, by_rows):
    parts = []
    per_row = lengths.shape[1] - 1
    shape = (BLOCK, LEADS) if by_rows else (LEADS, BLOCK)
    for row in range(lengths.shape[0]):
        _, starts, first = span_scalars(lengths, row)
        at = places(first, core, shape, 0 if by_rows else 1)
        slot = lax.broadcasted_iota(jnp.int32, shape, 1 if by_rows else 0)
        hit = sum(
            ((slot == row * per_row + j) & (at == starts[j])).astype(jnp.int32) for j in range(per_row)
        )
        parts.append(hit.astype(f32))
    return jnp.concatenate(parts, axis=0 if by_rows else 1)


def lane_masks():
    return lax.broadcasted_iota(jnp.int32, (BLOCK, PAIR), 1) < HEAD_DIM


def forward_pass(x, lengths, core, norms, wa, wu, wd, qkv, ctx, mid, acc, ready, save):
    tokens, features = x.shape
    pairs = features // PAIR
    for c in range(3):
        ready["a"](c)
        cols = pl.ds(c * features, features)
        qkv[:, cols] = mm(x[...], wa[:, cols]).astype(bf16)
    first = lane_masks()
    zero = jnp.zeros((BLOCK, PAIR), bf16)

    def block_step(b, carry):
        rows = pl.ds(pl.multiple_of(b * BLOCK, BLOCK), BLOCK)
        bias = mask_bias(lengths, b, core)
        for h in range(pairs):
            q = qkv[rows, pl.ds(h * PAIR, PAIR)]
            k = qkv[rows, pl.ds(features + h * PAIR, PAIR)]
            v = qkv[rows, pl.ds(2 * features + h * PAIR, PAIR)]
            total = None
            for side in range(2):
                own = first if side == 0 else ~first
                s = mm(q, jnp.where(own, k, zero), NT) * (HEAD_DIM**-0.5) + bias
                e = jnp.exp(s - jnp.max(s, axis=-1, keepdims=True))
                pr = (e * (1.0 / jnp.sum(e, axis=-1, keepdims=True))).astype(bf16)
                if save:
                    save["p"][b, h, :, pl.ds(side * BLOCK, BLOCK)] = pr
                part = mm(pr, jnp.where(own, v, zero))
                total = part if total is None else total + part
            ctx[rows, pl.ds(h * PAIR, PAIR)] = total.astype(bf16)
        return carry

    lax.fori_loop(0, tokens // BLOCK, block_step, 0)
    ready["a"](3)
    zn, r = normalize(x[...].astype(f32) + mm(ctx[...], wa[:, pl.ds(3 * features, features)]))
    if save:
        save["keep"]("qkv", "p", "ctx")
        save["rstd0"][...] = r
        save["zh0"][...] = zn.astype(bf16)
    mid[...] = (zn * norms[0, 0:1, :] + norms[0, 1:2, :]).astype(bf16)
    acc[...] = mid[...].astype(f32)
    if save:
        save["keep"]("zh0", "mid")
    for c in range(wu.shape[1] // features):
        cols = pl.ds(c * features, features)
        ready["u"](c)
        act, slope = gelu_and_slope(mm(mid[...], wu[:, cols]))
        act = act.astype(bf16)
        if save:
            save["a"][:, cols] = act
            save["slope"][:, cols] = slope.astype(bf16)
            save["keep_cols"](c)
        ready["d"](c)
        acc[...] += mm(act, wd[:, cols], NT)
    zn, r = normalize(acc[...])
    if save:
        save["rstd1"][...] = r
        save["zh1"][...] = zn.astype(bf16)
    return (zn * norms[1, 0:1, :] + norms[1, 1:2, :]).astype(bf16)


def backward_pass(
    dy, norms, wa, wu, wd, qkv, p, zh0, slope, zh1, rstd0, rstd1, df, du, do, dqkv, dctx, acc, dnorm, ready, keep
):
    tokens, features = dy.shape
    pairs = features // PAIR
    ready["zh1"]()
    dz, dgain, dshift = normalize_back(zh1[...].astype(f32), rstd1[...], norms[1, 0:1, :], dy.astype(f32))
    dnorm[2:3, :] = dgain
    dnorm[3:4, :] = dshift
    df[...] = dz.astype(bf16)
    acc[...] = dz
    keep("df")
    for c in range(wu.shape[1] // features):
        cols = pl.ds(c * features, features)
        ready["d"](c)
        da = mm(df[...], wd[:, cols])
        ready["slope"](c)
        g = (da * slope[:, cols].astype(f32)).astype(bf16)
        du[:, cols] = g
        ready["u"](c)
        acc[...] += mm(g, wu[:, cols], NT)
    keep("du")
    ready["zh0"]()
    d_mid = acc[...].astype(bf16).astype(f32)
    dz, dgain, dshift = normalize_back(zh0[...].astype(f32), rstd0[...], norms[0, 0:1, :], d_mid)
    dnorm[0:1, :] = dgain
    dnorm[1:2, :] = dshift
    do[...] = dz.astype(bf16)
    acc[...] = dz
    keep("do")
    ready["a"](3)
    dctx[...] = mm(do[...], wa[:, pl.ds(3 * features, features)], NT).astype(bf16)
    ready["qkv"]()
    first = lane_masks()
    zero = jnp.zeros((BLOCK, PAIR), bf16)
    scale = HEAD_DIM**-0.5

    def block_step(b, carry):
        rows = pl.ds(pl.multiple_of(b * BLOCK, BLOCK), BLOCK)
        for h in range(pairs):
            q = qkv[rows, pl.ds(h * PAIR, PAIR)]
            k = qkv[rows, pl.ds(features + h * PAIR, PAIR)]
            v = qkv[rows, pl.ds(2 * features + h * PAIR, PAIR)]
            dc = dctx[rows, pl.ds(h * PAIR, PAIR)]
            dq = dk = dv = None
            for side in range(2):
                own = first if side == 0 else ~first
                pr = p[b, h, :, pl.ds(side * BLOCK, BLOCK)]
                prf = pr.astype(f32)
                dp = mm(dc, jnp.where(own, v, zero), NT)
                r = jnp.sum(dp * prf, axis=-1, keepdims=True)
                ds = (prf * (dp - r)).astype(bf16)
                parts = (
                    mm(ds, jnp.where(own, k, zero)),
                    mm(ds, jnp.where(own, q, zero), TN),
                    mm(pr, jnp.where(own, dc, zero), TN),
                )
                if dq is None:
                    dq, dk, dv = parts
                else:
                    dq, dk, dv = dq + parts[0], dk + parts[1], dv + parts[2]
            dqkv[rows, pl.ds(h * PAIR, PAIR)] = (dq * scale).astype(bf16)
            dqkv[rows, pl.ds(features + h * PAIR, PAIR)] = (dk * scale).astype(bf16)
            dqkv[rows, pl.ds(2 * features + h * PAIR, PAIR)] = dv.astype(bf16)
        return carry

    lax.fori_loop(0, tokens // BLOCK, block_step, 0)
    keep("dqkv")
    for c in range(3):
        cols = pl.ds(c * features, features)
        ready["a"](c)
        acc[...] += mm(dqkv[:, cols], wa[:, cols], NT)


def start_kernel(
    rows_in, lengths, first_h, second_h, norm_in,
    main_h, aux_h, other_first_h, other_second_h, norms, lead_out,
    wa, wu, wd, halves, main, aux, qkv, ctx, mid, acc, norm_pair, lead_own, lead_in,
    load, w_ss, w_rs, d_ss, d_rs, n_ss, n_rs, m_ss, m_rs, x_ss, x_rs, l_ss, l_rs, out_sem,
):
    sec = lax.axis_index("section")
    core = sec % 2
    at_head = sec // 2
    inside = (sec == 0) | (sec == 3)
    tokens, features = main.shape
    pieces = wu.shape[1] // features
    half = wd.shape[1] // 2
    even, odd = core == 0, core == 1
    sibling = {"section": sec + 1 - 2 * core}
    barrier = pltpu.get_barrier_semaphore()
    for step in range(1, 4):
        target = {"section": (sec + step) % 4}
        pl.semaphore_signal(barrier, inc=1, device_id=target, device_id_type=MESH)

    def cols(c):
        return pl.ds(c * features, features)

    def local_first(c, dst):
        return pltpu.make_async_copy(first_h.at[:, cols(c)], dst.at[:, cols(c)], load.at[c])

    def sent_first(c, dst):
        return remote(first_h.at[:, cols(c)], dst.at[:, cols(c)], w_ss.at[c], w_rs.at[c], sibling)

    def local_second(side):
        return pltpu.make_async_copy(second_h, wd.at[:, pl.ds(side * half, half)], load.at[pieces])

    def sent_second(side):
        return remote(second_h, wd.at[:, pl.ds(side * half, half)], d_ss, d_rs, sibling)

    for c in range(pieces):
        when(even, lambda: local_first(c, wa).start())
        when(odd, lambda: local_first(c, wu).start())
    when(even, lambda: local_second(0).start())
    when(odd, lambda: local_second(1).start())

    for row in range(lengths.shape[0]):
        _, _, first = span_scalars(lengths, row)
        packed = rows_in[pl.ds(row * SEQ, SEQ), :]
        for side in range(2):
            at = places(first, side, (BLOCK, SEQ), 0)
            hot = at == lax.broadcasted_iota(jnp.int32, (BLOCK, SEQ), 1)
            halves[side, pl.ds(row * BLOCK, BLOCK), :] = mm(hot.astype(f32).astype(bf16), packed).astype(bf16)
    norm_pair[core] = norm_in[...]

    sent_main = remote(halves.at[1 - core], main, m_ss, m_rs, sibling)
    sent_norm = remote(norm_pair.at[core], norm_pair.at[core], n_ss, n_rs, sibling)
    norm_from = remote(norm_pair.at[1 - core], norm_pair.at[1 - core], n_ss, n_rs, sibling)
    sent_aux = [
        remote(halves.at[side], aux, x_ss.at[side], x_rs, {"section": 4 + side - 2 * sec})
        for side in range(2)
    ]
    pl.semaphore_wait(barrier, 3)
    when(inside, lambda: sent_main.start())
    sent_norm.start()
    for c in range(pieces):
        when(even, lambda: sent_first(c, wa).start())
        when(odd, lambda: sent_first(c, wu).start())
    when(even, lambda: sent_second(0).start())
    when(odd, lambda: sent_second(1).start())
    when(~inside, lambda: [copy.start() for copy in sent_aux])

    @pl.when(inside)
    def _():
        main[...] = halves[core]

    when(~inside, lambda: sent_main.wait_recv())
    norm_from.wait_recv()
    norms[...] = norm_pair[...]

    def ready_a(c):
        when(even, lambda: local_first(c, wa).wait())
        when(odd, lambda: sent_first(c, wa).wait_recv())

    def ready_u(c):
        when(odd, lambda: local_first(c, wu).wait())
        when(even, lambda: sent_first(c, wu).wait_recv())

    def ready_d(c):
        if c == 0:
            when(even, lambda: local_second(0).wait())
            when(odd, lambda: sent_second(0).wait_recv())
        if c == pieces // 2:
            when(odd, lambda: local_second(1).wait())
            when(even, lambda: sent_second(1).wait_recv())

    ready = dict(a=ready_a, u=ready_u, d=ready_d)
    y = forward_pass(main, lengths, core, norms, wa, wu, wd, qkv, ctx, mid, acc, ready, None)
    lead_own[...] = mm(lead_picks(lengths, core, False).astype(bf16), y).astype(bf16)
    hop = remote(lead_own, lead_in, l_ss, l_rs, {"section": (sec + 2) % 4})
    when(at_head == 0, lambda: hop.start())

    def write(src, dst, i):
        return pltpu.make_async_copy(src, dst, out_sem.at[i])

    def store_pair(first_ref, side):
        write(first_ref, other_first_h, 0).start()
        write(wd.at[:, pl.ds(side * half, half)], other_second_h, 1).start()

    when(even, lambda: store_pair(wu, 1))
    when(odd, lambda: store_pair(wa, 0))
    write(main, main_h, 2).start()
    sent_aux[0].wait_recv()
    write(aux, aux_h, 3).start()

    @pl.when(at_head == 0)
    def _():
        lead_out[...] = jnp.zeros_like(lead_out)
        hop.wait_send()

    @pl.when(at_head == 1)
    def _():
        hop.wait_recv()
        lead_out[...] = lead_in[...]

    when(inside, lambda: sent_main.wait_send())
    sent_norm.wait_send()
    for c in range(pieces):
        sent_first(c, wa).wait_send()
    sent_second(0).wait_send()
    when(~inside, lambda: [copy.wait_send() for copy in sent_aux])
    write(wa, other_first_h, 0).wait()
    write(wd.at[:, pl.ds(0, half)], other_second_h, 1).wait()
    write(main, main_h, 2).wait()
    write(aux, aux_h, 3).wait()


ANY = pl.BlockSpec(memory_space=pl.ANY)
IN_VMEM = pl.BlockSpec(memory_space=pltpu.VMEM)
IN_SMEM = pl.BlockSpec(memory_space=pltpu.SMEM)
S = jax.ShapeDtypeStruct


def vm(*shape):
    return pltpu.VMEM(shape, bf16)


def dma(*shape):
    return pltpu.SemaphoreType.DMA(shape)


def params(number):
    if number is None:
        return pltpu.CompilerParams(vmem_limit_bytes=VMEM_LIMIT)
    return pltpu.CompilerParams(vmem_limit_bytes=VMEM_LIMIT, collective_id=number, has_side_effects=True)


def start(rows_in, lengths, first, second, norm_own):
    features, ff = first.shape
    tokens = rows_in.shape[0] // 2
    square = S((tokens, features), bf16)
    one = pltpu.SemaphoreType.DMA
    return pl.pallas_call(
        start_kernel,
        out_shape=[
            square, square, S(first.shape, bf16), S(second.shape, bf16), S((2, 2, features), f32),
            S((LEADS, features), bf16),
        ],
        in_specs=[IN_VMEM, IN_SMEM, ANY, ANY, IN_VMEM],
        out_specs=[ANY] * 4 + [IN_VMEM] * 2,
        scratch_shapes=[
            vm(features, ff), vm(features, ff), vm(features, ff), vm(2, tokens, features),
            vm(tokens, features), vm(tokens, features), vm(tokens, 3 * features), vm(tokens, features),
            vm(tokens, features), pltpu.VMEM((tokens, features), f32), pltpu.VMEM((2, 2, features), f32),
            vm(LEADS, features), vm(LEADS, features),
            dma(ff // features + 1), dma(ff // features), dma(ff // features), one, one, one, one, one, one,
            dma(2), one, one, one, dma(4),
        ],
        compiler_params=params(1),
        name="start_and_forward",
    )(rows_in, lengths, first, second, norm_own)


def weight_loads(core, first_h, second_h, other_first_h, other_second_h, wa, wu, wd, a_sem, u_sem, d_sem):
    features = wa.shape[0]
    half = wd.shape[1] // 2

    def cols(c):
        return pl.ds(c * features, features)

    def copy(kind, c, own):
        if kind == "a":
            return pltpu.make_async_copy((first_h if own else other_first_h).at[:, cols(c)], wa.at[:, cols(c)], a_sem.at[c])
        if kind == "u":
            return pltpu.make_async_copy((first_h if own else other_first_h).at[:, cols(c)], wu.at[:, cols(c)], u_sem.at[c])
        from_own = second_h if own else other_second_h
        in_half = c % (half // features)
        return pltpu.make_async_copy(from_own.at[:, cols(in_half)], wd.at[:, cols(c)], d_sem.at[c])

    def begin(kind, c):
        core_of = 0 if kind == "a" else 1 if kind == "u" else (c * features) // half
        when(core == core_of, lambda: copy(kind, c, True).start())
        when(core != core_of, lambda: copy(kind, c, False).start())

    def ready(kind, c):
        copy(kind, c, True).wait()

    return begin, ready


def middle_kernel(
    lengths, main, aux, lead, norms, first_h, second_h, other_first_h, other_second_h,
    x_h, y_h, qkv_h, p_h, ctx_h, zh0_h, mid_h, a_h, slope_h, zh1_h, rstd0, rstd1, lead_grads,
    wa, wu, wd, x, y, qkv, p, ctx, zh0, mid, a, slope, zh1, df, do, dctx, dqkv, acc, dnorm, lead_own, lead_in,
    a_sem, u_sem, d_sem, out_sem, col_sem, l_ss, l_rs,
):
    sec = lax.axis_index("section")
    core = sec % 2
    at_head = sec // 2
    tokens, features = main.shape
    pieces = wu.shape[1] // features
    peer = {"section": (sec + 2) % 4}
    barrier = pltpu.get_barrier_semaphore()
    pl.semaphore_signal(barrier, inc=1, device_id=peer, device_id_type=MESH)
    begin, ready_w = weight_loads(
        core, first_h, second_h, other_first_h, other_second_h, wa, wu, wd, a_sem, u_sem, d_sem
    )
    for c in range(pieces):
        begin("a", c)
    for c in range(pieces):
        begin("u", c)
        begin("d", c)
    refs = dict(
        x=(x, x_h), y=(y, y_h), qkv=(qkv, qkv_h), p=(p, p_h), ctx=(ctx, ctx_h), zh0=(zh0, zh0_h), mid=(mid, mid_h),
        zh1=(zh1, zh1_h),
    )
    order = list(refs)

    def store(name):
        return pltpu.make_async_copy(*refs[name], out_sem.at[order.index(name)])

    def store_cols(c, which):
        src, dst = ((a, a_h), (slope, slope_h))[which]
        cols = pl.ds(c * features, features)
        return pltpu.make_async_copy(src.at[:, cols], dst.at[:, cols], col_sem.at[which, c])

    def keep(*names):
        for name in names:
            store(name).start()

    picks = lead_picks(lengths, core, True)
    leading = jnp.max(picks, axis=1, keepdims=True) > 0

    @pl.when(at_head == 1)
    def _():
        x[...] = jnp.where(leading, mm(picks.astype(bf16), lead[...]).astype(bf16), aux[...])

    @pl.when(at_head == 0)
    def _():
        x[...] = main[...]

    keep("x")
    ready = dict(a=lambda c: ready_w("a", c), u=lambda c: ready_w("u", c), d=lambda c: ready_w("d", c))
    save = dict(
        p=p, a=a, slope=slope, zh0=zh0, zh1=zh1, rstd0=rstd0, rstd1=rstd1, keep=keep,
        keep_cols=lambda c: [store_cols(c, 0).start(), store_cols(c, 1).start()],
    )
    y[...] = forward_pass(x, lengths, core, norms, wa, wu, wd, qkv, ctx, mid, acc, ready, save)
    keep("zh1", "y")
    none = {k: (lambda *_: None) for k in ("a", "u", "d", "zh1", "zh0", "slope", "qkv")}
    backward_pass(
        main[...], norms, wa, wu, wd, qkv, p, zh0, slope, zh1, rstd0, rstd1, df, a, do, dqkv, dctx, acc, dnorm,
        none | dict(slope=lambda c: store_cols(c, 0).wait()), lambda name: None,
    )
    pick = lead_picks(lengths, core, False).astype(bf16)
    hi = acc[...].astype(bf16)
    lo = (acc[...] - hi.astype(f32)).astype(bf16)
    lead_own[...] = mm(pick, hi) + mm(pick, lo)
    pl.semaphore_wait(barrier, 1)
    hop = remote(lead_own, lead_in, l_ss, l_rs, peer)
    when(at_head == 1, lambda: hop.start())
    for name in order:
        store(name).wait()
    for c in range(pieces):
        store_cols(c, 1).wait()

    @pl.when(at_head == 1)
    def _():
        lead_grads[...] = jnp.zeros_like(lead_grads)
        hop.wait_send()

    @pl.when(at_head == 0)
    def _():
        hop.wait_recv()
        lead_grads[...] = lead_in[...]


def middle(lengths, main, aux, lead, norms, weights):
    tokens, features = main.shape
    ff = weights[0].shape[1]
    pieces = ff // features
    blocks, pairs = tokens // BLOCK, features // PAIR
    square = S((tokens, features), bf16)
    shapes = dict(
        x=square, y=square, qkv=S((tokens, 3 * features), bf16), p=S((blocks, pairs, BLOCK, 2 * BLOCK), bf16),
        ctx=square, zh0=square, mid=square, a=S((tokens, ff), bf16), slope=S((tokens, ff), bf16), zh1=square,
        rstd0=S((tokens, 1), f32), rstd1=S((tokens, 1), f32), lead_grads=S((LEADS, features), f32),
    )
    small = ("rstd0", "rstd1", "lead_grads")
    wide = vm(features, ff)
    outs = pl.pallas_call(
        middle_kernel,
        out_shape=list(shapes.values()),
        in_specs=[IN_SMEM] + [IN_VMEM] * 4 + [ANY] * 4,
        out_specs=[IN_VMEM if k in small else ANY for k in shapes],
        scratch_shapes=[wide, wide, wide]
        + [pltpu.VMEM(s.shape, s.dtype) for k, s in shapes.items() if k not in small]
        + [
            vm(tokens, features), vm(tokens, features), vm(tokens, features), vm(tokens, 3 * features),
            pltpu.VMEM((tokens, features), f32), pltpu.VMEM((4, features), f32),
            pltpu.VMEM((LEADS, features), f32), pltpu.VMEM((LEADS, features), f32),
            dma(pieces), dma(pieces), dma(pieces), dma(8), dma(2, pieces),
            pltpu.SemaphoreType.DMA, pltpu.SemaphoreType.DMA,
        ],
        compiler_params=params(2),
        name="forward_and_backward",
    )(lengths, main, aux, lead, norms, *weights)
    return dict(zip(shapes, outs))


def last_kernel(
    lengths, main, aux, lead_grads, norms, rstd0, rstd1, first_h, second_h, other_first_h, other_second_h,
    y_h, qkv_h, p_h, zh0_h, slope_h, zh1_h,
    own_h, across_h, df_h, rights, dnorm,
    wa, wu, wd, y, qkv, p, zh0, slope, zh1, df, du, do, dctx, dqkv, acc, own, across,
    a_sem, u_sem, d_sem, in_sem, col_sem, out_sem,
):
    sec = lax.axis_index("section")
    core = sec % 2
    at_head = sec // 2
    tokens, features = main.shape
    ff = wu.shape[1]
    pieces = ff // features
    begin, ready_w = weight_loads(
        core, first_h, second_h, other_first_h, other_second_h, wa, wu, wd, a_sem, u_sem, d_sem
    )
    loads = dict(zh1=(zh1_h, zh1), zh0=(zh0_h, zh0), qkv=(qkv_h, qkv), p=(p_h, p), y=(y_h, y))
    names = list(loads)

    def load(name):
        return pltpu.make_async_copy(*loads[name], in_sem.at[names.index(name)])

    def load_slope(c):
        cols = pl.ds(c * features, features)
        return pltpu.make_async_copy(slope_h.at[:, cols], slope.at[:, cols], col_sem.at[c])

    load("zh1").start()
    for c in range(pieces):
        begin("d", c)
        load_slope(c).start()
        begin("u", c)
    load("zh0").start()
    begin("a", pieces - 1)
    load("qkv").start()
    load("p").start()
    for c in range(pieces - 1):
        begin("a", c)
    load("y").start()
    stores = dict(
        df=(df, df_h), du=(du, rights.at[1, :, pl.ds(0, ff)]), do=(do, rights.at[0, :, pl.ds(3 * features, features)]),
        dqkv=(dqkv, rights.at[0, :, pl.ds(0, 3 * features)]), own=(own, own_h), across=(across, across_h),
    )
    order = list(stores)

    def store(name):
        return pltpu.make_async_copy(*stores[name], out_sem.at[order.index(name)])

    picks = lead_picks(lengths, core, True)
    leading = jnp.max(picks, axis=1, keepdims=True) > 0
    picks = picks.astype(bf16)

    @pl.when(at_head == 1)
    def _():
        own[...] = main[...]

    @pl.when(at_head == 0)
    def _():
        hi = lead_grads[...].astype(bf16)
        lo = (lead_grads[...] - hi.astype(f32)).astype(bf16)
        own[...] = (mm(picks, hi) + mm(picks, lo) + aux[...].astype(f32)).astype(bf16)

    ready = dict(
        a=lambda c: ready_w("a", c), u=lambda c: ready_w("u", c), d=lambda c: ready_w("d", c), slope=lambda c: load_slope(c).wait(),
        zh1=lambda: load("zh1").wait(), zh0=lambda: load("zh0").wait(), qkv=lambda: [load("qkv").wait(), load("p").wait()],
    )
    backward_pass(
        own[...], norms, wa, wu, wd, qkv, p, zh0, slope, zh1, rstd0, rstd1, df, du, do, dqkv, dctx, acc, dnorm,
        ready, lambda name: store(name).start(),
    )
    load("y").wait()
    dx = acc[...].astype(bf16)

    @pl.when(at_head == 1)
    def _():
        own[...] = y[...]
        across[...] = jnp.where(leading, jnp.zeros_like(dx), dx)

    @pl.when(at_head == 0)
    def _():
        own[...] = dx
        across[...] = y[...]

    store("own").start()
    store("across").start()
    for name in order:
        store(name).wait()


def last(lengths, main, aux, lead_grads, norms, weights, saved):
    tokens, features = main.shape
    ff = weights[0].shape[1]
    pieces = ff // features
    square = S((tokens, features), bf16)
    wide = vm(features, ff)
    held = [saved[k] for k in ("y", "qkv", "p", "zh0", "slope", "zh1")]
    return pl.pallas_call(
        last_kernel,
        out_shape=[square, square, square, S((2, tokens, ff), bf16), S((4, features), f32)],
        in_specs=[IN_SMEM] + [IN_VMEM] * 6 + [ANY] * 10,
        out_specs=[ANY] * 4 + [IN_VMEM],
        scratch_shapes=[wide, wide, wide]
        + [pltpu.VMEM(s.shape, s.dtype) for s in held]
        + [
            vm(tokens, features), vm(tokens, ff), vm(tokens, features), vm(tokens, features), vm(tokens, 3 * features),
            pltpu.VMEM((tokens, features), f32), vm(tokens, features), vm(tokens, features),
            dma(pieces), dma(pieces), dma(pieces), dma(5), dma(pieces), dma(6),
        ],
        compiler_params=params(None),
        name="last_backward",
    )(lengths, main, aux, lead_grads, norms, saved["rstd0"], saved["rstd1"], *weights, *held)


PANEL = 128
SPLIT = 1
RING = 4


def reduce_kernel(
    chain, x_h, ctx_h, df_h, mid_h, rights, a_h, own_h, across_h, dnorm, out_h, norm_out, halves_h,
    left, left_t, own_ring, sib_ring, sib_send, sib_recv, part, y1, c1, zin1, mid1, zin2, mid2, d2, y2, final, halves,
    left_sem, own_sem, ring_sem, out_sem, sib_ss, sib_rs, y1_ss, y1_rs, z1_ss, z1_rs, m1_ss, m1_rs,
    z2_ss, z2_rs, m2_ss, m2_rs, y2_ss, y2_rs, f_ss, f_rs, o_ss, o_rs, c_ss, c_rs, h_sem,
):
    sec = lax.axis_index("section")
    dp = lax.axis_index("dp")
    core = sec % 2
    panels, rows, _ = final.shape
    half = rows // 2
    features = rows * SPLIT
    spot = dp // 2
    side = spot // (chain // 2)
    depth = chain // 2 - 1
    dist = side * (spot - chain // 2) + (1 - side) * (chain // 2 - 1 - spot)
    inner = dist == 0
    y = dp % 2
    sibling = {"section": sec + 1 - 2 * core}
    across_y = {"dp": dp + 1 - 2 * y}
    inward = {"dp": dp + 2 - 4 * side}
    outward = {"dp": dp - 2 + 4 * side}
    has_out = dist < depth

    barrier = pltpu.get_barrier_semaphore()
    inside = (sec == 0) | (sec == 3)
    beyond = {"section": 2 - sec // 2}
    others = [{"section": (sec + step) % 4} for step in (1, 2, 3)]
    for target in (*others, across_y, inward):
        pl.semaphore_signal(barrier, inc=1, device_id=target, device_id_type=MESH)

    @pl.when(has_out)
    def _():
        pl.semaphore_signal(barrier, inc=1, device_id=outward, device_id_type=MESH)

    def rows_at(which):
        return pl.ds(pl.multiple_of(which * half, half), half)

    mine, theirs = rows_at(y), rows_at(1 - y)
    kept, rest = rows_at(side), rows_at(1 - side)

    def to_sibling(j):
        return remote(sib_send.at[j % RING], sib_recv.at[j], sib_ss.at[j % RING], sib_rs.at[j], sibling)

    def one_y(j):
        i = j // 2
        return remote(part.at[j, theirs], y1.at[i], y1_ss.at[i], y1_rs.at[i], across_y)

    def one_in(j):
        i = j // 2
        return remote(c1.at[i], zin1.at[i], z1_ss.at[i], z1_rs.at[i], inward)

    def one_mid(j):
        i = j // 2
        return remote(c1.at[i], mid1.at[i], m1_ss.at[i], m1_rs.at[i], inward)

    def one_out(j):
        return remote(final.at[j, mine], final.at[j, mine], f_ss.at[0, j], f_rs.at[0, j], outward)

    def one_back(j):
        return remote(final.at[j, mine], final.at[j, mine], f_ss.at[1, j], f_rs.at[1, j], across_y)

    def one_back_in(j):
        return remote(final.at[j, theirs], final.at[j, theirs], f_ss.at[1, j], f_rs.at[1, j], across_y)

    def two_in(j):
        i = j // 2
        return remote(part.at[j], zin2.at[i], z2_ss.at[i], z2_rs.at[i], inward)

    def two_mid(j):
        i = j // 2
        return remote(part.at[j, rest], mid2.at[i], m2_ss.at[i], m2_rs.at[i], inward)

    def two_y(j):
        i = j // 2
        return remote(d2.at[i], y2.at[i], y2_ss.at[i], y2_rs.at[i], across_y)

    def two_swap(j):
        return remote(final.at[j, kept], final.at[j, kept], f_ss.at[2, j], f_rs.at[1, j], inward)

    def two_swap_in(j):
        return remote(final.at[j, rest], final.at[j, rest], f_ss.at[2, j], f_rs.at[1, j], inward)

    def two_out_kept(j):
        return remote(final.at[j, kept], final.at[j, kept], f_ss.at[0, j], f_rs.at[0, j], outward)

    def two_out_rest(j):
        return remote(final.at[j, rest], final.at[j, rest], f_ss.at[1, j], f_rs.at[1, j], outward)

    def left_of(who, j):
        p = (j - 1) // SPLIT
        even = p // (3 * features // PANEL) + p // (4 * features // PANEL)
        odd = 3 - p // (4 * features // PANEL)
        return who * odd + (1 - who) * even

    wide = rights.shape[2] // PANEL

    def strip(j):
        return pl.ds(pl.multiple_of((j - 1) % SPLIT * rows, rows), rows)

    class Fetch:
        def __init__(self, who, j, ring, sem):
            self.who, self.p, self.slot, self.sem = who, (j - 1) // SPLIT, ring.at[j % RING], sem.at[j % RING]

        def upper(self):
            cols = pl.ds(pl.multiple_of(self.p * PANEL, PANEL), PANEL)
            return pltpu.make_async_copy(rights.at[self.who, :, cols], self.slot, self.sem)

        def lower(self):
            col = self.p - wide + self.who * (wide // 2)
            cols = pl.ds(pl.multiple_of(col * PANEL, PANEL), PANEL)
            return pltpu.make_async_copy(a_h.at[:, cols], self.slot, self.sem)

        def start(self):
            when(self.p < wide, lambda: self.upper().start())
            when(self.p >= wide, lambda: self.lower().start())

        def wait(self):
            when(self.p < wide, lambda: self.upper().wait())
            when(self.p >= wide, lambda: self.lower().wait())

    fetch = Fetch

    def to_out(j):
        cols = pl.ds(pl.multiple_of((j - 1) // SPLIT * PANEL, PANEL), PANEL)
        return pltpu.make_async_copy(final.at[j], out_h.at[strip(j), cols], out_sem.at[j])

    own_copy = pltpu.make_async_copy(own_h, halves.at[core], h_sem.at[0])
    own_send = remote(own_h, halves.at[core], o_ss, o_rs, sibling)
    own_from = remote(own_h, halves.at[1 - core], o_ss, o_rs, sibling)
    across_send = remote(across_h, halves.at[core], c_ss, c_rs.at[core], beyond)
    across_from = [remote(across_h, halves.at[side], c_ss, c_rs.at[side], beyond) for side in range(2)]
    lefts = [pltpu.make_async_copy(h, left.at[i], left_sem.at[i]) for i, h in enumerate((x_h, ctx_h, df_h, mid_h))]
    for i in (0, 3, 1, 2):
        lefts[i].start()
    for j in range(1, RING):
        fetch(core, j, own_ring, own_sem).upper().start()
        fetch(1 - core, j, sib_ring, ring_sem).upper().start()

    def turn(i):
        grid = (features, features)
        eye = lax.broadcasted_iota(jnp.int32, grid, 0) == lax.broadcasted_iota(jnp.int32, grid, 1)
        left_t[i] = mm(eye.astype(bf16), left[i], NT).astype(bf16)

    def norm_panel(other):
        chosen = jnp.where(core == other, dnorm[2:4, :], dnorm[0:2, :])
        strips = [
            chosen[r : r + 1, c * PANEL : (c + 1) * PANEL]
            for r in range(2)
            for c in range(features // PANEL)
        ]
        return jnp.concatenate(strips + [jnp.zeros((16 - len(strips), PANEL), f32)], axis=0)

    pl.semaphore_wait(barrier, 5 + has_out.astype(jnp.int32))
    when(inside, lambda: own_copy.start())
    when(~inside, lambda: own_send.start())
    across_send.start()

    def stage_send(j):
        when(j >= RING, lambda: to_sibling(j - RING).wait_send())

        @pl.when(j == 0)
        def _():
            sib_send[0] = jnp.zeros((rows, PANEL), bf16)
            sib_send[0, 0:16, :] = norm_panel(0).astype(bf16)

        @pl.when(j > 0)
        def _():
            fetch(1 - core, j, sib_ring, ring_sem).wait()
            sib_send[j % RING] = mm(left_t[left_of(1 - core, j), strip(j), :], sib_ring[j % RING]).astype(bf16)

        to_sibling(j).start()
        nxt = j + RING
        when(
            (j >= 0) & (nxt < panels),
            lambda: fetch(1 - core, nxt, sib_ring, ring_sem).start(),
        )

    def stage_part(j):
        to_sibling(j).wait_recv()

        @pl.when(j == 0)
        def _():
            part[0] = jnp.zeros((rows, PANEL), bf16)
            part[0, 0:16, :] = (norm_panel(1) + sib_recv[0, 0:16, :].astype(f32)).astype(bf16)

        @pl.when(j > 0)
        def _():
            fetch(core, j, own_ring, own_sem).wait()
            own = mm(left_t[left_of(core, j), strip(j), :], own_ring[j % RING])
            part[j] = (own + sib_recv[j].astype(f32)).astype(bf16)

        nxt = j + RING
        when((nxt < panels), lambda: fetch(core, nxt, own_ring, own_sem).start())
        when(j % 2 == 0, lambda: one_y(j).start())
        when((j % 2 == 1) & (dist == depth) & (depth > 0), lambda: two_in(j).start())
        when((j % 2 == 1) & (dist == depth) & (depth == 0), lambda: two_mid(j).start())

    def one_halves(j):
        one_y(j).wait_recv()
        c1[j // 2] = (part[j, mine, :].astype(f32) + y1[j // 2].astype(f32)).astype(bf16)
        when((dist == depth) & (dist > 0), lambda: one_in(j).start())
        when((dist == depth) & inner, lambda: one_mid(j).start())

    def one_chain(j):
        one_in(j).wait_recv()
        c1[j // 2] = (c1[j // 2].astype(f32) + zin1[j // 2].astype(f32)).astype(bf16)
        when(dist > 0, lambda: one_in(j).start())
        when(inner, lambda: one_mid(j).start())

    def one_total(j):
        one_mid(j).wait_recv()
        final[j, mine, :] = (c1[j // 2].astype(f32) + mid1[j // 2].astype(f32)).astype(bf16)
        when(has_out, lambda: one_out(j).start())
        one_back(j).start()

    def one_spread(j):
        one_out(j).wait_recv()
        when(has_out, lambda: one_out(j).start())
        one_back(j).start()

    def two_chain(j):
        two_in(j).wait_recv()
        part[j] = (part[j].astype(f32) + zin2[j // 2].astype(f32)).astype(bf16)
        when(dist > 0, lambda: two_in(j).start())
        when(inner, lambda: two_mid(j).start())

    def two_halves(j):
        two_mid(j).wait_recv()
        d2[j // 2] = (part[j, kept, :].astype(f32) + mid2[j // 2].astype(f32)).astype(bf16)
        two_y(j).start()

    def two_total(j):
        two_y(j).wait_recv()
        final[j, kept, :] = (d2[j // 2].astype(f32) + y2[j // 2].astype(f32)).astype(bf16)
        two_swap(j).start()
        when(has_out, lambda: two_out_kept(j).start())

    def two_swapped(j):
        two_swap_in(j).wait_recv()
        when(has_out, lambda: two_out_rest(j).start())

    def two_spread_kept(j):
        two_out_kept(j).wait_recv()
        when(has_out, lambda: two_out_kept(j).start())

    def two_spread_rest(j):
        two_out_rest(j).wait_recv()
        when(has_out, lambda: two_out_rest(j).start())

    def finish(j):
        when(j % 2 == 0, lambda: one_back_in(j).wait_recv())

        @pl.when(j == 0)
        def _():
            norm_out[...] = final[0, 0:16, :].astype(f32)

        when(j > 0, lambda: to_out(j).start())

    last_lag = 7 + 4 * depth

    def step(t, carry):
        def at(lag, kind, cond, run):
            j = t - lag
            ok = (j >= 0) & (j < panels)
            if kind is not None:
                ok = ok & (j % 2 == kind)
            if cond is not None:
                ok = ok & cond
            when(ok, run, j)

        at(last_lag, 1, dist > 0, two_spread_rest) if depth == 0 else at(7 + 2 * (depth + dist), 1, dist > 0, two_spread_rest)
        at(5 + 2 * (depth + dist), 1, dist > 0, two_spread_kept)
        at(5 + 2 * (depth + dist), 0, dist > 0, one_spread)
        at(7 + 2 * depth, 1, inner, two_swapped)
        at(5 + 2 * depth, 1, inner, two_total)
        at(5 + 2 * depth, 0, inner, one_total)
        at(3 + 2 * depth, 1, inner, two_halves)
        at(3 + 2 * (depth - dist), 0, dist < depth, one_chain)
        at(1 + 2 * (depth - dist), 1, dist < depth, two_chain)
        at(3, 0, None, one_halves)
        at(1, None, None, stage_part)
        at(0, None, None, stage_send)
        at(last_lag + 1, None, None, finish)
        when(t == 0, lambda: [lefts[0].wait(), turn(0), lefts[3].wait(), turn(3)])
        when(t == 4 * SPLIT, lambda: [lefts[1].wait(), turn(1), lefts[2].wait(), turn(2)])
        return carry

    lax.fori_loop(0, panels + last_lag + 1, step, 0)

    @pl.when(inside)
    def _():
        own_copy.wait()
        own_from.wait_recv()

    @pl.when(~inside)
    def _():
        own_send.wait_send()
        across_from[0].wait_recv()
        across_from[1].wait_recv()

    across_send.wait_send()
    rows_done = pltpu.make_async_copy(halves, halves_h, h_sem.at[1])
    rows_done.start()

    def drain(j, carry):
        when(j >= panels - RING, lambda: to_sibling(j).wait_send())
        when(j > 0, lambda: to_out(j).wait())

        @pl.when(j % 2 == 0)
        def _():
            one_y(j).wait_send()
            when(dist > 0, lambda: one_in(j).wait_send())
            when(inner, lambda: one_mid(j).wait_send())
            when(has_out, lambda: one_out(j).wait_send())
            one_back(j).wait_send()

        @pl.when(j % 2 == 1)
        def _():
            when(dist > 0, lambda: two_in(j).wait_send())

            @pl.when(inner)
            def _():
                two_mid(j).wait_send()
                two_y(j).wait_send()
                two_swap(j).wait_send()

            @pl.when(has_out)
            def _():
                two_out_kept(j).wait_send()
                two_out_rest(j).wait_send()

        return carry

    lax.fori_loop(0, panels, drain, 0)
    rows_done.wait()


def reduce_gradients(lefts, rights, acts, own, across, dnorm, chain):
    rows = lefts[0].shape[0]
    features = lefts[0].shape[1]
    width = rights.shape[2] + acts.shape[1] // 2
    panels = SPLIT * width // PANEL + 1
    unit = features // SPLIT
    evens, odds = (panels + 1) // 2, panels // 2
    any_ = ANY
    V = lambda *s: pltpu.VMEM(s, bf16)
    D = lambda *s: pltpu.SemaphoreType.DMA(s)
    h = unit // 2
    return pl.pallas_call(
        functools.partial(reduce_kernel, chain),
        out_shape=[
            jax.ShapeDtypeStruct((features, width), bf16),
            jax.ShapeDtypeStruct((16, PANEL), f32),
            jax.ShapeDtypeStruct((2, *own.shape), bf16),
        ],
        in_specs=[any_] * 8 + [IN_VMEM],
        out_specs=[any_, IN_VMEM, any_],
        scratch_shapes=[
            V(4, rows, features), V(4, features, rows), V(RING, rows, PANEL), V(RING, rows, PANEL),
            V(RING, unit, PANEL), V(panels, unit, PANEL), V(panels, unit, PANEL),
            V(evens, h, PANEL), V(evens, h, PANEL), V(evens, h, PANEL), V(evens, h, PANEL),
            V(odds, unit, PANEL), V(odds, h, PANEL), V(odds, h, PANEL), V(odds, h, PANEL),
            V(panels, unit, PANEL), V(2, *own.shape),
            D(4), D(RING), D(RING), D(panels), D(RING), D(panels), D(evens), D(evens), D(evens), D(evens), D(evens), D(evens),
            D(odds), D(odds), D(odds), D(odds), D(odds), D(odds), D(3, panels), D(2, panels),
            pltpu.SemaphoreType.DMA, pltpu.SemaphoreType.DMA, pltpu.SemaphoreType.DMA, D(2), D(2),
        ],
        compiler_params=params(3),
        name="reduce_gradients",
    )(*lefts, rights, acts, own, across, dnorm)


def finish_kernel(lengths, total, halves, norm_in, first_out, second_out, rows_out, gain_out, shift_out):
    step = pl.program_id(0)
    features = rows_out.shape[1]
    wide = first_out.shape[1]
    first_out[...] = total[:, pl.ds(0, wide)].astype(f32)
    second_out[...] = total[:, pl.ds(wide, second_out.shape[1])].astype(f32)
    row = step // 2
    _, _, first = span_scalars(lengths, row)
    at = lax.broadcasted_iota(jnp.int32, (BLOCK, BLOCK), 0) + (step % 2) * BLOCK
    out = None
    for side in range(2):
        hot = at == places(first, side, (BLOCK, BLOCK), 1)
        part = mm(hot.astype(f32).astype(bf16), halves[side])
        out = part if out is None else out + part
    rows_out[...] = out
    strips = features // PANEL
    for r, ref in enumerate((gain_out, shift_out)):
        ref[...] = jnp.concatenate([norm_in[r * strips + c : r * strips + c + 1, :] for c in range(strips)], axis=1)


def finish(lengths, total, halves, norm_in, ff):
    features, width = total.shape
    tokens = halves.shape[1]
    steps = 2 * tokens // BLOCK
    part = features // steps
    row_spec = pl.BlockSpec((1, features), lambda i: (0, 0))
    return pl.pallas_call(
        finish_kernel,
        grid=(steps,),
        out_shape=[
            S((features, ff), f32), S((features, width - ff), f32), S((2 * tokens, features), f32),
            S((1, features), f32), S((1, features), f32),
        ],
        in_specs=[
            IN_SMEM, pl.BlockSpec((part, width), lambda i: (i, 0)),
            pl.BlockSpec((2, BLOCK, features), lambda i: (0, i // 2, 0)), IN_VMEM,
        ],
        out_specs=[
            pl.BlockSpec((part, ff), lambda i: (i, 0)), pl.BlockSpec((part, width - ff), lambda i: (i, 0)),
            pl.BlockSpec((BLOCK, features), lambda i: (i, 0)), row_spec, row_spec,
        ],
        compiler_params=params(None),
        name="finish",
    )(lengths, total, halves, norm_in)


def per_device(section_rows, span_lengths, first_weights, second_weights, norm_gain, norm_shift):
    first, second = first_weights[0], second_weights[0]
    norm_own = jnp.concatenate([norm_gain, norm_shift], axis=0)
    main, aux, other_first, other_second, norms, lead = start(section_rows[0], span_lengths, first, second, norm_own)
    weights = (first, second, other_first, other_second)
    saved = middle(span_lengths, main, aux, lead, norms, weights)
    own, across, df, rights, dnorm = last(span_lengths, main, aux, saved["lead_grads"], norms, weights, saved)
    lefts = (saved["x"], saved["ctx"], df, saved["mid"])
    total, norm_total, halves = reduce_gradients(
        lefts, rights, saved["a"], own, across, dnorm, lax.axis_size("dp") // 2
    )
    d_first, d_second, rows, gain, shift = finish(span_lengths, total, halves, norm_total, first.shape[1])
    return rows[None], d_first[None], d_second[None], gain, shift


def solution(mesh):
    in_specs = (
        P("section", "dp", None),
        P("dp", None),
        P("section", None, None),
        P("section", None, None),
        P("section", None),
        P("section", None),
    )
    out_specs = (
        P("section", "dp", None),
        P("section", None, None),
        P("section", None, None),
        P("section", None),
        P("section", None),
    )
    return jax.shard_map(
        per_device, mesh=mesh, in_specs=in_specs, out_specs=out_specs, check_vma=False
    )
```

```python
import functools

import jax
import jax.numpy as jnp
from jax import lax
from jax.experimental import pallas as pl
from jax.experimental.pallas import tpu as pltpu
from jax.sharding import PartitionSpec as P

HEAD_DIM = 64
PAIR = 2 * HEAD_DIM
BLOCK = 256
SEQ = 512
LEADS = 16
VMEM_LIMIT = 60 << 20
MESH = pl.DeviceIdType.MESH
f32 = jnp.float32
bf16 = jnp.bfloat16
epsilon = 1e-12
NN = (((1,), (0,)), ((), ()))
NT = (((1,), (1,)), ((), ()))
TN = (((0,), (0,)), ((), ()))
LOG2E = 1.4426950408889634


def mm(a, b, dims=NN):
    return lax.dot_general(a, b, dims, preferred_element_type=f32)


def when(cond, step, *args):
    @pl.when(cond)
    def _():
        step(*args)


def remote(src, dst, ss, rs, target):
    return pltpu.make_async_remote_copy(
        src_ref=src, dst_ref=dst, send_sem=ss, recv_sem=rs, device_id=target, device_id_type=MESH
    )


def gelu_and_slope(u):
    bell = jnp.exp2(u * u * (-0.5 * LOG2E))
    t = 1.0 / (1.0 + (0.3275911 * 0.5**0.5) * jnp.abs(u))
    poly = t * (0.127414796 + t * (-0.142248368 + t * (0.7107068705 + t * (-0.7265760135 + t * 0.5307027145))))
    tail = poly * bell
    cdf = jnp.where(u < 0, tail, 1.0 - tail)
    return u * cdf, cdf + u * bell * 0.3989422804014327


def normalize(z):
    centered = z - jnp.mean(z, axis=-1, keepdims=True)
    rstd = lax.rsqrt(jnp.mean(centered * centered, axis=-1, keepdims=True) + epsilon)
    return centered * rstd, rstd


def normalize_back(zh, rstd, gain, dy):
    g = dy * gain
    mean_g = jnp.mean(g, axis=-1, keepdims=True)
    mean_gz = jnp.mean(g * zh, axis=-1, keepdims=True)
    dz = rstd * (g - mean_g - zh * mean_gz)
    return dz, jnp.sum(dy * zh, axis=0, keepdims=True), jnp.sum(dy, axis=0, keepdims=True)


def span_scalars(lengths, row):
    ends, starts, first, total = [], [], 0, 0
    for j in range(lengths.shape[1]):
        size = lengths[row, j]
        starts.append(total)
        first = first + jnp.where(size == BLOCK, total, 0)
        total = total + size
        ends.append(total)
    return ends, starts, first


def places(first, core, shape, axis):
    at = lax.broadcasted_iota(jnp.int32, shape, axis) + (first + core * BLOCK)
    return jnp.where(at >= SEQ, at - SEQ, at)


def mask_bias(lengths, row, core):
    ends, _, first = span_scalars(lengths, row)

    def segment(at):
        return sum((at >= end).astype(jnp.int32) for end in ends)

    rows = segment(places(first, core, (BLOCK, BLOCK), 0))
    cols = segment(places(first, core, (BLOCK, BLOCK), 1))
    return jnp.where(rows == cols, 0.0, -1e30)


def lead_picks(lengths, core, by_rows):
    parts = []
    per_row = lengths.shape[1] - 1
    shape = (BLOCK, LEADS) if by_rows else (LEADS, BLOCK)
    for row in range(lengths.shape[0]):
        _, starts, first = span_scalars(lengths, row)
        at = places(first, core, shape, 0 if by_rows else 1)
        slot = lax.broadcasted_iota(jnp.int32, shape, 1 if by_rows else 0)
        hit = sum(
            ((slot == row * per_row + j) & (at == starts[j])).astype(jnp.int32) for j in range(per_row)
        )
        parts.append(hit.astype(f32))
    return jnp.concatenate(parts, axis=0 if by_rows else 1)


def lane_masks():
    return lax.broadcasted_iota(jnp.int32, (BLOCK, PAIR), 1) < HEAD_DIM


def forward_pass(x, lengths, core, norms, wa, wu, wd, qkv, ctx, mid, acc, ready, save):
    tokens, features = x.shape
    pairs = features // PAIR
    for c in range(3):
        ready["a"](c)
        cols = pl.ds(c * features, features)
        qkv[:, cols] = mm(x[...], wa[:, cols]).astype(bf16)
    first = lane_masks()
    zero = jnp.zeros((BLOCK, PAIR), bf16)

    def block_step(b, carry):
        rows = pl.ds(pl.multiple_of(b * BLOCK, BLOCK), BLOCK)
        bias = mask_bias(lengths, b, core)
        for h in range(pairs):
            q = qkv[rows, pl.ds(h * PAIR, PAIR)]
            k = qkv[rows, pl.ds(features + h * PAIR, PAIR)]
            v = qkv[rows, pl.ds(2 * features + h * PAIR, PAIR)]
            total = None
            for side in range(2):
                own = first if side == 0 else ~first
                s = mm(q, jnp.where(own, k, zero), NT) * (HEAD_DIM**-0.5) + bias
                e = jnp.exp(s - jnp.max(s, axis=-1, keepdims=True))
                pr = (e * (1.0 / jnp.sum(e, axis=-1, keepdims=True))).astype(bf16)
                if save:
                    save["p"][b, h, :, pl.ds(side * BLOCK, BLOCK)] = pr
                part = mm(pr, jnp.where(own, v, zero))
                total = part if total is None else total + part
            ctx[rows, pl.ds(h * PAIR, PAIR)] = total.astype(bf16)
        return carry

    lax.fori_loop(0, tokens // BLOCK, block_step, 0)
    ready["a"](3)
    zn, r = normalize(x[...].astype(f32) + mm(ctx[...], wa[:, pl.ds(3 * features, features)]))
    if save:
        save["keep"]("qkv", "p", "ctx")
        save["rstd0"][...] = r
        save["zh0"][...] = zn.astype(bf16)
    mid[...] = (zn * norms[0, 0:1, :] + norms[0, 1:2, :]).astype(bf16)
    acc[...] = mid[...].astype(f32)
    if save:
        save["keep"]("zh0", "mid")
    for c in range(wu.shape[1] // features):
        cols = pl.ds(c * features, features)
        ready["u"](c)
        act, slope = gelu_and_slope(mm(mid[...], wu[:, cols]))
        act = act.astype(bf16)
        if save:
            save["a"][:, cols] = act
            save["slope"][:, cols] = slope.astype(bf16)
            save["keep_cols"](c)
        ready["d"](c)
        acc[...] += mm(act, wd[:, cols], NT)
    zn, r = normalize(acc[...])
    if save:
        save["rstd1"][...] = r
        save["zh1"][...] = zn.astype(bf16)
    return (zn * norms[1, 0:1, :] + norms[1, 1:2, :]).astype(bf16)


def feed_forward_back(dy, norms, wu, wd, slope, zh1, rstd1, df, du, acc, dnorm, ready):
    features = wu.shape[0]
    dz, dgain, dshift = normalize_back(zh1[...].astype(f32), rstd1[...], norms[1, 0:1, :], dy.astype(f32))
    dnorm[2:3, :] = dgain
    dnorm[3:4, :] = dshift
    df[...] = dz.astype(bf16)
    acc[...] = dz
    for c in range(wu.shape[1] // features):
        cols = pl.ds(c * features, features)
        ready["d"](c)
        da = mm(df[...], wd[:, cols])
        ready["du"](c)
        g = (da * slope[:, cols].astype(f32)).astype(bf16)
        du[:, cols] = g
        ready["u"](c)
        acc[...] += mm(g, wu[:, cols], NT)


def attention_back(d_mid, norms, wa, qkv, p, zh0, rstd0, do, dqkv, dctx, acc, dnorm, ready, keep, patch=None):
    tokens, features = d_mid.shape
    pairs = features // PAIR
    ready["zh0"]()
    dz, dgain, dshift = normalize_back(zh0[...].astype(f32), rstd0[...], norms[0, 0:1, :], d_mid.astype(f32))
    dnorm[0:1, :] = dgain
    dnorm[1:2, :] = dshift
    do[...] = dz.astype(bf16)
    acc[...] = dz
    keep("do")
    ready["a"](3)
    dctx[...] = mm(do[...], wa[:, pl.ds(3 * features, features)], NT).astype(bf16)
    ready["qkv"]()
    first = lane_masks()
    zero = jnp.zeros((BLOCK, PAIR), bf16)
    scale = HEAD_DIM**-0.5

    def block_step(b, carry):
        rows = pl.ds(pl.multiple_of(b * BLOCK, BLOCK), BLOCK)
        for h in range(pairs):
            q = qkv[rows, pl.ds(h * PAIR, PAIR)]
            k = qkv[rows, pl.ds(features + h * PAIR, PAIR)]
            v = qkv[rows, pl.ds(2 * features + h * PAIR, PAIR)]
            dc = dctx[rows, pl.ds(h * PAIR, PAIR)]
            dq = dk = dv = None
            for side in range(2):
                own = first if side == 0 else ~first
                pr = p[b, h, :, pl.ds(side * BLOCK, BLOCK)]
                prf = pr.astype(f32)
                dp = mm(dc, jnp.where(own, v, zero), NT)
                r = jnp.sum(dp * prf, axis=-1, keepdims=True)
                ds = (prf * (dp - r)).astype(bf16)
                parts = (
                    mm(ds, jnp.where(own, k, zero)),
                    mm(ds, jnp.where(own, q, zero), TN),
                    mm(pr, jnp.where(own, dc, zero), TN),
                )
                if dq is None:
                    dq, dk, dv = parts
                else:
                    dq, dk, dv = dq + parts[0], dk + parts[1], dv + parts[2]
            dqkv[rows, pl.ds(h * PAIR, PAIR)] = (dq * scale).astype(bf16)
            dqkv[rows, pl.ds(features + h * PAIR, PAIR)] = (dk * scale).astype(bf16)
            dqkv[rows, pl.ds(2 * features + h * PAIR, PAIR)] = dv.astype(bf16)
        return carry

    lax.fori_loop(0, tokens // BLOCK, block_step, 0)
    keep("dqkv")
    if patch:
        patch()
    for c in range(3):
        cols = pl.ds(c * features, features)
        ready["a"](c)
        acc[...] += mm(dqkv[:, cols], wa[:, cols], NT)


def lead_forward(x, lengths, core, norms, wa, wu, wd, kv, ready):
    tokens, features = x.shape
    per_row = lengths.shape[1] - 1
    own = mm(lead_picks(lengths, core, False).astype(bf16), x[...]).astype(bf16)
    for c in (1, 2):
        ready["a"](c)
        kv[:, pl.ds((c - 1) * features, features)] = mm(x[...], wa[:, pl.ds(c * features, features)]).astype(bf16)
    ready["a"](0)
    q = mm(own, wa[:, pl.ds(0, features)]).astype(bf16)
    parts = []
    for row in range(tokens // BLOCK):
        ends, _, first = span_scalars(lengths, row)
        at = places(first, core, (LEADS, BLOCK), 1)
        keys = sum((at >= end).astype(jnp.int32) for end in ends)
        span = lax.broadcasted_iota(jnp.int32, (LEADS, BLOCK), 0) - row * per_row
        parts.append(jnp.where((span == keys) & (span < per_row), 0.0, -1e30))
    bias = jnp.concatenate(parts, axis=1)
    ctx = []
    for h in range(features // PAIR):
        k = kv[:, pl.ds(h * PAIR, PAIR)]
        v = kv[:, pl.ds(features + h * PAIR, PAIR)]
        lanes = lax.broadcasted_iota(jnp.int32, (LEADS, PAIR), 1) < HEAD_DIM
        total = None
        for side in range(2):
            mine = lanes if side == 0 else ~lanes
            s = mm(jnp.where(mine, q[:, h * PAIR : (h + 1) * PAIR], jnp.zeros((), bf16)), k, NT) * (HEAD_DIM**-0.5) + bias
            e = jnp.exp(s - jnp.max(s, axis=-1, keepdims=True))
            part = mm((e * (1.0 / jnp.sum(e, axis=-1, keepdims=True))).astype(bf16), v)
            total = jnp.where(lanes, part, 0.0) if side == 0 else jnp.where(lanes, total, part)
        ctx.append(total.astype(bf16))
    ready["a"](3)
    zn, _ = normalize(own.astype(f32) + mm(jnp.concatenate(ctx, axis=1), wa[:, pl.ds(3 * features, features)]))
    mid = (zn * norms[0, 0:1, :] + norms[0, 1:2, :]).astype(bf16)
    out = mid.astype(f32)
    for c in range(wu.shape[1] // features):
        cols = pl.ds(c * features, features)
        ready["u"](c)
        act, _ = gelu_and_slope(mm(mid, wu[:, cols]))
        ready["d"](c)
        out = out + mm(act.astype(bf16), wd[:, cols], NT)
    zn, _ = normalize(out)
    return (zn * norms[1, 0:1, :] + norms[1, 1:2, :]).astype(bf16)


def start_kernel(
    rows_in, lengths, first_h, second_h, norm_in,
    main_h, aux_h, other_first_h, other_second_h, norms, lead_out,
    wa, wu, wd, halves, main, aux, kv, norm_pair, lead_own, lead_in,
    load, w_ss, w_rs, d_ss, d_rs, n_ss, n_rs, m_ss, m_rs, x_ss, x_rs, l_ss, l_rs, out_sem,
):
    sec = lax.axis_index("section")
    core = sec % 2
    at_head = sec // 2
    inside = (sec == 0) | (sec == 3)
    tokens, features = main.shape
    pieces = wu.shape[1] // features
    half = wd.shape[1] // 2
    even, odd = core == 0, core == 1
    sibling = {"section": sec + 1 - 2 * core}
    barrier = pltpu.get_barrier_semaphore()
    for step in range(1, 4):
        target = {"section": (sec + step) % 4}
        pl.semaphore_signal(barrier, inc=1, device_id=target, device_id_type=MESH)

    def cols(c):
        return pl.ds(c * features, features)

    def local_first(c, dst):
        return pltpu.make_async_copy(first_h.at[:, cols(c)], dst.at[:, cols(c)], load.at[c])

    def sent_first(c, dst):
        return remote(first_h.at[:, cols(c)], dst.at[:, cols(c)], w_ss.at[c], w_rs.at[c], sibling)

    def local_second(side):
        return pltpu.make_async_copy(second_h, wd.at[:, pl.ds(side * half, half)], load.at[pieces])

    def sent_second(side):
        return remote(second_h, wd.at[:, pl.ds(side * half, half)], d_ss, d_rs, sibling)

    turns = (1, 2, 0, *range(3, pieces))
    for c in range(pieces):
        when(even, lambda: local_first(turns[c], wa).start())
        when(odd, lambda: local_first(c, wu).start())
    when(even, lambda: local_second(0).start())
    when(odd, lambda: local_second(1).start())

    for row in range(lengths.shape[0]):
        _, _, first = span_scalars(lengths, row)
        packed = rows_in[pl.ds(row * SEQ, SEQ), :]
        for side in range(2):
            at = places(first, side, (BLOCK, SEQ), 0)
            hot = at == lax.broadcasted_iota(jnp.int32, (BLOCK, SEQ), 1)
            halves[side, pl.ds(row * BLOCK, BLOCK), :] = mm(hot.astype(f32).astype(bf16), packed).astype(bf16)
    norm_pair[core] = norm_in[...]

    sent_main = remote(halves.at[1 - core], main, m_ss, m_rs, sibling)
    sent_norm = remote(norm_pair.at[core], norm_pair.at[core], n_ss, n_rs, sibling)
    norm_from = remote(norm_pair.at[1 - core], norm_pair.at[1 - core], n_ss, n_rs, sibling)
    sent_aux = [
        remote(halves.at[side], aux, x_ss.at[side], x_rs, {"section": 4 + side - 2 * sec})
        for side in range(2)
    ]
    pl.semaphore_wait(barrier, 3)
    when(inside, lambda: sent_main.start())
    sent_norm.start()
    when(~inside, lambda: [copy.start() for copy in sent_aux])
    for c in range(pieces):
        when(even, lambda: sent_first(turns[c], wa).start())
        when(odd, lambda: sent_first(c, wu).start())
    when(even, lambda: sent_second(0).start())
    when(odd, lambda: sent_second(1).start())

    @pl.when(inside)
    def _():
        main[...] = halves[core]

    when(~inside, lambda: sent_main.wait_recv())
    norm_from.wait_recv()
    norms[...] = norm_pair[...]

    def ready_a(c):
        when(even, lambda: local_first(c, wa).wait())
        when(odd, lambda: sent_first(c, wa).wait_recv())

    def ready_u(c):
        when(odd, lambda: local_first(c, wu).wait())
        when(even, lambda: sent_first(c, wu).wait_recv())

    def ready_d(c):
        if c == 0:
            when(even, lambda: local_second(0).wait())
            when(odd, lambda: sent_second(0).wait_recv())
        if c == pieces // 2:
            when(odd, lambda: local_second(1).wait())
            when(even, lambda: sent_second(1).wait_recv())

    lead_own[...] = lead_forward(main, lengths, core, norms, wa, wu, wd, kv, dict(a=ready_a, u=ready_u, d=ready_d))
    hop = remote(lead_own, lead_in, l_ss, l_rs, {"section": (sec + 2) % 4})
    when(at_head == 0, lambda: hop.start())

    def write(src, dst, i):
        return pltpu.make_async_copy(src, dst, out_sem.at[i])

    def store_pair(first_ref, side):
        write(first_ref, other_first_h, 0).start()
        write(wd.at[:, pl.ds(side * half, half)], other_second_h, 1).start()

    when(even, lambda: store_pair(wu, 1))
    when(odd, lambda: store_pair(wa, 0))
    write(main, main_h, 2).start()
    sent_aux[0].wait_recv()
    write(aux, aux_h, 3).start()

    @pl.when(at_head == 0)
    def _():
        lead_out[...] = jnp.zeros_like(lead_out)
        hop.wait_send()

    @pl.when(at_head == 1)
    def _():
        hop.wait_recv()
        lead_out[...] = lead_in[...]

    when(inside, lambda: sent_main.wait_send())
    sent_norm.wait_send()
    for c in range(pieces):
        sent_first(c, wa).wait_send()
    sent_second(0).wait_send()
    when(~inside, lambda: [copy.wait_send() for copy in sent_aux])
    write(wa, other_first_h, 0).wait()
    write(wd.at[:, pl.ds(0, half)], other_second_h, 1).wait()
    write(main, main_h, 2).wait()
    write(aux, aux_h, 3).wait()


ANY = pl.BlockSpec(memory_space=pl.ANY)
IN_VMEM = pl.BlockSpec(memory_space=pltpu.VMEM)
IN_SMEM = pl.BlockSpec(memory_space=pltpu.SMEM)
S = jax.ShapeDtypeStruct


def vm(*shape):
    return pltpu.VMEM(shape, bf16)


def dma(*shape):
    return pltpu.SemaphoreType.DMA(shape)


def params(number):
    if number is None:
        return pltpu.CompilerParams(vmem_limit_bytes=VMEM_LIMIT)
    return pltpu.CompilerParams(vmem_limit_bytes=VMEM_LIMIT, collective_id=number, has_side_effects=True)


def start(rows_in, lengths, first, second, norm_own):
    features, ff = first.shape
    tokens = rows_in.shape[0] // 2
    square = S((tokens, features), bf16)
    one = pltpu.SemaphoreType.DMA
    return pl.pallas_call(
        start_kernel,
        out_shape=[
            square, square, S(first.shape, bf16), S(second.shape, bf16), S((2, 2, features), f32),
            S((LEADS, features), bf16),
        ],
        in_specs=[IN_VMEM, IN_SMEM, ANY, ANY, IN_VMEM],
        out_specs=[ANY] * 4 + [IN_VMEM] * 2,
        scratch_shapes=[
            vm(features, ff), vm(features, ff), vm(features, ff), vm(2, tokens, features),
            vm(tokens, features), vm(tokens, features), vm(tokens, 2 * features), pltpu.VMEM((2, 2, features), f32),
            vm(LEADS, features), vm(LEADS, features),
            dma(ff // features + 1), dma(ff // features), dma(ff // features), one, one, one, one, one, one,
            dma(2), one, one, one, dma(4),
        ],
        compiler_params=params(1),
        name="start_and_forward",
    )(rows_in, lengths, first, second, norm_own)


def weight_loads(core, first_h, second_h, other_first_h, other_second_h, wa, wu, wd, a_sem, u_sem, d_sem):
    features = wa.shape[0]
    half = wd.shape[1] // 2

    def cols(c):
        return pl.ds(c * features, features)

    def copy(kind, c, own):
        if kind == "a":
            return pltpu.make_async_copy((first_h if own else other_first_h).at[:, cols(c)], wa.at[:, cols(c)], a_sem.at[c])
        if kind == "u":
            return pltpu.make_async_copy((first_h if own else other_first_h).at[:, cols(c)], wu.at[:, cols(c)], u_sem.at[c])
        from_own = second_h if own else other_second_h
        in_half = c % (half // features)
        return pltpu.make_async_copy(from_own.at[:, cols(in_half)], wd.at[:, cols(c)], d_sem.at[c])

    def begin(kind, c):
        core_of = 0 if kind == "a" else 1 if kind == "u" else (c * features) // half
        when(core == core_of, lambda: copy(kind, c, True).start())
        when(core != core_of, lambda: copy(kind, c, False).start())

    def ready(kind, c):
        copy(kind, c, True).wait()

    return begin, ready


def middle_kernel(
    lengths, main, aux, lead, norms, first_h, second_h, other_first_h, other_second_h,
    x_h, y_h, qkv_h, p_h, ctx_h, zh0_h, mid_h, a_h, df_h, du_h, dmid_h, rstd0, lead_grads, lead_slope, lead_zh, lead_rstd, dnorm,
    wa, wu, wd, x, y, qkv, p, ctx, zh0, mid, a, df, slope, dmid, zh1, rstd1, do, dctx, dqkv, acc, lead_own, lead_in,
    a_sem, u_sem, d_sem, out_sem, col_sem, l_ss, l_rs,
):
    sec = lax.axis_index("section")
    core = sec % 2
    at_head = sec // 2
    tokens, features = main.shape
    pieces = wu.shape[1] // features
    peer = {"section": (sec + 2) % 4}
    barrier = pltpu.get_barrier_semaphore()
    pl.semaphore_signal(barrier, inc=1, device_id=peer, device_id_type=MESH)
    begin, ready_w = weight_loads(
        core, first_h, second_h, other_first_h, other_second_h, wa, wu, wd, a_sem, u_sem, d_sem
    )
    for c in range(pieces):
        begin("a", c)
    for c in range(pieces):
        begin("u", c)
        begin("d", c)
    refs = dict(
        x=(x, x_h), y=(y, y_h), qkv=(qkv, qkv_h), p=(p, p_h), ctx=(ctx, ctx_h), zh0=(zh0, zh0_h), mid=(mid, mid_h),
        df=(df, df_h), du=(slope, du_h), dmid=(dmid, dmid_h),
    )
    order = list(refs)

    def store(name):
        return pltpu.make_async_copy(*refs[name], out_sem.at[order.index(name)])

    def store_cols(c):
        cols = pl.ds(c * features, features)
        return pltpu.make_async_copy(a.at[:, cols], a_h.at[:, cols], col_sem.at[c])

    def keep(*names):
        for name in names:
            store(name).start()

    picks = lead_picks(lengths, core, True)
    leading = jnp.max(picks, axis=1, keepdims=True) > 0

    @pl.when(at_head == 1)
    def _():
        x[...] = jnp.where(leading, mm(picks.astype(bf16), lead[...]).astype(bf16), aux[...])

    @pl.when(at_head == 0)
    def _():
        x[...] = main[...]

    keep("x")
    ready = dict(a=lambda c: ready_w("a", c), u=lambda c: ready_w("u", c), d=lambda c: ready_w("d", c))
    save = dict(
        p=p, a=a, slope=slope, zh0=zh0, zh1=zh1, rstd0=rstd0, rstd1=rstd1, keep=keep,
        keep_cols=lambda c: store_cols(c).start(),
    )
    y[...] = forward_pass(x, lengths, core, norms, wa, wu, wd, qkv, ctx, mid, acc, ready, save)
    keep("y")
    pick = lead_picks(lengths, core, False).astype(bf16)
    lead_zh[...] = mm(pick, zh1[...]).astype(bf16)
    left = jnp.broadcast_to(rstd1[...], (tokens, PAIR))
    total = jnp.zeros((LEADS, PAIR), f32)
    for _ in range(3):
        high = left.astype(bf16)
        left = left - high.astype(f32)
        total = total + mm(pick, high)
    lead_rstd[...] = total[:, 0:1]
    for c in range(pieces):
        cols = pl.ds(c * features, features)
        lead_slope[:, cols] = mm(pick, slope[:, cols]).astype(bf16)

    @pl.when(at_head == 1)
    def _():
        dmid[...] = main[...]

    @pl.when(at_head == 0)
    def _():
        dmid[...] = aux[...]

    none = {k: (lambda *_: None) for k in ("a", "u", "d", "du", "zh0", "qkv")}
    feed_forward_back(dmid[...], norms, wu, wd, slope, zh1, rstd1, df, slope, acc, dnorm, none)
    dmid[...] = acc[...].astype(bf16)
    keep("df", "du", "dmid")
    attention_back(dmid[...], norms, wa, qkv, p, zh0, rstd0, do, dqkv, dctx, acc, dnorm, none, lambda name: None)
    hi = acc[...].astype(bf16)
    lo = (acc[...] - hi.astype(f32)).astype(bf16)
    lead_own[...] = mm(pick, hi) + mm(pick, lo)
    pl.semaphore_wait(barrier, 1)
    hop = remote(lead_own, lead_in, l_ss, l_rs, peer)
    when(at_head == 1, lambda: hop.start())
    for name in order:
        store(name).wait()
    for c in range(pieces):
        store_cols(c).wait()

    @pl.when(at_head == 1)
    def _():
        lead_grads[...] = jnp.zeros_like(lead_grads)
        hop.wait_send()

    @pl.when(at_head == 0)
    def _():
        hop.wait_recv()
        lead_grads[...] = lead_in[...]


def middle(lengths, main, aux, lead, norms, weights):
    tokens, features = main.shape
    ff = weights[0].shape[1]
    pieces = ff // features
    blocks, pairs = tokens // BLOCK, features // PAIR
    square = S((tokens, features), bf16)
    shapes = dict(
        x=square, y=square, qkv=S((tokens, 3 * features), bf16), p=S((blocks, pairs, BLOCK, 2 * BLOCK), bf16),
        ctx=square, zh0=square, mid=square, a=S((tokens, ff), bf16), df=square, du=S((tokens, ff), bf16), dmid=square,
        rstd0=S((tokens, 1), f32), lead_grads=S((LEADS, features), f32), lead_slope=S((LEADS, ff), bf16),
        lead_zh=S((LEADS, features), bf16), lead_rstd=S((LEADS, 1), f32), dnorm=S((4, features), f32),
    )
    small = ("rstd0", "lead_grads", "lead_slope", "lead_zh", "lead_rstd", "dnorm")
    wide = vm(features, ff)
    outs = pl.pallas_call(
        middle_kernel,
        out_shape=list(shapes.values()),
        in_specs=[IN_SMEM] + [IN_VMEM] * 4 + [ANY] * 4,
        out_specs=[IN_VMEM if k in small else ANY for k in shapes],
        scratch_shapes=[wide, wide, wide]
        + [pltpu.VMEM(s.shape, s.dtype) for k, s in shapes.items() if k not in small]
        + [
            vm(tokens, features), pltpu.VMEM((tokens, 1), f32), vm(tokens, features), vm(tokens, features),
            vm(tokens, 3 * features), pltpu.VMEM((tokens, features), f32),
            pltpu.VMEM((LEADS, features), f32), pltpu.VMEM((LEADS, features), f32),
            dma(pieces), dma(pieces), dma(pieces), dma(10), dma(pieces),
            pltpu.SemaphoreType.DMA, pltpu.SemaphoreType.DMA,
        ],
        compiler_params=params(2),
        name="forward_and_backward",
    )(lengths, main, aux, lead, norms, *weights)
    return dict(zip(shapes, outs))


def last_kernel(
    lengths, main, aux, lead_grads, lead_slope, lead_zh, lead_rstd, dnorm_in, norms, rstd0,
    first_h, second_h, other_first_h, other_second_h, y_h, qkv_h, p_h, zh0_h, df_h, du_h, dmid_h,
    own_h, across_h, df_out, rights, dnorm,
    wa, wu, wd, y, qkv, p, zh0, df, du, dmid, do, dctx, dqkv, acc, own, across,
    a_sem, u_sem, d_sem, in_sem, out_sem,
):
    sec = lax.axis_index("section")
    core = sec % 2
    at_head = sec // 2
    tokens, features = main.shape
    ff = wu.shape[1]
    pieces = ff // features
    begin, ready_w = weight_loads(
        core, first_h, second_h, other_first_h, other_second_h, wa, wu, wd, a_sem, u_sem, d_sem
    )
    loads = dict(
        df=(df_h, df), du=(du_h, du), dmid=(dmid_h, dmid), zh0=(zh0_h, zh0), qkv=(qkv_h, qkv), p=(p_h, p), y=(y_h, y)
    )
    names = list(loads)

    def load(name):
        return pltpu.make_async_copy(*loads[name], in_sem.at[names.index(name)])

    for c in range(pieces):
        begin("d", c)
        begin("u", c)
    for name in ("dmid", "zh0"):
        load(name).start()
    begin("a", pieces - 1)
    for name in ("qkv", "p", "df", "du"):
        load(name).start()
    for c in range(pieces - 1):
        begin("a", c)
    load("y").start()
    stores = dict(
        df=(df, df_out), du=(du, rights.at[1, :, pl.ds(0, ff)]), do=(do, rights.at[0, :, pl.ds(3 * features, features)]),
        dqkv=(dqkv, rights.at[0, :, pl.ds(0, 3 * features)]), own=(own, own_h), across=(across, across_h),
    )
    order = list(stores)

    def store(name):
        return pltpu.make_async_copy(*stores[name], out_sem.at[order.index(name)])

    picks = lead_picks(lengths, core, True)
    leading = jnp.max(picks, axis=1, keepdims=True) > 0
    picks = picks.astype(bf16)
    pick = lead_picks(lengths, core, False).astype(bf16)

    @pl.when(at_head == 1)
    def _():
        own[...] = main[...]

    @pl.when(at_head == 0)
    def _():
        own[...] = aux[...]

    base = mm(pick, own[...])
    dy = (base + lead_grads[...]).astype(bf16).astype(f32)
    zh = lead_zh[...].astype(f32)
    extra = dy - base
    dnorm[2:3, :] = dnorm_in[2:3, :] + jnp.sum(extra * zh, axis=0, keepdims=True)
    dnorm[3:4, :] = dnorm_in[3:4, :] + jnp.sum(extra, axis=0, keepdims=True)
    dz, _, _ = normalize_back(zh, lead_rstd[...], norms[1, 0:1, :], dy)
    lead_df = dz.astype(bf16)
    lead_du = []
    for c in range(pieces):
        cols = pl.ds(c * features, features)
        ready_w("d", c)
        g = (mm(lead_df, wd[:, cols]) * lead_slope[:, cols].astype(f32)).astype(bf16)
        lead_du.append(g)
        ready_w("u", c)
        dz = dz + mm(g, wu[:, cols], NT)
    load("dmid").wait()
    dmid[...] = jnp.where(leading, mm(picks, dz.astype(bf16)).astype(bf16), dmid[...])
    ready = dict(
        a=lambda c: ready_w("a", c), zh0=lambda: load("zh0").wait(), qkv=lambda: [load("qkv").wait(), load("p").wait()],
    )

    def keep(name):
        store(name).start()

    def patch():
        load("df").wait()
        df[...] = jnp.where(leading, mm(picks, lead_df).astype(bf16), df[...])
        keep("df")
        load("du").wait()
        for c in range(pieces):
            cols = pl.ds(c * features, features)
            du[:, cols] = jnp.where(leading, mm(picks, lead_du[c]).astype(bf16), du[:, cols])
        keep("du")

    attention_back(dmid[...], norms, wa, qkv, p, zh0, rstd0, do, dqkv, dctx, acc, dnorm, ready, keep, patch)
    load("y").wait()
    dx = acc[...].astype(bf16)

    @pl.when(at_head == 1)
    def _():
        own[...] = y[...]
        across[...] = jnp.where(leading, jnp.zeros_like(dx), dx)

    @pl.when(at_head == 0)
    def _():
        own[...] = dx
        across[...] = y[...]

    store("own").start()
    store("across").start()
    for name in order:
        store(name).wait()


def last(lengths, main, aux, norms, weights, saved):
    tokens, features = main.shape
    ff = weights[0].shape[1]
    pieces = ff // features
    square = S((tokens, features), bf16)
    wide = vm(features, ff)
    leads = [saved[k] for k in ("lead_grads", "lead_slope", "lead_zh", "lead_rstd", "dnorm")]
    held = [saved[k] for k in ("y", "qkv", "p", "zh0", "df", "du", "dmid")]
    return pl.pallas_call(
        last_kernel,
        out_shape=[square, square, square, S((2, tokens, ff), bf16), S((4, features), f32)],
        in_specs=[IN_SMEM] + [IN_VMEM] * 9 + [ANY] * 11,
        out_specs=[ANY] * 4 + [IN_VMEM],
        scratch_shapes=[wide, wide, wide]
        + [pltpu.VMEM(s.shape, s.dtype) for s in held]
        + [
            vm(tokens, features), vm(tokens, features), vm(tokens, 3 * features),
            pltpu.VMEM((tokens, features), f32), vm(tokens, features), vm(tokens, features),
            dma(pieces), dma(pieces), dma(pieces), dma(7), dma(6),
        ],
        compiler_params=params(None),
        name="last_backward",
    )(lengths, main, aux, *leads, norms, saved["rstd0"], *weights, *held)


PANEL = 128
SPLIT = 1
RING = 4


def reduce_kernel(
    chain, x_h, ctx_h, df_h, mid_h, rights, a_h, own_h, across_h, dnorm, out_h, norm_out, halves_h,
    left, left_t, own_ring, sib_ring, sib_send, sib_recv, part, y1, c1, zin1, mid1, zin2, mid2, d2, y2, final, halves,
    left_sem, own_sem, ring_sem, out_sem, sib_ss, sib_rs, y1_ss, y1_rs, z1_ss, z1_rs, m1_ss, m1_rs,
    z2_ss, z2_rs, m2_ss, m2_rs, y2_ss, y2_rs, f_ss, f_rs, o_ss, o_rs, c_ss, c_rs, h_sem,
):
    sec = lax.axis_index("section")
    dp = lax.axis_index("dp")
    core = sec % 2
    panels, rows, _ = final.shape
    half = rows // 2
    features = rows * SPLIT
    spot = dp // 2
    side = spot // (chain // 2)
    depth = chain // 2 - 1
    dist = side * (spot - chain // 2) + (1 - side) * (chain // 2 - 1 - spot)
    inner = dist == 0
    y = dp % 2
    sibling = {"section": sec + 1 - 2 * core}
    across_y = {"dp": dp + 1 - 2 * y}
    inward = {"dp": dp + 2 - 4 * side}
    outward = {"dp": dp - 2 + 4 * side}
    has_out = dist < depth

    barrier = pltpu.get_barrier_semaphore()
    inside = (sec == 0) | (sec == 3)
    beyond = {"section": 2 - sec // 2}
    others = [{"section": (sec + step) % 4} for step in (1, 2, 3)]
    for target in (*others, across_y, inward):
        pl.semaphore_signal(barrier, inc=1, device_id=target, device_id_type=MESH)

    @pl.when(has_out)
    def _():
        pl.semaphore_signal(barrier, inc=1, device_id=outward, device_id_type=MESH)

    def rows_at(which):
        return pl.ds(pl.multiple_of(which * half, half), half)

    mine, theirs = rows_at(y), rows_at(1 - y)
    kept, rest = rows_at(side), rows_at(1 - side)

    def to_sibling(j):
        return remote(sib_send.at[j % RING], sib_recv.at[j], sib_ss.at[j % RING], sib_rs.at[j], sibling)

    def one_y(j):
        i = j // 2
        return remote(part.at[j, theirs], y1.at[i], y1_ss.at[i], y1_rs.at[i], across_y)

    def one_in(j):
        i = j // 2
        return remote(c1.at[i], zin1.at[i], z1_ss.at[i], z1_rs.at[i], inward)

    def one_mid(j):
        i = j // 2
        return remote(c1.at[i], mid1.at[i], m1_ss.at[i], m1_rs.at[i], inward)

    def one_out(j):
        return remote(final.at[j, mine], final.at[j, mine], f_ss.at[0, j], f_rs.at[0, j], outward)

    def one_back(j):
        return remote(final.at[j, mine], final.at[j, mine], f_ss.at[1, j], f_rs.at[1, j], across_y)

    def one_back_in(j):
        return remote(final.at[j, theirs], final.at[j, theirs], f_ss.at[1, j], f_rs.at[1, j], across_y)

    def two_in(j):
        i = j // 2
        return remote(part.at[j], zin2.at[i], z2_ss.at[i], z2_rs.at[i], inward)

    def two_mid(j):
        i = j // 2
        return remote(part.at[j, rest], mid2.at[i], m2_ss.at[i], m2_rs.at[i], inward)

    def two_y(j):
        i = j // 2
        return remote(d2.at[i], y2.at[i], y2_ss.at[i], y2_rs.at[i], across_y)

    def two_swap(j):
        return remote(final.at[j, kept], final.at[j, kept], f_ss.at[2, j], f_rs.at[1, j], inward)

    def two_swap_in(j):
        return remote(final.at[j, rest], final.at[j, rest], f_ss.at[2, j], f_rs.at[1, j], inward)

    def two_out_kept(j):
        return remote(final.at[j, kept], final.at[j, kept], f_ss.at[0, j], f_rs.at[0, j], outward)

    def two_out_rest(j):
        return remote(final.at[j, rest], final.at[j, rest], f_ss.at[1, j], f_rs.at[1, j], outward)

    def left_of(who, j):
        p = (j - 1) // SPLIT
        even = p // (3 * features // PANEL) + p // (4 * features // PANEL)
        odd = 3 - p // (4 * features // PANEL)
        return who * odd + (1 - who) * even

    wide = rights.shape[2] // PANEL

    def strip(j):
        return pl.ds(pl.multiple_of((j - 1) % SPLIT * rows, rows), rows)

    class Fetch:
        def __init__(self, who, j, ring, sem):
            self.who, self.p, self.slot, self.sem = who, (j - 1) // SPLIT, ring.at[j % RING], sem.at[j % RING]

        def upper(self):
            cols = pl.ds(pl.multiple_of(self.p * PANEL, PANEL), PANEL)
            return pltpu.make_async_copy(rights.at[self.who, :, cols], self.slot, self.sem)

        def lower(self):
            col = self.p - wide + self.who * (wide // 2)
            cols = pl.ds(pl.multiple_of(col * PANEL, PANEL), PANEL)
            return pltpu.make_async_copy(a_h.at[:, cols], self.slot, self.sem)

        def start(self):
            when(self.p < wide, lambda: self.upper().start())
            when(self.p >= wide, lambda: self.lower().start())

        def wait(self):
            when(self.p < wide, lambda: self.upper().wait())
            when(self.p >= wide, lambda: self.lower().wait())

    fetch = Fetch

    def to_out(j):
        cols = pl.ds(pl.multiple_of((j - 1) // SPLIT * PANEL, PANEL), PANEL)
        return pltpu.make_async_copy(final.at[j], out_h.at[strip(j), cols], out_sem.at[j])

    own_copy = pltpu.make_async_copy(own_h, halves.at[core], h_sem.at[0])
    own_send = remote(own_h, halves.at[core], o_ss, o_rs, sibling)
    own_from = remote(own_h, halves.at[1 - core], o_ss, o_rs, sibling)
    across_send = remote(across_h, halves.at[core], c_ss, c_rs.at[core], beyond)
    across_from = [remote(across_h, halves.at[side], c_ss, c_rs.at[side], beyond) for side in range(2)]
    lefts = [pltpu.make_async_copy(h, left.at[i], left_sem.at[i]) for i, h in enumerate((x_h, ctx_h, df_h, mid_h))]
    for i in (0, 3, 1, 2):
        lefts[i].start()
    for j in range(1, RING):
        fetch(core, j, own_ring, own_sem).upper().start()
        fetch(1 - core, j, sib_ring, ring_sem).upper().start()

    def turn(i):
        grid = (features, features)
        eye = lax.broadcasted_iota(jnp.int32, grid, 0) == lax.broadcasted_iota(jnp.int32, grid, 1)
        left_t[i] = mm(eye.astype(bf16), left[i], NT).astype(bf16)

    def norm_panel(other):
        chosen = jnp.where(core == other, dnorm[2:4, :], dnorm[0:2, :])
        strips = [
            chosen[r : r + 1, c * PANEL : (c + 1) * PANEL]
            for r in range(2)
            for c in range(features // PANEL)
        ]
        return jnp.concatenate(strips + [jnp.zeros((16 - len(strips), PANEL), f32)], axis=0)

    pl.semaphore_wait(barrier, 5 + has_out.astype(jnp.int32))
    when(inside, lambda: own_copy.start())
    when(~inside, lambda: own_send.start())
    across_send.start()

    def stage_send(j):
        when(j >= RING, lambda: to_sibling(j - RING).wait_send())

        @pl.when(j == 0)
        def _():
            sib_send[0] = jnp.zeros((rows, PANEL), bf16)
            sib_send[0, 0:16, :] = norm_panel(0).astype(bf16)

        @pl.when(j > 0)
        def _():
            fetch(1 - core, j, sib_ring, ring_sem).wait()
            sib_send[j % RING] = mm(left_t[left_of(1 - core, j), strip(j), :], sib_ring[j % RING]).astype(bf16)

        to_sibling(j).start()
        nxt = j + RING
        when(
            (j >= 0) & (nxt < panels),
            lambda: fetch(1 - core, nxt, sib_ring, ring_sem).start(),
        )

    def stage_part(j):
        to_sibling(j).wait_recv()

        @pl.when(j == 0)
        def _():
            part[0] = jnp.zeros((rows, PANEL), bf16)
            part[0, 0:16, :] = (norm_panel(1) + sib_recv[0, 0:16, :].astype(f32)).astype(bf16)

        @pl.when(j > 0)
        def _():
            fetch(core, j, own_ring, own_sem).wait()
            own = mm(left_t[left_of(core, j), strip(j), :], own_ring[j % RING])
            part[j] = (own + sib_recv[j].astype(f32)).astype(bf16)

        nxt = j + RING
        when((nxt < panels), lambda: fetch(core, nxt, own_ring, own_sem).start())
        when(j % 2 == 0, lambda: one_y(j).start())
        when((j % 2 == 1) & (dist == depth) & (depth > 0), lambda: two_in(j).start())
        when((j % 2 == 1) & (dist == depth) & (depth == 0), lambda: two_mid(j).start())

    def one_halves(j):
        one_y(j).wait_recv()
        c1[j // 2] = (part[j, mine, :].astype(f32) + y1[j // 2].astype(f32)).astype(bf16)
        when((dist == depth) & (dist > 0), lambda: one_in(j).start())
        when((dist == depth) & inner, lambda: one_mid(j).start())

    def one_chain(j):
        one_in(j).wait_recv()
        c1[j // 2] = (c1[j // 2].astype(f32) + zin1[j // 2].astype(f32)).astype(bf16)
        when(dist > 0, lambda: one_in(j).start())
        when(inner, lambda: one_mid(j).start())

    def one_total(j):
        one_mid(j).wait_recv()
        final[j, mine, :] = (c1[j // 2].astype(f32) + mid1[j // 2].astype(f32)).astype(bf16)
        when(has_out, lambda: one_out(j).start())
        one_back(j).start()

    def one_spread(j):
        one_out(j).wait_recv()
        when(has_out, lambda: one_out(j).start())
        one_back(j).start()

    def two_chain(j):
        two_in(j).wait_recv()
        part[j] = (part[j].astype(f32) + zin2[j // 2].astype(f32)).astype(bf16)
        when(dist > 0, lambda: two_in(j).start())
        when(inner, lambda: two_mid(j).start())

    def two_halves(j):
        two_mid(j).wait_recv()
        d2[j // 2] = (part[j, kept, :].astype(f32) + mid2[j // 2].astype(f32)).astype(bf16)
        two_y(j).start()

    def two_total(j):
        two_y(j).wait_recv()
        final[j, kept, :] = (d2[j // 2].astype(f32) + y2[j // 2].astype(f32)).astype(bf16)
        two_swap(j).start()
        when(has_out, lambda: two_out_kept(j).start())

    def two_swapped(j):
        two_swap_in(j).wait_recv()
        when(has_out, lambda: two_out_rest(j).start())

    def two_spread_kept(j):
        two_out_kept(j).wait_recv()
        when(has_out, lambda: two_out_kept(j).start())

    def two_spread_rest(j):
        two_out_rest(j).wait_recv()
        when(has_out, lambda: two_out_rest(j).start())

    def finish(j):
        when(j % 2 == 0, lambda: one_back_in(j).wait_recv())

        @pl.when(j == 0)
        def _():
            norm_out[...] = final[0, 0:16, :].astype(f32)

        when(j > 0, lambda: to_out(j).start())

    last_lag = 7 + 4 * depth

    def step(t, carry):
        def at(lag, kind, cond, run):
            j = t - lag
            ok = (j >= 0) & (j < panels)
            if kind is not None:
                ok = ok & (j % 2 == kind)
            if cond is not None:
                ok = ok & cond
            when(ok, run, j)

        at(last_lag, 1, dist > 0, two_spread_rest) if depth == 0 else at(7 + 2 * (depth + dist), 1, dist > 0, two_spread_rest)
        at(5 + 2 * (depth + dist), 1, dist > 0, two_spread_kept)
        at(5 + 2 * (depth + dist), 0, dist > 0, one_spread)
        at(7 + 2 * depth, 1, inner, two_swapped)
        at(5 + 2 * depth, 1, inner, two_total)
        at(5 + 2 * depth, 0, inner, one_total)
        at(3 + 2 * depth, 1, inner, two_halves)
        at(3 + 2 * (depth - dist), 0, dist < depth, one_chain)
        at(1 + 2 * (depth - dist), 1, dist < depth, two_chain)
        at(3, 0, None, one_halves)
        at(1, None, None, stage_part)
        at(0, None, None, stage_send)
        at(last_lag + 1, None, None, finish)
        when(t == 0, lambda: [lefts[0].wait(), turn(0), lefts[3].wait(), turn(3)])
        when(t == 4 * SPLIT, lambda: [lefts[1].wait(), turn(1), lefts[2].wait(), turn(2)])
        return carry

    lax.fori_loop(0, panels + last_lag + 1, step, 0)

    @pl.when(inside)
    def _():
        own_copy.wait()
        own_from.wait_recv()

    @pl.when(~inside)
    def _():
        own_send.wait_send()
        across_from[0].wait_recv()
        across_from[1].wait_recv()

    across_send.wait_send()
    rows_done = pltpu.make_async_copy(halves, halves_h, h_sem.at[1])
    rows_done.start()

    def drain(j, carry):
        when(j >= panels - RING, lambda: to_sibling(j).wait_send())
        when(j > 0, lambda: to_out(j).wait())

        @pl.when(j % 2 == 0)
        def _():
            one_y(j).wait_send()
            when(dist > 0, lambda: one_in(j).wait_send())
            when(inner, lambda: one_mid(j).wait_send())
            when(has_out, lambda: one_out(j).wait_send())
            one_back(j).wait_send()

        @pl.when(j % 2 == 1)
        def _():
            when(dist > 0, lambda: two_in(j).wait_send())

            @pl.when(inner)
            def _():
                two_mid(j).wait_send()
                two_y(j).wait_send()
                two_swap(j).wait_send()

            @pl.when(has_out)
            def _():
                two_out_kept(j).wait_send()
                two_out_rest(j).wait_send()

        return carry

    lax.fori_loop(0, panels, drain, 0)
    rows_done.wait()


def reduce_gradients(lefts, rights, acts, own, across, dnorm, chain):
    rows = lefts[0].shape[0]
    features = lefts[0].shape[1]
    width = rights.shape[2] + acts.shape[1] // 2
    panels = SPLIT * width // PANEL + 1
    unit = features // SPLIT
    evens, odds = (panels + 1) // 2, panels // 2
    any_ = ANY
    V = lambda *s: pltpu.VMEM(s, bf16)
    D = lambda *s: pltpu.SemaphoreType.DMA(s)
    h = unit // 2
    return pl.pallas_call(
        functools.partial(reduce_kernel, chain),
        out_shape=[
            jax.ShapeDtypeStruct((features, width), bf16),
            jax.ShapeDtypeStruct((16, PANEL), f32),
            jax.ShapeDtypeStruct((2, *own.shape), bf16),
        ],
        in_specs=[any_] * 8 + [IN_VMEM],
        out_specs=[any_, IN_VMEM, any_],
        scratch_shapes=[
            V(4, rows, features), V(4, features, rows), V(RING, rows, PANEL), V(RING, rows, PANEL),
            V(RING, unit, PANEL), V(panels, unit, PANEL), V(panels, unit, PANEL),
            V(evens, h, PANEL), V(evens, h, PANEL), V(evens, h, PANEL), V(evens, h, PANEL),
            V(odds, unit, PANEL), V(odds, h, PANEL), V(odds, h, PANEL), V(odds, h, PANEL),
            V(panels, unit, PANEL), V(2, *own.shape),
            D(4), D(RING), D(RING), D(panels), D(RING), D(panels), D(evens), D(evens), D(evens), D(evens), D(evens), D(evens),
            D(odds), D(odds), D(odds), D(odds), D(odds), D(odds), D(3, panels), D(2, panels),
            pltpu.SemaphoreType.DMA, pltpu.SemaphoreType.DMA, pltpu.SemaphoreType.DMA, D(2), D(2),
        ],
        compiler_params=params(3),
        name="reduce_gradients",
    )(*lefts, rights, acts, own, across, dnorm)


def finish_kernel(lengths, total, halves, norm_in, first_out, second_out, rows_out, gain_out, shift_out):
    step = pl.program_id(0)
    features = rows_out.shape[1]
    wide = first_out.shape[1]
    first_out[...] = total[:, pl.ds(0, wide)].astype(f32)
    second_out[...] = total[:, pl.ds(wide, second_out.shape[1])].astype(f32)
    size = rows_out.shape[0]
    row = step // (SEQ // size)
    _, _, first = span_scalars(lengths, row)
    at = lax.broadcasted_iota(jnp.int32, (size, BLOCK), 0) + step % (SEQ // size) * size
    out = None
    for side in range(2):
        hot = at == places(first, side, (size, BLOCK), 1)
        part = mm(hot.astype(f32).astype(bf16), halves[side])
        out = part if out is None else out + part
    rows_out[...] = out
    strips = features // PANEL
    for r, ref in enumerate((gain_out, shift_out)):
        ref[...] = jnp.concatenate([norm_in[r * strips + c : r * strips + c + 1, :] for c in range(strips)], axis=1)


def finish(lengths, total, halves, norm_in, ff):
    features, width = total.shape
    tokens = halves.shape[1]
    size = PANEL
    steps = 2 * tokens // size
    part = features // steps
    row_spec = pl.BlockSpec((1, features), lambda i: (0, 0))
    return pl.pallas_call(
        finish_kernel,
        grid=(steps,),
        out_shape=[
            S((features, ff), f32), S((features, width - ff), f32), S((2 * tokens, features), f32),
            S((1, features), f32), S((1, features), f32),
        ],
        in_specs=[
            IN_SMEM, pl.BlockSpec((part, width), lambda i: (i, 0)),
            pl.BlockSpec((2, BLOCK, features), lambda i: (0, i // (SEQ // size), 0)), IN_VMEM,
        ],
        out_specs=[
            pl.BlockSpec((part, ff), lambda i: (i, 0)), pl.BlockSpec((part, width - ff), lambda i: (i, 0)),
            pl.BlockSpec((size, features), lambda i: (i, 0)), row_spec, row_spec,
        ],
        compiler_params=params(None),
        name="finish",
    )(lengths, total, halves, norm_in)


def per_device(section_rows, span_lengths, first_weights, second_weights, norm_gain, norm_shift):
    first, second = first_weights[0], second_weights[0]
    norm_own = jnp.concatenate([norm_gain, norm_shift], axis=0)
    main, aux, other_first, other_second, norms, lead = start(section_rows[0], span_lengths, first, second, norm_own)
    weights = (first, second, other_first, other_second)
    saved = middle(span_lengths, main, aux, lead, norms, weights)
    own, across, df, rights, dnorm = last(span_lengths, main, aux, norms, weights, saved)
    lefts = (saved["x"], saved["ctx"], df, saved["mid"])
    total, norm_total, halves = reduce_gradients(
        lefts, rights, saved["a"], own, across, dnorm, lax.axis_size("dp") // 2
    )
    d_first, d_second, rows, gain, shift = finish(span_lengths, total, halves, norm_total, first.shape[1])
    return rows[None], d_first[None], d_second[None], gain, shift


def solution(mesh):
    in_specs = (
        P("section", "dp", None),
        P("dp", None),
        P("section", None, None),
        P("section", None, None),
        P("section", None),
        P("section", None),
    )
    out_specs = (
        P("section", "dp", None),
        P("section", None, None),
        P("section", None, None),
        P("section", None),
        P("section", None),
    )
    return jax.shard_map(
        per_device, mesh=mesh, in_specs=in_specs, out_specs=out_specs, check_vma=False
    )
```

```python
import functools

import jax
import jax.numpy as jnp
from jax import lax
from jax.experimental import pallas as pl
from jax.experimental.pallas import tpu as pltpu
from jax.sharding import PartitionSpec as P

HEAD_DIM = 64
PAIR = 2 * HEAD_DIM
BLOCK = 256
SEQ = 512
LEADS = 16
VMEM_LIMIT = 60 << 20
MESH = pl.DeviceIdType.MESH
f32 = jnp.float32
bf16 = jnp.bfloat16
epsilon = 1e-12
NN = (((1,), (0,)), ((), ()))
NT = (((1,), (1,)), ((), ()))
TN = (((0,), (0,)), ((), ()))
LOG2E = 1.4426950408889634


def mm(a, b, dims=NN):
    return lax.dot_general(a, b, dims, preferred_element_type=f32)


def when(cond, step, *args):
    @pl.when(cond)
    def _():
        step(*args)


def remote(src, dst, ss, rs, target):
    return pltpu.make_async_remote_copy(
        src_ref=src, dst_ref=dst, send_sem=ss, recv_sem=rs, device_id=target, device_id_type=MESH
    )


def gelu_and_slope(u):
    bell = jnp.exp2(u * u * (-0.5 * LOG2E))
    t = 1.0 / (1.0 + (0.3275911 * 0.5**0.5) * jnp.abs(u))
    poly = t * (0.127414796 + t * (-0.142248368 + t * (0.7107068705 + t * (-0.7265760135 + t * 0.5307027145))))
    tail = poly * bell
    cdf = jnp.where(u < 0, tail, 1.0 - tail)
    return u * cdf, cdf + u * bell * 0.3989422804014327


def normalize(z):
    centered = z - jnp.mean(z, axis=-1, keepdims=True)
    rstd = lax.rsqrt(jnp.mean(centered * centered, axis=-1, keepdims=True) + epsilon)
    return centered * rstd, rstd


def normalize_back(zh, rstd, gain, dy):
    g = dy * gain
    mean_g = jnp.mean(g, axis=-1, keepdims=True)
    mean_gz = jnp.mean(g * zh, axis=-1, keepdims=True)
    dz = rstd * (g - mean_g - zh * mean_gz)
    return dz, jnp.sum(dy * zh, axis=0, keepdims=True), jnp.sum(dy, axis=0, keepdims=True)


def span_scalars(lengths, row):
    ends, starts, first, total = [], [], 0, 0
    for j in range(lengths.shape[1]):
        size = lengths[row, j]
        starts.append(total)
        first = first + jnp.where(size == BLOCK, total, 0)
        total = total + size
        ends.append(total)
    return ends, starts, first


def places(first, core, shape, axis):
    at = lax.broadcasted_iota(jnp.int32, shape, axis) + (first + core * BLOCK)
    return jnp.where(at >= SEQ, at - SEQ, at)


def mask_bias(lengths, row, core):
    ends, _, first = span_scalars(lengths, row)

    def segment(at):
        return sum((at >= end).astype(jnp.int32) for end in ends)

    rows = segment(places(first, core, (BLOCK, BLOCK), 0))
    cols = segment(places(first, core, (BLOCK, BLOCK), 1))
    return jnp.where(rows == cols, 0.0, -1e30)


def lead_picks(lengths, core, by_rows):
    parts = []
    per_row = lengths.shape[1] - 1
    shape = (BLOCK, LEADS) if by_rows else (LEADS, BLOCK)
    for row in range(lengths.shape[0]):
        _, starts, first = span_scalars(lengths, row)
        at = places(first, core, shape, 0 if by_rows else 1)
        slot = lax.broadcasted_iota(jnp.int32, shape, 1 if by_rows else 0)
        hit = sum(
            ((slot == row * per_row + j) & (at == starts[j])).astype(jnp.int32) for j in range(per_row)
        )
        parts.append(hit.astype(f32))
    return jnp.concatenate(parts, axis=0 if by_rows else 1)


def lane_masks():
    return lax.broadcasted_iota(jnp.int32, (BLOCK, PAIR), 1) < HEAD_DIM


def forward_pass(x, lengths, core, norms, wa, wu, wd, qkv, ctx, mid, acc, ready, save):
    tokens, features = x.shape
    pairs = features // PAIR
    for c in range(3):
        ready["a"](c)
        cols = pl.ds(c * features, features)
        qkv[:, cols] = mm(x[...], wa[:, cols]).astype(bf16)
    first = lane_masks()
    zero = jnp.zeros((BLOCK, PAIR), bf16)

    def block_step(b, carry):
        rows = pl.ds(pl.multiple_of(b * BLOCK, BLOCK), BLOCK)
        bias = mask_bias(lengths, b, core)
        for h in range(pairs):
            q = qkv[rows, pl.ds(h * PAIR, PAIR)]
            k = qkv[rows, pl.ds(features + h * PAIR, PAIR)]
            v = qkv[rows, pl.ds(2 * features + h * PAIR, PAIR)]
            total = None
            for side in range(2):
                own = first if side == 0 else ~first
                s = mm(q, jnp.where(own, k, zero), NT) * (HEAD_DIM**-0.5) + bias
                e = jnp.exp(s - jnp.max(s, axis=-1, keepdims=True))
                pr = (e * (1.0 / jnp.sum(e, axis=-1, keepdims=True))).astype(bf16)
                if save:
                    save["p"][b, h, :, pl.ds(side * BLOCK, BLOCK)] = pr
                part = mm(pr, jnp.where(own, v, zero))
                total = part if total is None else total + part
            ctx[rows, pl.ds(h * PAIR, PAIR)] = total.astype(bf16)
        return carry

    lax.fori_loop(0, tokens // BLOCK, block_step, 0)
    ready["a"](3)
    zn, r = normalize(x[...].astype(f32) + mm(ctx[...], wa[:, pl.ds(3 * features, features)]))
    if save:
        save["keep"]("qkv", "p", "ctx")
        save["rstd0"][...] = r
        save["zh0"][...] = zn.astype(bf16)
    mid[...] = (zn * norms[0, 0:1, :] + norms[0, 1:2, :]).astype(bf16)
    acc[...] = mid[...].astype(f32)
    if save:
        save["keep"]("zh0", "mid")
    for c in range(wu.shape[1] // features):
        cols = pl.ds(c * features, features)
        ready["u"](c)
        act, slope = gelu_and_slope(mm(mid[...], wu[:, cols]))
        act = act.astype(bf16)
        if save:
            save["a"][:, cols] = act
            save["slope"][:, cols] = slope.astype(bf16)
            save["keep_cols"](c)
        ready["d"](c)
        acc[...] += mm(act, wd[:, cols], NT)
    zn, r = normalize(acc[...])
    if save:
        save["rstd1"][...] = r
        save["zh1"][...] = zn.astype(bf16)
    return (zn * norms[1, 0:1, :] + norms[1, 1:2, :]).astype(bf16)


def feed_forward_back(dy, norms, wu, wd, slope, zh1, rstd1, df, du, acc, dnorm, ready):
    features = wu.shape[0]
    dz, dgain, dshift = normalize_back(zh1[...].astype(f32), rstd1[...], norms[1, 0:1, :], dy.astype(f32))
    dnorm[2:3, :] = dgain
    dnorm[3:4, :] = dshift
    df[...] = dz.astype(bf16)
    acc[...] = dz
    for c in range(wu.shape[1] // features):
        cols = pl.ds(c * features, features)
        ready["d"](c)
        da = mm(df[...], wd[:, cols])
        ready["du"](c)
        g = (da * slope[:, cols].astype(f32)).astype(bf16)
        du[:, cols] = g
        ready["u"](c)
        acc[...] += mm(g, wu[:, cols], NT)


def attention_back_begin(d_mid, norms, wa, zh0, rstd0, do, dctx, acc, dnorm):
    tokens, features = acc.shape
    dgain = dshift = None
    for b in range(tokens // BLOCK):
        rows = pl.ds(b * BLOCK, BLOCK)
        dz, dg, ds = normalize_back(
            zh0[rows, :].astype(f32), rstd0[rows, :], norms[0, 0:1, :], d_mid[rows, :].astype(f32)
        )
        dgain, dshift = (dg, ds) if b == 0 else (dgain + dg, dshift + ds)
        acc[rows, :] = dz
        do[rows, :] = dz.astype(bf16)
        dctx[rows, :] = mm(dz.astype(bf16), wa[:, pl.ds(3 * features, features)], NT).astype(bf16)
    dnorm[0:1, :] = dgain
    dnorm[1:2, :] = dshift


def attention_back_item(b, h, qkv, p, dctx):
    features = dctx.shape[1]
    first = lane_masks()
    zero = jnp.zeros((BLOCK, PAIR), bf16)
    scale = HEAD_DIM**-0.5
    rows = pl.ds(pl.multiple_of(b * BLOCK, BLOCK), BLOCK)
    at = [pl.ds(pl.multiple_of(part * features + h * PAIR, PAIR), PAIR) for part in range(3)]
    q, k, v = (qkv[rows, cols] for cols in at)
    dc = dctx[rows, at[0]]
    dq = dk = dv = None
    for side in range(2):
        own = first if side == 0 else ~first
        pr = p[b, h, :, pl.ds(side * BLOCK, BLOCK)]
        prf = pr.astype(f32)
        dp = mm(dc, jnp.where(own, v, zero), NT)
        r = jnp.sum(dp * prf, axis=-1, keepdims=True)
        ds = (prf * (dp - r)).astype(bf16)
        parts = (
            mm(ds, jnp.where(own, k, zero)),
            mm(ds, jnp.where(own, q, zero), TN),
            mm(pr, jnp.where(own, dc, zero), TN),
        )
        if dq is None:
            dq, dk, dv = parts
        else:
            dq, dk, dv = dq + parts[0], dk + parts[1], dv + parts[2]
    qkv[rows, at[0]] = (dq * scale).astype(bf16)
    qkv[rows, at[1]] = (dk * scale).astype(bf16)
    qkv[rows, at[2]] = dv.astype(bf16)


def attention_back_end(part, wa, dqkv, acc):
    features = wa.shape[0]
    cols = pl.ds(part * features, features)
    for b in range(acc.shape[0] // BLOCK):
        rows = pl.ds(b * BLOCK, BLOCK)
        acc[rows, :] += mm(dqkv[rows, cols], wa[:, cols], NT)


def lead_forward(x, lengths, core, norms, wa, wu, wd, kv, ready):
    tokens, features = x.shape
    per_row = lengths.shape[1] - 1
    own = mm(lead_picks(lengths, core, False).astype(bf16), x[...]).astype(bf16)
    for c in (1, 2):
        ready["a"](c)
        kv[:, pl.ds((c - 1) * features, features)] = mm(x[...], wa[:, pl.ds(c * features, features)]).astype(bf16)
    ready["a"](0)
    q = mm(own, wa[:, pl.ds(0, features)]).astype(bf16)
    parts = []
    for row in range(tokens // BLOCK):
        ends, _, first = span_scalars(lengths, row)
        at = places(first, core, (LEADS, BLOCK), 1)
        keys = sum((at >= end).astype(jnp.int32) for end in ends)
        span = lax.broadcasted_iota(jnp.int32, (LEADS, BLOCK), 0) - row * per_row
        parts.append(jnp.where((span == keys) & (span < per_row), 0.0, -1e30))
    bias = jnp.concatenate(parts, axis=1)
    ctx = []
    for h in range(features // PAIR):
        k = kv[:, pl.ds(h * PAIR, PAIR)]
        v = kv[:, pl.ds(features + h * PAIR, PAIR)]
        lanes = lax.broadcasted_iota(jnp.int32, (LEADS, PAIR), 1) < HEAD_DIM
        total = None
        for side in range(2):
            mine = lanes if side == 0 else ~lanes
            s = mm(jnp.where(mine, q[:, h * PAIR : (h + 1) * PAIR], jnp.zeros((), bf16)), k, NT) * (HEAD_DIM**-0.5) + bias
            e = jnp.exp(s - jnp.max(s, axis=-1, keepdims=True))
            part = mm((e * (1.0 / jnp.sum(e, axis=-1, keepdims=True))).astype(bf16), v)
            total = jnp.where(lanes, part, 0.0) if side == 0 else jnp.where(lanes, total, part)
        ctx.append(total.astype(bf16))
    ready["a"](3)
    zn, _ = normalize(own.astype(f32) + mm(jnp.concatenate(ctx, axis=1), wa[:, pl.ds(3 * features, features)]))
    mid = (zn * norms[0, 0:1, :] + norms[0, 1:2, :]).astype(bf16)
    out = mid.astype(f32)
    for c in range(wu.shape[1] // features):
        cols = pl.ds(c * features, features)
        ready["u"](c)
        act, _ = gelu_and_slope(mm(mid, wu[:, cols]))
        ready["d"](c)
        out = out + mm(act.astype(bf16), wd[:, cols], NT)
    zn, _ = normalize(out)
    return (zn * norms[1, 0:1, :] + norms[1, 1:2, :]).astype(bf16)


def start_kernel(
    rows_in, lengths, first_h, second_h, norm_in,
    main_h, aux_h, other_first_h, other_second_h, norms, lead_out,
    wa, wu, wd, halves, main, aux, kv, norm_pair, lead_own, lead_in,
    load, w_ss, w_rs, d_ss, d_rs, n_ss, n_rs, m_ss, m_rs, x_ss, x_rs, l_ss, l_rs, out_sem,
):
    sec = lax.axis_index("section")
    core = sec % 2
    at_head = sec // 2
    inside = (sec == 0) | (sec == 3)
    tokens, features = main.shape
    pieces = wu.shape[1] // features
    half = wd.shape[1] // 2
    even, odd = core == 0, core == 1
    sibling = {"section": sec + 1 - 2 * core}
    barrier = pltpu.get_barrier_semaphore()
    for step in range(1, 4):
        target = {"section": (sec + step) % 4}
        pl.semaphore_signal(barrier, inc=1, device_id=target, device_id_type=MESH)

    def cols(c):
        return pl.ds(c * features, features)

    def local_first(c, dst):
        return pltpu.make_async_copy(first_h.at[:, cols(c)], dst.at[:, cols(c)], load.at[c])

    def sent_first(c, dst):
        return remote(first_h.at[:, cols(c)], dst.at[:, cols(c)], w_ss.at[c], w_rs.at[c], sibling)

    def local_second(side):
        return pltpu.make_async_copy(second_h, wd.at[:, pl.ds(side * half, half)], load.at[pieces])

    def sent_second(side):
        return remote(second_h, wd.at[:, pl.ds(side * half, half)], d_ss, d_rs, sibling)

    turns = (1, 2, 0, *range(3, pieces))
    for c in range(pieces):
        when(even, lambda: local_first(turns[c], wa).start())
        when(odd, lambda: local_first(c, wu).start())
    when(even, lambda: local_second(0).start())
    when(odd, lambda: local_second(1).start())

    for row in range(lengths.shape[0]):
        _, _, first = span_scalars(lengths, row)
        packed = rows_in[pl.ds(row * SEQ, SEQ), :]
        for side in range(2):
            at = places(first, side, (BLOCK, SEQ), 0)
            hot = at == lax.broadcasted_iota(jnp.int32, (BLOCK, SEQ), 1)
            halves[side, pl.ds(row * BLOCK, BLOCK), :] = mm(hot.astype(f32).astype(bf16), packed).astype(bf16)
    norm_pair[core] = norm_in[...]

    sent_main = remote(halves.at[1 - core], main, m_ss, m_rs, sibling)
    sent_norm = remote(norm_pair.at[core], norm_pair.at[core], n_ss, n_rs, sibling)
    norm_from = remote(norm_pair.at[1 - core], norm_pair.at[1 - core], n_ss, n_rs, sibling)
    sent_aux = [
        remote(halves.at[side], aux, x_ss.at[side], x_rs, {"section": 4 + side - 2 * sec})
        for side in range(2)
    ]
    pl.semaphore_wait(barrier, 3)
    when(inside, lambda: sent_main.start())
    sent_norm.start()
    when(~inside, lambda: [copy.start() for copy in sent_aux])
    for c in range(pieces):
        when(even, lambda: sent_first(turns[c], wa).start())
        when(odd, lambda: sent_first(c, wu).start())
    when(even, lambda: sent_second(0).start())
    when(odd, lambda: sent_second(1).start())

    @pl.when(inside)
    def _():
        main[...] = halves[core]

    when(~inside, lambda: sent_main.wait_recv())
    norm_from.wait_recv()
    norms[...] = norm_pair[...]

    def ready_a(c):
        when(even, lambda: local_first(c, wa).wait())
        when(odd, lambda: sent_first(c, wa).wait_recv())

    def ready_u(c):
        when(odd, lambda: local_first(c, wu).wait())
        when(even, lambda: sent_first(c, wu).wait_recv())

    def ready_d(c):
        if c == 0:
            when(even, lambda: local_second(0).wait())
            when(odd, lambda: sent_second(0).wait_recv())
        if c == pieces // 2:
            when(odd, lambda: local_second(1).wait())
            when(even, lambda: sent_second(1).wait_recv())

    lead_own[...] = lead_forward(main, lengths, core, norms, wa, wu, wd, kv, dict(a=ready_a, u=ready_u, d=ready_d))
    hop = remote(lead_own, lead_in, l_ss, l_rs, {"section": (sec + 2) % 4})
    when(at_head == 0, lambda: hop.start())

    def write(src, dst, i):
        return pltpu.make_async_copy(src, dst, out_sem.at[i])

    def store_pair(first_ref, side):
        write(first_ref, other_first_h, 0).start()
        write(wd.at[:, pl.ds(side * half, half)], other_second_h, 1).start()

    when(even, lambda: store_pair(wu, 1))
    when(odd, lambda: store_pair(wa, 0))
    write(main, main_h, 2).start()
    sent_aux[0].wait_recv()
    write(aux, aux_h, 3).start()

    @pl.when(at_head == 0)
    def _():
        lead_out[...] = jnp.zeros_like(lead_out)
        hop.wait_send()

    @pl.when(at_head == 1)
    def _():
        hop.wait_recv()
        lead_out[...] = lead_in[...]

    when(inside, lambda: sent_main.wait_send())
    sent_norm.wait_send()
    for c in range(pieces):
        sent_first(c, wa).wait_send()
    sent_second(0).wait_send()
    when(~inside, lambda: [copy.wait_send() for copy in sent_aux])
    write(wa, other_first_h, 0).wait()
    write(wd.at[:, pl.ds(0, half)], other_second_h, 1).wait()
    write(main, main_h, 2).wait()
    write(aux, aux_h, 3).wait()


ANY = pl.BlockSpec(memory_space=pl.ANY)
IN_VMEM = pl.BlockSpec(memory_space=pltpu.VMEM)
IN_SMEM = pl.BlockSpec(memory_space=pltpu.SMEM)
S = jax.ShapeDtypeStruct


def vm(*shape):
    return pltpu.VMEM(shape, bf16)


def dma(*shape):
    return pltpu.SemaphoreType.DMA(shape)


def params(number):
    if number is None:
        return pltpu.CompilerParams(vmem_limit_bytes=VMEM_LIMIT)
    return pltpu.CompilerParams(vmem_limit_bytes=VMEM_LIMIT, collective_id=number, has_side_effects=True)


def start(rows_in, lengths, first, second, norm_own):
    features, ff = first.shape
    tokens = rows_in.shape[0] // 2
    square = S((tokens, features), bf16)
    one = pltpu.SemaphoreType.DMA
    return pl.pallas_call(
        start_kernel,
        out_shape=[
            square, square, S(first.shape, bf16), S(second.shape, bf16), S((2, 2, features), f32),
            S((LEADS, features), bf16),
        ],
        in_specs=[IN_VMEM, IN_SMEM, ANY, ANY, IN_VMEM],
        out_specs=[ANY] * 4 + [IN_VMEM] * 2,
        scratch_shapes=[
            vm(features, ff), vm(features, ff), vm(features, ff), vm(2, tokens, features),
            vm(tokens, features), vm(tokens, features), vm(tokens, 2 * features), pltpu.VMEM((2, 2, features), f32),
            vm(LEADS, features), vm(LEADS, features),
            dma(ff // features + 1), dma(ff // features), dma(ff // features), one, one, one, one, one, one,
            dma(2), one, one, one, dma(4),
        ],
        compiler_params=params(1),
        name="start_and_forward",
    )(rows_in, lengths, first, second, norm_own)


def weight_loads(core, first_h, second_h, other_first_h, other_second_h, wa, wu, wd, a_sem, u_sem, d_sem):
    features = wa.shape[0]
    half = wd.shape[1] // 2

    def cols(c):
        return pl.ds(c * features, features)

    def copy(kind, c, own):
        if kind == "a":
            return pltpu.make_async_copy((first_h if own else other_first_h).at[:, cols(c)], wa.at[:, cols(c)], a_sem.at[c])
        if kind == "u":
            return pltpu.make_async_copy((first_h if own else other_first_h).at[:, cols(c)], wu.at[:, cols(c)], u_sem.at[c])
        from_own = second_h if own else other_second_h
        in_half = c % (half // features)
        return pltpu.make_async_copy(from_own.at[:, cols(in_half)], wd.at[:, cols(c)], d_sem.at[c])

    def begin(kind, c):
        core_of = 0 if kind == "a" else 1 if kind == "u" else (c * features) // half
        when(core == core_of, lambda: copy(kind, c, True).start())
        when(core != core_of, lambda: copy(kind, c, False).start())

    def ready(kind, c):
        copy(kind, c, True).wait()

    return begin, ready


def middle_kernel(
    lengths, main, aux, lead, norms, first_h, second_h, other_first_h, other_second_h,
    x_h, y_h, qkv_h, p_h, ctx_h, zh0_h, mid_h, a_h, df_h, du_h, dmid_h, rstd0, dnorm,
    wa, wu, wd, x, y, qkv, p, ctx, zh0, mid, a, df, slope, dmid, zh1, rstd1, do, dctx, acc, d_att, lead_slope, lead_own, lead_in,
    a_sem, u_sem, d_sem, out_sem, col_sem, l_ss, l_rs,
):
    sec = lax.axis_index("section")
    core = sec % 2
    at_head = sec // 2
    tokens, features = main.shape
    pieces = wu.shape[1] // features
    peer = {"section": (sec + 2) % 4}
    barrier = pltpu.get_barrier_semaphore()
    pl.semaphore_signal(barrier, inc=1, device_id=peer, device_id_type=MESH)
    begin, ready_w = weight_loads(
        core, first_h, second_h, other_first_h, other_second_h, wa, wu, wd, a_sem, u_sem, d_sem
    )
    for c in range(pieces):
        begin("a", c)
    for c in range(pieces):
        begin("u", c)
        begin("d", c)
    refs = dict(
        x=(x, x_h), y=(y, y_h), qkv=(qkv, qkv_h), p=(p, p_h), ctx=(ctx, ctx_h), zh0=(zh0, zh0_h), mid=(mid, mid_h),
        df=(df, df_h), du=(slope, du_h), dmid=(dmid, dmid_h),
    )
    order = list(refs)

    def store(name):
        return pltpu.make_async_copy(*refs[name], out_sem.at[order.index(name)])

    def store_cols(c):
        cols = pl.ds(c * features, features)
        return pltpu.make_async_copy(a.at[:, cols], a_h.at[:, cols], col_sem.at[c])

    def keep(*names):
        for name in names:
            store(name).start()

    picks = lead_picks(lengths, core, True)
    leading = jnp.max(picks, axis=1, keepdims=True) > 0

    @pl.when(at_head == 1)
    def _():
        x[...] = jnp.where(leading, mm(picks.astype(bf16), lead[...]).astype(bf16), aux[...])

    @pl.when(at_head == 0)
    def _():
        x[...] = main[...]

    keep("x")
    ready = dict(a=lambda c: ready_w("a", c), u=lambda c: ready_w("u", c), d=lambda c: ready_w("d", c))
    save = dict(
        p=p, a=a, slope=slope, zh0=zh0, zh1=zh1, rstd0=rstd0, rstd1=rstd1, keep=keep,
        keep_cols=lambda c: store_cols(c).start(),
    )
    y[...] = forward_pass(x, lengths, core, norms, wa, wu, wd, qkv, ctx, mid, acc, ready, save)
    keep("y")
    pick = lead_picks(lengths, core, False).astype(bf16)
    lead_zh = mm(pick, zh1[...])
    left = jnp.broadcast_to(rstd1[...], (tokens, PAIR))
    total = jnp.zeros((LEADS, PAIR), f32)
    for _ in range(3):
        high = left.astype(bf16)
        left = left - high.astype(f32)
        total = total + mm(pick, high)
    lead_rstd = total[:, 0:1]
    for c in range(pieces):
        cols = pl.ds(c * features, features)
        lead_slope[:, cols] = mm(pick, slope[:, cols]).astype(bf16)

    @pl.when(at_head == 1)
    def _():
        dmid[...] = main[...]

    @pl.when(at_head == 0)
    def _():
        dmid[...] = aux[...]

    base = mm(pick, dmid[...])
    none = {k: (lambda *_: None) for k in ("u", "d", "du")}
    feed_forward_back(dmid[...], norms, wu, wd, slope, zh1, rstd1, df, slope, acc, dnorm, none)
    dmid[...] = acc[...].astype(bf16)
    dnorm[0:2, :] = jnp.zeros((2, features), f32)
    pl.semaphore_wait(barrier, 1)
    hop = remote(lead_own, lead_in, l_ss, l_rs, peer)

    @pl.when(at_head == 1)
    def _():
        keep("df", "du", "dmid")
        attention_back_begin(dmid, norms, wa, zh0, rstd0, do, dctx, acc, d_att)
        for name in ("qkv", "p"):
            store(name).wait()

        def block_step(b, carry):
            for h in range(features // PAIR):
                attention_back_item(b, h, qkv, p, dctx)
            return carry

        lax.fori_loop(0, tokens // BLOCK, block_step, 0)
        for part in range(3):
            attention_back_end(part, wa, qkv, acc)
        hi = acc[...].astype(bf16)
        lo = (acc[...] - hi.astype(f32)).astype(bf16)
        lead_own[...] = mm(pick, hi) + mm(pick, lo)
        hop.start()
        hop.wait_send()

    @pl.when(at_head == 0)
    def _():
        for name in ("qkv", "p"):
            store(name).wait()
        hop.wait_recv()
        dy = (base + lead_in[...]).astype(bf16).astype(f32)
        extra = dy - base
        dnorm[2:3, :] += jnp.sum(extra * lead_zh, axis=0, keepdims=True)
        dnorm[3:4, :] += jnp.sum(extra, axis=0, keepdims=True)
        dz, _, _ = normalize_back(lead_zh, lead_rstd, norms[1, 0:1, :], dy)
        hot = picks.astype(bf16)
        lead_df = dz.astype(bf16)
        df[...] = jnp.where(leading, mm(hot, lead_df).astype(bf16), df[...])
        keep("df")
        for c in range(pieces):
            cols = pl.ds(c * features, features)
            g = (mm(lead_df, wd[:, cols]) * lead_slope[:, cols].astype(f32)).astype(bf16)
            slope[:, cols] = jnp.where(leading, mm(hot, g).astype(bf16), slope[:, cols])
            dz = dz + mm(g, wu[:, cols], NT)
        keep("du")
        dmid[...] = jnp.where(leading, mm(hot, dz.astype(bf16)).astype(bf16), dmid[...])
        keep("dmid")

    for name in order:
        if name not in ("qkv", "p"):
            store(name).wait()
    for c in range(pieces):
        store_cols(c).wait()


def middle(lengths, main, aux, lead, norms, weights):
    tokens, features = main.shape
    ff = weights[0].shape[1]
    pieces = ff // features
    blocks, pairs = tokens // BLOCK, features // PAIR
    square = S((tokens, features), bf16)
    shapes = dict(
        x=square, y=square, qkv=S((tokens, 3 * features), bf16), p=S((blocks, pairs, BLOCK, 2 * BLOCK), bf16),
        ctx=square, zh0=square, mid=square, a=S((tokens, ff), bf16), df=square, du=S((tokens, ff), bf16), dmid=square,
        rstd0=S((tokens, 1), f32), dnorm=S((4, features), f32),
    )
    small = ("rstd0", "dnorm")
    wide = vm(features, ff)
    outs = pl.pallas_call(
        middle_kernel,
        out_shape=list(shapes.values()),
        in_specs=[IN_SMEM] + [IN_VMEM] * 4 + [ANY] * 4,
        out_specs=[IN_VMEM if k in small else ANY for k in shapes],
        scratch_shapes=[wide, wide, wide]
        + [pltpu.VMEM(s.shape, s.dtype) for k, s in shapes.items() if k not in small]
        + [
            vm(tokens, features), pltpu.VMEM((tokens, 1), f32), vm(tokens, features), vm(tokens, features),
            pltpu.VMEM((tokens, features), f32), pltpu.VMEM((2, features), f32), vm(LEADS, ff),
            pltpu.VMEM((LEADS, features), f32), pltpu.VMEM((LEADS, features), f32),
            dma(pieces), dma(pieces), dma(pieces), dma(10), dma(pieces),
            pltpu.SemaphoreType.DMA, pltpu.SemaphoreType.DMA,
        ],
        compiler_params=params(2),
        name="forward_and_backward",
    )(lengths, main, aux, lead, norms, *weights)
    return dict(zip(shapes, outs))


PANEL = 128
RING = 4


def reduce_kernel(
    chain, lengths, dnorm_in, norms, rstd0, x_h, ctx_h, mid_h, a_h, df_h, du_h, dmid_h, zh0_h, qkv_h, p_h, y_h,
    first_h, other_first_h,
    out_h, norm_out, halves_h,
    left, left_t, own_ring, sib_ring, sib_send, part, y1, zin1, mid1, zin2, mid2, y2, final, halves,
    wa, qkv, p, do, dctx, acc, y_buf, dnorm,
    left_sem, own_sem, ring_sem, out_sem, sib_ss, sib_rs, y1_ss, y1_rs, z1_ss, z1_rs, m1_ss, m1_rs,
    z2_ss, z2_rs, m2_ss, m2_rs, y2_ss, y2_rs, f_ss, f_rs, o_ss, o_rs, c_ss, c_rs, h_sem, a_sem, in_sem,
):
    sec = lax.axis_index("section")
    dp = lax.axis_index("dp")
    core = sec % 2
    panels, rows, _ = final.shape
    tokens = acc.shape[0]
    half = rows // 2
    features = rows
    last = panels - 1
    spot = dp // 2
    side = spot // (chain // 2)
    depth = chain // 2 - 1
    dist = side * (spot - chain // 2) + (1 - side) * (chain // 2 - 1 - spot)
    inner = dist == 0
    y = dp % 2
    sibling = {"section": sec + 1 - 2 * core}
    across_y = {"dp": dp + 1 - 2 * y}
    inward = {"dp": dp + 2 - 4 * side}
    outward = {"dp": dp - 2 + 4 * side}
    has_out = dist < depth

    barrier = pltpu.get_barrier_semaphore()
    at_head = sec // 2
    dx_buf = dctx
    inside = (sec == 0) | (sec == 3)
    beyond = {"section": 2 - sec // 2}
    others = [{"section": (sec + step) % 4} for step in (1, 2, 3)]
    for target in (*others, across_y, inward):
        pl.semaphore_signal(barrier, inc=1, device_id=target, device_id_type=MESH)

    @pl.when(has_out)
    def _():
        pl.semaphore_signal(barrier, inc=1, device_id=outward, device_id_type=MESH)

    def rows_at(which):
        return pl.ds(pl.multiple_of(which * half, half), half)

    mine, theirs = rows_at(y), rows_at(1 - y)
    kept, rest = rows_at(side), rows_at(1 - side)

    def to_sibling(j):
        return remote(sib_send.at[j % RING], part.at[j], sib_ss.at[j % RING], sib_rs.at[j], sibling)

    def one_y(j):
        i = j // 2
        return remote(part.at[j, theirs], y1.at[i], y1_ss.at[i], y1_rs.at[i], across_y)

    def one_in(j):
        i = j // 2
        return remote(part.at[j, mine], zin1.at[i], z1_ss.at[i], z1_rs.at[i], inward)

    def one_mid(j):
        i = j // 2
        return remote(part.at[j, mine], mid1.at[i], m1_ss.at[i], m1_rs.at[i], inward)

    def one_out(j):
        return remote(final.at[j, mine], final.at[j, mine], f_ss.at[0, j], f_rs.at[0, j], outward)

    def one_back(j):
        return remote(final.at[j, mine], final.at[j, mine], f_ss.at[1, j], f_rs.at[1, j], across_y)

    def one_back_in(j):
        return remote(final.at[j, theirs], final.at[j, theirs], f_ss.at[1, j], f_rs.at[1, j], across_y)

    def two_in(j):
        i = j // 2
        return remote(part.at[j], zin2.at[i], z2_ss.at[i], z2_rs.at[i], inward)

    def two_mid(j):
        i = j // 2
        return remote(part.at[j, rest], mid2.at[i], m2_ss.at[i], m2_rs.at[i], inward)

    def two_y(j):
        i = j // 2
        return remote(part.at[j, kept], y2.at[i], y2_ss.at[i], y2_rs.at[i], across_y)

    def two_swap(j):
        return remote(final.at[j, kept], final.at[j, kept], f_ss.at[2, j], f_rs.at[1, j], inward)

    def two_swap_in(j):
        return remote(final.at[j, rest], final.at[j, rest], f_ss.at[2, j], f_rs.at[1, j], inward)

    def two_out_kept(j):
        return remote(final.at[j, kept], final.at[j, kept], f_ss.at[0, j], f_rs.at[0, j], outward)

    def two_out_rest(j):
        return remote(final.at[j, rest], final.at[j, rest], f_ss.at[1, j], f_rs.at[1, j], outward)

    down = a_h.shape[1] // (2 * PANEL)
    outer_cols = features // PANEL
    raw = dict(x=(x_h, 0), ctx=(ctx_h, 1), df=(df_h, 2), mid=(mid_h, 3))

    def left_of(who, j):
        late = jnp.minimum(j // down, 1)
        even = 2 * (1 - late) + late * (1 - jnp.minimum(j // (down + outer_cols), 1))
        odd = 2 * (1 - late) + 3 * late
        return who * odd + (1 - who) * even

    def columns(col):
        return pl.ds(pl.multiple_of(col * PANEL, PANEL), PANEL)

    def fetch_down(who, j, ring, sem):
        return pltpu.make_async_copy(a_h.at[:, columns(who * down + j)], ring.at[j % RING], sem.at[j % RING])

    def fetch_up(j, ring, sem):
        return pltpu.make_async_copy(du_h.at[:, columns(j - down)], ring.at[j % RING], sem.at[j % RING])

    def fetch(who, j, ring, sem):
        when(j < down, lambda: fetch_down(who, j, ring, sem).start())
        when((j >= down) & (j < last) & (who == 1), lambda: fetch_up(j, ring, sem).start())

    def right(who, j, ring, sem, use):
        def from_ring():
            pltpu.make_async_copy(a_h.at[:, columns(0)], ring.at[j % RING], sem.at[j % RING]).wait()
            use(ring[j % RING])

        when((j < down) | ((j < last) & (who == 1)), from_ring)
        when((j >= down) & (j < down + outer_cols) & (who == 0), lambda: use(do[:, columns(j - down)]))
        when(
            (j >= down + outer_cols) & (j < last) & (who == 0), lambda: use(qkv[:, columns(j - down - outer_cols)])
        )

    def to_out(j):
        late = jnp.minimum(j // down, 1)
        even = jnp.where(j < down + outer_cols, j - down + 3 * outer_cols, j - down - outer_cols)
        col = (1 - late) * (4 * outer_cols + j) + late * (core * (j - down) + (1 - core) * even)
        return pltpu.make_async_copy(final.at[j], out_h.at[:, columns(col)], out_sem.at[j])


    def own_send(src):
        return remote(src, halves.at[core], o_ss, o_rs, sibling)

    def own_from():
        return remote(dx_buf, halves.at[1 - core], o_ss, o_rs, sibling)

    def across_send(src):
        return remote(src, halves.at[core], c_ss, c_rs.at[core], beyond)

    def across_from(side):
        return remote(dx_buf, halves.at[side], c_ss, c_rs.at[side], beyond)

    def load_left(name):
        return pltpu.make_async_copy(raw[name][0], left, left_sem)

    loads = dict(dmid=(dmid_h, do), zh0=(zh0_h, dctx), qkv=(qkv_h, qkv), p=(p_h, p), y=(y_h, y_buf))
    names = list(loads)

    def load(name):
        return pltpu.make_async_copy(*loads[name], in_sem.at[names.index(name)])

    def load_wa(own, c):
        cols = pl.ds(c * features, features)
        return pltpu.make_async_copy((first_h if own else other_first_h).at[:, cols], wa.at[:, cols], a_sem.at[c])

    load_left("df").start()
    for j in range(RING):
        fetch_down(core, j, own_ring, own_sem).start()
        fetch_down(1 - core, j, sib_ring, ring_sem).start()
    load("dmid").start()
    load("zh0").start()
    for c in (3, 0, 1, 2):
        when(core == 0, lambda: load_wa(True, c).start())
        when(core == 1, lambda: load_wa(False, c).start())
    for name in ("qkv", "p", "y"):
        load(name).start()

    def turn(i):
        for b in range(features // BLOCK):
            grid = (BLOCK, features)
            eye = lax.broadcasted_iota(jnp.int32, grid, 0) + b * BLOCK == lax.broadcasted_iota(jnp.int32, grid, 1)
            left_t[i, pl.ds(b * BLOCK, BLOCK), :] = mm(eye.astype(f32).astype(bf16), left[...], NT).astype(bf16)

    def norm_panel(other):
        chosen = jnp.where(core == other, dnorm[2:4, :], dnorm[0:2, :])
        strips = [
            chosen[r : r + 1, c * PANEL : (c + 1) * PANEL]
            for r in range(2)
            for c in range(features // PANEL)
        ]
        return jnp.concatenate(strips + [jnp.zeros((16 - len(strips), PANEL), f32)], axis=0)

    pl.semaphore_wait(barrier, 5 + has_out.astype(jnp.int32))

    def stage_send(j):
        when(j >= RING, lambda: to_sibling(j - RING).wait_send())

        @pl.when(j == last)
        def _():
            sib_send[last % RING] = jnp.zeros((rows, PANEL), bf16)
            sib_send[last % RING, 0:16, :] = norm_panel(0).astype(bf16)

        def use(block):
            sib_send[j % RING] = mm(left_t[left_of(1 - core, j)], block).astype(bf16)

        right(1 - core, j, sib_ring, ring_sem, use)
        to_sibling(j).start()
        fetch(1 - core, j + RING, sib_ring, ring_sem)

    def stage_part(j):
        to_sibling(j).wait_recv()

        @pl.when(j == last)
        def _():
            part[last, 0:16, :] = (norm_panel(1) + part[last, 0:16, :].astype(f32)).astype(bf16)

        def use(block):
            own = mm(left_t[left_of(core, j)], block)
            part[j] = (own + part[j].astype(f32)).astype(bf16)

        right(core, j, own_ring, own_sem, use)
        fetch(core, j + RING, own_ring, own_sem)
        when(j % 2 == 0, lambda: one_y(j).start())
        when((j % 2 == 1) & (dist == depth) & (depth > 0), lambda: two_in(j).start())
        when((j % 2 == 1) & (dist == depth) & (depth == 0), lambda: two_mid(j).start())

    def one_halves(j):
        one_y(j).wait_recv()
        part[j, mine, :] = (part[j, mine, :].astype(f32) + y1[j // 2].astype(f32)).astype(bf16)
        when((dist == depth) & (dist > 0), lambda: one_in(j).start())
        when((dist == depth) & inner, lambda: one_mid(j).start())

    def one_chain(j):
        one_in(j).wait_recv()
        part[j, mine, :] = (part[j, mine, :].astype(f32) + zin1[j // 2].astype(f32)).astype(bf16)
        when(dist > 0, lambda: one_in(j).start())
        when(inner, lambda: one_mid(j).start())

    def one_total(j):
        one_mid(j).wait_recv()
        final[j, mine, :] = (part[j, mine, :].astype(f32) + mid1[j // 2].astype(f32)).astype(bf16)
        when(has_out, lambda: one_out(j).start())
        one_back(j).start()

    def one_spread(j):
        one_out(j).wait_recv()
        when(has_out, lambda: one_out(j).start())
        one_back(j).start()

    def two_chain(j):
        two_in(j).wait_recv()
        part[j] = (part[j].astype(f32) + zin2[j // 2].astype(f32)).astype(bf16)
        when(dist > 0, lambda: two_in(j).start())
        when(inner, lambda: two_mid(j).start())

    def two_halves(j):
        two_mid(j).wait_recv()
        part[j, kept, :] = (part[j, kept, :].astype(f32) + mid2[j // 2].astype(f32)).astype(bf16)
        two_y(j).start()

    def two_total(j):
        two_y(j).wait_recv()
        final[j, kept, :] = (part[j, kept, :].astype(f32) + y2[j // 2].astype(f32)).astype(bf16)
        two_swap(j).start()
        when(has_out, lambda: two_out_kept(j).start())

    def two_swapped(j):
        two_swap_in(j).wait_recv()
        when(has_out, lambda: two_out_rest(j).start())

    def two_spread_kept(j):
        two_out_kept(j).wait_recv()
        when(has_out, lambda: two_out_kept(j).start())

    def two_spread_rest(j):
        two_out_rest(j).wait_recv()
        when(has_out, lambda: two_out_rest(j).start())

    def finish(j):
        when(j % 2 == 0, lambda: one_back_in(j).wait_recv())

        @pl.when(j == last)
        def _():
            norm_out[...] = final[last, 0:16, :].astype(f32)

        when(j < last, lambda: to_out(j).start())

    last_lag = 7 + 4 * depth

    pairs = features // PAIR
    items = tokens // BLOCK * pairs

    def turn_next(name, following):
        load_left(name).wait()
        turn(raw[name][1])
        if following:
            load_left(following).start()

    def attention_begin():
        load("dmid").wait()
        load("zh0").wait()
        load_wa(True, 3).wait()
        attention_back_begin(do, norms, wa, dctx, rstd0, do, dctx, acc, dnorm)

    def send_rows():
        load("y").wait()

        @pl.when(at_head == 1)
        def _():
            leading = jnp.max(lead_picks(lengths, core, True), axis=1, keepdims=True) > 0
            dx_buf[...] = jnp.where(leading, 0.0, acc[...]).astype(bf16)

        @pl.when(at_head == 0)
        def _():
            dx_buf[...] = acc[...].astype(bf16)

        def go(own, across):
            across_send(across).start()
            when(~inside, lambda: own_send(own).start())

            @pl.when(inside)
            def _():
                halves[core] = own[...]

        when(at_head == 1, go, y_buf, dx_buf)
        when(at_head == 0, go, dx_buf, y_buf)

    dnorm[...] = dnorm_in[...]
    turn_next("df", "mid")

    def step(t, carry):
        def at(lag, kind, cond, run):
            j = t - lag
            ok = (j >= 0) & (j < panels)
            if kind is not None:
                ok = ok & (j % 2 == kind)
            if cond is not None:
                ok = ok & cond
            when(ok, run, j)

        at(7 + 2 * (depth + dist), 1, dist > 0, two_spread_rest)
        at(5 + 2 * (depth + dist), 1, dist > 0, two_spread_kept)
        at(5 + 2 * (depth + dist), 0, dist > 0, one_spread)
        at(7 + 2 * depth, 1, inner, two_swapped)
        at(5 + 2 * depth, 1, inner, two_total)
        at(5 + 2 * depth, 0, inner, one_total)
        at(3 + 2 * depth, 1, inner, two_halves)
        at(3 + 2 * (depth - dist), 0, dist < depth, one_chain)
        at(1 + 2 * (depth - dist), 1, dist < depth, two_chain)
        at(3, 0, None, one_halves)
        at(1, None, None, stage_part)
        at(0, None, None, stage_send)
        at(last_lag + 1, None, None, finish)
        when(t == 0, attention_begin)
        item = t - 1
        when(t == 1, lambda: [load("qkv").wait(), load("p").wait()])
        when((item >= 0) & (item < items), lambda: attention_back_item(item // pairs, item % pairs, qkv, p, dctx))
        when(t == 2, turn_next, "mid", "ctx")
        when(t == 4, turn_next, "ctx", "x")
        when(t == 6, turn_next, "x", None)
        for c in range(3):
            when(t == items + 1 + c, lambda: [load_wa(True, c).wait(), attention_back_end(c, wa, qkv, acc)])
        when(t == items + 4, send_rows)
        return carry

    lax.fori_loop(0, panels + last_lag + 1, step, 0)

    @pl.when(inside)
    def _():
        own_from().wait_recv()

    @pl.when(~inside)
    def _():
        own_send(dx_buf).wait_send()
        across_from(0).wait_recv()
        across_from(1).wait_recv()

    across_send(dx_buf).wait_send()
    rows_done = pltpu.make_async_copy(halves, halves_h, h_sem)
    rows_done.start()

    def drain(j, carry):
        when(j >= panels - RING, lambda: to_sibling(j).wait_send())
        when(j < last, lambda: to_out(j).wait())

        @pl.when(j % 2 == 0)
        def _():
            one_y(j).wait_send()
            when(dist > 0, lambda: one_in(j).wait_send())
            when(inner, lambda: one_mid(j).wait_send())
            when(has_out, lambda: one_out(j).wait_send())
            one_back(j).wait_send()

        @pl.when(j % 2 == 1)
        def _():
            when(dist > 0, lambda: two_in(j).wait_send())

            @pl.when(inner)
            def _():
                two_mid(j).wait_send()
                two_y(j).wait_send()
                two_swap(j).wait_send()

            @pl.when(has_out)
            def _():
                two_out_kept(j).wait_send()
                two_out_rest(j).wait_send()

        return carry

    lax.fori_loop(0, panels, drain, 0)
    rows_done.wait()


def reduce_gradients(lengths, norms, weights, saved, chain):
    tokens, features = saved["x"].shape
    ff = saved["a"].shape[1]
    width = ff + ff // 2
    panels = width // PANEL + 1
    evens, odds = (panels + 1) // 2, panels // 2
    h = features // 2
    one = pltpu.SemaphoreType.DMA
    arrays = [saved[k] for k in ("x", "ctx", "mid", "a", "df", "du", "dmid", "zh0", "qkv", "p", "y")]
    return pl.pallas_call(
        functools.partial(reduce_kernel, chain),
        out_shape=[S((features, width), bf16), S((16, PANEL), f32), S((2, tokens, features), bf16)],
        in_specs=[IN_SMEM] + [IN_VMEM] * 3 + [ANY] * 13,
        out_specs=[ANY, IN_VMEM, ANY],
        scratch_shapes=[
            vm(tokens, features), vm(4, features, tokens), vm(RING, tokens, PANEL), vm(RING, tokens, PANEL),
            vm(RING, features, PANEL), vm(panels, features, PANEL),
            vm(evens, h, PANEL), vm(evens, h, PANEL), vm(evens, h, PANEL),
            vm(odds, features, PANEL), vm(odds, h, PANEL), vm(odds, h, PANEL),
            vm(panels, features, PANEL), vm(2, tokens, features),
            vm(features, ff), vm(tokens, 3 * features), pltpu.VMEM(saved["p"].shape, bf16), vm(tokens, features),
            vm(tokens, features), pltpu.VMEM((tokens, features), f32), vm(tokens, features),
            pltpu.VMEM((4, features), f32),
            one, dma(RING), dma(RING), dma(panels), dma(RING), dma(panels),
            dma(evens), dma(evens), dma(evens), dma(evens), dma(evens), dma(evens),
            dma(odds), dma(odds), dma(odds), dma(odds), dma(odds), dma(odds), dma(3, panels), dma(2, panels),
            one, one, one, dma(2), one, dma(ff // features), dma(5),
        ],
        compiler_params=params(3),
        name="reduce_gradients",
    )(lengths, saved["dnorm"], norms, saved["rstd0"], *arrays, weights[0], weights[2])


def finish_kernel(lengths, total, halves, norm_in, first_out, second_out, rows_out, gain_out, shift_out):
    step = pl.program_id(0)
    features = rows_out.shape[1]
    wide = first_out.shape[1]
    first_out[...] = total[:, pl.ds(0, wide)].astype(f32)
    second_out[...] = total[:, pl.ds(wide, second_out.shape[1])].astype(f32)
    size = rows_out.shape[0]
    row = step // (SEQ // size)
    _, _, first = span_scalars(lengths, row)
    at = lax.broadcasted_iota(jnp.int32, (size, BLOCK), 0) + step % (SEQ // size) * size
    out = None
    for side in range(2):
        hot = at == places(first, side, (size, BLOCK), 1)
        part = mm(hot.astype(f32).astype(bf16), halves[side])
        out = part if out is None else out + part
    rows_out[...] = out
    strips = features // PANEL
    for r, ref in enumerate((gain_out, shift_out)):
        ref[...] = jnp.concatenate([norm_in[r * strips + c : r * strips + c + 1, :] for c in range(strips)], axis=1)


def finish(lengths, total, halves, norm_in, ff):
    features, width = total.shape
    tokens = halves.shape[1]
    size = BLOCK
    steps = 2 * tokens // size
    part = features // steps
    row_spec = pl.BlockSpec((1, features), lambda i: (0, 0))
    return pl.pallas_call(
        finish_kernel,
        grid=(steps,),
        out_shape=[
            S((features, ff), f32), S((features, width - ff), f32), S((2 * tokens, features), f32),
            S((1, features), f32), S((1, features), f32),
        ],
        in_specs=[
            IN_SMEM, pl.BlockSpec((part, width), lambda i: (i, 0)),
            pl.BlockSpec((2, BLOCK, features), lambda i: (0, i // (SEQ // size), 0)), IN_VMEM,
        ],
        out_specs=[
            pl.BlockSpec((part, ff), lambda i: (i, 0)), pl.BlockSpec((part, width - ff), lambda i: (i, 0)),
            pl.BlockSpec((size, features), lambda i: (i, 0)), row_spec, row_spec,
        ],
        compiler_params=params(None),
        name="finish",
    )(lengths, total, halves, norm_in)


def per_device(section_rows, span_lengths, first_weights, second_weights, norm_gain, norm_shift):
    first, second = first_weights[0], second_weights[0]
    norm_own = jnp.concatenate([norm_gain, norm_shift], axis=0)
    main, aux, other_first, other_second, norms, lead = start(section_rows[0], span_lengths, first, second, norm_own)
    weights = (first, second, other_first, other_second)
    saved = middle(span_lengths, main, aux, lead, norms, weights)
    total, norm_total, halves = reduce_gradients(
        span_lengths, norms, weights, saved, lax.axis_size("dp") // 2
    )
    d_first, d_second, rows, gain, shift = finish(span_lengths, total, halves, norm_total, first.shape[1])
    return rows[None], d_first[None], d_second[None], gain, shift


def solution(mesh):
    in_specs = (
        P("section", "dp", None),
        P("dp", None),
        P("section", None, None),
        P("section", None, None),
        P("section", None),
        P("section", None),
    )
    out_specs = (
        P("section", "dp", None),
        P("section", None, None),
        P("section", None, None),
        P("section", None),
        P("section", None),
    )
    return jax.shard_map(
        per_device, mesh=mesh, in_specs=in_specs, out_specs=out_specs, check_vma=False
    )
```

```python
import functools

import jax
import jax.numpy as jnp
from jax import lax
from jax.experimental import pallas as pl
from jax.experimental.pallas import tpu as pltpu
from jax.sharding import PartitionSpec as P

HEAD_DIM = 64
PAIR = 2 * HEAD_DIM
BLOCK = 256
SEQ = 512
LEADS = 16
VMEM_LIMIT = 60 << 20
MESH = pl.DeviceIdType.MESH
f32 = jnp.float32
bf16 = jnp.bfloat16
epsilon = 1e-12
NN = (((1,), (0,)), ((), ()))
NT = (((1,), (1,)), ((), ()))
TN = (((0,), (0,)), ((), ()))
LOG2E = 1.4426950408889634


def mm(a, b, dims=NN):
    return lax.dot_general(a, b, dims, preferred_element_type=f32)


def when(cond, step, *args):
    @pl.when(cond)
    def _():
        step(*args)


def remote(src, dst, ss, rs, target):
    return pltpu.make_async_remote_copy(
        src_ref=src, dst_ref=dst, send_sem=ss, recv_sem=rs, device_id=target, device_id_type=MESH
    )


def gelu_and_slope(u):
    bell = jnp.exp2(u * u * (-0.5 * LOG2E))
    t = 1.0 / (1.0 + (0.3275911 * 0.5**0.5) * jnp.abs(u))
    poly = t * (0.127414796 + t * (-0.142248368 + t * (0.7107068705 + t * (-0.7265760135 + t * 0.5307027145))))
    tail = poly * bell
    cdf = jnp.where(u < 0, tail, 1.0 - tail)
    return u * cdf, cdf + u * bell * 0.3989422804014327


def normalize(z):
    centered = z - jnp.mean(z, axis=-1, keepdims=True)
    rstd = lax.rsqrt(jnp.mean(centered * centered, axis=-1, keepdims=True) + epsilon)
    return centered * rstd, rstd


def normalize_back(zh, rstd, gain, dy):
    g = dy * gain
    mean_g = jnp.mean(g, axis=-1, keepdims=True)
    mean_gz = jnp.mean(g * zh, axis=-1, keepdims=True)
    dz = rstd * (g - mean_g - zh * mean_gz)
    return dz, jnp.sum(dy * zh, axis=0, keepdims=True), jnp.sum(dy, axis=0, keepdims=True)


def span_scalars(lengths, row):
    ends, starts, first, total = [], [], 0, 0
    for j in range(lengths.shape[1]):
        size = lengths[row, j]
        starts.append(total)
        first = first + jnp.where(size == BLOCK, total, 0)
        total = total + size
        ends.append(total)
    return ends, starts, first


def places(first, core, shape, axis):
    at = lax.broadcasted_iota(jnp.int32, shape, axis) + (first + core * BLOCK)
    return jnp.where(at >= SEQ, at - SEQ, at)


def mask_bias(lengths, row, core):
    ends, _, first = span_scalars(lengths, row)

    def segment(at):
        return sum((at >= end).astype(jnp.int32) for end in ends)

    rows = segment(places(first, core, (BLOCK, BLOCK), 0))
    cols = segment(places(first, core, (BLOCK, BLOCK), 1))
    return jnp.where(rows == cols, 0.0, -1e30)


def lead_picks(lengths, core, by_rows):
    parts = []
    per_row = lengths.shape[1] - 1
    shape = (BLOCK, LEADS) if by_rows else (LEADS, BLOCK)
    for row in range(lengths.shape[0]):
        _, starts, first = span_scalars(lengths, row)
        at = places(first, core, shape, 0 if by_rows else 1)
        slot = lax.broadcasted_iota(jnp.int32, shape, 1 if by_rows else 0)
        hit = sum(
            ((slot == row * per_row + j) & (at == starts[j])).astype(jnp.int32) for j in range(per_row)
        )
        parts.append(hit.astype(f32))
    return jnp.concatenate(parts, axis=0 if by_rows else 1)


def lane_masks():
    return lax.broadcasted_iota(jnp.int32, (BLOCK, PAIR), 1) < HEAD_DIM


def forward_pass(x, lengths, core, norms, wa, wu, wd, qkv, ctx, mid, acc, ready, save):
    tokens, features = x.shape
    pairs = features // PAIR
    first = lane_masks()
    zero = jnp.zeros((BLOCK, PAIR), bf16)

    def block_step(b, carry):
        rows = pl.ds(pl.multiple_of(b * BLOCK, BLOCK), BLOCK)
        bias = mask_bias(lengths, b, core)
        for h in range(pairs):
            q = qkv[rows, pl.ds(h * PAIR, PAIR)]
            k = qkv[rows, pl.ds(features + h * PAIR, PAIR)]
            v = qkv[rows, pl.ds(2 * features + h * PAIR, PAIR)]
            total = None
            for side in range(2):
                own = first if side == 0 else ~first
                s = mm(q, jnp.where(own, k, zero), NT) * (HEAD_DIM**-0.5) + bias
                e = jnp.exp(s - jnp.max(s, axis=-1, keepdims=True))
                pr = (e * (1.0 / jnp.sum(e, axis=-1, keepdims=True))).astype(bf16)
                save["p"][b, h, :, pl.ds(side * BLOCK, BLOCK)] = pr
                part = mm(pr, jnp.where(own, v, zero))
                total = part if total is None else total + part
            ctx[rows, pl.ds(h * PAIR, PAIR)] = total.astype(bf16)
        return carry

    lax.fori_loop(0, tokens // BLOCK, block_step, 0)
    ready["a"](3)
    zn, r = normalize(x[...].astype(f32) + mm(ctx[...], wa[:, pl.ds(3 * features, features)]))
    save["keep"]("p", "ctx")
    save["rstd0"][...] = r
    save["zh0"][...] = zn.astype(bf16)
    mid[...] = (zn * norms[0, 0:1, :] + norms[0, 1:2, :]).astype(bf16)
    acc[...] = mid[...].astype(f32)
    save["keep"]("zh0", "mid")
    pieces = wu.shape[1] // features
    cols = [pl.ds(c * features, features) for c in range(pieces)]
    ready["u"](0)
    ahead = mm(mid[...], wu[:, cols[0]])
    for c in range(pieces):
        u = ahead
        if c + 1 < pieces:
            ready["u"](c + 1)
            ahead = mm(mid[...], wu[:, cols[c + 1]])
        act, slope = gelu_and_slope(u)
        act = act.astype(bf16)
        save["a"][:, cols[c]] = act
        save["slope"][:, cols[c]] = slope.astype(bf16)
        save["keep_cols"](c)
        ready["d"](c)
        acc[...] += mm(act, wd[:, cols[c]], NT)
    zn, r = normalize(acc[...])
    save["rstd1"][...] = r
    save["zh1"][...] = zn.astype(bf16)
    return (zn * norms[1, 0:1, :] + norms[1, 1:2, :]).astype(bf16)


def feed_forward_back(dy, norms, wu, wd, slope, zh1, rstd1, df, du, acc, dnorm, ready):
    features = wu.shape[0]
    dz, dgain, dshift = normalize_back(zh1[...].astype(f32), rstd1[...], norms[1, 0:1, :], dy.astype(f32))
    dnorm[2:3, :] = dgain
    dnorm[3:4, :] = dshift
    df[...] = dz.astype(bf16)
    acc[...] = dz
    for c in range(wu.shape[1] // features):
        cols = pl.ds(c * features, features)
        ready["d"](c)
        da = mm(df[...], wd[:, cols])
        ready["du"](c)
        g = (da * slope[:, cols].astype(f32)).astype(bf16)
        du[:, cols] = g
        ready["u"](c)
        acc[...] += mm(g, wu[:, cols], NT)


def attention_back_begin(d_mid, norms, wa, zh0, rstd0, do, dctx, acc, dnorm):
    tokens, features = acc.shape
    dgain = dshift = None
    for b in range(tokens // BLOCK):
        rows = pl.ds(b * BLOCK, BLOCK)
        dz, dg, ds = normalize_back(
            zh0[rows, :].astype(f32), rstd0[rows, :], norms[0, 0:1, :], d_mid[rows, :].astype(f32)
        )
        dgain, dshift = (dg, ds) if b == 0 else (dgain + dg, dshift + ds)
        acc[rows, :] = dz
        do[rows, :] = dz.astype(bf16)
        dctx[rows, :] = mm(dz.astype(bf16), wa[:, pl.ds(3 * features, features)], NT).astype(bf16)
    dnorm[0:1, :] = dgain
    dnorm[1:2, :] = dshift


def attention_back_item(b, h, qkv, p, dctx, out):
    features = dctx.shape[1]
    first = lane_masks()
    zero = jnp.zeros((BLOCK, PAIR), bf16)
    scale = HEAD_DIM**-0.5
    rows = pl.ds(pl.multiple_of(b * BLOCK, BLOCK), BLOCK)
    at = [pl.ds(pl.multiple_of(part * features + h * PAIR, PAIR), PAIR) for part in range(3)]
    q, k, v = (qkv[rows, cols] for cols in at)
    dc = dctx[rows, at[0]]
    dq = dk = dv = None
    for side in range(2):
        own = first if side == 0 else ~first
        pr = p[b, h, :, pl.ds(side * BLOCK, BLOCK)]
        prf = pr.astype(f32)
        dp = mm(dc, jnp.where(own, v, zero), NT)
        r = jnp.sum(dp * prf, axis=-1, keepdims=True)
        ds = (prf * (dp - r)).astype(bf16)
        parts = (
            mm(ds, jnp.where(own, k, zero)),
            mm(ds, jnp.where(own, q, zero), TN),
            mm(pr, jnp.where(own, dc, zero), TN),
        )
        if dq is None:
            dq, dk, dv = parts
        else:
            dq, dk, dv = dq + parts[0], dk + parts[1], dv + parts[2]
    out[rows, at[0]] = (dq * scale).astype(bf16)
    out[rows, at[1]] = (dk * scale).astype(bf16)
    out[rows, at[2]] = dv.astype(bf16)


def attention_back_end(part, wa, dqkv, acc):
    features = wa.shape[0]
    cols = pl.ds(part * features, features)
    for b in range(acc.shape[0] // BLOCK):
        rows = pl.ds(b * BLOCK, BLOCK)
        acc[rows, :] += mm(dqkv[rows, cols], wa[:, cols], NT)


def lead_forward(x, lengths, core, norms, wa, wu, wd, kv, ready):
    tokens, features = x.shape
    per_row = lengths.shape[1] - 1
    own = mm(lead_picks(lengths, core, False).astype(bf16), x[...]).astype(bf16)
    for c in (1, 2):
        ready["a"](c)
        kv[:, pl.ds(c * features, features)] = mm(x[...], wa[:, pl.ds(c * features, features)]).astype(bf16)
    ready["a"](0)
    q = mm(own, wa[:, pl.ds(0, features)]).astype(bf16)
    parts = []
    for row in range(tokens // BLOCK):
        ends, _, first = span_scalars(lengths, row)
        at = places(first, core, (LEADS, BLOCK), 1)
        keys = sum((at >= end).astype(jnp.int32) for end in ends)
        span = lax.broadcasted_iota(jnp.int32, (LEADS, BLOCK), 0) - row * per_row
        parts.append(jnp.where((span == keys) & (span < per_row), 0.0, -1e30))
    bias = jnp.concatenate(parts, axis=1)
    ctx = []
    for h in range(features // PAIR):
        k = kv[:, pl.ds(features + h * PAIR, PAIR)]
        v = kv[:, pl.ds(2 * features + h * PAIR, PAIR)]
        lanes = lax.broadcasted_iota(jnp.int32, (LEADS, PAIR), 1) < HEAD_DIM
        total = None
        for side in range(2):
            mine = lanes if side == 0 else ~lanes
            s = mm(jnp.where(mine, q[:, h * PAIR : (h + 1) * PAIR], jnp.zeros((), bf16)), k, NT) * (HEAD_DIM**-0.5) + bias
            e = jnp.exp(s - jnp.max(s, axis=-1, keepdims=True))
            part = mm((e * (1.0 / jnp.sum(e, axis=-1, keepdims=True))).astype(bf16), v)
            total = jnp.where(lanes, part, 0.0) if side == 0 else jnp.where(lanes, total, part)
        ctx.append(total.astype(bf16))
    ready["a"](3)
    zn, _ = normalize(own.astype(f32) + mm(jnp.concatenate(ctx, axis=1), wa[:, pl.ds(3 * features, features)]))
    mid = (zn * norms[0, 0:1, :] + norms[0, 1:2, :]).astype(bf16)
    out = mid.astype(f32)
    for c in range(wu.shape[1] // features):
        cols = pl.ds(c * features, features)
        ready["u"](c)
        act, _ = gelu_and_slope(mm(mid, wu[:, cols]))
        ready["d"](c)
        out = out + mm(act.astype(bf16), wd[:, cols], NT)
    zn, _ = normalize(out)
    return (zn * norms[1, 0:1, :] + norms[1, 1:2, :]).astype(bf16)


def front_kernel(
    rows_h, lengths, first_h, second_h, gain_in, shift_in,
    x_h, y_h, qkv_h, p_h, ctx_h, zh0_h, mid_h, a_h, df_h, du_h, dmid_h, other_first_h, rstd0, dnorm, norms,
    wa, wu, wd, x, qkv, p, ctx, zh0, mid, a, slope, up, zh1, rstd1, do, dctx, acc, d_att,
    lead_slope, grad_own, grad_in, row_own, row_in, norm_pair,
    row_sem, load, w_ss, w_rs, d_ss, d_rs, n_ss, n_rs, m_ss, m_rs, x_ss, x_rs, r_ss, r_rs, l_ss, l_rs, out_sem, col_sem, other_sem,
):
    sec = lax.axis_index("section")
    core = sec % 2
    at_head = sec // 2
    tokens, features = x.shape
    blocks = tokens // BLOCK
    pieces = wu.shape[1] // features
    half = wd.shape[1] // 2
    even, odd = core == 0, core == 1
    head, backbone = at_head == 1, at_head == 0
    sibling = {"section": sec + 1 - 2 * core}
    peer = {"section": (sec + 2) % 4}
    halves = (do, dctx)
    y, df, dmid = mid, ctx, x
    barrier = pltpu.get_barrier_semaphore()
    for step in range(1, 4):
        target = {"section": (sec + step) % 4}
        pl.semaphore_signal(barrier, inc=1, device_id=target, device_id_type=MESH)

    def cols(c):
        return pl.ds(c * features, features)

    def block(b):
        return pl.ds(b * BLOCK, BLOCK)

    def local_first(c, dst):
        return pltpu.make_async_copy(first_h.at[:, cols(c)], dst.at[:, cols(c)], load.at[c])

    def sent_first(c, dst):
        return remote(first_h.at[:, cols(c)], dst.at[:, cols(c)], w_ss.at[c], w_rs.at[c], sibling)

    def local_second(side):
        return pltpu.make_async_copy(second_h, wd.at[:, pl.ds(side * half, half)], load.at[pieces])

    def sent_second(side):
        return remote(second_h, wd.at[:, pl.ds(side * half, half)], d_ss, d_rs, sibling)

    def row_load(row):
        return pltpu.make_async_copy(
            rows_h.at[pl.ds(row * SEQ, SEQ)], slope.at[pl.ds(0, SEQ), cols(row)], row_sem.at[row]
        )

    for row in range(blocks):
        row_load(row).start()
    turns = (1, 2, 0, *range(3, pieces))
    for c in range(pieces):
        when(even, lambda: local_first(turns[c], wa).start())
        when(odd, lambda: local_first(c, wu).start())
    when(even, lambda: local_second(0).start())
    when(odd, lambda: local_second(1).start())

    for row in range(blocks):
        _, _, first = span_scalars(lengths, row)
        row_load(row).wait()
        packed = slope[0:SEQ, cols(row)]
        for side in range(2):
            at = places(first, side, (BLOCK, SEQ), 0)
            hot = at == lax.broadcasted_iota(jnp.int32, (BLOCK, SEQ), 1)
            halves[side][block(row), :] = mm(hot.astype(f32).astype(bf16), packed).astype(bf16)
    norm_pair[core, 0:1, :] = gain_in[...]
    norm_pair[core, 1:2, :] = shift_in[...]

    def inner_send(dst):
        return remote(halves[1] if dst is x else halves[0], dst, m_ss, m_rs, sibling)

    def cross_send(dst, side, b):
        target = {"section": 2 + side} if dst is x else {"section": side}
        return remote(halves[side].at[block(b)], dst.at[block(b)], x_ss.at[side, b], x_rs.at[b], target)

    sent_norm = remote(norm_pair.at[core], norm_pair.at[core], n_ss, n_rs, sibling)
    norm_from = remote(norm_pair.at[1 - core], norm_pair.at[1 - core], n_ss, n_rs, sibling)
    pl.semaphore_wait(barrier, 3)
    pairs_of = [(side, b) for b in range(blocks) for side in range(2)]
    when(sec == 1, lambda: [cross_send(x, *at).start() for at in pairs_of])
    when(sec == 0, lambda: inner_send(x).start())
    sent_norm.start()
    for c in range(pieces):
        when(even, lambda: sent_first(turns[c], wa).start())
        when(odd, lambda: sent_first(c, wu).start())
    when(even, lambda: sent_second(0).start())
    when(odd, lambda: sent_second(1).start())
    when(sec == 3, lambda: inner_send(up).start())
    when(sec == 2, lambda: [cross_send(up, *at).start() for at in pairs_of])

    @pl.when(sec == 0)
    def _():
        x[...] = halves[0][...]

    @pl.when(sec == 3)
    def _():
        up[...] = halves[1][...]

    norm_from.wait_recv()
    norms[...] = norm_pair[...]

    def ready_a(c):
        when(even, lambda: local_first(c, wa).wait())
        when(odd, lambda: sent_first(c, wa).wait_recv())

    def ready_u(c):
        when(odd, lambda: local_first(c, wu).wait())
        when(even, lambda: sent_first(c, wu).wait_recv())

    def ready_d(c):
        if c == 0:
            when(even, lambda: local_second(0).wait())
            when(odd, lambda: sent_second(0).wait_recv())
        if c == pieces // 2:
            when(odd, lambda: local_second(1).wait())
            when(even, lambda: sent_second(1).wait_recv())

    refs = dict(
        x=(x, x_h), y=(y, y_h), qkv=(qkv, qkv_h), p=(p, p_h), ctx=(ctx, ctx_h), zh0=(zh0, zh0_h), mid=(mid, mid_h),
        df=(df, df_h), du=(slope, du_h), dmid=(dmid, dmid_h),
    )
    order = list(refs)

    def store(name):
        return pltpu.make_async_copy(*refs[name], out_sem.at[order.index(name)])

    def store_cols(c):
        return pltpu.make_async_copy(a.at[:, cols(c)], a_h.at[:, cols(c)], col_sem.at[c])

    def keep(*names):
        for name in names:
            store(name).start()

    picks = lead_picks(lengths, core, True)
    leading = jnp.max(picks, axis=1, keepdims=True) > 0
    hot_leads = picks.astype(bf16)
    pick = lead_picks(lengths, core, False).astype(bf16)
    row_hop = remote(row_own, row_in, r_ss, r_rs, peer)

    @pl.when(backbone)
    def _():
        when(odd, lambda: inner_send(x).wait_recv())
        ready = dict(a=ready_a, u=ready_u, d=ready_d)
        row_own[...] = lead_forward(x, lengths, core, norms, wa, wu, wd, qkv, ready)
        row_hop.start()
        qkv[:, cols(0)] = mm(x[...], wa[:, cols(0)]).astype(bf16)

    @pl.when(head)
    def _():
        for c in range(3):
            ready_a(c)
        row_hop.wait_recv()
        for b in range(blocks):
            cross_send(x, 0, b).wait_recv()
            at = slice(b * BLOCK, (b + 1) * BLOCK)
            x[block(b), :] = jnp.where(leading[at], mm(hot_leads[at], row_in[...]).astype(bf16), x[block(b), :])
            for c in range(3):
                qkv[block(b), cols(c)] = mm(x[block(b), :], wa[:, cols(c)]).astype(bf16)

    keep("x", "qkv")
    at_first = {k: f for k, f in (("a", ready_a), ("u", ready_u), ("d", ready_d))}
    ready = {k: (lambda c, f=f: when(head, f, c)) for k, f in at_first.items()}
    save = dict(
        p=p, a=a, slope=slope, zh0=zh0, zh1=zh1, rstd0=rstd0, rstd1=rstd1, keep=keep,
        keep_cols=lambda c: store_cols(c).start(),
    )
    out = forward_pass(x, lengths, core, norms, wa, wu, wd, qkv, ctx, mid, acc, ready, save)
    for name in ("mid", "ctx", "x"):
        store(name).wait()
    y[...] = out
    keep("y")
    other = pltpu.make_async_copy(wa, other_first_h, other_sem)
    when(odd, lambda: other.start())
    lead_zh = mm(pick, zh1[...])
    left = jnp.broadcast_to(rstd1[...], (tokens, PAIR))
    total = jnp.zeros((LEADS, PAIR), f32)
    for _ in range(3):
        high = left.astype(bf16)
        left = left - high.astype(f32)
        total = total + mm(pick, high)
    lead_rstd = total[:, 0:1]

    @pl.when(backbone)
    def _():
        for b in range(blocks):
            cross_send(up, 0, b).wait_recv()
        row_hop.wait_send()
        for c in range(pieces):
            lead_slope[:, cols(c)] = mm(pick, slope[:, cols(c)]).astype(bf16)

    when(sec == 2, lambda: inner_send(up).wait_recv())
    when(sec == 0, lambda: inner_send(x).wait_send())
    when(sec == 3, lambda: inner_send(up).wait_send())
    when((sec == 1) | (sec == 2), lambda: [cross_send(x, *at).wait_send() for at in pairs_of])
    sent_norm.wait_send()
    for c in range(pieces):
        sent_first(c, wa).wait_send()
    sent_second(0).wait_send()
    none = {k: (lambda *_: None) for k in ("u", "d", "du")}
    feed_forward_back(up[...], norms, wu, wd, slope, zh1, rstd1, df, slope, acc, dnorm, none)
    dmid[...] = acc[...].astype(bf16)
    dnorm[0:2, :] = jnp.zeros((2, features), f32)
    for c in range(pieces):
        store_cols(c).wait()
    grad_hop = remote(grad_own, grad_in, l_ss, l_rs, peer)

    @pl.when(head)
    def _():
        keep("df", "du", "dmid")
        attention_back_begin(dmid, norms, wa, zh0, rstd0, do, dctx, acc, d_att)

        def block_step(b, carry):
            for h in range(features // PAIR):
                attention_back_item(b, h, qkv, p, dctx, a)
            return carry

        lax.fori_loop(0, blocks, block_step, 0)
        for part in range(3):
            attention_back_end(part, wa, a, acc)
        hi = acc[...].astype(bf16)
        lo = (acc[...] - hi.astype(f32)).astype(bf16)
        grad_own[...] = mm(pick, hi) + mm(pick, lo)
        grad_hop.start()
        grad_hop.wait_send()

    @pl.when(backbone)
    def _():
        base = mm(pick, up[...])
        grad_hop.wait_recv()
        dy = (base + grad_in[...]).astype(bf16).astype(f32)
        extra = dy - base
        dnorm[2:3, :] += jnp.sum(extra * lead_zh, axis=0, keepdims=True)
        dnorm[3:4, :] += jnp.sum(extra, axis=0, keepdims=True)
        dz, _, _ = normalize_back(lead_zh, lead_rstd, norms[1, 0:1, :], dy)
        lead_df = dz.astype(bf16)
        df[...] = jnp.where(leading, mm(hot_leads, lead_df).astype(bf16), df[...])
        keep("df")
        for c in range(pieces):
            g = (mm(lead_df, wd[:, cols(c)]) * lead_slope[:, cols(c)].astype(f32)).astype(bf16)
            slope[:, cols(c)] = jnp.where(leading, mm(hot_leads, g).astype(bf16), slope[:, cols(c)])
            dz = dz + mm(g, wu[:, cols(c)], NT)
        keep("du")
        dmid[...] = jnp.where(leading, mm(hot_leads, dz.astype(bf16)).astype(bf16), dmid[...])
        keep("dmid")

    for name in order:
        if name not in ("mid", "ctx", "x"):
            store(name).wait()
    when(odd, lambda: other.wait())


ANY = pl.BlockSpec(memory_space=pl.ANY)
IN_VMEM = pl.BlockSpec(memory_space=pltpu.VMEM)
IN_SMEM = pl.BlockSpec(memory_space=pltpu.SMEM)
S = jax.ShapeDtypeStruct


def vm(*shape):
    return pltpu.VMEM(shape, bf16)


def dma(*shape):
    return pltpu.SemaphoreType.DMA(shape)


def params(number):
    if number is None:
        return pltpu.CompilerParams(vmem_limit_bytes=VMEM_LIMIT)
    return pltpu.CompilerParams(vmem_limit_bytes=VMEM_LIMIT, collective_id=number, has_side_effects=True)


def front(rows_in, lengths, first, second, gain, shift):
    features, ff = first.shape
    tokens = rows_in.shape[0] // 2
    pieces = ff // features
    blocks, pairs = tokens // BLOCK, features // PAIR
    square = S((tokens, features), bf16)
    one = pltpu.SemaphoreType.DMA
    shapes = dict(
        x=square, y=square, qkv=S((tokens, 3 * features), bf16), p=S((blocks, pairs, BLOCK, 2 * BLOCK), bf16),
        ctx=square, zh0=square, mid=square, a=S((tokens, ff), bf16), df=square, du=S((tokens, ff), bf16), dmid=square,
        other_first=S(first.shape, bf16), rstd0=S((tokens, 1), f32), dnorm=S((4, features), f32),
        norms=S((2, 2, features), f32),
    )
    small = ("rstd0", "dnorm", "norms")
    wide = vm(features, ff)
    outs = pl.pallas_call(
        front_kernel,
        out_shape=list(shapes.values()),
        in_specs=[ANY, IN_SMEM, ANY, ANY, IN_VMEM, IN_VMEM],
        out_specs=[IN_VMEM if k in small else ANY for k in shapes],
        scratch_shapes=[wide, wide, wide]
        + [pltpu.VMEM(shapes[k].shape, bf16) for k in ("x", "qkv", "p", "ctx", "zh0", "mid", "a", "du")]
        + [
            vm(tokens, features), vm(tokens, features), pltpu.VMEM((tokens, 1), f32), vm(tokens, features),
            vm(tokens, features), pltpu.VMEM((tokens, features), f32), pltpu.VMEM((2, features), f32), vm(LEADS, ff),
            pltpu.VMEM((LEADS, features), f32), pltpu.VMEM((LEADS, features), f32), vm(LEADS, features), vm(LEADS, features),
            pltpu.VMEM((2, 2, features), f32),
            dma(blocks), dma(pieces + 1), dma(pieces), dma(pieces), one, one, one, one, one, one, dma(2, blocks), dma(blocks),
            one, one, one, one, dma(10), dma(pieces), one,
        ],
        compiler_params=params(1),
        name="front",
    )(rows_in, lengths, first, second, gain, shift)
    return dict(zip(shapes, outs))


PANEL = 128
RING = 4


def reduce_kernel(
    chain, lengths, dnorm_in, norms, rstd0, x_h, ctx_h, mid_h, a_h, df_h, du_h, dmid_h, zh0_h, qkv_h, p_h, y_h,
    first_h, other_first_h,
    out_h, norm_out, halves_h,
    left, left_t, own_ring, sib_ring, sib_send, part, y1, zin1, mid1, zin2, mid2, y2, final, halves,
    wa, qkv, p, do, dctx, acc, y_buf, dnorm,
    left_sem, own_sem, ring_sem, out_sem, sib_ss, sib_rs, y1_ss, y1_rs, z1_ss, z1_rs, m1_ss, m1_rs,
    z2_ss, z2_rs, m2_ss, m2_rs, y2_ss, y2_rs, f_ss, f_rs, o_ss, o_rs, c_ss, c_rs, h_sem, a_sem, in_sem,
):
    sec = lax.axis_index("section")
    dp = lax.axis_index("dp")
    core = sec % 2
    panels, rows, _ = final.shape
    tokens = acc.shape[0]
    half = rows // 2
    features = rows
    last = panels - 1
    spot = dp // 2
    side = spot // (chain // 2)
    depth = chain // 2 - 1
    dist = side * (spot - chain // 2) + (1 - side) * (chain // 2 - 1 - spot)
    inner = dist == 0
    y = dp % 2
    sibling = {"section": sec + 1 - 2 * core}
    across_y = {"dp": dp + 1 - 2 * y}
    inward = {"dp": dp + 2 - 4 * side}
    outward = {"dp": dp - 2 + 4 * side}
    has_out = dist < depth

    barrier = pltpu.get_barrier_semaphore()
    at_head = sec // 2
    dx_buf = dctx
    inside = (sec == 0) | (sec == 3)
    beyond = {"section": 2 - sec // 2}
    others = [{"section": (sec + step) % 4} for step in (1, 2, 3)]
    for target in (*others, across_y, inward):
        pl.semaphore_signal(barrier, inc=1, device_id=target, device_id_type=MESH)

    @pl.when(has_out)
    def _():
        pl.semaphore_signal(barrier, inc=1, device_id=outward, device_id_type=MESH)

    def rows_at(which):
        return pl.ds(pl.multiple_of(which * half, half), half)

    mine, theirs = rows_at(y), rows_at(1 - y)
    kept, rest = rows_at(side), rows_at(1 - side)

    def to_sibling(j):
        return remote(sib_send.at[j % RING], part.at[j], sib_ss.at[j % RING], sib_rs.at[j], sibling)

    def one_y(j):
        i = j // 2
        return remote(part.at[j, theirs], y1.at[i], y1_ss.at[i], y1_rs.at[i], across_y)

    def one_in(j):
        i = j // 2
        return remote(part.at[j, mine], zin1.at[i], z1_ss.at[i], z1_rs.at[i], inward)

    def one_mid(j):
        i = j // 2
        return remote(part.at[j, mine], mid1.at[i], m1_ss.at[i], m1_rs.at[i], inward)

    def one_out(j):
        return remote(final.at[j, mine], final.at[j, mine], f_ss.at[0, j], f_rs.at[0, j], outward)

    def one_back(j):
        return remote(final.at[j, mine], final.at[j, mine], f_ss.at[1, j], f_rs.at[1, j], across_y)

    def one_back_in(j):
        return remote(final.at[j, theirs], final.at[j, theirs], f_ss.at[1, j], f_rs.at[1, j], across_y)

    def two_in(j):
        i = j // 2
        return remote(part.at[j], zin2.at[i], z2_ss.at[i], z2_rs.at[i], inward)

    def two_mid(j):
        i = j // 2
        return remote(part.at[j, rest], mid2.at[i], m2_ss.at[i], m2_rs.at[i], inward)

    def two_y(j):
        i = j // 2
        return remote(part.at[j, kept], y2.at[i], y2_ss.at[i], y2_rs.at[i], across_y)

    def two_swap(j):
        return remote(final.at[j, kept], final.at[j, kept], f_ss.at[2, j], f_rs.at[1, j], inward)

    def two_swap_in(j):
        return remote(final.at[j, rest], final.at[j, rest], f_ss.at[2, j], f_rs.at[1, j], inward)

    def two_out_kept(j):
        return remote(final.at[j, kept], final.at[j, kept], f_ss.at[0, j], f_rs.at[0, j], outward)

    def two_out_rest(j):
        return remote(final.at[j, rest], final.at[j, rest], f_ss.at[1, j], f_rs.at[1, j], outward)

    down = a_h.shape[1] // (2 * PANEL)
    outer_cols = features // PANEL
    raw = dict(x=(x_h, 0), ctx=(ctx_h, 1), df=(df_h, 2), mid=(mid_h, 3))

    def left_of(who, j):
        late = jnp.minimum(j // down, 1)
        even = 2 * (1 - late) + late * (1 - jnp.minimum(j // (down + outer_cols), 1))
        odd = 2 * (1 - late) + 3 * late
        return who * odd + (1 - who) * even

    def columns(col):
        return pl.ds(pl.multiple_of(col * PANEL, PANEL), PANEL)

    def fetch_down(who, j, ring, sem):
        return pltpu.make_async_copy(a_h.at[:, columns(who * down + j)], ring.at[j % RING], sem.at[j % RING])

    def fetch_up(j, ring, sem):
        return pltpu.make_async_copy(du_h.at[:, columns(j - down)], ring.at[j % RING], sem.at[j % RING])

    def fetch(who, j, ring, sem):
        when(j < down, lambda: fetch_down(who, j, ring, sem).start())
        when((j >= down) & (j < last) & (who == 1), lambda: fetch_up(j, ring, sem).start())

    def right(who, j, ring, sem, use):
        def from_ring():
            pltpu.make_async_copy(a_h.at[:, columns(0)], ring.at[j % RING], sem.at[j % RING]).wait()
            use(ring[j % RING])

        when((j < down) | ((j < last) & (who == 1)), from_ring)
        when((j >= down) & (j < down + outer_cols) & (who == 0), lambda: use(do[:, columns(j - down)]))
        when(
            (j >= down + outer_cols) & (j < last) & (who == 0), lambda: use(qkv[:, columns(j - down - outer_cols)])
        )

    def to_out(j):
        late = jnp.minimum(j // down, 1)
        even = jnp.where(j < down + outer_cols, j - down + 3 * outer_cols, j - down - outer_cols)
        col = (1 - late) * (4 * outer_cols + j) + late * (core * (j - down) + (1 - core) * even)
        return pltpu.make_async_copy(final.at[j], out_h.at[:, columns(col)], out_sem.at[j])


    def own_send(src):
        return remote(src, halves.at[core], o_ss, o_rs, sibling)

    def own_from():
        return remote(dx_buf, halves.at[1 - core], o_ss, o_rs, sibling)

    def across_send(src):
        return remote(src, halves.at[core], c_ss, c_rs.at[core], beyond)

    def across_from(side):
        return remote(dx_buf, halves.at[side], c_ss, c_rs.at[side], beyond)

    def load_left(name):
        return pltpu.make_async_copy(raw[name][0], left, left_sem)

    loads = dict(dmid=(dmid_h, do), zh0=(zh0_h, dctx), qkv=(qkv_h, qkv), p=(p_h, p), y=(y_h, y_buf))
    names = list(loads)

    def load(name):
        return pltpu.make_async_copy(*loads[name], in_sem.at[names.index(name)])

    def load_wa(own, c):
        cols = pl.ds(c * features, features)
        return pltpu.make_async_copy((first_h if own else other_first_h).at[:, cols], wa.at[:, cols], a_sem.at[c])

    load_left("df").start()
    for j in range(RING):
        fetch_down(core, j, own_ring, own_sem).start()
        fetch_down(1 - core, j, sib_ring, ring_sem).start()
    load("dmid").start()
    load("zh0").start()
    for c in (3, 0, 1, 2):
        when(core == 0, lambda: load_wa(True, c).start())
        when(core == 1, lambda: load_wa(False, c).start())
    for name in ("qkv", "p", "y"):
        load(name).start()

    def turn(i):
        for b in range(features // BLOCK):
            grid = (BLOCK, features)
            eye = lax.broadcasted_iota(jnp.int32, grid, 0) + b * BLOCK == lax.broadcasted_iota(jnp.int32, grid, 1)
            left_t[i, pl.ds(b * BLOCK, BLOCK), :] = mm(eye.astype(f32).astype(bf16), left[...], NT).astype(bf16)

    def norm_panel(other):
        chosen = jnp.where(core == other, dnorm[2:4, :], dnorm[0:2, :])
        strips = [
            chosen[r : r + 1, c * PANEL : (c + 1) * PANEL]
            for r in range(2)
            for c in range(features // PANEL)
        ]
        return jnp.concatenate(strips + [jnp.zeros((16 - len(strips), PANEL), f32)], axis=0)

    pl.semaphore_wait(barrier, 5 + has_out.astype(jnp.int32))

    def stage_send(j):
        when(j >= RING, lambda: to_sibling(j - RING).wait_send())

        @pl.when(j == last)
        def _():
            sib_send[last % RING] = jnp.zeros((rows, PANEL), bf16)
            sib_send[last % RING, 0:16, :] = norm_panel(0).astype(bf16)

        def use(block):
            sib_send[j % RING] = mm(left_t[left_of(1 - core, j)], block).astype(bf16)

        right(1 - core, j, sib_ring, ring_sem, use)
        to_sibling(j).start()
        fetch(1 - core, j + RING, sib_ring, ring_sem)

    def stage_part(j):
        to_sibling(j).wait_recv()

        @pl.when(j == last)
        def _():
            part[last, 0:16, :] = (norm_panel(1) + part[last, 0:16, :].astype(f32)).astype(bf16)

        def use(block):
            own = mm(left_t[left_of(core, j)], block)
            part[j] = (own + part[j].astype(f32)).astype(bf16)

        right(core, j, own_ring, own_sem, use)
        fetch(core, j + RING, own_ring, own_sem)
        when(j % 2 == 0, lambda: one_y(j).start())
        when((j % 2 == 1) & (dist == depth) & (depth > 0), lambda: two_in(j).start())
        when((j % 2 == 1) & (dist == depth) & (depth == 0), lambda: two_mid(j).start())

    def one_halves(j):
        one_y(j).wait_recv()
        part[j, mine, :] = (part[j, mine, :].astype(f32) + y1[j // 2].astype(f32)).astype(bf16)
        when((dist == depth) & (dist > 0), lambda: one_in(j).start())
        when((dist == depth) & inner, lambda: one_mid(j).start())

    def one_chain(j):
        one_in(j).wait_recv()
        part[j, mine, :] = (part[j, mine, :].astype(f32) + zin1[j // 2].astype(f32)).astype(bf16)
        when(dist > 0, lambda: one_in(j).start())
        when(inner, lambda: one_mid(j).start())

    def one_total(j):
        one_mid(j).wait_recv()
        final[j, mine, :] = (part[j, mine, :].astype(f32) + mid1[j // 2].astype(f32)).astype(bf16)
        when(has_out, lambda: one_out(j).start())
        one_back(j).start()

    def one_spread(j):
        one_out(j).wait_recv()
        when(has_out, lambda: one_out(j).start())
        one_back(j).start()

    def two_chain(j):
        two_in(j).wait_recv()
        part[j] = (part[j].astype(f32) + zin2[j // 2].astype(f32)).astype(bf16)
        when(dist > 0, lambda: two_in(j).start())
        when(inner, lambda: two_mid(j).start())

    def two_halves(j):
        two_mid(j).wait_recv()
        part[j, kept, :] = (part[j, kept, :].astype(f32) + mid2[j // 2].astype(f32)).astype(bf16)
        two_y(j).start()

    def two_total(j):
        two_y(j).wait_recv()
        final[j, kept, :] = (part[j, kept, :].astype(f32) + y2[j // 2].astype(f32)).astype(bf16)
        two_swap(j).start()
        when(has_out, lambda: two_out_kept(j).start())

    def two_swapped(j):
        two_swap_in(j).wait_recv()
        when(has_out, lambda: two_out_rest(j).start())

    def two_spread_kept(j):
        two_out_kept(j).wait_recv()
        when(has_out, lambda: two_out_kept(j).start())

    def two_spread_rest(j):
        two_out_rest(j).wait_recv()
        when(has_out, lambda: two_out_rest(j).start())

    def finish(j):
        when(j % 2 == 0, lambda: one_back_in(j).wait_recv())

        @pl.when(j == last)
        def _():
            norm_out[...] = final[last, 0:16, :].astype(f32)

        when(j < last, lambda: to_out(j).start())

    last_lag = 7 + 4 * depth

    pairs = features // PAIR
    items = tokens // BLOCK * pairs

    def turn_next(name, following):
        load_left(name).wait()
        turn(raw[name][1])
        if following:
            load_left(following).start()

    def attention_begin():
        load("dmid").wait()
        load("zh0").wait()
        load_wa(True, 3).wait()
        attention_back_begin(do, norms, wa, dctx, rstd0, do, dctx, acc, dnorm)

    def send_rows():
        load("y").wait()

        @pl.when(at_head == 1)
        def _():
            leading = jnp.max(lead_picks(lengths, core, True), axis=1, keepdims=True) > 0
            dx_buf[...] = jnp.where(leading, 0.0, acc[...]).astype(bf16)

        @pl.when(at_head == 0)
        def _():
            dx_buf[...] = acc[...].astype(bf16)

        def go(own, across):
            across_send(across).start()
            when(~inside, lambda: own_send(own).start())

            @pl.when(inside)
            def _():
                halves[core] = own[...]

        when(at_head == 1, go, y_buf, dx_buf)
        when(at_head == 0, go, dx_buf, y_buf)

    dnorm[...] = dnorm_in[...]
    turn_next("df", "mid")

    def step(t, carry):
        def at(lag, kind, cond, run):
            j = t - lag
            ok = (j >= 0) & (j < panels)
            if kind is not None:
                ok = ok & (j % 2 == kind)
            if cond is not None:
                ok = ok & cond
            when(ok, run, j)

        at(7 + 2 * (depth + dist), 1, dist > 0, two_spread_rest)
        at(5 + 2 * (depth + dist), 1, dist > 0, two_spread_kept)
        at(5 + 2 * (depth + dist), 0, dist > 0, one_spread)
        at(7 + 2 * depth, 1, inner, two_swapped)
        at(5 + 2 * depth, 1, inner, two_total)
        at(5 + 2 * depth, 0, inner, one_total)
        at(3 + 2 * depth, 1, inner, two_halves)
        at(3 + 2 * (depth - dist), 0, dist < depth, one_chain)
        at(1 + 2 * (depth - dist), 1, dist < depth, two_chain)
        at(3, 0, None, one_halves)
        at(1, None, None, stage_part)
        at(0, None, None, stage_send)
        at(last_lag + 1, None, None, finish)
        when(t == 0, attention_begin)
        item = t - 1
        when(t == 1, lambda: [load("qkv").wait(), load("p").wait()])
        when((item >= 0) & (item < items), lambda: attention_back_item(item // pairs, item % pairs, qkv, p, dctx, qkv))
        when(t == 2, turn_next, "mid", "ctx")
        when(t == 4, turn_next, "ctx", "x")
        when(t == 6, turn_next, "x", None)
        for c in range(3):
            when(t == items + 1 + c, lambda: [load_wa(True, c).wait(), attention_back_end(c, wa, qkv, acc)])
        when(t == items + 4, send_rows)
        return carry

    lax.fori_loop(0, panels + last_lag + 1, step, 0)

    @pl.when(inside)
    def _():
        own_from().wait_recv()

    @pl.when(~inside)
    def _():
        own_send(dx_buf).wait_send()
        across_from(0).wait_recv()
        across_from(1).wait_recv()

    across_send(dx_buf).wait_send()
    rows_done = pltpu.make_async_copy(halves, halves_h, h_sem)
    rows_done.start()

    def drain(j, carry):
        when(j >= panels - RING, lambda: to_sibling(j).wait_send())
        when(j < last, lambda: to_out(j).wait())

        @pl.when(j % 2 == 0)
        def _():
            one_y(j).wait_send()
            when(dist > 0, lambda: one_in(j).wait_send())
            when(inner, lambda: one_mid(j).wait_send())
            when(has_out, lambda: one_out(j).wait_send())
            one_back(j).wait_send()

        @pl.when(j % 2 == 1)
        def _():
            when(dist > 0, lambda: two_in(j).wait_send())

            @pl.when(inner)
            def _():
                two_mid(j).wait_send()
                two_y(j).wait_send()
                two_swap(j).wait_send()

            @pl.when(has_out)
            def _():
                two_out_kept(j).wait_send()
                two_out_rest(j).wait_send()

        return carry

    lax.fori_loop(0, panels, drain, 0)
    rows_done.wait()


def reduce_gradients(lengths, first, saved, chain):
    tokens, features = saved["x"].shape
    ff = saved["a"].shape[1]
    width = ff + ff // 2
    panels = width // PANEL + 1
    evens, odds = (panels + 1) // 2, panels // 2
    h = features // 2
    one = pltpu.SemaphoreType.DMA
    arrays = [saved[k] for k in ("x", "ctx", "mid", "a", "df", "du", "dmid", "zh0", "qkv", "p", "y")]
    return pl.pallas_call(
        functools.partial(reduce_kernel, chain),
        out_shape=[S((features, width), bf16), S((16, PANEL), f32), S((2, tokens, features), bf16)],
        in_specs=[IN_SMEM] + [IN_VMEM] * 3 + [ANY] * 13,
        out_specs=[ANY, IN_VMEM, ANY],
        scratch_shapes=[
            vm(tokens, features), vm(4, features, tokens), vm(RING, tokens, PANEL), vm(RING, tokens, PANEL),
            vm(RING, features, PANEL), vm(panels, features, PANEL),
            vm(evens, h, PANEL), vm(evens, h, PANEL), vm(evens, h, PANEL),
            vm(odds, features, PANEL), vm(odds, h, PANEL), vm(odds, h, PANEL),
            vm(panels, features, PANEL), vm(2, tokens, features),
            vm(features, ff), vm(tokens, 3 * features), pltpu.VMEM(saved["p"].shape, bf16), vm(tokens, features),
            vm(tokens, features), pltpu.VMEM((tokens, features), f32), vm(tokens, features),
            pltpu.VMEM((4, features), f32),
            one, dma(RING), dma(RING), dma(panels), dma(RING), dma(panels),
            dma(evens), dma(evens), dma(evens), dma(evens), dma(evens), dma(evens),
            dma(odds), dma(odds), dma(odds), dma(odds), dma(odds), dma(odds), dma(3, panels), dma(2, panels),
            one, one, one, dma(2), one, dma(ff // features), dma(5),
        ],
        compiler_params=params(3),
        name="reduce_gradients",
    )(lengths, saved["dnorm"], saved["norms"], saved["rstd0"], *arrays, first, saved["other_first"])


def finish_kernel(lengths, total, halves, norm_in, first_out, second_out, rows_out, gain_out, shift_out):
    step = pl.program_id(0)
    features = rows_out.shape[1]
    wide = first_out.shape[1]
    first_out[...] = total[:, pl.ds(0, wide)].astype(f32)
    second_out[...] = total[:, pl.ds(wide, second_out.shape[1])].astype(f32)
    size = rows_out.shape[0]
    row = step // (SEQ // size)
    _, _, first = span_scalars(lengths, row)
    at = lax.broadcasted_iota(jnp.int32, (size, BLOCK), 0) + step % (SEQ // size) * size
    out = None
    for side in range(2):
        hot = at == places(first, side, (size, BLOCK), 1)
        part = mm(hot.astype(f32).astype(bf16), halves[side])
        out = part if out is None else out + part
    rows_out[...] = out
    strips = features // PANEL
    for r, ref in enumerate((gain_out, shift_out)):
        ref[...] = jnp.concatenate([norm_in[r * strips + c : r * strips + c + 1, :] for c in range(strips)], axis=1)


def finish(lengths, total, halves, norm_in, ff):
    features, width = total.shape
    tokens = halves.shape[1]
    size = BLOCK
    steps = 2 * tokens // size
    part = features // steps
    row_spec = pl.BlockSpec((1, features), lambda i: (0, 0))
    return pl.pallas_call(
        finish_kernel,
        grid=(steps,),
        out_shape=[
            S((features, ff), f32), S((features, width - ff), f32), S((2 * tokens, features), f32),
            S((1, features), f32), S((1, features), f32),
        ],
        in_specs=[
            IN_SMEM, pl.BlockSpec((part, width), lambda i: (i, 0)),
            pl.BlockSpec((2, BLOCK, features), lambda i: (0, i // (SEQ // size), 0)), IN_VMEM,
        ],
        out_specs=[
            pl.BlockSpec((part, ff), lambda i: (i, 0)), pl.BlockSpec((part, width - ff), lambda i: (i, 0)),
            pl.BlockSpec((size, features), lambda i: (i, 0)), row_spec, row_spec,
        ],
        compiler_params=params(None),
        name="finish",
    )(lengths, total, halves, norm_in)


def per_device(section_rows, span_lengths, first_weights, second_weights, norm_gain, norm_shift):
    first, second = first_weights[0], second_weights[0]
    saved = front(section_rows[0], span_lengths, first, second, norm_gain, norm_shift)
    total, norm_total, halves = reduce_gradients(span_lengths, first, saved, lax.axis_size("dp") // 2)
    d_first, d_second, rows, gain, shift = finish(span_lengths, total, halves, norm_total, first.shape[1])
    return rows[None], d_first[None], d_second[None], gain, shift


def solution(mesh):
    in_specs = (
        P("section", "dp", None),
        P("dp", None),
        P("section", None, None),
        P("section", None, None),
        P("section", None),
        P("section", None),
    )
    out_specs = (
        P("section", "dp", None),
        P("section", None, None),
        P("section", None, None),
        P("section", None),
        P("section", None),
    )
    return jax.shard_map(
        per_device, mesh=mesh, in_specs=in_specs, out_specs=out_specs, check_vma=False
    )
```

```python
import functools

import jax
import jax.numpy as jnp
from jax import lax
from jax.experimental import pallas as pl
from jax.experimental.pallas import tpu as pltpu
from jax.sharding import PartitionSpec as P

HEAD_DIM = 64
PAIR = 2 * HEAD_DIM
BLOCK = 256
SEQ = 512
LEADS = 16
VMEM_LIMIT = 60 << 20
MESH = pl.DeviceIdType.MESH
f32 = jnp.float32
bf16 = jnp.bfloat16
epsilon = 1e-12
NN = (((1,), (0,)), ((), ()))
NT = (((1,), (1,)), ((), ()))
TN = (((0,), (0,)), ((), ()))
LOG2E = 1.4426950408889634


def mm(a, b, dims=NN):
    return lax.dot_general(a, b, dims, preferred_element_type=f32)


def when(cond, step, *args):
    @pl.when(cond)
    def _():
        step(*args)


def remote(src, dst, ss, rs, target):
    return pltpu.make_async_remote_copy(
        src_ref=src, dst_ref=dst, send_sem=ss, recv_sem=rs, device_id=target, device_id_type=MESH
    )


def gelu_and_slope(u):
    bell = jnp.exp2(u * u * (-0.5 * LOG2E))
    t = 1.0 / (1.0 + (0.3275911 * 0.5**0.5) * jnp.abs(u))
    poly = t * (0.127414796 + t * (-0.142248368 + t * (0.7107068705 + t * (-0.7265760135 + t * 0.5307027145))))
    tail = poly * bell
    cdf = jnp.where(u < 0, tail, 1.0 - tail)
    return u * cdf, cdf + u * bell * 0.3989422804014327


def normalize(z):
    centered = z - jnp.mean(z, axis=-1, keepdims=True)
    rstd = lax.rsqrt(jnp.mean(centered * centered, axis=-1, keepdims=True) + epsilon)
    return centered * rstd, rstd


def normalize_back(zh, rstd, gain, dy):
    g = dy * gain
    mean_g = jnp.mean(g, axis=-1, keepdims=True)
    mean_gz = jnp.mean(g * zh, axis=-1, keepdims=True)
    dz = rstd * (g - mean_g - zh * mean_gz)
    return dz, jnp.sum(dy * zh, axis=0, keepdims=True), jnp.sum(dy, axis=0, keepdims=True)


def span_scalars(lengths, row):
    ends, starts, first, total = [], [], 0, 0
    for j in range(lengths.shape[1]):
        size = lengths[row, j]
        starts.append(total)
        first = first + jnp.where(size == BLOCK, total, 0)
        total = total + size
        ends.append(total)
    return ends, starts, first


def places(first, core, shape, axis):
    at = lax.broadcasted_iota(jnp.int32, shape, axis) + (first + core * BLOCK)
    return jnp.where(at >= SEQ, at - SEQ, at)


def mask_bias(lengths, row, core):
    ends, _, first = span_scalars(lengths, row)

    def segment(at):
        return sum((at >= end).astype(jnp.int32) for end in ends)

    rows = segment(places(first, core, (BLOCK, BLOCK), 0))
    cols = segment(places(first, core, (BLOCK, BLOCK), 1))
    return jnp.where(rows == cols, 0.0, -1e30)


def lead_picks(lengths, core, by_rows):
    parts = []
    per_row = lengths.shape[1] - 1
    shape = (BLOCK, LEADS) if by_rows else (LEADS, BLOCK)
    for row in range(lengths.shape[0]):
        _, starts, first = span_scalars(lengths, row)
        at = places(first, core, shape, 0 if by_rows else 1)
        slot = lax.broadcasted_iota(jnp.int32, shape, 1 if by_rows else 0)
        hit = sum(
            ((slot == row * per_row + j) & (at == starts[j])).astype(jnp.int32) for j in range(per_row)
        )
        parts.append(hit.astype(f32))
    return jnp.concatenate(parts, axis=0 if by_rows else 1)


def lane_masks():
    return lax.broadcasted_iota(jnp.int32, (BLOCK, PAIR), 1) < HEAD_DIM


def forward_pass(x, lengths, core, norms, wa, wu, wd, qkv, ctx, mid, acc, ready, save):
    tokens, features = x.shape
    pairs = features // PAIR
    first = lane_masks()
    zero = jnp.zeros((BLOCK, PAIR), bf16)

    def block_step(b, carry):
        rows = pl.ds(pl.multiple_of(b * BLOCK, BLOCK), BLOCK)
        bias = mask_bias(lengths, b, core)
        for h in range(pairs):
            q = qkv[rows, pl.ds(h * PAIR, PAIR)]
            k = qkv[rows, pl.ds(features + h * PAIR, PAIR)]
            v = qkv[rows, pl.ds(2 * features + h * PAIR, PAIR)]
            total = None
            for side in range(2):
                own = first if side == 0 else ~first
                s = mm(q, jnp.where(own, k, zero), NT) * (HEAD_DIM**-0.5) + bias
                e = jnp.exp(s - jnp.max(s, axis=-1, keepdims=True))
                pr = (e * (1.0 / jnp.sum(e, axis=-1, keepdims=True))).astype(bf16)
                save["p"][b, h, :, pl.ds(side * BLOCK, BLOCK)] = pr
                part = mm(pr, jnp.where(own, v, zero))
                total = part if total is None else total + part
            ctx[rows, pl.ds(h * PAIR, PAIR)] = total.astype(bf16)
        return carry

    lax.fori_loop(0, tokens // BLOCK, block_step, 0)
    ready["a"](3)
    zn, r = normalize(x[...].astype(f32) + mm(ctx[...], wa[:, pl.ds(3 * features, features)]))
    save["keep"]("p", "ctx")
    save["rstd0"][...] = r
    save["zh0"][...] = zn.astype(bf16)
    mid[...] = (zn * norms[0, 0:1, :] + norms[0, 1:2, :]).astype(bf16)
    acc[...] = mid[...].astype(f32)
    save["keep"]("zh0", "mid")
    pieces = wu.shape[1] // features
    cols = [pl.ds(c * features, features) for c in range(pieces)]
    ready["u"](0)
    ahead = mm(mid[...], wu[:, cols[0]])
    for c in range(pieces):
        u = ahead
        if c + 1 < pieces:
            ready["u"](c + 1)
            ahead = mm(mid[...], wu[:, cols[c + 1]])
        act, slope = gelu_and_slope(u)
        act = act.astype(bf16)
        save["a"][:, cols[c]] = act
        save["slope"][:, cols[c]] = slope.astype(bf16)
        save["keep_cols"](c)
        ready["d"](c)
        acc[...] += mm(act, wd[:, cols[c]], NT)
    zn, r = normalize(acc[...])
    save["rstd1"][...] = r
    save["zh1"][...] = zn.astype(bf16)
    return (zn * norms[1, 0:1, :] + norms[1, 1:2, :]).astype(bf16)


def feed_forward_back(dy, norms, wu, wd, slope, zh1, rstd1, df, du, acc, dnorm, ready):
    features = wu.shape[0]
    dz, dgain, dshift = normalize_back(zh1[...].astype(f32), rstd1[...], norms[1, 0:1, :], dy.astype(f32))
    dnorm[2:3, :] = dgain
    dnorm[3:4, :] = dshift
    df[...] = dz.astype(bf16)
    acc[...] = dz
    for c in range(wu.shape[1] // features):
        cols = pl.ds(c * features, features)
        ready["d"](c)
        da = mm(df[...], wd[:, cols])
        ready["du"](c)
        g = (da * slope[:, cols].astype(f32)).astype(bf16)
        du[:, cols] = g
        ready["u"](c)
        acc[...] += mm(g, wu[:, cols], NT)


def attention_back_begin(d_mid, norms, wa, zh0, rstd0, do, dctx, acc, dnorm):
    tokens, features = acc.shape
    dgain = dshift = None
    for b in range(tokens // BLOCK):
        rows = pl.ds(b * BLOCK, BLOCK)
        dz, dg, ds = normalize_back(
            zh0[rows, :].astype(f32), rstd0[rows, :], norms[0, 0:1, :], d_mid[rows, :].astype(f32)
        )
        dgain, dshift = (dg, ds) if b == 0 else (dgain + dg, dshift + ds)
        acc[rows, :] = dz
        do[rows, :] = dz.astype(bf16)
        dctx[rows, :] = mm(dz.astype(bf16), wa[:, pl.ds(3 * features, features)], NT).astype(bf16)
    dnorm[0:1, :] = dgain
    dnorm[1:2, :] = dshift


def attention_back_item(b, h, qkv, p, dctx):
    features = dctx.shape[1]
    first = lane_masks()
    zero = jnp.zeros((BLOCK, PAIR), bf16)
    scale = HEAD_DIM**-0.5
    rows = pl.ds(pl.multiple_of(b * BLOCK, BLOCK), BLOCK)
    at = [pl.ds(pl.multiple_of(part * features + h * PAIR, PAIR), PAIR) for part in range(3)]
    q, k, v = (qkv[rows, cols] for cols in at)
    dc = dctx[rows, at[0]]
    dq = dk = dv = None
    for side in range(2):
        own = first if side == 0 else ~first
        pr = p[b, h, :, pl.ds(side * BLOCK, BLOCK)]
        prf = pr.astype(f32)
        dp = mm(dc, jnp.where(own, v, zero), NT)
        r = jnp.sum(dp * prf, axis=-1, keepdims=True)
        ds = (prf * (dp - r)).astype(bf16)
        parts = (
            mm(ds, jnp.where(own, k, zero)),
            mm(ds, jnp.where(own, q, zero), TN),
            mm(pr, jnp.where(own, dc, zero), TN),
        )
        if dq is None:
            dq, dk, dv = parts
        else:
            dq, dk, dv = dq + parts[0], dk + parts[1], dv + parts[2]
    qkv[rows, at[0]] = (dq * scale).astype(bf16)
    qkv[rows, at[1]] = (dk * scale).astype(bf16)
    qkv[rows, at[2]] = dv.astype(bf16)


def attention_back_end(part, wa, dqkv, acc):
    features = wa.shape[0]
    cols = pl.ds(part * features, features)
    for b in range(acc.shape[0] // BLOCK):
        rows = pl.ds(b * BLOCK, BLOCK)
        acc[rows, :] += mm(dqkv[rows, cols], wa[:, cols], NT)


def head_lanes(features):
    lane = lax.broadcasted_iota(jnp.int32, (LEADS, features), 1)
    return [(lane >= h * HEAD_DIM) & (lane < (h + 1) * HEAD_DIM) for h in range(features // HEAD_DIM)]


def spread_heads(rows):
    wide = rows.astype(f32)
    return jnp.concatenate([jnp.where(own, wide, 0.0) for own in head_lanes(rows.shape[1])], axis=0).astype(bf16)


def fold_heads(wide):
    total = None
    for h, own in enumerate(head_lanes(wide.shape[1])):
        part = jnp.where(own, wide[h * LEADS : (h + 1) * LEADS, :], 0.0)
        total = part if total is None else total + part
    return total


def lead_probs(queries, keys, lengths, core):
    tokens, features = keys.shape
    per_row = lengths.shape[1] - 1
    parts = []
    for row in range(tokens // BLOCK):
        ends, _, first = span_scalars(lengths, row)
        at = places(first, core, (LEADS, BLOCK), 1)
        segment = sum((at >= end).astype(jnp.int32) for end in ends)
        span = lax.broadcasted_iota(jnp.int32, (LEADS, BLOCK), 0) - row * per_row
        parts.append(jnp.where((span == segment) & (span < per_row), 0.0, -1e30))
    bias = jnp.concatenate([jnp.concatenate(parts, axis=1)] * (features // HEAD_DIM), axis=0)
    s = mm(spread_heads(queries), keys, NT) * (HEAD_DIM**-0.5) + bias
    e = jnp.exp(s - jnp.max(s, axis=-1, keepdims=True))
    return (e * (1.0 / jnp.sum(e, axis=-1, keepdims=True))).astype(bf16)


def lead_forward(x, lengths, core, norms, wa, wu, wd, qkv, ready):
    features = x.shape[1]
    pieces = wu.shape[1] // features
    cols = [pl.ds(c * features, features) for c in range(4)]
    own = mm(lead_picks(lengths, core, False).astype(bf16), x[...]).astype(bf16)
    for c in (1, 2):
        ready["a"](c)
        qkv[:, cols[c]] = mm(x[...], wa[:, cols[c]]).astype(bf16)
    ready["a"](0)
    probs = lead_probs(mm(own, wa[:, cols[0]]).astype(bf16), qkv[:, cols[1]], lengths, core)
    ctx = fold_heads(mm(probs, qkv[:, cols[2]])).astype(bf16)
    ready["a"](3)
    zn, _ = normalize(own.astype(f32) + mm(ctx, wa[:, cols[3]]))
    mid = (zn * norms[0, 0:1, :] + norms[0, 1:2, :]).astype(bf16)
    out = mid.astype(f32)
    for step in range(pieces):
        c = (step + core * (pieces // 2)) % pieces
        at = pl.ds(pl.multiple_of(c * features, features), features)
        ready["u"](c)
        act, _ = gelu_and_slope(mm(mid, wu[:, at]))
        if step % (pieces // 2) == 0:
            ready["half"](step)
        out = out + mm(act.astype(bf16), wd[:, at], NT)
    zn, _ = normalize(out)
    return (zn * norms[1, 0:1, :] + norms[1, 1:2, :]).astype(bf16)


def lead_back(pick, lengths, core, wa, qkv, p, ctx, dctx, dz):
    tokens, features = ctx.shape
    scale = HEAD_DIM**-0.5
    heads = features // HEAD_DIM
    cols = [pl.ds(c * features, features) for c in range(3)]
    q16, v16 = (mm(pick, qkv[:, cols[c]]).astype(bf16) for c in (0, 2))
    low = lead_probs(q16, qkv[:, cols[1]], lengths, core)
    probs = low.astype(f32)
    dp = mm(spread_heads(mm(pick, dctx[...]).astype(bf16)), qkv[:, cols[2]], NT)
    ds = (probs * (dp - jnp.sum(dp * probs, axis=-1, keepdims=True))).astype(bf16)
    dq = (fold_heads(mm(ds, qkv[:, cols[1]])) * scale).astype(bf16)
    seen = []
    for h in range(heads):
        keys = pl.ds(h % 2 * BLOCK, BLOCK)
        seen.append(
            jnp.concatenate(
                [mm(pick[:, b * BLOCK : (b + 1) * BLOCK], p[b, h // 2, :, keys], NT) for b in range(tokens // BLOCK)],
                axis=1,
            )
        )
    seen = jnp.concatenate(seen, axis=0)
    product = dctx[...].astype(f32) * ctx[...].astype(f32)
    high = product.astype(bf16)
    low = (product - high.astype(f32)).astype(bf16)
    lane = lax.broadcasted_iota(jnp.int32, (LEADS, features), 1)
    head = lax.broadcasted_iota(jnp.int32, (LEADS, features), 0) * HEAD_DIM
    select = ((lane >= head) & (lane < head + HEAD_DIM)).astype(f32).astype(bf16)
    sums = mm(select, high, NT) + mm(select, low, NT)
    sums = jnp.concatenate([jnp.broadcast_to(sums[h : h + 1, :], (LEADS, tokens)) for h in range(heads)], axis=0)
    ds = (seen * (mm(spread_heads(v16), dctx[...], NT) - sums)).astype(bf16)
    dk = (fold_heads(mm(ds, qkv[:, cols[0]])) * scale).astype(bf16)
    dv = fold_heads(mm(seen.astype(bf16), dctx[...])).astype(bf16)
    high = dz[...].astype(bf16)
    low = (dz[...] - high.astype(f32)).astype(bf16)
    out = mm(pick, high) + mm(pick, low)
    for c, part in enumerate((dq, dk, dv)):
        out = out + mm(part, wa[:, cols[c]], NT)
    return out


def front_kernel(
    rows_h, lengths, first_h, second_h, gain_in, shift_in,
    x_h, y_h, qkv_h, p_h, ctx_h, zh0_h, mid_h, a_h, df_h, du_h, dmid_h, other_first_h, rstd0, dnorm, norms,
    wa, wu, wd, x, qkv, p, ctx, zh0, mid, a, slope, up, zh1, rstd1, do, dctx, acc, d_att,
    lead_slope, grad_own, grad_in, row_own, row_in, norm_pair,
    row_sem, load, w_ss, w_rs, d_ss, d_rs, n_ss, n_rs, m_ss, m_rs, x_ss, x_rs, r_ss, r_rs, l_ss, l_rs, out_sem, col_sem, other_sem,
):
    sec = lax.axis_index("section")
    core = sec % 2
    at_head = sec // 2
    tokens, features = x.shape
    blocks = tokens // BLOCK
    pieces = wu.shape[1] // features
    half = wd.shape[1] // 2
    even, odd = core == 0, core == 1
    head, backbone = at_head == 1, at_head == 0
    sibling = {"section": sec + 1 - 2 * core}
    peer = {"section": (sec + 2) % 4}
    halves = (do, dctx)
    y, df, dmid = mid, mid, x
    barrier = pltpu.get_barrier_semaphore()
    for step in range(1, 4):
        target = {"section": (sec + step) % 4}
        pl.semaphore_signal(barrier, inc=1, device_id=target, device_id_type=MESH)

    def cols(c):
        return pl.ds(c * features, features)

    def block(b):
        return pl.ds(b * BLOCK, BLOCK)

    def piece(c):
        return pl.ds(c * features if isinstance(c, int) else pl.multiple_of(c * features, features), features)

    def local_first(c, dst):
        return pltpu.make_async_copy(first_h.at[:, piece(c)], dst.at[:, piece(c)], load.at[c])

    def sent_first(c, dst):
        return remote(first_h.at[:, piece(c)], dst.at[:, piece(c)], w_ss.at[c], w_rs.at[c], sibling)

    def local_second(side):
        return pltpu.make_async_copy(second_h, wd.at[:, pl.ds(side * half, half)], load.at[pieces])

    def sent_second(side):
        return remote(second_h, wd.at[:, pl.ds(side * half, half)], d_ss, d_rs, sibling)

    def row_load(row):
        return pltpu.make_async_copy(
            rows_h.at[pl.ds(row * SEQ, SEQ)], slope.at[pl.ds(0, SEQ), cols(row)], row_sem.at[row]
        )

    for row in range(blocks):
        row_load(row).start()
    turns = (1, 2, 0, *range(3, pieces))
    for c in range(pieces):
        when(even, lambda: local_first(turns[c], wa).start())
        when(odd, lambda: local_first(c, wu).start())
    when(even, lambda: local_second(0).start())
    when(odd, lambda: local_second(1).start())

    for row in range(blocks):
        _, _, first = span_scalars(lengths, row)
        row_load(row).wait()
        packed = slope[0:SEQ, cols(row)]
        for side in range(2):
            at = places(first, side, (BLOCK, SEQ), 0)
            hot = at == lax.broadcasted_iota(jnp.int32, (BLOCK, SEQ), 1)
            halves[side][block(row), :] = mm(hot.astype(f32).astype(bf16), packed).astype(bf16)
    norm_pair[core, 0:1, :] = gain_in[...]
    norm_pair[core, 1:2, :] = shift_in[...]

    def inner_send(dst):
        return remote(halves[1] if dst is x else halves[0], dst, m_ss, m_rs, sibling)

    def cross_send(dst, side, b):
        target = {"section": 2 + side} if dst is x else {"section": side}
        return remote(halves[side].at[block(b)], dst.at[block(b)], x_ss.at[side, b], x_rs.at[b], target)

    sent_norm = remote(norm_pair.at[core], norm_pair.at[core], n_ss, n_rs, sibling)
    norm_from = remote(norm_pair.at[1 - core], norm_pair.at[1 - core], n_ss, n_rs, sibling)
    pl.semaphore_wait(barrier, 3)
    pairs_of = [(side, b) for b in range(blocks) for side in range(2)]
    when(sec == 1, lambda: [cross_send(x, *at).start() for at in pairs_of])
    when(sec == 0, lambda: inner_send(x).start())
    sent_norm.start()
    for c in range(pieces):
        when(even, lambda: sent_first(turns[c], wa).start())
        when(odd, lambda: sent_first(c, wu).start())
    when(even, lambda: sent_second(0).start())
    when(odd, lambda: sent_second(1).start())
    when(sec == 3, lambda: inner_send(up).start())
    when(sec == 2, lambda: [cross_send(up, *at).start() for at in pairs_of])

    @pl.when(sec == 0)
    def _():
        x[...] = halves[0][...]

    @pl.when(sec == 3)
    def _():
        up[...] = halves[1][...]

    norm_from.wait_recv()
    norms[...] = norm_pair[...]

    def ready_a(c):
        when(even, lambda: local_first(c, wa).wait())
        when(odd, lambda: sent_first(c, wa).wait_recv())

    def ready_u(c):
        when(odd, lambda: local_first(c, wu).wait())
        when(even, lambda: sent_first(c, wu).wait_recv())

    def ready_d(c):
        if c == 0:
            when(even, lambda: local_second(0).wait())
            when(odd, lambda: sent_second(0).wait_recv())
        if c == pieces // 2:
            when(odd, lambda: local_second(1).wait())
            when(even, lambda: sent_second(1).wait_recv())

    def ready_half(step):
        if step == 0:
            when(even, lambda: local_second(0).wait())
            when(odd, lambda: local_second(1).wait())
        else:
            when(even, lambda: sent_second(1).wait_recv())
            when(odd, lambda: sent_second(0).wait_recv())

    refs = dict(
        x=(x, x_h), y=(y, y_h), qkv=(qkv, qkv_h), p=(p, p_h), ctx=(ctx, ctx_h), zh0=(zh0, zh0_h), mid=(mid, mid_h),
        df=(df, df_h), du=(slope, du_h), dmid=(dmid, dmid_h),
    )
    order = list(refs)

    def store(name):
        return pltpu.make_async_copy(*refs[name], out_sem.at[order.index(name)])

    def store_cols(c):
        return pltpu.make_async_copy(a.at[:, cols(c)], a_h.at[:, cols(c)], col_sem.at[c])

    def keep(*names):
        for name in names:
            store(name).start()

    picks = lead_picks(lengths, core, True)
    leading = jnp.max(picks, axis=1, keepdims=True) > 0
    hot_leads = picks.astype(bf16)
    pick = lead_picks(lengths, core, False).astype(bf16)
    row_hop = remote(row_own, row_in, r_ss, r_rs, peer)

    @pl.when(backbone)
    def _():
        when(odd, lambda: inner_send(x).wait_recv())
        ready = dict(a=ready_a, u=ready_u, half=ready_half)
        row_own[...] = lead_forward(x, lengths, core, norms, wa, wu, wd, qkv, ready)
        row_hop.start()
        qkv[:, cols(0)] = mm(x[...], wa[:, cols(0)]).astype(bf16)

    @pl.when(head)
    def _():
        for c in range(3):
            ready_a(c)
        row_hop.wait_recv()
        for b in range(blocks):
            cross_send(x, 0, b).wait_recv()
            at = slice(b * BLOCK, (b + 1) * BLOCK)
            x[block(b), :] = jnp.where(leading[at], mm(hot_leads[at], row_in[...]).astype(bf16), x[block(b), :])
            for c in range(3):
                qkv[block(b), cols(c)] = mm(x[block(b), :], wa[:, cols(c)]).astype(bf16)

    keep("x", "qkv")
    at_first = {k: f for k, f in (("a", ready_a), ("u", ready_u), ("d", ready_d))}
    ready = {k: (lambda c, f=f: when(head, f, c)) for k, f in at_first.items()}
    save = dict(
        p=p, a=a, slope=slope, zh0=zh0, zh1=zh1, rstd0=rstd0, rstd1=rstd1, keep=keep,
        keep_cols=lambda c: store_cols(c).start(),
    )
    out = forward_pass(x, lengths, core, norms, wa, wu, wd, qkv, ctx, mid, acc, ready, save)
    for name in ("mid", "x"):
        store(name).wait()
    y[...] = out
    keep("y")
    other = pltpu.make_async_copy(wa, other_first_h, other_sem)
    when(odd, lambda: other.start())
    lead_zh = mm(pick, zh1[...])
    left = jnp.broadcast_to(rstd1[...], (tokens, PAIR))
    total = jnp.zeros((LEADS, PAIR), f32)
    for _ in range(3):
        high = left.astype(bf16)
        left = left - high.astype(f32)
        total = total + mm(pick, high)
    lead_rstd = total[:, 0:1]

    @pl.when(backbone)
    def _():
        for b in range(blocks):
            cross_send(up, 0, b).wait_recv()
        row_hop.wait_send()
        for c in range(pieces):
            lead_slope[:, cols(c)] = mm(pick, slope[:, cols(c)]).astype(bf16)

    when(sec == 2, lambda: inner_send(up).wait_recv())
    when(sec == 0, lambda: inner_send(x).wait_send())
    when(sec == 3, lambda: inner_send(up).wait_send())
    when((sec == 1) | (sec == 2), lambda: [cross_send(x, *at).wait_send() for at in pairs_of])
    sent_norm.wait_send()
    for c in range(pieces):
        sent_first(c, wa).wait_send()
    sent_second(0).wait_send()
    none = {k: (lambda *_: None) for k in ("u", "d", "du")}
    store("y").wait()
    feed_forward_back(up[...], norms, wu, wd, slope, zh1, rstd1, df, slope, acc, dnorm, none)
    dmid[...] = acc[...].astype(bf16)
    dnorm[0:2, :] = jnp.zeros((2, features), f32)
    grad_hop = remote(grad_own, grad_in, l_ss, l_rs, peer)

    @pl.when(head)
    def _():
        keep("df", "du", "dmid")
        attention_back_begin(dmid, norms, wa, zh0, rstd0, do, dctx, acc, d_att)
        grad_own[...] = lead_back(pick, lengths, core, wa, qkv, p, ctx, dctx, acc)
        grad_hop.start()
        grad_hop.wait_send()

    @pl.when(backbone)
    def _():
        base = mm(pick, up[...])
        grad_hop.wait_recv()
        dy = (base + grad_in[...]).astype(bf16).astype(f32)
        extra = dy - base
        dnorm[2:3, :] += jnp.sum(extra * lead_zh, axis=0, keepdims=True)
        dnorm[3:4, :] += jnp.sum(extra, axis=0, keepdims=True)
        dz, _, _ = normalize_back(lead_zh, lead_rstd, norms[1, 0:1, :], dy)
        lead_df = dz.astype(bf16)
        df[...] = jnp.where(leading, mm(hot_leads, lead_df).astype(bf16), df[...])
        keep("df")
        for c in range(pieces):
            g = (mm(lead_df, wd[:, cols(c)]) * lead_slope[:, cols(c)].astype(f32)).astype(bf16)
            slope[:, cols(c)] = jnp.where(leading, mm(hot_leads, g).astype(bf16), slope[:, cols(c)])
            dz = dz + mm(g, wu[:, cols(c)], NT)
        keep("du")
        dmid[...] = jnp.where(leading, mm(hot_leads, dz.astype(bf16)).astype(bf16), dmid[...])
        keep("dmid")

    for name in order:
        if name not in ("mid", "x", "y"):
            store(name).wait()
    for c in range(pieces):
        store_cols(c).wait()
    when(odd, lambda: other.wait())


ANY = pl.BlockSpec(memory_space=pl.ANY)
IN_VMEM = pl.BlockSpec(memory_space=pltpu.VMEM)
IN_SMEM = pl.BlockSpec(memory_space=pltpu.SMEM)
S = jax.ShapeDtypeStruct


def vm(*shape):
    return pltpu.VMEM(shape, bf16)


def dma(*shape):
    return pltpu.SemaphoreType.DMA(shape)


def params(number):
    if number is None:
        return pltpu.CompilerParams(vmem_limit_bytes=VMEM_LIMIT)
    return pltpu.CompilerParams(vmem_limit_bytes=VMEM_LIMIT, collective_id=number, has_side_effects=True)


def front(rows_in, lengths, first, second, gain, shift):
    features, ff = first.shape
    tokens = rows_in.shape[0] // 2
    pieces = ff // features
    blocks, pairs = tokens // BLOCK, features // PAIR
    square = S((tokens, features), bf16)
    one = pltpu.SemaphoreType.DMA
    shapes = dict(
        x=square, y=square, qkv=S((tokens, 3 * features), bf16), p=S((blocks, pairs, BLOCK, 2 * BLOCK), bf16),
        ctx=square, zh0=square, mid=square, a=S((tokens, ff), bf16), df=square, du=S((tokens, ff), bf16), dmid=square,
        other_first=S(first.shape, bf16), rstd0=S((tokens, 1), f32), dnorm=S((4, features), f32),
        norms=S((2, 2, features), f32),
    )
    small = ("rstd0", "dnorm", "norms")
    wide = vm(features, ff)
    outs = pl.pallas_call(
        front_kernel,
        out_shape=list(shapes.values()),
        in_specs=[ANY, IN_SMEM, ANY, ANY, IN_VMEM, IN_VMEM],
        out_specs=[IN_VMEM if k in small else ANY for k in shapes],
        scratch_shapes=[wide, wide, wide]
        + [pltpu.VMEM(shapes[k].shape, bf16) for k in ("x", "qkv", "p", "ctx", "zh0", "mid", "a", "du")]
        + [
            vm(tokens, features), vm(tokens, features), pltpu.VMEM((tokens, 1), f32), vm(tokens, features),
            vm(tokens, features), pltpu.VMEM((tokens, features), f32), pltpu.VMEM((2, features), f32), vm(LEADS, ff),
            pltpu.VMEM((LEADS, features), f32), pltpu.VMEM((LEADS, features), f32), vm(LEADS, features), vm(LEADS, features),
            pltpu.VMEM((2, 2, features), f32),
            dma(blocks), dma(pieces + 1), dma(pieces), dma(pieces), one, one, one, one, one, one, dma(2, blocks), dma(blocks),
            one, one, one, one, dma(10), dma(pieces), one,
        ],
        compiler_params=params(1),
        name="front",
    )(rows_in, lengths, first, second, gain, shift)
    return dict(zip(shapes, outs))


PANEL = 128
RING = 4


def reduce_kernel(
    chain, lengths, dnorm_in, norms, rstd0, x_h, ctx_h, mid_h, a_h, df_h, du_h, dmid_h, zh0_h, qkv_h, p_h, y_h,
    first_h, other_first_h,
    out_h, norm_out, halves_h,
    left, left_t, own_ring, sib_ring, sib_send, part, y1, zin1, mid1, zin2, mid2, y2, final, halves,
    wa, qkv, p, do, dctx, acc, y_buf, dnorm,
    left_sem, own_sem, ring_sem, out_sem, sib_ss, sib_rs, y1_ss, y1_rs, z1_ss, z1_rs, m1_ss, m1_rs,
    z2_ss, z2_rs, m2_ss, m2_rs, y2_ss, y2_rs, f_ss, f_rs, o_ss, o_rs, c_ss, c_rs, h_sem, a_sem, in_sem,
):
    sec = lax.axis_index("section")
    dp = lax.axis_index("dp")
    core = sec % 2
    panels, rows, _ = final.shape
    tokens = acc.shape[0]
    half = rows // 2
    features = rows
    last = panels - 1
    spot = dp // 2
    side = spot // (chain // 2)
    depth = chain // 2 - 1
    dist = side * (spot - chain // 2) + (1 - side) * (chain // 2 - 1 - spot)
    inner = dist == 0
    y = dp % 2
    sibling = {"section": sec + 1 - 2 * core}
    across_y = {"dp": dp + 1 - 2 * y}
    inward = {"dp": dp + 2 - 4 * side}
    outward = {"dp": dp - 2 + 4 * side}
    has_out = dist < depth

    barrier = pltpu.get_barrier_semaphore()
    at_head = sec // 2
    dx_buf = dctx
    inside = (sec == 0) | (sec == 3)
    beyond = {"section": 2 - sec // 2}
    others = [{"section": (sec + step) % 4} for step in (1, 2, 3)]
    for target in (*others, across_y, inward):
        pl.semaphore_signal(barrier, inc=1, device_id=target, device_id_type=MESH)

    @pl.when(has_out)
    def _():
        pl.semaphore_signal(barrier, inc=1, device_id=outward, device_id_type=MESH)

    def rows_at(which):
        return pl.ds(pl.multiple_of(which * half, half), half)

    mine, theirs = rows_at(y), rows_at(1 - y)
    kept, rest = rows_at(side), rows_at(1 - side)

    def to_sibling(j):
        return remote(sib_send.at[j % RING], part.at[j], sib_ss.at[j % RING], sib_rs.at[j], sibling)

    def one_y(j):
        i = j // 2
        return remote(part.at[j, theirs], y1.at[i], y1_ss.at[i], y1_rs.at[i], across_y)

    def one_in(j):
        i = j // 2
        return remote(part.at[j, mine], zin1.at[i], z1_ss.at[i], z1_rs.at[i], inward)

    def one_mid(j):
        i = j // 2
        return remote(part.at[j, mine], mid1.at[i], m1_ss.at[i], m1_rs.at[i], inward)

    def one_out(j):
        return remote(final.at[j, mine], final.at[j, mine], f_ss.at[0, j], f_rs.at[0, j], outward)

    def one_back(j):
        return remote(final.at[j, mine], final.at[j, mine], f_ss.at[1, j], f_rs.at[1, j], across_y)

    def one_back_in(j):
        return remote(final.at[j, theirs], final.at[j, theirs], f_ss.at[1, j], f_rs.at[1, j], across_y)

    def two_in(j):
        i = j // 2
        return remote(part.at[j], zin2.at[i], z2_ss.at[i], z2_rs.at[i], inward)

    def two_mid(j):
        i = j // 2
        return remote(part.at[j, rest], mid2.at[i], m2_ss.at[i], m2_rs.at[i], inward)

    def two_y(j):
        i = j // 2
        return remote(part.at[j, kept], y2.at[i], y2_ss.at[i], y2_rs.at[i], across_y)

    def two_swap(j):
        return remote(final.at[j, kept], final.at[j, kept], f_ss.at[2, j], f_rs.at[1, j], inward)

    def two_swap_in(j):
        return remote(final.at[j, rest], final.at[j, rest], f_ss.at[2, j], f_rs.at[1, j], inward)

    def two_out_kept(j):
        return remote(final.at[j, kept], final.at[j, kept], f_ss.at[0, j], f_rs.at[0, j], outward)

    def two_out_rest(j):
        return remote(final.at[j, rest], final.at[j, rest], f_ss.at[1, j], f_rs.at[1, j], outward)

    down = a_h.shape[1] // (2 * PANEL)
    outer_cols = features // PANEL
    raw = dict(x=(x_h, 0), ctx=(ctx_h, 1), df=(df_h, 2), mid=(mid_h, 3))

    def left_of(who, j):
        late = jnp.minimum(j // down, 1)
        even = 2 * (1 - late) + late * (1 - jnp.minimum(j // (down + outer_cols), 1))
        odd = 2 * (1 - late) + 3 * late
        return who * odd + (1 - who) * even

    def columns(col):
        return pl.ds(pl.multiple_of(col * PANEL, PANEL), PANEL)

    def fetch_down(who, j, ring, sem):
        return pltpu.make_async_copy(a_h.at[:, columns(who * down + j)], ring.at[j % RING], sem.at[j % RING])

    def fetch_up(j, ring, sem):
        return pltpu.make_async_copy(du_h.at[:, columns(j - down)], ring.at[j % RING], sem.at[j % RING])

    def fetch(who, j, ring, sem):
        when(j < down, lambda: fetch_down(who, j, ring, sem).start())
        when((j >= down) & (j < last) & (who == 1), lambda: fetch_up(j, ring, sem).start())

    def right(who, j, ring, sem, use):
        def from_ring():
            pltpu.make_async_copy(a_h.at[:, columns(0)], ring.at[j % RING], sem.at[j % RING]).wait()
            use(ring[j % RING])

        when((j < down) | ((j < last) & (who == 1)), from_ring)
        when((j >= down) & (j < down + outer_cols) & (who == 0), lambda: use(do[:, columns(j - down)]))
        when(
            (j >= down + outer_cols) & (j < last) & (who == 0), lambda: use(qkv[:, columns(j - down - outer_cols)])
        )

    def to_out(j):
        late = jnp.minimum(j // down, 1)
        even = jnp.where(j < down + outer_cols, j - down + 3 * outer_cols, j - down - outer_cols)
        col = (1 - late) * (4 * outer_cols + j) + late * (core * (j - down) + (1 - core) * even)
        return pltpu.make_async_copy(final.at[j], out_h.at[:, columns(col)], out_sem.at[j])


    def own_send(src):
        return remote(src, halves.at[core], o_ss, o_rs, sibling)

    def own_from():
        return remote(dx_buf, halves.at[1 - core], o_ss, o_rs, sibling)

    def across_send(src):
        return remote(src, halves.at[core], c_ss, c_rs.at[core], beyond)

    def across_from(side):
        return remote(dx_buf, halves.at[side], c_ss, c_rs.at[side], beyond)

    def load_left(name):
        return pltpu.make_async_copy(raw[name][0], left, left_sem)

    loads = dict(dmid=(dmid_h, do), zh0=(zh0_h, dctx), qkv=(qkv_h, qkv), p=(p_h, p), y=(y_h, y_buf))
    names = list(loads)

    def load(name):
        return pltpu.make_async_copy(*loads[name], in_sem.at[names.index(name)])

    def load_wa(own, c):
        cols = pl.ds(c * features, features)
        return pltpu.make_async_copy((first_h if own else other_first_h).at[:, cols], wa.at[:, cols], a_sem.at[c])

    load_left("df").start()
    for j in range(RING):
        fetch_down(core, j, own_ring, own_sem).start()
        fetch_down(1 - core, j, sib_ring, ring_sem).start()
    load("dmid").start()
    load("zh0").start()
    for c in (3, 0, 1, 2):
        when(core == 0, lambda: load_wa(True, c).start())
        when(core == 1, lambda: load_wa(False, c).start())
    for name in ("qkv", "p", "y"):
        load(name).start()

    def turn(i):
        for b in range(features // BLOCK):
            grid = (BLOCK, features)
            eye = lax.broadcasted_iota(jnp.int32, grid, 0) + b * BLOCK == lax.broadcasted_iota(jnp.int32, grid, 1)
            left_t[i, pl.ds(b * BLOCK, BLOCK), :] = mm(eye.astype(f32).astype(bf16), left[...], NT).astype(bf16)

    def norm_panel(other):
        chosen = jnp.where(core == other, dnorm[2:4, :], dnorm[0:2, :])
        strips = [
            chosen[r : r + 1, c * PANEL : (c + 1) * PANEL]
            for r in range(2)
            for c in range(features // PANEL)
        ]
        return jnp.concatenate(strips + [jnp.zeros((16 - len(strips), PANEL), f32)], axis=0)

    pl.semaphore_wait(barrier, 5 + has_out.astype(jnp.int32))

    def stage_send(j):
        when(j >= RING, lambda: to_sibling(j - RING).wait_send())

        @pl.when(j == last)
        def _():
            sib_send[last % RING] = jnp.zeros((rows, PANEL), bf16)
            sib_send[last % RING, 0:16, :] = norm_panel(0).astype(bf16)

        def use(block):
            sib_send[j % RING] = mm(left_t[left_of(1 - core, j)], block).astype(bf16)

        right(1 - core, j, sib_ring, ring_sem, use)
        to_sibling(j).start()
        fetch(1 - core, j + RING, sib_ring, ring_sem)

    def stage_part(j):
        to_sibling(j).wait_recv()

        @pl.when(j == last)
        def _():
            part[last, 0:16, :] = (norm_panel(1) + part[last, 0:16, :].astype(f32)).astype(bf16)

        def use(block):
            own = mm(left_t[left_of(core, j)], block)
            part[j] = (own + part[j].astype(f32)).astype(bf16)

        right(core, j, own_ring, own_sem, use)
        fetch(core, j + RING, own_ring, own_sem)
        when(j % 2 == 0, lambda: one_y(j).start())
        when((j % 2 == 1) & (dist == depth) & (depth > 0), lambda: two_in(j).start())
        when((j % 2 == 1) & (dist == depth) & (depth == 0), lambda: two_mid(j).start())

    def one_halves(j):
        one_y(j).wait_recv()
        part[j, mine, :] = (part[j, mine, :].astype(f32) + y1[j // 2].astype(f32)).astype(bf16)
        when((dist == depth) & (dist > 0), lambda: one_in(j).start())
        when((dist == depth) & inner, lambda: one_mid(j).start())

    def one_chain(j):
        one_in(j).wait_recv()
        part[j, mine, :] = (part[j, mine, :].astype(f32) + zin1[j // 2].astype(f32)).astype(bf16)
        when(dist > 0, lambda: one_in(j).start())
        when(inner, lambda: one_mid(j).start())

    def one_total(j):
        one_mid(j).wait_recv()
        final[j, mine, :] = (part[j, mine, :].astype(f32) + mid1[j // 2].astype(f32)).astype(bf16)
        when(has_out, lambda: one_out(j).start())
        one_back(j).start()

    def one_spread(j):
        one_out(j).wait_recv()
        when(has_out, lambda: one_out(j).start())
        one_back(j).start()

    def two_chain(j):
        two_in(j).wait_recv()
        part[j] = (part[j].astype(f32) + zin2[j // 2].astype(f32)).astype(bf16)
        when(dist > 0, lambda: two_in(j).start())
        when(inner, lambda: two_mid(j).start())

    def two_halves(j):
        two_mid(j).wait_recv()
        part[j, kept, :] = (part[j, kept, :].astype(f32) + mid2[j // 2].astype(f32)).astype(bf16)
        two_y(j).start()

    def two_total(j):
        two_y(j).wait_recv()
        final[j, kept, :] = (part[j, kept, :].astype(f32) + y2[j // 2].astype(f32)).astype(bf16)
        two_swap(j).start()
        when(has_out, lambda: two_out_kept(j).start())

    def two_swapped(j):
        two_swap_in(j).wait_recv()
        when(has_out, lambda: two_out_rest(j).start())

    def two_spread_kept(j):
        two_out_kept(j).wait_recv()
        when(has_out, lambda: two_out_kept(j).start())

    def two_spread_rest(j):
        two_out_rest(j).wait_recv()
        when(has_out, lambda: two_out_rest(j).start())

    def finish(j):
        when(j % 2 == 0, lambda: one_back_in(j).wait_recv())

        @pl.when(j == last)
        def _():
            norm_out[...] = final[last, 0:16, :].astype(f32)

        when(j < last, lambda: to_out(j).start())

    last_lag = 7 + 4 * depth

    pairs = features // PAIR
    items = tokens // BLOCK * pairs
    begin = 4

    def turn_next(name, following):
        load_left(name).wait()
        turn(raw[name][1])
        if following:
            load_left(following).start()

    def attention_begin():
        load("dmid").wait()
        load("zh0").wait()
        load_wa(True, 3).wait()
        attention_back_begin(do, norms, wa, dctx, rstd0, do, dctx, acc, dnorm)

    def send_rows():
        load("y").wait()

        @pl.when(at_head == 1)
        def _():
            leading = jnp.max(lead_picks(lengths, core, True), axis=1, keepdims=True) > 0
            dx_buf[...] = jnp.where(leading, 0.0, acc[...]).astype(bf16)

        @pl.when(at_head == 0)
        def _():
            dx_buf[...] = acc[...].astype(bf16)

        def go(own, across):
            across_send(across).start()
            when(~inside, lambda: own_send(own).start())

            @pl.when(inside)
            def _():
                halves[core] = own[...]

        when(at_head == 1, go, y_buf, dx_buf)
        when(at_head == 0, go, dx_buf, y_buf)

    dnorm[...] = dnorm_in[...]
    turn_next("df", "mid")

    def step(t, carry):
        def at(lag, kind, cond, run):
            j = t - lag
            ok = (j >= 0) & (j < panels)
            if kind is not None:
                ok = ok & (j % 2 == kind)
            if cond is not None:
                ok = ok & cond
            when(ok, run, j)

        at(7 + 2 * (depth + dist), 1, dist > 0, two_spread_rest)
        at(5 + 2 * (depth + dist), 1, dist > 0, two_spread_kept)
        at(5 + 2 * (depth + dist), 0, dist > 0, one_spread)
        at(7 + 2 * depth, 1, inner, two_swapped)
        at(5 + 2 * depth, 1, inner, two_total)
        at(5 + 2 * depth, 0, inner, one_total)
        at(3 + 2 * depth, 1, inner, two_halves)
        at(3 + 2 * (depth - dist), 0, dist < depth, one_chain)
        at(1 + 2 * (depth - dist), 1, dist < depth, two_chain)
        at(3, 0, None, one_halves)
        at(1, None, None, stage_part)
        at(0, None, None, stage_send)
        at(last_lag + 1, None, None, finish)
        when(t == begin, attention_begin)
        item = t - begin - 1
        when(t == begin + 1, lambda: [load("qkv").wait(), load("p").wait()])
        when((item >= 0) & (item < items), lambda: attention_back_item(item // pairs, item % pairs, qkv, p, dctx))
        when(t == 8, turn_next, "mid", "ctx")
        when(t == 9, turn_next, "ctx", "x")
        when(t == 10, turn_next, "x", None)
        for c in range(3):
            when(t == begin + items + 1 + c, lambda: [load_wa(True, c).wait(), attention_back_end(c, wa, qkv, acc)])
        when(t == begin + items + 4, send_rows)
        return carry

    lax.fori_loop(0, panels + last_lag + 1, step, 0)

    @pl.when(inside)
    def _():
        own_from().wait_recv()

    @pl.when(~inside)
    def _():
        own_send(dx_buf).wait_send()
        across_from(0).wait_recv()
        across_from(1).wait_recv()

    across_send(dx_buf).wait_send()
    rows_done = pltpu.make_async_copy(halves, halves_h, h_sem)
    rows_done.start()

    def drain(j, carry):
        when(j >= panels - RING, lambda: to_sibling(j).wait_send())
        when(j < last, lambda: to_out(j).wait())

        @pl.when(j % 2 == 0)
        def _():
            one_y(j).wait_send()
            when(dist > 0, lambda: one_in(j).wait_send())
            when(inner, lambda: one_mid(j).wait_send())
            when(has_out, lambda: one_out(j).wait_send())
            one_back(j).wait_send()

        @pl.when(j % 2 == 1)
        def _():
            when(dist > 0, lambda: two_in(j).wait_send())

            @pl.when(inner)
            def _():
                two_mid(j).wait_send()
                two_y(j).wait_send()
                two_swap(j).wait_send()

            @pl.when(has_out)
            def _():
                two_out_kept(j).wait_send()
                two_out_rest(j).wait_send()

        return carry

    lax.fori_loop(0, panels, drain, 0)
    rows_done.wait()


def reduce_gradients(lengths, first, saved, chain):
    tokens, features = saved["x"].shape
    ff = saved["a"].shape[1]
    width = ff + ff // 2
    panels = width // PANEL + 1
    evens, odds = (panels + 1) // 2, panels // 2
    h = features // 2
    one = pltpu.SemaphoreType.DMA
    arrays = [saved[k] for k in ("x", "ctx", "mid", "a", "df", "du", "dmid", "zh0", "qkv", "p", "y")]
    return pl.pallas_call(
        functools.partial(reduce_kernel, chain),
        out_shape=[S((features, width), bf16), S((16, PANEL), f32), S((2, tokens, features), bf16)],
        in_specs=[IN_SMEM] + [IN_VMEM] * 3 + [ANY] * 13,
        out_specs=[ANY, IN_VMEM, ANY],
        scratch_shapes=[
            vm(tokens, features), vm(4, features, tokens), vm(RING, tokens, PANEL), vm(RING, tokens, PANEL),
            vm(RING, features, PANEL), vm(panels, features, PANEL),
            vm(evens, h, PANEL), vm(evens, h, PANEL), vm(evens, h, PANEL),
            vm(odds, features, PANEL), vm(odds, h, PANEL), vm(odds, h, PANEL),
            vm(panels, features, PANEL), vm(2, tokens, features),
            vm(features, ff), vm(tokens, 3 * features), pltpu.VMEM(saved["p"].shape, bf16), vm(tokens, features),
            vm(tokens, features), pltpu.VMEM((tokens, features), f32), vm(tokens, features),
            pltpu.VMEM((4, features), f32),
            one, dma(RING), dma(RING), dma(panels), dma(RING), dma(panels),
            dma(evens), dma(evens), dma(evens), dma(evens), dma(evens), dma(evens),
            dma(odds), dma(odds), dma(odds), dma(odds), dma(odds), dma(odds), dma(3, panels), dma(2, panels),
            one, one, one, dma(2), one, dma(ff // features), dma(5),
        ],
        compiler_params=params(3),
        name="reduce_gradients",
    )(lengths, saved["dnorm"], saved["norms"], saved["rstd0"], *arrays, first, saved["other_first"])


def finish_kernel(lengths, total, halves, norm_in, first_out, second_out, rows_out, gain_out, shift_out):
    step = pl.program_id(0)
    features = rows_out.shape[1]
    wide = first_out.shape[1]
    first_out[...] = total[:, pl.ds(0, wide)].astype(f32)
    second_out[...] = total[:, pl.ds(wide, second_out.shape[1])].astype(f32)
    size = rows_out.shape[0]
    row = step // (SEQ // size)
    _, _, first = span_scalars(lengths, row)
    at = lax.broadcasted_iota(jnp.int32, (size, BLOCK), 0) + step % (SEQ // size) * size
    out = None
    for side in range(2):
        hot = at == places(first, side, (size, BLOCK), 1)
        part = mm(hot.astype(f32).astype(bf16), halves[side])
        out = part if out is None else out + part
    rows_out[...] = out
    strips = features // PANEL
    for r, ref in enumerate((gain_out, shift_out)):
        ref[...] = jnp.concatenate([norm_in[r * strips + c : r * strips + c + 1, :] for c in range(strips)], axis=1)


def finish(lengths, total, halves, norm_in, ff):
    features, width = total.shape
    tokens = halves.shape[1]
    size = SEQ
    steps = 2 * tokens // size
    part = features // steps
    row_spec = pl.BlockSpec((1, features), lambda i: (0, 0))
    return pl.pallas_call(
        finish_kernel,
        grid=(steps,),
        out_shape=[
            S((features, ff), f32), S((features, width - ff), f32), S((2 * tokens, features), f32),
            S((1, features), f32), S((1, features), f32),
        ],
        in_specs=[
            IN_SMEM, pl.BlockSpec((part, width), lambda i: (i, 0)),
            pl.BlockSpec((2, BLOCK, features), lambda i: (0, i // (SEQ // size), 0)), IN_VMEM,
        ],
        out_specs=[
            pl.BlockSpec((part, ff), lambda i: (i, 0)), pl.BlockSpec((part, width - ff), lambda i: (i, 0)),
            pl.BlockSpec((size, features), lambda i: (i, 0)), row_spec, row_spec,
        ],
        compiler_params=params(None),
        name="finish",
    )(lengths, total, halves, norm_in)


def per_device(section_rows, span_lengths, first_weights, second_weights, norm_gain, norm_shift):
    first, second = first_weights[0], second_weights[0]
    saved = front(section_rows[0], span_lengths, first, second, norm_gain, norm_shift)
    total, norm_total, halves = reduce_gradients(span_lengths, first, saved, lax.axis_size("dp") // 2)
    d_first, d_second, rows, gain, shift = finish(span_lengths, total, halves, norm_total, first.shape[1])
    return rows[None], d_first[None], d_second[None], gain, shift


def solution(mesh):
    in_specs = (
        P("section", "dp", None),
        P("dp", None),
        P("section", None, None),
        P("section", None, None),
        P("section", None),
        P("section", None),
    )
    out_specs = (
        P("section", "dp", None),
        P("section", None, None),
        P("section", None, None),
        P("section", None),
        P("section", None),
    )
    return jax.shard_map(
        per_device, mesh=mesh, in_specs=in_specs, out_specs=out_specs, check_vma=False
    )
```

```python
import functools

import jax
import jax.numpy as jnp
from jax import lax
from jax.experimental import pallas as pl
from jax.experimental.pallas import tpu as pltpu
from jax.sharding import PartitionSpec as P

HEAD_DIM = 64
PAIR = 2 * HEAD_DIM
BLOCK = 256
SEQ = 512
LEADS = 16
VMEM_LIMIT = 60 << 20
MESH = pl.DeviceIdType.MESH
f32 = jnp.float32
bf16 = jnp.bfloat16
epsilon = 1e-12
NN = (((1,), (0,)), ((), ()))
NT = (((1,), (1,)), ((), ()))
TN = (((0,), (0,)), ((), ()))
LOG2E = 1.4426950408889634


def mm(a, b, dims=NN):
    return lax.dot_general(a, b, dims, preferred_element_type=f32)


def when(cond, step, *args):
    @pl.when(cond)
    def _():
        step(*args)


def remote(src, dst, ss, rs, target):
    return pltpu.make_async_remote_copy(
        src_ref=src, dst_ref=dst, send_sem=ss, recv_sem=rs, device_id=target, device_id_type=MESH
    )


def gelu_and_slope(u):
    bell = jnp.exp2(u * u * (-0.5 * LOG2E))
    t = 1.0 / (1.0 + (0.3275911 * 0.5**0.5) * jnp.abs(u))
    poly = t * (0.127414796 + t * (-0.142248368 + t * (0.7107068705 + t * (-0.7265760135 + t * 0.5307027145))))
    tail = poly * bell
    cdf = jnp.where(u < 0, tail, 1.0 - tail)
    return u * cdf, cdf + u * bell * 0.3989422804014327


def normalize(z):
    centered = z - jnp.mean(z, axis=-1, keepdims=True)
    rstd = lax.rsqrt(jnp.mean(centered * centered, axis=-1, keepdims=True) + epsilon)
    return centered * rstd, rstd


def normalize_back(zh, rstd, gain, dy):
    g = dy * gain
    mean_g = jnp.mean(g, axis=-1, keepdims=True)
    mean_gz = jnp.mean(g * zh, axis=-1, keepdims=True)
    dz = rstd * (g - mean_g - zh * mean_gz)
    return dz, jnp.sum(dy * zh, axis=0, keepdims=True), jnp.sum(dy, axis=0, keepdims=True)


def span_scalars(lengths, row):
    ends, starts, first, total = [], [], 0, 0
    for j in range(lengths.shape[1]):
        size = lengths[row, j]
        starts.append(total)
        first = first + jnp.where(size == BLOCK, total, 0)
        total = total + size
        ends.append(total)
    return ends, starts, first


def places(first, core, shape, axis):
    at = lax.broadcasted_iota(jnp.int32, shape, axis) + (first + core * BLOCK)
    return jnp.where(at >= SEQ, at - SEQ, at)


def mask_bias(lengths, row, core):
    ends, _, first = span_scalars(lengths, row)

    def segment(at):
        return sum((at >= end).astype(jnp.int32) for end in ends)

    rows = segment(places(first, core, (BLOCK, BLOCK), 0))
    cols = segment(places(first, core, (BLOCK, BLOCK), 1))
    return jnp.where(rows == cols, 0.0, -1e30)


def lead_picks(lengths, core, by_rows):
    parts = []
    per_row = lengths.shape[1] - 1
    shape = (BLOCK, LEADS) if by_rows else (LEADS, BLOCK)
    for row in range(lengths.shape[0]):
        _, starts, first = span_scalars(lengths, row)
        at = places(first, core, shape, 0 if by_rows else 1)
        slot = lax.broadcasted_iota(jnp.int32, shape, 1 if by_rows else 0)
        hit = sum(
            ((slot == row * per_row + j) & (at == starts[j])).astype(jnp.int32) for j in range(per_row)
        )
        parts.append(hit.astype(f32))
    return jnp.concatenate(parts, axis=0 if by_rows else 1)


def lane_masks():
    return lax.broadcasted_iota(jnp.int32, (BLOCK, PAIR), 1) < HEAD_DIM


def forward_pass(x, lengths, core, norms, wa, wu, wd, qkv, ctx, mid, acc, ready, arrive, save):
    tokens, features = x.shape
    pairs = features // PAIR
    first = lane_masks()
    zero = jnp.zeros((BLOCK, PAIR), bf16)

    def block_step(b, carry):
        rows = pl.ds(pl.multiple_of(b * BLOCK, BLOCK), BLOCK)
        arrive(b)
        for c in range(3):
            cols = pl.ds(c * features, features)
            qkv[rows, cols] = mm(x[rows, :], wa[:, cols]).astype(bf16)
        bias = mask_bias(lengths, b, core)
        for h in range(pairs):
            q = qkv[rows, pl.ds(h * PAIR, PAIR)]
            k = qkv[rows, pl.ds(features + h * PAIR, PAIR)]
            v = qkv[rows, pl.ds(2 * features + h * PAIR, PAIR)]
            total = None
            for side in range(2):
                own = first if side == 0 else ~first
                s = mm(q, jnp.where(own, k, zero), NT) * (HEAD_DIM**-0.5) + bias
                e = jnp.exp(s - jnp.max(s, axis=-1, keepdims=True))
                pr = (e * (1.0 / jnp.sum(e, axis=-1, keepdims=True))).astype(bf16)
                save["p"][b, h, :, pl.ds(side * BLOCK, BLOCK)] = pr
                part = mm(pr, jnp.where(own, v, zero))
                total = part if total is None else total + part
            ctx[rows, pl.ds(h * PAIR, PAIR)] = total.astype(bf16)
        return carry

    lax.fori_loop(0, tokens // BLOCK, block_step, 0)
    ready["a"](3)
    zn, r = normalize(x[...].astype(f32) + mm(ctx[...], wa[:, pl.ds(3 * features, features)]))
    save["keep"]("x", "qkv", "p", "ctx")
    save["rstd0"][...] = r
    save["zh0"][...] = zn.astype(bf16)
    mid[...] = (zn * norms[0, 0:1, :] + norms[0, 1:2, :]).astype(bf16)
    acc[...] = mid[...].astype(f32)
    save["keep"]("zh0", "mid")
    pieces = wu.shape[1] // features
    cols = [pl.ds(c * features, features) for c in range(pieces)]
    ready["u"](0)
    ahead = mm(mid[...], wu[:, cols[0]])
    for c in range(pieces):
        u = ahead
        if c + 1 < pieces:
            ready["u"](c + 1)
            ahead = mm(mid[...], wu[:, cols[c + 1]])
        act, slope = gelu_and_slope(u)
        act = act.astype(bf16)
        save["a"][:, cols[c]] = act
        save["slope"][:, cols[c]] = slope.astype(bf16)
        save["keep_cols"](c)
        ready["d"](c)
        acc[...] += mm(act, wd[:, cols[c]], NT)
    zn, r = normalize(acc[...])
    save["rstd1"][...] = r
    save["zh1"][...] = zn.astype(bf16)
    return (zn * norms[1, 0:1, :] + norms[1, 1:2, :]).astype(bf16)


def feed_forward_back(dy, norms, wu, wd, slope, zh1, rstd1, df, du, acc, dnorm, ready):
    features = wu.shape[0]
    dz, dgain, dshift = normalize_back(zh1[...].astype(f32), rstd1[...], norms[1, 0:1, :], dy.astype(f32))
    dnorm[2:3, :] = dgain
    dnorm[3:4, :] = dshift
    df[...] = dz.astype(bf16)
    acc[...] = dz
    for c in range(wu.shape[1] // features):
        cols = pl.ds(c * features, features)
        ready["d"](c)
        da = mm(df[...], wd[:, cols])
        ready["du"](c)
        g = (da * slope[:, cols].astype(f32)).astype(bf16)
        du[:, cols] = g
        ready["u"](c)
        acc[...] += mm(g, wu[:, cols], NT)


def attention_back_begin(d_mid, norms, wa, zh0, rstd0, do, dctx, acc, dnorm):
    tokens, features = acc.shape
    dgain = dshift = None
    for b in range(tokens // BLOCK):
        rows = pl.ds(b * BLOCK, BLOCK)
        dz, dg, ds = normalize_back(
            zh0[rows, :].astype(f32), rstd0[rows, :], norms[0, 0:1, :], d_mid[rows, :].astype(f32)
        )
        dgain, dshift = (dg, ds) if b == 0 else (dgain + dg, dshift + ds)
        acc[rows, :] = dz
        do[rows, :] = dz.astype(bf16)
        dctx[rows, :] = mm(dz.astype(bf16), wa[:, pl.ds(3 * features, features)], NT).astype(bf16)
    dnorm[0:1, :] = dgain
    dnorm[1:2, :] = dshift


def attention_back_item(b, h, qkv, p, dctx):
    features = dctx.shape[1]
    first = lane_masks()
    zero = jnp.zeros((BLOCK, PAIR), bf16)
    scale = HEAD_DIM**-0.5
    rows = pl.ds(pl.multiple_of(b * BLOCK, BLOCK), BLOCK)
    at = [pl.ds(pl.multiple_of(part * features + h * PAIR, PAIR), PAIR) for part in range(3)]
    q, k, v = (qkv[rows, cols] for cols in at)
    dc = dctx[rows, at[0]]
    dq = dk = dv = None
    for side in range(2):
        own = first if side == 0 else ~first
        pr = p[b, h, :, pl.ds(side * BLOCK, BLOCK)]
        prf = pr.astype(f32)
        dp = mm(dc, jnp.where(own, v, zero), NT)
        r = jnp.sum(dp * prf, axis=-1, keepdims=True)
        ds = (prf * (dp - r)).astype(bf16)
        parts = (
            mm(ds, jnp.where(own, k, zero)),
            mm(ds, jnp.where(own, q, zero), TN),
            mm(pr, jnp.where(own, dc, zero), TN),
        )
        if dq is None:
            dq, dk, dv = parts
        else:
            dq, dk, dv = dq + parts[0], dk + parts[1], dv + parts[2]
    qkv[rows, at[0]] = (dq * scale).astype(bf16)
    qkv[rows, at[1]] = (dk * scale).astype(bf16)
    qkv[rows, at[2]] = dv.astype(bf16)


def attention_back_end(part, wa, dqkv, acc):
    features = wa.shape[0]
    cols = pl.ds(part * features, features)
    for b in range(acc.shape[0] // BLOCK):
        rows = pl.ds(b * BLOCK, BLOCK)
        acc[rows, :] += mm(dqkv[rows, cols], wa[:, cols], NT)


def head_lanes(features):
    lane = lax.broadcasted_iota(jnp.int32, (LEADS, features), 1)
    return [(lane >= h * HEAD_DIM) & (lane < (h + 1) * HEAD_DIM) for h in range(features // HEAD_DIM)]


def spread_heads(rows):
    wide = rows.astype(f32)
    return jnp.concatenate([jnp.where(own, wide, 0.0) for own in head_lanes(rows.shape[1])], axis=0).astype(bf16)


def fold_heads(wide):
    total = None
    for h, own in enumerate(head_lanes(wide.shape[1])):
        part = jnp.where(own, wide[h * LEADS : (h + 1) * LEADS, :], 0.0)
        total = part if total is None else total + part
    return total


def lead_probs(queries, keys, lengths, core):
    tokens, features = keys.shape
    per_row = lengths.shape[1] - 1
    parts = []
    for row in range(tokens // BLOCK):
        ends, _, first = span_scalars(lengths, row)
        at = places(first, core, (LEADS, BLOCK), 1)
        segment = sum((at >= end).astype(jnp.int32) for end in ends)
        span = lax.broadcasted_iota(jnp.int32, (LEADS, BLOCK), 0) - row * per_row
        parts.append(jnp.where((span == segment) & (span < per_row), 0.0, -1e30))
    bias = jnp.concatenate([jnp.concatenate(parts, axis=1)] * (features // HEAD_DIM), axis=0)
    s = mm(spread_heads(queries), keys, NT) * (HEAD_DIM**-0.5) + bias
    e = jnp.exp(s - jnp.max(s, axis=-1, keepdims=True))
    return (e * (1.0 / jnp.sum(e, axis=-1, keepdims=True))).astype(bf16)


def lead_forward(x, lengths, core, norms, wa, wu, wd, qkv, ready):
    features = x.shape[1]
    pieces = wu.shape[1] // features
    cols = [pl.ds(c * features, features) for c in range(4)]
    own = mm(lead_picks(lengths, core, False).astype(bf16), x[...]).astype(bf16)
    for c in (1, 2):
        ready["a"](c)
        qkv[:, cols[c]] = mm(x[...], wa[:, cols[c]]).astype(bf16)
    ready["a"](0)
    probs = lead_probs(mm(own, wa[:, cols[0]]).astype(bf16), qkv[:, cols[1]], lengths, core)
    ctx = fold_heads(mm(probs, qkv[:, cols[2]])).astype(bf16)
    ready["a"](3)
    zn, _ = normalize(own.astype(f32) + mm(ctx, wa[:, cols[3]]))
    mid = (zn * norms[0, 0:1, :] + norms[0, 1:2, :]).astype(bf16)
    out = mid.astype(f32)
    for step in range(pieces):
        c = (step + core * (pieces // 2)) % pieces
        at = pl.ds(pl.multiple_of(c * features, features), features)
        ready["u"](c)
        act, _ = gelu_and_slope(mm(mid, wu[:, at]))
        if step % (pieces // 2) == 0:
            ready["half"](step)
        out = out + mm(act.astype(bf16), wd[:, at], NT)
    zn, _ = normalize(out)
    return (zn * norms[1, 0:1, :] + norms[1, 1:2, :]).astype(bf16)


def lead_back(pick, lengths, core, wa, qkv, p, ctx, dctx, dz):
    tokens, features = ctx.shape
    scale = HEAD_DIM**-0.5
    heads = features // HEAD_DIM
    cols = [pl.ds(c * features, features) for c in range(3)]
    q16, v16 = (mm(pick, qkv[:, cols[c]]).astype(bf16) for c in (0, 2))
    low = lead_probs(q16, qkv[:, cols[1]], lengths, core)
    probs = low.astype(f32)
    dp = mm(spread_heads(mm(pick, dctx[...]).astype(bf16)), qkv[:, cols[2]], NT)
    ds = (probs * (dp - jnp.sum(dp * probs, axis=-1, keepdims=True))).astype(bf16)
    dq = (fold_heads(mm(ds, qkv[:, cols[1]])) * scale).astype(bf16)
    seen = []
    for h in range(heads):
        keys = pl.ds(h % 2 * BLOCK, BLOCK)
        seen.append(
            jnp.concatenate(
                [mm(pick[:, b * BLOCK : (b + 1) * BLOCK], p[b, h // 2, :, keys], NT) for b in range(tokens // BLOCK)],
                axis=1,
            )
        )
    seen = jnp.concatenate(seen, axis=0)
    product = dctx[...].astype(f32) * ctx[...].astype(f32)
    high = product.astype(bf16)
    low = (product - high.astype(f32)).astype(bf16)
    lane = lax.broadcasted_iota(jnp.int32, (LEADS, features), 1)
    head = lax.broadcasted_iota(jnp.int32, (LEADS, features), 0) * HEAD_DIM
    select = ((lane >= head) & (lane < head + HEAD_DIM)).astype(f32).astype(bf16)
    sums = mm(select, high, NT) + mm(select, low, NT)
    sums = jnp.concatenate([jnp.broadcast_to(sums[h : h + 1, :], (LEADS, tokens)) for h in range(heads)], axis=0)
    ds = (seen * (mm(spread_heads(v16), dctx[...], NT) - sums)).astype(bf16)
    dk = (fold_heads(mm(ds, qkv[:, cols[0]])) * scale).astype(bf16)
    dv = fold_heads(mm(seen.astype(bf16), dctx[...])).astype(bf16)
    high = dz[...].astype(bf16)
    low = (dz[...] - high.astype(f32)).astype(bf16)
    out = mm(pick, high) + mm(pick, low)
    for c, part in enumerate((dq, dk, dv)):
        out = out + mm(part, wa[:, cols[c]], NT)
    return out


def front_kernel(
    rows_h, lengths, first_h, second_h, gain_in, shift_in,
    x_h, y_h, qkv_h, p_h, ctx_h, zh0_h, mid_h, a_h, df_h, du_h, dmid_h, other_first_h, rstd0, dnorm, norms,
    wa, wu, wd, x, qkv, p, ctx, zh0, mid, a, slope, up, zh1, rstd1, do, dctx, acc, d_att,
    lead_slope, hot_ref, grad_own, grad_in, row_own, row_in, norm_pair,
    row_sem, load, w_ss, w_rs, d_ss, d_rs, n_ss, n_rs, m_ss, m_rs, x_ss, x_rs, r_ss, r_rs, l_ss, l_rs, out_sem, col_sem, du_sem, other_sem,
):
    sec = lax.axis_index("section")
    core = sec % 2
    at_head = sec // 2
    tokens, features = x.shape
    blocks = tokens // BLOCK
    pieces = wu.shape[1] // features
    half = wd.shape[1] // 2
    even, odd = core == 0, core == 1
    head, backbone = at_head == 1, at_head == 0
    sibling = {"section": sec + 1 - 2 * core}
    peer = {"section": (sec + 2) % 4}
    halves = (do, dctx)
    y, df, dmid = mid, mid, x
    barrier = pltpu.get_barrier_semaphore()
    for step in range(1, 4):
        target = {"section": (sec + step) % 4}
        pl.semaphore_signal(barrier, inc=1, device_id=target, device_id_type=MESH)

    def cols(c):
        return pl.ds(c * features, features)

    def block(b):
        return pl.ds(b * BLOCK if isinstance(b, int) else pl.multiple_of(b * BLOCK, BLOCK), BLOCK)

    def piece(c):
        return pl.ds(c * features if isinstance(c, int) else pl.multiple_of(c * features, features), features)

    def local_first(c, dst):
        return pltpu.make_async_copy(first_h.at[:, piece(c)], dst.at[:, piece(c)], load.at[c])

    def sent_first(c, dst):
        return remote(first_h.at[:, piece(c)], dst.at[:, piece(c)], w_ss.at[c], w_rs.at[c], sibling)

    def local_second(side):
        return pltpu.make_async_copy(second_h, wd.at[:, pl.ds(side * half, half)], load.at[pieces])

    def sent_second(side):
        return remote(second_h, wd.at[:, pl.ds(side * half, half)], d_ss, d_rs, sibling)

    def row_load(row):
        return pltpu.make_async_copy(
            rows_h.at[pl.ds(row * SEQ, SEQ)], slope.at[pl.ds(0, SEQ), cols(row)], row_sem.at[row]
        )

    for row in range(blocks):
        row_load(row).start()
    turns = (1, 2, 0, *range(3, pieces))
    for c in range(pieces):
        when(even, lambda: local_first(turns[c], wa).start())
        when(odd, lambda: local_first(c, wu).start())
    when(even, lambda: local_second(0).start())
    when(odd, lambda: local_second(1).start())

    def inner_send(dst):
        return remote(halves[1] if dst is x else halves[0], dst, m_ss, m_rs, sibling)

    def cross_send(dst, side, b):
        target = {"section": 2 + side} if dst is x else {"section": side}
        return remote(halves[side].at[block(b)], dst.at[block(b)], x_ss.at[side, b], x_rs.at[b], target)

    def send_weights():
        for c in range(pieces):
            when(even, lambda: sent_first(turns[c], wa).start())
            when(odd, lambda: sent_first(c, wu).start())
        when(even, lambda: sent_second(0).start())
        when(odd, lambda: sent_second(1).start())

    for row in range(blocks):
        _, _, first = span_scalars(lengths, row)
        row_load(row).wait()
        packed = slope[0:SEQ, cols(row)]
        for side in range(2):
            at = places(first, side, (BLOCK, SEQ), 0)
            hot = at == lax.broadcasted_iota(jnp.int32, (BLOCK, SEQ), 1)
            halves[side][block(row), :] = mm(hot.astype(f32).astype(bf16), packed).astype(bf16)
        if row == 0:
            pl.semaphore_wait(barrier, 3)
        when(sec == 1, lambda: [cross_send(x, side, row).start() for side in range(2)])
        when(sec == 2, lambda: [cross_send(up, side, row).start() for side in range(2)])
        if row == 0:
            when(odd, send_weights)
    when(sec == 0, lambda: inner_send(x).start())
    norm_pair[core, 0:1, :] = gain_in[...]
    norm_pair[core, 1:2, :] = shift_in[...]
    sent_norm = remote(norm_pair.at[core], norm_pair.at[core], n_ss, n_rs, sibling)
    norm_from = remote(norm_pair.at[1 - core], norm_pair.at[1 - core], n_ss, n_rs, sibling)
    sent_norm.start()
    when(even, send_weights)
    when(sec == 3, lambda: inner_send(up).start())
    pairs_of = [(side, b) for b in range(blocks) for side in range(2)]

    @pl.when(sec == 0)
    def _():
        x[...] = halves[0][...]

    @pl.when(sec == 3)
    def _():
        up[...] = halves[1][...]

    norm_from.wait_recv()
    norms[...] = norm_pair[...]

    def ready_a(c):
        when(even, lambda: local_first(c, wa).wait())
        when(odd, lambda: sent_first(c, wa).wait_recv())

    def ready_u(c):
        when(odd, lambda: local_first(c, wu).wait())
        when(even, lambda: sent_first(c, wu).wait_recv())

    def ready_d(c):
        if c == 0:
            when(even, lambda: local_second(0).wait())
            when(odd, lambda: sent_second(0).wait_recv())
        if c == pieces // 2:
            when(odd, lambda: local_second(1).wait())
            when(even, lambda: sent_second(1).wait_recv())

    def ready_half(step):
        if step == 0:
            when(even, lambda: local_second(0).wait())
            when(odd, lambda: local_second(1).wait())
        else:
            when(even, lambda: sent_second(1).wait_recv())
            when(odd, lambda: sent_second(0).wait_recv())

    refs = dict(
        x=(x, x_h), y=(y, y_h), qkv=(qkv, qkv_h), p=(p, p_h), ctx=(ctx, ctx_h), zh0=(zh0, zh0_h), mid=(mid, mid_h),
        df=(df, df_h), dmid=(dmid, dmid_h),
    )
    order = list(refs)

    def store(name):
        return pltpu.make_async_copy(*refs[name], out_sem.at[order.index(name)])

    def store_cols(c):
        return pltpu.make_async_copy(a.at[:, cols(c)], a_h.at[:, cols(c)], col_sem.at[c])

    def store_du(c):
        return pltpu.make_async_copy(slope.at[:, cols(c)], du_h.at[:, cols(c)], du_sem.at[c])

    def keep(*names):
        for name in names:
            store(name).start()

    picks = lead_picks(lengths, core, True)
    leading = jnp.max(picks, axis=1, keepdims=True) > 0
    hot_leads = picks.astype(bf16)
    pick = lead_picks(lengths, core, False).astype(bf16)
    row_hop = remote(row_own, row_in, r_ss, r_rs, peer)

    @pl.when(backbone)
    def _():
        when(odd, lambda: inner_send(x).wait_recv())
        ready = dict(a=ready_a, u=ready_u, half=ready_half)
        row_own[...] = lead_forward(x, lengths, core, norms, wa, wu, wd, qkv, ready)
        row_hop.start()

    @pl.when(head)
    def _():
        for c in range(3):
            ready_a(c)
        row_hop.wait_recv()

    hot_ref[...] = hot_leads

    def patched(b):
        cross_send(x, 0, b).wait_recv()
        hot = hot_ref[block(b), :]
        is_lead = jnp.max(hot.astype(f32), axis=1, keepdims=True) > 0
        x[block(b), :] = jnp.where(is_lead, mm(hot, row_in[...]).astype(bf16), x[block(b), :])

    def arrive(b):
        when(head, patched, b)

    at_first = {k: f for k, f in (("a", ready_a), ("u", ready_u), ("d", ready_d))}
    ready = {k: (lambda c, f=f: when(head, f, c)) for k, f in at_first.items()}
    save = dict(
        p=p, a=a, slope=slope, zh0=zh0, zh1=zh1, rstd0=rstd0, rstd1=rstd1, keep=keep,
        keep_cols=lambda c: store_cols(c).start(),
    )
    out = forward_pass(x, lengths, core, norms, wa, wu, wd, qkv, ctx, mid, acc, ready, arrive, save)
    for name in ("mid", "x"):
        store(name).wait()
    y[...] = out
    keep("y")
    other = pltpu.make_async_copy(wa, other_first_h, other_sem)
    when(odd, lambda: other.start())
    lead_zh = mm(pick, zh1[...])
    left = jnp.broadcast_to(rstd1[...], (tokens, PAIR))
    total = jnp.zeros((LEADS, PAIR), f32)
    for _ in range(3):
        high = left.astype(bf16)
        left = left - high.astype(f32)
        total = total + mm(pick, high)
    lead_rstd = total[:, 0:1]

    @pl.when(backbone)
    def _():
        for b in range(blocks):
            cross_send(up, 0, b).wait_recv()
        row_hop.wait_send()
        for c in range(pieces):
            lead_slope[:, cols(c)] = mm(pick, slope[:, cols(c)]).astype(bf16)

    when(sec == 2, lambda: inner_send(up).wait_recv())
    when(sec == 0, lambda: inner_send(x).wait_send())
    when(sec == 3, lambda: inner_send(up).wait_send())
    when((sec == 1) | (sec == 2), lambda: [cross_send(x, *at).wait_send() for at in pairs_of])
    sent_norm.wait_send()
    for c in range(pieces):
        sent_first(c, wa).wait_send()
    sent_second(0).wait_send()
    none = {k: (lambda *_: None) for k in ("u", "d", "du")}
    store("y").wait()
    feed_forward_back(up[...], norms, wu, wd, slope, zh1, rstd1, df, slope, acc, dnorm, none)
    dmid[...] = acc[...].astype(bf16)
    dnorm[0:2, :] = jnp.zeros((2, features), f32)
    grad_hop = remote(grad_own, grad_in, l_ss, l_rs, peer)

    @pl.when(head)
    def _():
        keep("df", "dmid")
        for c in range(pieces):
            store_du(c).start()
        attention_back_begin(dmid, norms, wa, zh0, rstd0, do, dctx, acc, d_att)
        grad_own[...] = lead_back(pick, lengths, core, wa, qkv, p, ctx, dctx, acc)
        grad_hop.start()
        grad_hop.wait_send()

    @pl.when(backbone)
    def _():
        base = mm(pick, up[...])
        grad_hop.wait_recv()
        dy = (base + grad_in[...]).astype(bf16).astype(f32)
        extra = dy - base
        dnorm[2:3, :] += jnp.sum(extra * lead_zh, axis=0, keepdims=True)
        dnorm[3:4, :] += jnp.sum(extra, axis=0, keepdims=True)
        dz, _, _ = normalize_back(lead_zh, lead_rstd, norms[1, 0:1, :], dy)
        lead_df = dz.astype(bf16)
        df[...] = jnp.where(leading, mm(hot_leads, lead_df).astype(bf16), df[...])
        keep("df")
        lead_du = []
        for c in range(pieces):
            g = (mm(lead_df, wd[:, cols(c)]) * lead_slope[:, cols(c)].astype(f32)).astype(bf16)
            lead_du.append(g)
            dz = dz + mm(g, wu[:, cols(c)], NT)
        for c in range(pieces):
            slope[:, cols(c)] = jnp.where(leading, mm(hot_leads, lead_du[c]).astype(bf16), slope[:, cols(c)])
            store_du(c).start()
        dmid[...] = jnp.where(leading, mm(hot_leads, dz.astype(bf16)).astype(bf16), dmid[...])
        keep("dmid")

    for name in order:
        if name not in ("mid", "x", "y"):
            store(name).wait()
    for c in range(pieces):
        store_cols(c).wait()
        store_du(c).wait()
    when(odd, lambda: other.wait())


ANY = pl.BlockSpec(memory_space=pl.ANY)
IN_VMEM = pl.BlockSpec(memory_space=pltpu.VMEM)
IN_SMEM = pl.BlockSpec(memory_space=pltpu.SMEM)
S = jax.ShapeDtypeStruct


def vm(*shape):
    return pltpu.VMEM(shape, bf16)


def dma(*shape):
    return pltpu.SemaphoreType.DMA(shape)


def params(number):
    if number is None:
        return pltpu.CompilerParams(vmem_limit_bytes=VMEM_LIMIT)
    return pltpu.CompilerParams(vmem_limit_bytes=VMEM_LIMIT, collective_id=number, has_side_effects=True)


def front(rows_in, lengths, first, second, gain, shift):
    features, ff = first.shape
    tokens = rows_in.shape[0] // 2
    pieces = ff // features
    blocks, pairs = tokens // BLOCK, features // PAIR
    square = S((tokens, features), bf16)
    one = pltpu.SemaphoreType.DMA
    shapes = dict(
        x=square, y=square, qkv=S((tokens, 3 * features), bf16), p=S((blocks, pairs, BLOCK, 2 * BLOCK), bf16),
        ctx=square, zh0=square, mid=square, a=S((tokens, ff), bf16), df=square, du=S((tokens, ff), bf16), dmid=square,
        other_first=S(first.shape, bf16), rstd0=S((tokens, 1), f32), dnorm=S((4, features), f32),
        norms=S((2, 2, features), f32),
    )
    small = ("rstd0", "dnorm", "norms")
    wide = vm(features, ff)
    outs = pl.pallas_call(
        front_kernel,
        out_shape=list(shapes.values()),
        in_specs=[ANY, IN_SMEM, ANY, ANY, IN_VMEM, IN_VMEM],
        out_specs=[IN_VMEM if k in small else ANY for k in shapes],
        scratch_shapes=[wide, wide, wide]
        + [pltpu.VMEM(shapes[k].shape, bf16) for k in ("x", "qkv", "p", "ctx", "zh0", "mid", "a", "du")]
        + [
            vm(tokens, features), vm(tokens, features), pltpu.VMEM((tokens, 1), f32), vm(tokens, features),
            vm(tokens, features), pltpu.VMEM((tokens, features), f32), pltpu.VMEM((2, features), f32), vm(LEADS, ff), vm(tokens, LEADS),
            pltpu.VMEM((LEADS, features), f32), pltpu.VMEM((LEADS, features), f32), vm(LEADS, features), vm(LEADS, features),
            pltpu.VMEM((2, 2, features), f32),
            dma(blocks), dma(pieces + 1), dma(pieces), dma(pieces), one, one, one, one, one, one, dma(2, blocks), dma(blocks),
            one, one, one, one, dma(9), dma(pieces), dma(pieces), one,
        ],
        compiler_params=params(1),
        name="front",
    )(rows_in, lengths, first, second, gain, shift)
    return dict(zip(shapes, outs))


PANEL = 128
RING = 4


def reduce_kernel(
    chain, lengths, dnorm_in, norms, rstd0, x_h, ctx_h, mid_h, a_h, df_h, du_h, dmid_h, zh0_h, qkv_h, p_h, y_h,
    first_h, other_first_h,
    out_h, norm_out, halves_h,
    left, left_t, own_ring, sib_ring, sib_send, part, y1, zin1, mid1, zin2, mid2, y2, final, halves,
    wa, qkv, p, do, dctx, acc, y_buf, dnorm, norm,
    left_sem, own_sem, ring_sem, out_sem, sib_ss, sib_rs, y1_ss, y1_rs, z1_ss, z1_rs, m1_ss, m1_rs,
    z2_ss, z2_rs, m2_ss, m2_rs, y2_ss, y2_rs, f_ss, f_rs, o_ss, o_rs, c_ss, c_rs, h_sem, a_sem, in_sem, n_ss, n_rs,
):
    sec = lax.axis_index("section")
    dp = lax.axis_index("dp")
    core = sec % 2
    panels, rows, _ = final.shape
    tokens = acc.shape[0]
    half = rows // 2
    features = rows
    last = panels
    spot = dp // 2
    side = spot // (chain // 2)
    depth = chain // 2 - 1
    dist = side * (spot - chain // 2) + (1 - side) * (chain // 2 - 1 - spot)
    inner = dist == 0
    y = dp % 2
    sibling = {"section": sec + 1 - 2 * core}
    across_y = {"dp": dp + 1 - 2 * y}
    inward = {"dp": dp + 2 - 4 * side}
    outward = {"dp": dp - 2 + 4 * side}
    has_out = dist < depth

    barrier = pltpu.get_barrier_semaphore()
    at_head = sec // 2
    dx_buf = dctx
    inside = (sec == 0) | (sec == 3)
    beyond = {"section": 2 - sec // 2}
    others = [{"section": (sec + step) % 4} for step in (1, 2, 3)]
    for target in (*others, across_y, inward):
        pl.semaphore_signal(barrier, inc=1, device_id=target, device_id_type=MESH)

    @pl.when(has_out)
    def _():
        pl.semaphore_signal(barrier, inc=1, device_id=outward, device_id_type=MESH)

    def rows_at(which):
        return pl.ds(pl.multiple_of(which * half, half), half)

    mine, theirs = rows_at(y), rows_at(1 - y)
    kept, rest = rows_at(side), rows_at(1 - side)

    def to_sibling(j):
        return remote(sib_send.at[j % RING], part.at[j], sib_ss.at[j % RING], sib_rs.at[j], sibling)

    def one_y(j):
        i = j // 2
        return remote(part.at[j, theirs], y1.at[i], y1_ss.at[i], y1_rs.at[i], across_y)

    def one_in(j):
        i = j // 2
        return remote(part.at[j, mine], zin1.at[i], z1_ss.at[i], z1_rs.at[i], inward)

    def one_mid(j):
        i = j // 2
        return remote(part.at[j, mine], mid1.at[i], m1_ss.at[i], m1_rs.at[i], inward)

    def one_out(j):
        return remote(final.at[j, mine], final.at[j, mine], f_ss.at[0, j], f_rs.at[0, j], outward)

    def one_back(j):
        return remote(final.at[j, mine], final.at[j, mine], f_ss.at[1, j], f_rs.at[1, j], across_y)

    def one_back_in(j):
        return remote(final.at[j, theirs], final.at[j, theirs], f_ss.at[1, j], f_rs.at[1, j], across_y)

    def two_in(j):
        i = j // 2
        return remote(part.at[j], zin2.at[i], z2_ss.at[i], z2_rs.at[i], inward)

    def two_mid(j):
        i = j // 2
        return remote(part.at[j, rest], mid2.at[i], m2_ss.at[i], m2_rs.at[i], inward)

    def two_y(j):
        i = j // 2
        return remote(part.at[j, kept], y2.at[i], y2_ss.at[i], y2_rs.at[i], across_y)

    def two_swap(j):
        return remote(final.at[j, kept], final.at[j, kept], f_ss.at[2, j], f_rs.at[1, j], inward)

    def two_swap_in(j):
        return remote(final.at[j, rest], final.at[j, rest], f_ss.at[2, j], f_rs.at[1, j], inward)

    def two_out_kept(j):
        return remote(final.at[j, kept], final.at[j, kept], f_ss.at[0, j], f_rs.at[0, j], outward)

    def two_out_rest(j):
        return remote(final.at[j, rest], final.at[j, rest], f_ss.at[1, j], f_rs.at[1, j], outward)

    down = a_h.shape[1] // (2 * PANEL)
    outer_cols = features // PANEL
    raw = dict(x=(x_h, 0), ctx=(ctx_h, 1), df=(df_h, 2), mid=(mid_h, 3))

    def left_of(who, j):
        late = jnp.minimum(j // down, 1)
        even = 2 * (1 - late) + late * (1 - jnp.minimum(j // (down + outer_cols), 1))
        odd = 2 * (1 - late) + 3 * late
        return who * odd + (1 - who) * even

    def columns(col):
        return pl.ds(pl.multiple_of(col * PANEL, PANEL), PANEL)

    def fetch_down(who, j, ring, sem):
        return pltpu.make_async_copy(a_h.at[:, columns(who * down + j)], ring.at[j % RING], sem.at[j % RING])

    def fetch_up(j, ring, sem):
        return pltpu.make_async_copy(du_h.at[:, columns(j - down)], ring.at[j % RING], sem.at[j % RING])

    def fetch(who, j, ring, sem):
        when(j < down, lambda: fetch_down(who, j, ring, sem).start())
        when((j >= down) & (j < last) & (who == 1), lambda: fetch_up(j, ring, sem).start())

    def right(who, j, ring, sem, use):
        def from_ring():
            pltpu.make_async_copy(a_h.at[:, columns(0)], ring.at[j % RING], sem.at[j % RING]).wait()
            use(ring[j % RING])

        when((j < down) | ((j < last) & (who == 1)), from_ring)
        when((j >= down) & (j < down + outer_cols) & (who == 0), lambda: use(do[:, columns(j - down)]))
        when(
            (j >= down + outer_cols) & (j < last) & (who == 0), lambda: use(qkv[:, columns(j - down - outer_cols)])
        )

    def to_out(j):
        late = jnp.minimum(j // down, 1)
        even = jnp.where(j < down + outer_cols, j - down + 3 * outer_cols, j - down - outer_cols)
        col = (1 - late) * (4 * outer_cols + j) + late * (core * (j - down) + (1 - core) * even)
        return pltpu.make_async_copy(final.at[j], out_h.at[:, columns(col)], out_sem.at[j])


    def own_send(src):
        return remote(src, halves.at[core], o_ss, o_rs, sibling)

    def own_from():
        return remote(dx_buf, halves.at[1 - core], o_ss, o_rs, sibling)

    def across_send(src):
        return remote(src, halves.at[core], c_ss, c_rs.at[core], beyond)

    def across_from(side):
        return remote(dx_buf, halves.at[side], c_ss, c_rs.at[side], beyond)

    def load_left(name):
        return pltpu.make_async_copy(raw[name][0], left, left_sem)

    loads = dict(dmid=(dmid_h, do), zh0=(zh0_h, dctx), qkv=(qkv_h, qkv), p=(p_h, p), y=(y_h, y_buf))
    names = list(loads)

    def load(name):
        return pltpu.make_async_copy(*loads[name], in_sem.at[names.index(name)])

    def load_wa(own, c):
        cols = pl.ds(c * features, features)
        return pltpu.make_async_copy((first_h if own else other_first_h).at[:, cols], wa.at[:, cols], a_sem.at[c])

    load_left("df").start()
    for j in range(RING):
        fetch_down(core, j, own_ring, own_sem).start()
        fetch_down(1 - core, j, sib_ring, ring_sem).start()
    load("dmid").start()
    load("zh0").start()
    for c in (3, 0, 1, 2):
        when(core == 0, lambda: load_wa(True, c).start())
        when(core == 1, lambda: load_wa(False, c).start())
    for name in ("qkv", "p", "y"):
        load(name).start()

    def turn(i):
        for b in range(features // BLOCK):
            grid = (BLOCK, features)
            eye = lax.broadcasted_iota(jnp.int32, grid, 0) + b * BLOCK == lax.broadcasted_iota(jnp.int32, grid, 1)
            left_t[i, pl.ds(b * BLOCK, BLOCK), :] = mm(eye.astype(f32).astype(bf16), left[...], NT).astype(bf16)

    def norm_panel(other):
        chosen = jnp.where(core == other, dnorm[2:4, :], dnorm[0:2, :])
        strips = [
            chosen[r : r + 1, c * PANEL : (c + 1) * PANEL]
            for r in range(2)
            for c in range(features // PANEL)
        ]
        return jnp.concatenate(strips + [jnp.zeros((16 - len(strips), PANEL), f32)], axis=0)

    pl.semaphore_wait(barrier, 5 + has_out.astype(jnp.int32))

    def stage_send(j):
        when(j >= RING, lambda: to_sibling(j - RING).wait_send())

        def use(block):
            sib_send[j % RING] = mm(left_t[left_of(1 - core, j)], block).astype(bf16)

        right(1 - core, j, sib_ring, ring_sem, use)
        to_sibling(j).start()
        fetch(1 - core, j + RING, sib_ring, ring_sem)

    def stage_part(j):
        to_sibling(j).wait_recv()

        def use(block):
            own = mm(left_t[left_of(core, j)], block)
            part[j] = (own + part[j].astype(f32)).astype(bf16)

        right(core, j, own_ring, own_sem, use)
        fetch(core, j + RING, own_ring, own_sem)
        when(j % 2 == 0, lambda: one_y(j).start())
        when((j % 2 == 1) & (dist == depth) & (depth > 0), lambda: two_in(j).start())
        when((j % 2 == 1) & (dist == depth) & (depth == 0), lambda: two_mid(j).start())

    def one_halves(j):
        one_y(j).wait_recv()
        part[j, mine, :] = (part[j, mine, :].astype(f32) + y1[j // 2].astype(f32)).astype(bf16)
        when((dist == depth) & (dist > 0), lambda: one_in(j).start())
        when((dist == depth) & inner, lambda: one_mid(j).start())

    def one_chain(j):
        one_in(j).wait_recv()
        part[j, mine, :] = (part[j, mine, :].astype(f32) + zin1[j // 2].astype(f32)).astype(bf16)
        when(dist > 0, lambda: one_in(j).start())
        when(inner, lambda: one_mid(j).start())

    def one_total(j):
        one_mid(j).wait_recv()
        final[j, mine, :] = (part[j, mine, :].astype(f32) + mid1[j // 2].astype(f32)).astype(bf16)
        when(has_out, lambda: one_out(j).start())
        one_back(j).start()

    def one_spread(j):
        one_out(j).wait_recv()
        when(has_out, lambda: one_out(j).start())
        one_back(j).start()

    def two_chain(j):
        two_in(j).wait_recv()
        part[j] = (part[j].astype(f32) + zin2[j // 2].astype(f32)).astype(bf16)
        when(dist > 0, lambda: two_in(j).start())
        when(inner, lambda: two_mid(j).start())

    def two_halves(j):
        two_mid(j).wait_recv()
        part[j, kept, :] = (part[j, kept, :].astype(f32) + mid2[j // 2].astype(f32)).astype(bf16)
        two_y(j).start()

    def two_total(j):
        two_y(j).wait_recv()
        final[j, kept, :] = (part[j, kept, :].astype(f32) + y2[j // 2].astype(f32)).astype(bf16)
        two_swap(j).start()
        when(has_out, lambda: two_out_kept(j).start())

    def two_swapped(j):
        two_swap_in(j).wait_recv()
        when(has_out, lambda: two_out_rest(j).start())

    def two_spread_kept(j):
        two_out_kept(j).wait_recv()
        when(has_out, lambda: two_out_kept(j).start())

    def two_spread_rest(j):
        two_out_rest(j).wait_recv()
        when(has_out, lambda: two_out_rest(j).start())

    def finish(j):
        when(j % 2 == 0, lambda: one_back_in(j).wait_recv())

        to_out(j).start()

    last_lag = 7 + 4 * depth

    pairs = features // PAIR
    items = tokens // BLOCK * pairs
    begin = 4

    def turn_next(name, following):
        load_left(name).wait()
        turn(raw[name][1])
        if following:
            load_left(following).start()

    def attention_begin():
        load("dmid").wait()
        load("zh0").wait()
        load_wa(True, 3).wait()
        attention_back_begin(do, norms, wa, dctx, rstd0, do, dctx, acc, dnorm)

    def send_rows():
        load("y").wait()

        @pl.when(at_head == 1)
        def _():
            leading = jnp.max(lead_picks(lengths, core, True), axis=1, keepdims=True) > 0
            dx_buf[...] = jnp.where(leading, 0.0, acc[...]).astype(bf16)

        @pl.when(at_head == 0)
        def _():
            dx_buf[...] = acc[...].astype(bf16)

        def go(own, across):
            across_send(across).start()
            when(~inside, lambda: own_send(own).start())

            @pl.when(inside)
            def _():
                halves[core] = own[...]

        when(at_head == 1, go, y_buf, dx_buf)
        when(at_head == 0, go, dx_buf, y_buf)

    def norm_hop(src, dst, i, target):
        return remote(norm.at[src], norm.at[dst], n_ss.at[i], n_rs.at[i], target)

    norm_sib = norm_hop(0, 1, 0, sibling)
    norm_y = norm_hop(2, 3, 1, across_y)
    norm_in_hop = norm_hop(7, 4, 2, inward)
    norm_mid = norm_hop(7, 5, 3, inward)
    norm_far = norm_hop(6, 6, 4, outward)

    def norm_steps(t):
        @pl.when(t == 0)
        def _():
            norm[0] = norm_panel(0)
            norm_sib.start()

        @pl.when(t == 2)
        def _():
            norm_sib.wait_recv()
            norm[2] = norm_panel(1) + norm[1]
            norm_y.start()

        @pl.when(t == 4)
        def _():
            norm_y.wait_recv()
            norm[7] = norm[2] + norm[3]

        @pl.when((t == 4 + 2 * (depth - dist)) & (dist < depth))
        def _():
            norm_in_hop.wait_recv()
            norm[7] = norm[7] + norm[4]

        @pl.when(t == 4 + 2 * (depth - dist))
        def _():
            when(dist > 0, lambda: norm_in_hop.start())
            when(inner, lambda: norm_mid.start())

        @pl.when((t == 6 + 2 * depth) & inner)
        def _():
            norm_mid.wait_recv()
            norm[6] = norm[7] + norm[5]
            when(has_out, lambda: norm_far.start())

        @pl.when((t == 6 + 2 * (depth + dist)) & (dist > 0))
        def _():
            norm_far.wait_recv()
            when(has_out, lambda: norm_far.start())

    dnorm[...] = dnorm_in[...]
    turn_next("df", "mid")

    def step(t, carry):
        def at(lag, kind, cond, run):
            j = t - lag
            ok = (j >= 0) & (j < panels)
            if kind is not None:
                ok = ok & (j % 2 == kind)
            if cond is not None:
                ok = ok & cond
            when(ok, run, j)

        at(7 + 2 * (depth + dist), 1, dist > 0, two_spread_rest)
        at(5 + 2 * (depth + dist), 1, dist > 0, two_spread_kept)
        at(5 + 2 * (depth + dist), 0, dist > 0, one_spread)
        at(7 + 2 * depth, 1, inner, two_swapped)
        at(5 + 2 * depth, 1, inner, two_total)
        at(5 + 2 * depth, 0, inner, one_total)
        at(3 + 2 * depth, 1, inner, two_halves)
        at(3 + 2 * (depth - dist), 0, dist < depth, one_chain)
        at(1 + 2 * (depth - dist), 1, dist < depth, two_chain)
        at(3, 0, None, one_halves)
        at(1, None, None, stage_part)
        at(0, None, None, stage_send)
        at(last_lag + 1, None, None, finish)
        when(t == begin, attention_begin)
        item = t - begin - 1
        when(t == begin + 1, lambda: [load("qkv").wait(), load("p").wait()])
        when((item >= 0) & (item < items), lambda: attention_back_item(item // pairs, item % pairs, qkv, p, dctx))
        when(t == 8, turn_next, "mid", "ctx")
        when(t == 9, turn_next, "ctx", "x")
        when(t == 10, turn_next, "x", None)
        for c in range(3):
            when(t == begin + items + 1 + c, lambda: [load_wa(True, c).wait(), attention_back_end(c, wa, qkv, acc)])
        when(t == begin + items + 4, send_rows)
        norm_steps(t - begin - 1)
        return carry

    lax.fori_loop(0, panels + last_lag + 1, step, 0)

    @pl.when(inside)
    def _():
        own_from().wait_recv()

    @pl.when(~inside)
    def _():
        own_send(dx_buf).wait_send()
        across_from(0).wait_recv()
        across_from(1).wait_recv()

    across_send(dx_buf).wait_send()
    norm_sib.wait_send()
    norm_y.wait_send()
    when(dist > 0, lambda: norm_in_hop.wait_send())
    when(inner, lambda: norm_mid.wait_send())
    when(has_out, lambda: norm_far.wait_send())
    norm_out[...] = norm[6]
    rows_done = pltpu.make_async_copy(halves, halves_h, h_sem)
    rows_done.start()

    def drain(j, carry):
        when(j >= panels - RING, lambda: to_sibling(j).wait_send())
        to_out(j).wait()

        @pl.when(j % 2 == 0)
        def _():
            one_y(j).wait_send()
            when(dist > 0, lambda: one_in(j).wait_send())
            when(inner, lambda: one_mid(j).wait_send())
            when(has_out, lambda: one_out(j).wait_send())
            one_back(j).wait_send()

        @pl.when(j % 2 == 1)
        def _():
            when(dist > 0, lambda: two_in(j).wait_send())

            @pl.when(inner)
            def _():
                two_mid(j).wait_send()
                two_y(j).wait_send()
                two_swap(j).wait_send()

            @pl.when(has_out)
            def _():
                two_out_kept(j).wait_send()
                two_out_rest(j).wait_send()

        return carry

    lax.fori_loop(0, panels, drain, 0)
    rows_done.wait()


def reduce_gradients(lengths, first, saved, chain):
    tokens, features = saved["x"].shape
    ff = saved["a"].shape[1]
    width = ff + ff // 2
    panels = width // PANEL
    evens, odds = (panels + 1) // 2, panels // 2
    h = features // 2
    one = pltpu.SemaphoreType.DMA
    arrays = [saved[k] for k in ("x", "ctx", "mid", "a", "df", "du", "dmid", "zh0", "qkv", "p", "y")]
    return pl.pallas_call(
        functools.partial(reduce_kernel, chain),
        out_shape=[S((features, width), bf16), S((16, PANEL), f32), S((2, tokens, features), bf16)],
        in_specs=[IN_SMEM] + [IN_VMEM] * 3 + [ANY] * 13,
        out_specs=[ANY, IN_VMEM, ANY],
        scratch_shapes=[
            vm(tokens, features), vm(4, features, tokens), vm(RING, tokens, PANEL), vm(RING, tokens, PANEL),
            vm(RING, features, PANEL), vm(panels, features, PANEL),
            vm(evens, h, PANEL), vm(evens, h, PANEL), vm(evens, h, PANEL),
            vm(odds, features, PANEL), vm(odds, h, PANEL), vm(odds, h, PANEL),
            vm(panels, features, PANEL), vm(2, tokens, features),
            vm(features, ff), vm(tokens, 3 * features), pltpu.VMEM(saved["p"].shape, bf16), vm(tokens, features),
            vm(tokens, features), pltpu.VMEM((tokens, features), f32), vm(tokens, features),
            pltpu.VMEM((4, features), f32), pltpu.VMEM((8, 16, PANEL), f32),
            one, dma(RING), dma(RING), dma(panels), dma(RING), dma(panels),
            dma(evens), dma(evens), dma(evens), dma(evens), dma(evens), dma(evens),
            dma(odds), dma(odds), dma(odds), dma(odds), dma(odds), dma(odds), dma(3, panels), dma(2, panels),
            one, one, one, dma(2), one, dma(ff // features), dma(5), dma(5), dma(5),
        ],
        compiler_params=params(3),
        name="reduce_gradients",
    )(lengths, saved["dnorm"], saved["norms"], saved["rstd0"], *arrays, first, saved["other_first"])


def finish_kernel(lengths, total, halves, norm_in, first_out, second_out, rows_out, gain_out, shift_out):
    step = pl.program_id(0)
    features = rows_out.shape[1]
    wide = first_out.shape[1]
    first_out[...] = total[:, pl.ds(0, wide)].astype(f32)
    second_out[...] = total[:, pl.ds(wide, second_out.shape[1])].astype(f32)
    size = rows_out.shape[0]
    row = step // (SEQ // size)
    _, _, first = span_scalars(lengths, row)
    at = lax.broadcasted_iota(jnp.int32, (size, BLOCK), 0) + step % (SEQ // size) * size
    out = None
    for side in range(2):
        hot = at == places(first, side, (size, BLOCK), 1)
        part = mm(hot.astype(f32).astype(bf16), halves[side])
        out = part if out is None else out + part
    rows_out[...] = out
    strips = features // PANEL
    for r, ref in enumerate((gain_out, shift_out)):
        ref[...] = jnp.concatenate([norm_in[r * strips + c : r * strips + c + 1, :] for c in range(strips)], axis=1)


def finish(lengths, total, halves, norm_in, ff):
    features, width = total.shape
    tokens = halves.shape[1]
    size = SEQ
    steps = 2 * tokens // size
    part = features // steps
    row_spec = pl.BlockSpec((1, features), lambda i: (0, 0))
    return pl.pallas_call(
        finish_kernel,
        grid=(steps,),
        out_shape=[
            S((features, ff), f32), S((features, width - ff), f32), S((2 * tokens, features), f32),
            S((1, features), f32), S((1, features), f32),
        ],
        in_specs=[
            IN_SMEM, pl.BlockSpec((part, width), lambda i: (i, 0)),
            pl.BlockSpec((2, BLOCK, features), lambda i: (0, i // (SEQ // size), 0)), IN_VMEM,
        ],
        out_specs=[
            pl.BlockSpec((part, ff), lambda i: (i, 0)), pl.BlockSpec((part, width - ff), lambda i: (i, 0)),
            pl.BlockSpec((size, features), lambda i: (i, 0)), row_spec, row_spec,
        ],
        compiler_params=params(None),
        name="finish",
    )(lengths, total, halves, norm_in)


def per_device(section_rows, span_lengths, first_weights, second_weights, norm_gain, norm_shift):
    first, second = first_weights[0], second_weights[0]
    saved = front(section_rows[0], span_lengths, first, second, norm_gain, norm_shift)
    total, norm_total, halves = reduce_gradients(span_lengths, first, saved, lax.axis_size("dp") // 2)
    d_first, d_second, rows, gain, shift = finish(span_lengths, total, halves, norm_total, first.shape[1])
    return rows[None], d_first[None], d_second[None], gain, shift


def solution(mesh):
    in_specs = (
        P("section", "dp", None),
        P("dp", None),
        P("section", None, None),
        P("section", None, None),
        P("section", None),
        P("section", None),
    )
    out_specs = (
        P("section", "dp", None),
        P("section", None, None),
        P("section", None, None),
        P("section", None),
        P("section", None),
    )
    return jax.shard_map(
        per_device, mesh=mesh, in_specs=in_specs, out_specs=out_specs, check_vma=False
    )
```

```python
import functools

import jax
import jax.numpy as jnp
from jax import lax
from jax.experimental import pallas as pl
from jax.experimental.pallas import tpu as pltpu
from jax.sharding import PartitionSpec as P

HEAD_DIM = 64
PAIR = 2 * HEAD_DIM
BLOCK = 256
SEQ = 512
LEADS = 16
VMEM_LIMIT = 60 << 20
MESH = pl.DeviceIdType.MESH
f32 = jnp.float32
bf16 = jnp.bfloat16
epsilon = 1e-12
NN = (((1,), (0,)), ((), ()))
NT = (((1,), (1,)), ((), ()))
TN = (((0,), (0,)), ((), ()))
LOG2E = 1.4426950408889634


def mm(a, b, dims=NN):
    return lax.dot_general(a, b, dims, preferred_element_type=f32)


def when(cond, step, *args):
    @pl.when(cond)
    def _():
        step(*args)


def remote(src, dst, ss, rs, target):
    return pltpu.make_async_remote_copy(
        src_ref=src, dst_ref=dst, send_sem=ss, recv_sem=rs, device_id=target, device_id_type=MESH
    )


def gelu_and_slope(u):
    bell = jnp.exp2(u * u * (-0.5 * LOG2E))
    t = 1.0 / (1.0 + (0.3275911 * 0.5**0.5) * jnp.abs(u))
    poly = t * (0.127414796 + t * (-0.142248368 + t * (0.7107068705 + t * (-0.7265760135 + t * 0.5307027145))))
    tail = poly * bell
    cdf = jnp.where(u < 0, tail, 1.0 - tail)
    return u * cdf, cdf + u * bell * 0.3989422804014327


def normalize(z):
    centered = z - jnp.mean(z, axis=-1, keepdims=True)
    rstd = lax.rsqrt(jnp.mean(centered * centered, axis=-1, keepdims=True) + epsilon)
    return centered * rstd, rstd


def normalize_back(zh, rstd, gain, dy):
    g = dy * gain
    mean_g = jnp.mean(g, axis=-1, keepdims=True)
    mean_gz = jnp.mean(g * zh, axis=-1, keepdims=True)
    dz = rstd * (g - mean_g - zh * mean_gz)
    return dz, jnp.sum(dy * zh, axis=0, keepdims=True), jnp.sum(dy, axis=0, keepdims=True)


def span_scalars(lengths, row):
    ends, starts, first, total = [], [], 0, 0
    for j in range(lengths.shape[1]):
        size = lengths[row, j]
        starts.append(total)
        first = first + jnp.where(size == BLOCK, total, 0)
        total = total + size
        ends.append(total)
    return ends, starts, first


def places(first, core, shape, axis):
    at = lax.broadcasted_iota(jnp.int32, shape, axis) + (first + core * BLOCK)
    return jnp.where(at >= SEQ, at - SEQ, at)


def mask_bias(lengths, row, core):
    ends, _, first = span_scalars(lengths, row)

    def segment(at):
        return sum((at >= end).astype(jnp.int32) for end in ends)

    rows = segment(places(first, core, (BLOCK, BLOCK), 0))
    cols = segment(places(first, core, (BLOCK, BLOCK), 1))
    return jnp.where(rows == cols, 0.0, -1e30)


def lead_picks(lengths, core, by_rows):
    parts = []
    per_row = lengths.shape[1] - 1
    shape = (BLOCK, LEADS) if by_rows else (LEADS, BLOCK)
    for row in range(lengths.shape[0]):
        _, starts, first = span_scalars(lengths, row)
        at = places(first, core, shape, 0 if by_rows else 1)
        slot = lax.broadcasted_iota(jnp.int32, shape, 1 if by_rows else 0)
        hit = sum(
            ((slot == row * per_row + j) & (at == starts[j])).astype(jnp.int32) for j in range(per_row)
        )
        parts.append(hit.astype(f32))
    return jnp.concatenate(parts, axis=0 if by_rows else 1)


def lane_masks():
    return lax.broadcasted_iota(jnp.int32, (BLOCK, PAIR), 1) < HEAD_DIM


def forward_pass(x, lengths, core, norms, wa, wu, wd, qkv, ctx, mid, acc, ready, arrive, save):
    tokens, features = x.shape
    pairs = features // PAIR
    first = lane_masks()
    zero = jnp.zeros((BLOCK, PAIR), bf16)

    def block_step(b, carry):
        rows = pl.ds(pl.multiple_of(b * BLOCK, BLOCK), BLOCK)
        arrive(b)
        for c in range(3):
            cols = pl.ds(c * features, features)
            qkv[rows, cols] = mm(x[rows, :], wa[:, cols]).astype(bf16)
        bias = mask_bias(lengths, b, core)
        for h in range(pairs):
            q = qkv[rows, pl.ds(h * PAIR, PAIR)]
            k = qkv[rows, pl.ds(features + h * PAIR, PAIR)]
            v = qkv[rows, pl.ds(2 * features + h * PAIR, PAIR)]
            total = None
            for side in range(2):
                own = first if side == 0 else ~first
                s = mm(q, jnp.where(own, k, zero), NT) * (HEAD_DIM**-0.5) + bias
                e = jnp.exp(s - jnp.max(s, axis=-1, keepdims=True))
                pr = (e * (1.0 / jnp.sum(e, axis=-1, keepdims=True))).astype(bf16)
                save["p"][b, h, :, pl.ds(side * BLOCK, BLOCK)] = pr
                part = mm(pr, jnp.where(own, v, zero))
                total = part if total is None else total + part
            ctx[rows, pl.ds(h * PAIR, PAIR)] = total.astype(bf16)
        return carry

    lax.fori_loop(0, tokens // BLOCK, block_step, 0)
    ready["a"](3)
    zn, r = normalize(x[...].astype(f32) + mm(ctx[...], wa[:, pl.ds(3 * features, features)]))
    save["keep"]("x", "qkv", "p", "ctx")
    save["rstd0"][...] = r
    save["zh0"][...] = zn.astype(bf16)
    mid[...] = (zn * norms[0, 0:1, :] + norms[0, 1:2, :]).astype(bf16)
    acc[...] = mid[...].astype(f32)
    save["keep"]("zh0", "mid")
    pieces = wu.shape[1] // features
    cols = [pl.ds(c * features, features) for c in range(pieces)]
    ready["u"](0)
    ahead = mm(mid[...], wu[:, cols[0]])
    for c in range(pieces):
        u = ahead
        if c + 1 < pieces:
            ready["u"](c + 1)
            ahead = mm(mid[...], wu[:, cols[c + 1]])
        act, slope = gelu_and_slope(u)
        act = act.astype(bf16)
        save["a"][:, cols[c]] = act
        save["slope"][:, cols[c]] = slope.astype(bf16)
        save["keep_cols"](c)
        ready["d"](c)
        acc[...] += mm(act, wd[:, cols[c]], NT)
    zn, r = normalize(acc[...])
    save["rstd1"][...] = r
    save["zh1"][...] = zn.astype(bf16)
    return (zn * norms[1, 0:1, :] + norms[1, 1:2, :]).astype(bf16)


def feed_forward_back(dy, norms, wu, wd, slope, zh1, rstd1, df, du, acc, dnorm, ready):
    features = wu.shape[0]
    dz, dgain, dshift = normalize_back(zh1[...].astype(f32), rstd1[...], norms[1, 0:1, :], dy.astype(f32))
    dnorm[2:3, :] = dgain
    dnorm[3:4, :] = dshift
    df[...] = dz.astype(bf16)
    acc[...] = dz
    for c in range(wu.shape[1] // features):
        cols = pl.ds(c * features, features)
        ready["d"](c)
        da = mm(df[...], wd[:, cols])
        ready["du"](c)
        g = (da * slope[:, cols].astype(f32)).astype(bf16)
        du[:, cols] = g
        ready["u"](c)
        acc[...] += mm(g, wu[:, cols], NT)


def attention_back_begin(d_mid, norms, wa, zh0, rstd0, do, dctx, acc, dnorm):
    tokens, features = acc.shape
    dgain = dshift = None
    for b in range(tokens // BLOCK):
        rows = pl.ds(b * BLOCK, BLOCK)
        dz, dg, ds = normalize_back(
            zh0[rows, :].astype(f32), rstd0[rows, :], norms[0, 0:1, :], d_mid[rows, :].astype(f32)
        )
        dgain, dshift = (dg, ds) if b == 0 else (dgain + dg, dshift + ds)
        acc[rows, :] = dz
        do[rows, :] = dz.astype(bf16)
        dctx[rows, :] = mm(dz.astype(bf16), wa[:, pl.ds(3 * features, features)], NT).astype(bf16)
    dnorm[0:1, :] = dgain
    dnorm[1:2, :] = dshift


def attention_back_item(b, h, qkv, p, dctx):
    features = dctx.shape[1]
    first = lane_masks()
    zero = jnp.zeros((BLOCK, PAIR), bf16)
    scale = HEAD_DIM**-0.5
    rows = pl.ds(pl.multiple_of(b * BLOCK, BLOCK), BLOCK)
    at = [pl.ds(pl.multiple_of(part * features + h * PAIR, PAIR), PAIR) for part in range(3)]
    q, k, v = (qkv[rows, cols] for cols in at)
    dc = dctx[rows, at[0]]
    dq = dk = dv = None
    for side in range(2):
        own = first if side == 0 else ~first
        pr = p[b, h, :, pl.ds(side * BLOCK, BLOCK)]
        prf = pr.astype(f32)
        dp = mm(dc, jnp.where(own, v, zero), NT)
        r = jnp.sum(dp * prf, axis=-1, keepdims=True)
        ds = (prf * (dp - r)).astype(bf16)
        parts = (
            mm(ds, jnp.where(own, k, zero)),
            mm(ds, jnp.where(own, q, zero), TN),
            mm(pr, jnp.where(own, dc, zero), TN),
        )
        if dq is None:
            dq, dk, dv = parts
        else:
            dq, dk, dv = dq + parts[0], dk + parts[1], dv + parts[2]
    qkv[rows, at[0]] = (dq * scale).astype(bf16)
    qkv[rows, at[1]] = (dk * scale).astype(bf16)
    qkv[rows, at[2]] = dv.astype(bf16)


def attention_back_end(part, wa, dqkv, acc):
    features = wa.shape[0]
    cols = pl.ds(part * features, features)
    for b in range(acc.shape[0] // BLOCK):
        rows = pl.ds(b * BLOCK, BLOCK)
        acc[rows, :] += mm(dqkv[rows, cols], wa[:, cols], NT)


def head_lanes(features):
    lane = lax.broadcasted_iota(jnp.int32, (LEADS, features), 1)
    return [(lane >= h * HEAD_DIM) & (lane < (h + 1) * HEAD_DIM) for h in range(features // HEAD_DIM)]


def spread_heads(rows):
    wide = rows.astype(f32)
    return jnp.concatenate([jnp.where(own, wide, 0.0) for own in head_lanes(rows.shape[1])], axis=0).astype(bf16)


def fold_heads(wide):
    total = None
    for h, own in enumerate(head_lanes(wide.shape[1])):
        part = jnp.where(own, wide[h * LEADS : (h + 1) * LEADS, :], 0.0)
        total = part if total is None else total + part
    return total


def lead_probs(queries, keys, lengths, core):
    tokens, features = keys.shape
    per_row = lengths.shape[1] - 1
    parts = []
    for row in range(tokens // BLOCK):
        ends, _, first = span_scalars(lengths, row)
        at = places(first, core, (LEADS, BLOCK), 1)
        segment = sum((at >= end).astype(jnp.int32) for end in ends)
        span = lax.broadcasted_iota(jnp.int32, (LEADS, BLOCK), 0) - row * per_row
        parts.append(jnp.where((span == segment) & (span < per_row), 0.0, -1e30))
    bias = jnp.concatenate([jnp.concatenate(parts, axis=1)] * (features // HEAD_DIM), axis=0)
    s = mm(spread_heads(queries), keys, NT) * (HEAD_DIM**-0.5) + bias
    e = jnp.exp(s - jnp.max(s, axis=-1, keepdims=True))
    return (e * (1.0 / jnp.sum(e, axis=-1, keepdims=True))).astype(bf16)


def lead_forward(x, lengths, core, norms, wa, wu, wd, qkv, ready):
    features = x.shape[1]
    pieces = wu.shape[1] // features
    cols = [pl.ds(c * features, features) for c in range(4)]
    own = mm(lead_picks(lengths, core, False).astype(bf16), x[...]).astype(bf16)
    for c in (1, 2):
        ready["a"](c)
        qkv[:, cols[c]] = mm(x[...], wa[:, cols[c]]).astype(bf16)
    ready["a"](0)
    probs = lead_probs(mm(own, wa[:, cols[0]]).astype(bf16), qkv[:, cols[1]], lengths, core)
    ctx = fold_heads(mm(probs, qkv[:, cols[2]])).astype(bf16)
    ready["a"](3)
    zn, _ = normalize(own.astype(f32) + mm(ctx, wa[:, cols[3]]))
    mid = (zn * norms[0, 0:1, :] + norms[0, 1:2, :]).astype(bf16)
    out = mid.astype(f32)
    for step in range(pieces):
        c = (step + core * (pieces // 2)) % pieces
        at = pl.ds(pl.multiple_of(c * features, features), features)
        ready["u"](c)
        act, _ = gelu_and_slope(mm(mid, wu[:, at]))
        if step % (pieces // 2) == 0:
            ready["half"](step)
        out = out + mm(act.astype(bf16), wd[:, at], NT)
    zn, _ = normalize(out)
    return (zn * norms[1, 0:1, :] + norms[1, 1:2, :]).astype(bf16)


def lead_back(pick, lengths, core, wa, qkv, p, ctx, dctx, dz):
    tokens, features = ctx.shape
    scale = HEAD_DIM**-0.5
    heads = features // HEAD_DIM
    cols = [pl.ds(c * features, features) for c in range(3)]
    q16, v16 = (mm(pick, qkv[:, cols[c]]).astype(bf16) for c in (0, 2))
    low = lead_probs(q16, qkv[:, cols[1]], lengths, core)
    probs = low.astype(f32)
    dp = mm(spread_heads(mm(pick, dctx[...]).astype(bf16)), qkv[:, cols[2]], NT)
    ds = (probs * (dp - jnp.sum(dp * probs, axis=-1, keepdims=True))).astype(bf16)
    dq = (fold_heads(mm(ds, qkv[:, cols[1]])) * scale).astype(bf16)
    seen = []
    for h in range(heads):
        keys = pl.ds(h % 2 * BLOCK, BLOCK)
        seen.append(
            jnp.concatenate(
                [mm(pick[:, b * BLOCK : (b + 1) * BLOCK], p[b, h // 2, :, keys], NT) for b in range(tokens // BLOCK)],
                axis=1,
            )
        )
    seen = jnp.concatenate(seen, axis=0)
    product = dctx[...].astype(f32) * ctx[...].astype(f32)
    high = product.astype(bf16)
    low = (product - high.astype(f32)).astype(bf16)
    lane = lax.broadcasted_iota(jnp.int32, (LEADS, features), 1)
    head = lax.broadcasted_iota(jnp.int32, (LEADS, features), 0) * HEAD_DIM
    select = ((lane >= head) & (lane < head + HEAD_DIM)).astype(f32).astype(bf16)
    sums = mm(select, high, NT) + mm(select, low, NT)
    sums = jnp.concatenate([jnp.broadcast_to(sums[h : h + 1, :], (LEADS, tokens)) for h in range(heads)], axis=0)
    ds = (seen * (mm(spread_heads(v16), dctx[...], NT) - sums)).astype(bf16)
    dk = (fold_heads(mm(ds, qkv[:, cols[0]])) * scale).astype(bf16)
    dv = fold_heads(mm(seen.astype(bf16), dctx[...])).astype(bf16)
    high = dz[...].astype(bf16)
    low = (dz[...] - high.astype(f32)).astype(bf16)
    out = mm(pick, high) + mm(pick, low)
    for c, part in enumerate((dq, dk, dv)):
        out = out + mm(part, wa[:, cols[c]], NT)
    return out


def front_kernel(
    rows_h, lengths, first_h, second_h, gain_in, shift_in,
    x_h, y_h, qkv_h, p_h, ctx_h, zh0_h, mid_h, a_h, df_h, du_h, dmid_h, other_first_h, rstd0, dnorm, norms,
    wa, wu, wd, x, qkv, p, ctx, zh0, mid, a, slope, up, zh1, rstd1, do, dctx, acc, d_att,
    lead_slope, lead_zh, lead_rstd, hot_ref, grad_own, grad_in, row_own, row_in, norm_pair,
    row_sem, load, w_ss, w_rs, d_ss, d_rs, n_ss, n_rs, m_ss, m_rs, x_ss, x_rs, r_ss, r_rs, l_ss, l_rs, out_sem, col_sem, du_sem, other_sem,
):
    sec = lax.axis_index("section")
    core = sec % 2
    at_head = sec // 2
    tokens, features = x.shape
    blocks = tokens // BLOCK
    pieces = wu.shape[1] // features
    half = wd.shape[1] // 2
    even, odd = core == 0, core == 1
    head, backbone = at_head == 1, at_head == 0
    sibling = {"section": sec + 1 - 2 * core}
    peer = {"section": (sec + 2) % 4}
    halves = (do, dctx)
    y, df, dmid = mid, mid, x
    barrier = pltpu.get_barrier_semaphore()
    for step in range(1, 4):
        target = {"section": (sec + step) % 4}
        pl.semaphore_signal(barrier, inc=1, device_id=target, device_id_type=MESH)

    def cols(c):
        return pl.ds(c * features, features)

    def block(b):
        return pl.ds(b * BLOCK if isinstance(b, int) else pl.multiple_of(b * BLOCK, BLOCK), BLOCK)

    def piece(c):
        return pl.ds(c * features if isinstance(c, int) else pl.multiple_of(c * features, features), features)

    def local_first(c, dst):
        return pltpu.make_async_copy(first_h.at[:, piece(c)], dst.at[:, piece(c)], load.at[c])

    def sent_first(c, dst):
        return remote(first_h.at[:, piece(c)], dst.at[:, piece(c)], w_ss.at[c], w_rs.at[c], sibling)

    def local_second(side):
        return pltpu.make_async_copy(second_h, wd.at[:, pl.ds(side * half, half)], load.at[pieces])

    def sent_second(side):
        return remote(second_h, wd.at[:, pl.ds(side * half, half)], d_ss, d_rs, sibling)

    def row_load(row):
        return pltpu.make_async_copy(
            rows_h.at[pl.ds(row * SEQ, SEQ)], slope.at[pl.ds(0, SEQ), cols(row)], row_sem.at[row]
        )

    for row in range(blocks):
        row_load(row).start()
    turns = (1, 2, 0, *range(3, pieces))
    for c in range(pieces):
        when(even, lambda: local_first(turns[c], wa).start())
        when(odd, lambda: local_first(c, wu).start())
    when(even, lambda: local_second(0).start())
    when(odd, lambda: local_second(1).start())

    def inner_send(dst):
        return remote(halves[1] if dst is x else halves[0], dst, m_ss, m_rs, sibling)

    def cross_send(dst, side, b):
        target = {"section": 2 + side} if dst is x else {"section": side}
        return remote(halves[side].at[block(b)], dst.at[block(b)], x_ss.at[side, b], x_rs.at[b], target)

    def send_weights():
        for c in range(pieces):
            when(even, lambda: sent_first(turns[c], wa).start())
            when(odd, lambda: sent_first(c, wu).start())
        when(even, lambda: sent_second(0).start())
        when(odd, lambda: sent_second(1).start())

    for row in range(blocks):
        _, _, first = span_scalars(lengths, row)
        row_load(row).wait()
        packed = slope[0:SEQ, cols(row)]
        for side in range(2):
            at = places(first, side, (BLOCK, SEQ), 0)
            hot = at == lax.broadcasted_iota(jnp.int32, (BLOCK, SEQ), 1)
            halves[side][block(row), :] = mm(hot.astype(f32).astype(bf16), packed).astype(bf16)
        if row == 0:
            pl.semaphore_wait(barrier, 3)
        if row < blocks - 1:
            when(sec == 1, lambda: [cross_send(x, side, row).start() for side in range(2)])
        when(sec == 2, lambda: [cross_send(up, side, row).start() for side in range(2)])
        if row == 0:
            when(odd, send_weights)
    when(sec == 0, lambda: inner_send(x).start())
    norm_pair[core, 0:1, :] = gain_in[...]
    norm_pair[core, 1:2, :] = shift_in[...]
    sent_norm = remote(norm_pair.at[core], norm_pair.at[core], n_ss, n_rs, sibling)
    norm_from = remote(norm_pair.at[1 - core], norm_pair.at[1 - core], n_ss, n_rs, sibling)
    sent_norm.start()
    when(even, send_weights)
    when(sec == 3, lambda: inner_send(up).start())
    pairs_of = [(side, b) for b in range(blocks) for side in range(2)]

    @pl.when(sec == 0)
    def _():
        x[...] = halves[0][...]

    @pl.when(sec == 3)
    def _():
        up[...] = halves[1][...]

    norm_from.wait_recv()
    norms[...] = norm_pair[...]

    def ready_a(c):
        when(even, lambda: local_first(c, wa).wait())
        when(odd, lambda: sent_first(c, wa).wait_recv())

    def ready_u(c):
        when(odd, lambda: local_first(c, wu).wait())
        when(even, lambda: sent_first(c, wu).wait_recv())

    def ready_d(c):
        if c == 0:
            when(even, lambda: local_second(0).wait())
            when(odd, lambda: sent_second(0).wait_recv())
        if c == pieces // 2:
            when(odd, lambda: local_second(1).wait())
            when(even, lambda: sent_second(1).wait_recv())

    def ready_half(step):
        if step == 0:
            when(even, lambda: local_second(0).wait())
            when(odd, lambda: local_second(1).wait())
        else:
            when(even, lambda: sent_second(1).wait_recv())
            when(odd, lambda: sent_second(0).wait_recv())

    refs = dict(
        x=(x, x_h), y=(y, y_h), qkv=(qkv, qkv_h), p=(p, p_h), ctx=(ctx, ctx_h), zh0=(zh0, zh0_h), mid=(mid, mid_h),
        df=(df, df_h), dmid=(dmid, dmid_h),
    )
    order = list(refs)

    def store(name):
        return pltpu.make_async_copy(*refs[name], out_sem.at[order.index(name)])

    def store_cols(c):
        return pltpu.make_async_copy(a.at[:, cols(c)], a_h.at[:, cols(c)], col_sem.at[c])

    def store_du(c):
        return pltpu.make_async_copy(slope.at[:, cols(c)], du_h.at[:, cols(c)], du_sem.at[c])

    def keep(*names):
        for name in names:
            store(name).start()

    picks = lead_picks(lengths, core, True)
    leading = jnp.max(picks, axis=1, keepdims=True) > 0
    hot_leads = picks.astype(bf16)
    pick = lead_picks(lengths, core, False).astype(bf16)
    row_hop = remote(row_own, row_in, r_ss, r_rs, peer)

    @pl.when(backbone)
    def _():
        when(odd, lambda: inner_send(x).wait_recv())
        ready = dict(a=ready_a, u=ready_u, half=ready_half)
        row_own[...] = lead_forward(x, lengths, core, norms, wa, wu, wd, qkv, ready)
        row_hop.start()
        when(sec == 1, lambda: [cross_send(x, side, blocks - 1).start() for side in range(2)])

    @pl.when(head)
    def _():
        for c in range(3):
            ready_a(c)
        row_hop.wait_recv()

    hot_ref[...] = hot_leads

    def patched(b):
        cross_send(x, 0, b).wait_recv()
        hot = hot_ref[block(b), :]
        is_lead = jnp.max(hot.astype(f32), axis=1, keepdims=True) > 0
        x[block(b), :] = jnp.where(is_lead, mm(hot, row_in[...]).astype(bf16), x[block(b), :])

    def arrive(b):
        when(head, patched, b)

    at_first = {k: f for k, f in (("a", ready_a), ("u", ready_u), ("d", ready_d))}
    ready = {k: (lambda c, f=f: when(head, f, c)) for k, f in at_first.items()}
    save = dict(
        p=p, a=a, slope=slope, zh0=zh0, zh1=zh1, rstd0=rstd0, rstd1=rstd1, keep=keep,
        keep_cols=lambda c: store_cols(c).start(),
    )
    out = forward_pass(x, lengths, core, norms, wa, wu, wd, qkv, ctx, mid, acc, ready, arrive, save)
    for name in ("mid", "x"):
        store(name).wait()
    y[...] = out
    keep("y")
    other = pltpu.make_async_copy(wa, other_first_h, other_sem)
    when(odd, lambda: other.start())

    @pl.when(backbone)
    def _():
        lead_zh[...] = mm(pick, zh1[...])
        left = jnp.broadcast_to(rstd1[...], (tokens, PAIR))
        total = jnp.zeros((LEADS, PAIR), f32)
        for _ in range(3):
            high = left.astype(bf16)
            left = left - high.astype(f32)
            total = total + mm(pick, high)
        lead_rstd[...] = total[:, 0:1]
        for b in range(blocks):
            cross_send(up, 0, b).wait_recv()
        row_hop.wait_send()
        for c in range(pieces):
            lead_slope[:, cols(c)] = mm(pick, slope[:, cols(c)]).astype(bf16)

    when(sec == 2, lambda: inner_send(up).wait_recv())
    when(sec == 0, lambda: inner_send(x).wait_send())
    when(sec == 3, lambda: inner_send(up).wait_send())
    when((sec == 1) | (sec == 2), lambda: [cross_send(x, *at).wait_send() for at in pairs_of])
    sent_norm.wait_send()
    for c in range(pieces):
        sent_first(c, wa).wait_send()
    sent_second(0).wait_send()
    none = {k: (lambda *_: None) for k in ("u", "d", "du")}
    store("y").wait()
    feed_forward_back(up[...], norms, wu, wd, slope, zh1, rstd1, df, slope, acc, dnorm, none)
    dmid[...] = acc[...].astype(bf16)
    dnorm[0:2, :] = jnp.zeros((2, features), f32)
    grad_hop = remote(grad_own, grad_in, l_ss, l_rs, peer)

    @pl.when(head)
    def _():
        keep("df", "dmid")
        for c in range(pieces):
            store_du(c).start()
        attention_back_begin(dmid, norms, wa, zh0, rstd0, do, dctx, acc, d_att)
        grad_own[...] = lead_back(pick, lengths, core, wa, qkv, p, ctx, dctx, acc)
        grad_hop.start()
        grad_hop.wait_send()

    @pl.when(backbone)
    def _():
        base = mm(pick, up[...])
        grad_hop.wait_recv()
        dy = (base + grad_in[...]).astype(bf16).astype(f32)
        extra = dy - base
        dnorm[2:3, :] += jnp.sum(extra * lead_zh[...], axis=0, keepdims=True)
        dnorm[3:4, :] += jnp.sum(extra, axis=0, keepdims=True)
        dz, _, _ = normalize_back(lead_zh[...], lead_rstd[...], norms[1, 0:1, :], dy)
        lead_df = dz.astype(bf16)
        df[...] = jnp.where(leading, mm(hot_leads, lead_df).astype(bf16), df[...])
        keep("df")
        lead_du = []
        for c in range(pieces):
            g = (mm(lead_df, wd[:, cols(c)]) * lead_slope[:, cols(c)].astype(f32)).astype(bf16)
            lead_du.append(g)
            dz = dz + mm(g, wu[:, cols(c)], NT)
        for c in range(pieces):
            slope[:, cols(c)] = jnp.where(leading, mm(hot_leads, lead_du[c]).astype(bf16), slope[:, cols(c)])
            store_du(c).start()
        dmid[...] = jnp.where(leading, mm(hot_leads, dz.astype(bf16)).astype(bf16), dmid[...])
        keep("dmid")

    for name in order:
        if name not in ("mid", "x", "y"):
            store(name).wait()
    for c in range(pieces):
        store_cols(c).wait()
        store_du(c).wait()
    when(odd, lambda: other.wait())


ANY = pl.BlockSpec(memory_space=pl.ANY)
IN_VMEM = pl.BlockSpec(memory_space=pltpu.VMEM)
IN_SMEM = pl.BlockSpec(memory_space=pltpu.SMEM)
S = jax.ShapeDtypeStruct


def vm(*shape):
    return pltpu.VMEM(shape, bf16)


def dma(*shape):
    return pltpu.SemaphoreType.DMA(shape)


def params(number):
    if number is None:
        return pltpu.CompilerParams(vmem_limit_bytes=VMEM_LIMIT)
    return pltpu.CompilerParams(vmem_limit_bytes=VMEM_LIMIT, collective_id=number, has_side_effects=True)


def front(rows_in, lengths, first, second, gain, shift):
    features, ff = first.shape
    tokens = rows_in.shape[0] // 2
    pieces = ff // features
    blocks, pairs = tokens // BLOCK, features // PAIR
    square = S((tokens, features), bf16)
    one = pltpu.SemaphoreType.DMA
    shapes = dict(
        x=square, y=square, qkv=S((tokens, 3 * features), bf16), p=S((blocks, pairs, BLOCK, 2 * BLOCK), bf16),
        ctx=square, zh0=square, mid=square, a=S((tokens, ff), bf16), df=square, du=S((tokens, ff), bf16), dmid=square,
        other_first=S(first.shape, bf16), rstd0=S((tokens, 1), f32), dnorm=S((4, features), f32),
        norms=S((2, 2, features), f32),
    )
    small = ("rstd0", "dnorm", "norms")
    wide = vm(features, ff)
    outs = pl.pallas_call(
        front_kernel,
        out_shape=list(shapes.values()),
        in_specs=[ANY, IN_SMEM, ANY, ANY, IN_VMEM, IN_VMEM],
        out_specs=[IN_VMEM if k in small else ANY for k in shapes],
        scratch_shapes=[wide, wide, wide]
        + [pltpu.VMEM(shapes[k].shape, bf16) for k in ("x", "qkv", "p", "ctx", "zh0", "mid", "a", "du")]
        + [
            vm(tokens, features), vm(tokens, features), pltpu.VMEM((tokens, 1), f32), vm(tokens, features),
            vm(tokens, features), pltpu.VMEM((tokens, features), f32), pltpu.VMEM((2, features), f32), vm(LEADS, ff), pltpu.VMEM((LEADS, features), f32),
            pltpu.VMEM((LEADS, 1), f32), vm(tokens, LEADS),
            pltpu.VMEM((LEADS, features), f32), pltpu.VMEM((LEADS, features), f32), vm(LEADS, features), vm(LEADS, features),
            pltpu.VMEM((2, 2, features), f32),
            dma(blocks), dma(pieces + 1), dma(pieces), dma(pieces), one, one, one, one, one, one, dma(2, blocks), dma(blocks),
            one, one, one, one, dma(9), dma(pieces), dma(pieces), one,
        ],
        compiler_params=params(1),
        name="front",
    )(rows_in, lengths, first, second, gain, shift)
    return dict(zip(shapes, outs))


PANEL = 128
RING = 4


def reduce_kernel(
    chain, lengths, dnorm_in, norms, rstd0, x_h, ctx_h, mid_h, a_h, df_h, du_h, dmid_h, zh0_h, qkv_h, p_h, y_h,
    first_h, other_first_h,
    out_h, norm_out, halves_h,
    left, left_t, own_ring, sib_ring, sib_send, part, y1, zin1, mid1, zin2, mid2, y2, final, halves,
    wa, qkv, p, do, dctx, acc, y_buf, dnorm, norm,
    left_sem, own_sem, ring_sem, out_sem, sib_ss, sib_rs, y1_ss, y1_rs, z1_ss, z1_rs, m1_ss, m1_rs,
    z2_ss, z2_rs, m2_ss, m2_rs, y2_ss, y2_rs, f_ss, f_rs, o_ss, o_rs, c_ss, c_rs, h_sem, a_sem, in_sem, n_ss, n_rs,
):
    sec = lax.axis_index("section")
    dp = lax.axis_index("dp")
    core = sec % 2
    panels, rows, _ = final.shape
    tokens = acc.shape[0]
    half = rows // 2
    features = rows
    last = panels
    spot = dp // 2
    side = spot // (chain // 2)
    depth = chain // 2 - 1
    dist = side * (spot - chain // 2) + (1 - side) * (chain // 2 - 1 - spot)
    inner = dist == 0
    y = dp % 2
    sibling = {"section": sec + 1 - 2 * core}
    across_y = {"dp": dp + 1 - 2 * y}
    inward = {"dp": dp + 2 - 4 * side}
    outward = {"dp": dp - 2 + 4 * side}
    has_out = dist < depth

    barrier = pltpu.get_barrier_semaphore()
    at_head = sec // 2
    dx_buf = dctx
    inside = (sec == 0) | (sec == 3)
    beyond = {"section": 2 - sec // 2}
    others = [{"section": (sec + step) % 4} for step in (1, 2, 3)]
    for target in (*others, across_y, inward):
        pl.semaphore_signal(barrier, inc=1, device_id=target, device_id_type=MESH)

    @pl.when(has_out)
    def _():
        pl.semaphore_signal(barrier, inc=1, device_id=outward, device_id_type=MESH)

    def rows_at(which):
        return pl.ds(pl.multiple_of(which * half, half), half)

    mine, theirs = rows_at(y), rows_at(1 - y)
    kept, rest = rows_at(side), rows_at(1 - side)

    def to_sibling(j):
        return remote(sib_send.at[j % RING], part.at[j], sib_ss.at[j % RING], sib_rs.at[j], sibling)

    def one_y(j):
        i = j // 2
        return remote(part.at[j, theirs], y1.at[i], y1_ss.at[i], y1_rs.at[i], across_y)

    def one_in(j):
        i = j // 2
        return remote(part.at[j, mine], zin1.at[i], z1_ss.at[i], z1_rs.at[i], inward)

    def one_mid(j):
        i = j // 2
        return remote(part.at[j, mine], mid1.at[i], m1_ss.at[i], m1_rs.at[i], inward)

    def one_out(j):
        return remote(final.at[j, mine], final.at[j, mine], f_ss.at[0, j], f_rs.at[0, j], outward)

    def one_back(j):
        return remote(final.at[j, mine], final.at[j, mine], f_ss.at[1, j], f_rs.at[1, j], across_y)

    def one_back_in(j):
        return remote(final.at[j, theirs], final.at[j, theirs], f_ss.at[1, j], f_rs.at[1, j], across_y)

    def two_in(j):
        i = j // 2
        return remote(part.at[j], zin2.at[i], z2_ss.at[i], z2_rs.at[i], inward)

    def two_mid(j):
        i = j // 2
        return remote(part.at[j, rest], mid2.at[i], m2_ss.at[i], m2_rs.at[i], inward)

    def two_y(j):
        i = j // 2
        return remote(part.at[j, kept], y2.at[i], y2_ss.at[i], y2_rs.at[i], across_y)

    def two_swap(j):
        return remote(final.at[j, kept], final.at[j, kept], f_ss.at[2, j], f_rs.at[1, j], inward)

    def two_swap_in(j):
        return remote(final.at[j, rest], final.at[j, rest], f_ss.at[2, j], f_rs.at[1, j], inward)

    def two_out_kept(j):
        return remote(final.at[j, kept], final.at[j, kept], f_ss.at[0, j], f_rs.at[0, j], outward)

    def two_out_rest(j):
        return remote(final.at[j, rest], final.at[j, rest], f_ss.at[1, j], f_rs.at[1, j], outward)

    down = a_h.shape[1] // (2 * PANEL)
    outer_cols = features // PANEL
    raw = dict(x=(x_h, 0), ctx=(ctx_h, 1), df=(df_h, 2), mid=(mid_h, 3))

    def left_of(who, j):
        late = jnp.minimum(j // down, 1)
        even = 2 * (1 - late) + late * (1 - jnp.minimum(j // (down + outer_cols), 1))
        odd = 2 * (1 - late) + 3 * late
        return who * odd + (1 - who) * even

    def columns(col):
        return pl.ds(pl.multiple_of(col * PANEL, PANEL), PANEL)

    def fetch_down(who, j, ring, sem):
        return pltpu.make_async_copy(a_h.at[:, columns(who * down + j)], ring.at[j % RING], sem.at[j % RING])

    def fetch_up(j, ring, sem):
        return pltpu.make_async_copy(du_h.at[:, columns(j - down)], ring.at[j % RING], sem.at[j % RING])

    def fetch(who, j, ring, sem):
        when(j < down, lambda: fetch_down(who, j, ring, sem).start())
        when((j >= down) & (j < last) & (who == 1), lambda: fetch_up(j, ring, sem).start())

    def right(who, j, ring, sem, use):
        def from_ring():
            pltpu.make_async_copy(a_h.at[:, columns(0)], ring.at[j % RING], sem.at[j % RING]).wait()
            use(ring[j % RING])

        when((j < down) | ((j < last) & (who == 1)), from_ring)
        when((j >= down) & (j < down + outer_cols) & (who == 0), lambda: use(do[:, columns(j - down)]))
        when(
            (j >= down + outer_cols) & (j < last) & (who == 0), lambda: use(qkv[:, columns(j - down - outer_cols)])
        )

    def to_out(j):
        late = jnp.minimum(j // down, 1)
        even = jnp.where(j < down + outer_cols, j - down + 3 * outer_cols, j - down - outer_cols)
        col = (1 - late) * (4 * outer_cols + j) + late * (core * (j - down) + (1 - core) * even)
        return pltpu.make_async_copy(final.at[j], out_h.at[:, columns(col)], out_sem.at[j])


    def own_send(src):
        return remote(src, halves.at[core], o_ss, o_rs, sibling)

    def own_from():
        return remote(dx_buf, halves.at[1 - core], o_ss, o_rs, sibling)

    def across_send(src):
        return remote(src, halves.at[core], c_ss, c_rs.at[core], beyond)

    def across_from(side):
        return remote(dx_buf, halves.at[side], c_ss, c_rs.at[side], beyond)

    def load_left(name):
        return pltpu.make_async_copy(raw[name][0], left, left_sem)

    loads = dict(dmid=(dmid_h, do), zh0=(zh0_h, dctx), qkv=(qkv_h, qkv), p=(p_h, p), y=(y_h, y_buf))
    names = list(loads)

    def load(name):
        return pltpu.make_async_copy(*loads[name], in_sem.at[names.index(name)])

    def load_wa(own, c):
        cols = pl.ds(c * features, features)
        return pltpu.make_async_copy((first_h if own else other_first_h).at[:, cols], wa.at[:, cols], a_sem.at[c])

    load_left("df").start()
    for j in range(RING):
        fetch_down(core, j, own_ring, own_sem).start()
        fetch_down(1 - core, j, sib_ring, ring_sem).start()
    load("dmid").start()
    load("zh0").start()
    for c in (3, 0, 1, 2):
        when(core == 0, lambda: load_wa(True, c).start())
        when(core == 1, lambda: load_wa(False, c).start())
    for name in ("qkv", "p", "y"):
        load(name).start()

    def turn(i):
        for b in range(features // BLOCK):
            grid = (BLOCK, features)
            eye = lax.broadcasted_iota(jnp.int32, grid, 0) + b * BLOCK == lax.broadcasted_iota(jnp.int32, grid, 1)
            left_t[i, pl.ds(b * BLOCK, BLOCK), :] = mm(eye.astype(f32).astype(bf16), left[...], NT).astype(bf16)

    def norm_panel(other):
        chosen = jnp.where(core == other, dnorm[2:4, :], dnorm[0:2, :])
        strips = [
            chosen[r : r + 1, c * PANEL : (c + 1) * PANEL]
            for r in range(2)
            for c in range(features // PANEL)
        ]
        return jnp.concatenate(strips + [jnp.zeros((16 - len(strips), PANEL), f32)], axis=0)

    pl.semaphore_wait(barrier, 5 + has_out.astype(jnp.int32))

    def stage_send(j):
        when(j >= RING, lambda: to_sibling(j - RING).wait_send())

        def use(block):
            sib_send[j % RING] = mm(left_t[left_of(1 - core, j)], block).astype(bf16)

        right(1 - core, j, sib_ring, ring_sem, use)
        to_sibling(j).start()
        fetch(1 - core, j + RING, sib_ring, ring_sem)

    def stage_part(j):
        to_sibling(j).wait_recv()

        def use(block):
            own = mm(left_t[left_of(core, j)], block)
            part[j] = (own + part[j].astype(f32)).astype(bf16)

        right(core, j, own_ring, own_sem, use)
        fetch(core, j + RING, own_ring, own_sem)
        when(j % 2 == 0, lambda: one_y(j).start())
        when((j % 2 == 1) & (dist == depth) & (depth > 0), lambda: two_in(j).start())
        when((j % 2 == 1) & (dist == depth) & (depth == 0), lambda: two_mid(j).start())

    def one_halves(j):
        one_y(j).wait_recv()
        part[j, mine, :] = (part[j, mine, :].astype(f32) + y1[j // 2].astype(f32)).astype(bf16)
        when((dist == depth) & (dist > 0), lambda: one_in(j).start())
        when((dist == depth) & inner, lambda: one_mid(j).start())

    def one_chain(j):
        one_in(j).wait_recv()
        part[j, mine, :] = (part[j, mine, :].astype(f32) + zin1[j // 2].astype(f32)).astype(bf16)
        when(dist > 0, lambda: one_in(j).start())
        when(inner, lambda: one_mid(j).start())

    def one_total(j):
        one_mid(j).wait_recv()
        final[j, mine, :] = (part[j, mine, :].astype(f32) + mid1[j // 2].astype(f32)).astype(bf16)
        when(has_out, lambda: one_out(j).start())
        one_back(j).start()

    def one_spread(j):
        one_out(j).wait_recv()
        when(has_out, lambda: one_out(j).start())
        one_back(j).start()

    def two_chain(j):
        two_in(j).wait_recv()
        part[j] = (part[j].astype(f32) + zin2[j // 2].astype(f32)).astype(bf16)
        when(dist > 0, lambda: two_in(j).start())
        when(inner, lambda: two_mid(j).start())

    def two_halves(j):
        two_mid(j).wait_recv()
        part[j, kept, :] = (part[j, kept, :].astype(f32) + mid2[j // 2].astype(f32)).astype(bf16)
        two_y(j).start()

    def two_total(j):
        two_y(j).wait_recv()
        final[j, kept, :] = (part[j, kept, :].astype(f32) + y2[j // 2].astype(f32)).astype(bf16)
        two_swap(j).start()
        when(has_out, lambda: two_out_kept(j).start())

    def two_swapped(j):
        two_swap_in(j).wait_recv()
        when(has_out, lambda: two_out_rest(j).start())

    def two_spread_kept(j):
        two_out_kept(j).wait_recv()
        when(has_out, lambda: two_out_kept(j).start())

    def two_spread_rest(j):
        two_out_rest(j).wait_recv()
        when(has_out, lambda: two_out_rest(j).start())

    def finish(j):
        when(j % 2 == 0, lambda: one_back_in(j).wait_recv())

        to_out(j).start()

    last_lag = 7 + 4 * depth

    pairs = features // PAIR
    items = tokens // BLOCK * pairs
    begin = 4

    def turn_next(name, following):
        load_left(name).wait()
        turn(raw[name][1])
        if following:
            load_left(following).start()

    def attention_begin():
        load("dmid").wait()
        load("zh0").wait()
        load_wa(True, 3).wait()
        attention_back_begin(do, norms, wa, dctx, rstd0, do, dctx, acc, dnorm)

    def send_rows():
        load("y").wait()

        @pl.when(at_head == 1)
        def _():
            leading = jnp.max(lead_picks(lengths, core, True), axis=1, keepdims=True) > 0
            dx_buf[...] = jnp.where(leading, 0.0, acc[...]).astype(bf16)

        @pl.when(at_head == 0)
        def _():
            dx_buf[...] = acc[...].astype(bf16)

        def go(own, across):
            across_send(across).start()
            when(~inside, lambda: own_send(own).start())

            @pl.when(inside)
            def _():
                halves[core] = own[...]

        when(at_head == 1, go, y_buf, dx_buf)
        when(at_head == 0, go, dx_buf, y_buf)

    def norm_hop(src, dst, i, target):
        return remote(norm.at[src], norm.at[dst], n_ss.at[i], n_rs.at[i], target)

    norm_sib = norm_hop(0, 1, 0, sibling)
    norm_y = norm_hop(2, 3, 1, across_y)
    norm_in_hop = norm_hop(7, 4, 2, inward)
    norm_mid = norm_hop(7, 5, 3, inward)
    norm_far = norm_hop(6, 6, 4, outward)

    def norm_steps(t):
        @pl.when(t == 0)
        def _():
            norm[0] = norm_panel(0)
            norm_sib.start()

        @pl.when(t == 2)
        def _():
            norm_sib.wait_recv()
            norm[2] = norm_panel(1) + norm[1]
            norm_y.start()

        @pl.when(t == 4)
        def _():
            norm_y.wait_recv()
            norm[7] = norm[2] + norm[3]

        @pl.when((t == 4 + 2 * (depth - dist)) & (dist < depth))
        def _():
            norm_in_hop.wait_recv()
            norm[7] = norm[7] + norm[4]

        @pl.when(t == 4 + 2 * (depth - dist))
        def _():
            when(dist > 0, lambda: norm_in_hop.start())
            when(inner, lambda: norm_mid.start())

        @pl.when((t == 6 + 2 * depth) & inner)
        def _():
            norm_mid.wait_recv()
            norm[6] = norm[7] + norm[5]
            when(has_out, lambda: norm_far.start())

        @pl.when((t == 6 + 2 * (depth + dist)) & (dist > 0))
        def _():
            norm_far.wait_recv()
            when(has_out, lambda: norm_far.start())

    dnorm[...] = dnorm_in[...]
    turn_next("df", "mid")

    def step(t, carry):
        def at(lag, kind, cond, run):
            j = t - lag
            ok = (j >= 0) & (j < panels)
            if kind is not None:
                ok = ok & (j % 2 == kind)
            if cond is not None:
                ok = ok & cond
            when(ok, run, j)

        at(7 + 2 * (depth + dist), 1, dist > 0, two_spread_rest)
        at(5 + 2 * (depth + dist), 1, dist > 0, two_spread_kept)
        at(5 + 2 * (depth + dist), 0, dist > 0, one_spread)
        at(7 + 2 * depth, 1, inner, two_swapped)
        at(5 + 2 * depth, 1, inner, two_total)
        at(5 + 2 * depth, 0, inner, one_total)
        at(3 + 2 * depth, 1, inner, two_halves)
        at(3 + 2 * (depth - dist), 0, dist < depth, one_chain)
        at(1 + 2 * (depth - dist), 1, dist < depth, two_chain)
        at(3, 0, None, one_halves)
        at(1, None, None, stage_part)
        at(0, None, None, stage_send)
        at(last_lag + 1, None, None, finish)
        when(t == begin, attention_begin)
        item = t - begin - 1
        when(t == begin + 1, lambda: [load("qkv").wait(), load("p").wait()])
        when((item >= 0) & (item < items), lambda: attention_back_item(item // pairs, item % pairs, qkv, p, dctx))
        when(t == 8, turn_next, "mid", "ctx")
        when(t == 9, turn_next, "ctx", "x")
        when(t == 10, turn_next, "x", None)
        for c in range(3):
            when(t == begin + items + 1 + c, lambda: [load_wa(True, c).wait(), attention_back_end(c, wa, qkv, acc)])
        when(t == begin + items + 4, send_rows)
        norm_steps(t - begin - 1)
        return carry

    lax.fori_loop(0, panels + last_lag + 1, step, 0)

    @pl.when(inside)
    def _():
        own_from().wait_recv()

    @pl.when(~inside)
    def _():
        own_send(dx_buf).wait_send()
        across_from(0).wait_recv()
        across_from(1).wait_recv()

    across_send(dx_buf).wait_send()
    norm_sib.wait_send()
    norm_y.wait_send()
    when(dist > 0, lambda: norm_in_hop.wait_send())
    when(inner, lambda: norm_mid.wait_send())
    when(has_out, lambda: norm_far.wait_send())
    norm_out[...] = norm[6]
    rows_done = pltpu.make_async_copy(halves, halves_h, h_sem)
    rows_done.start()

    def drain(j, carry):
        when(j >= panels - RING, lambda: to_sibling(j).wait_send())
        to_out(j).wait()

        @pl.when(j % 2 == 0)
        def _():
            one_y(j).wait_send()
            when(dist > 0, lambda: one_in(j).wait_send())
            when(inner, lambda: one_mid(j).wait_send())
            when(has_out, lambda: one_out(j).wait_send())
            one_back(j).wait_send()

        @pl.when(j % 2 == 1)
        def _():
            when(dist > 0, lambda: two_in(j).wait_send())

            @pl.when(inner)
            def _():
                two_mid(j).wait_send()
                two_y(j).wait_send()
                two_swap(j).wait_send()

            @pl.when(has_out)
            def _():
                two_out_kept(j).wait_send()
                two_out_rest(j).wait_send()

        return carry

    lax.fori_loop(0, panels, drain, 0)
    rows_done.wait()


def reduce_gradients(lengths, first, saved, chain):
    tokens, features = saved["x"].shape
    ff = saved["a"].shape[1]
    width = ff + ff // 2
    panels = width // PANEL
    evens, odds = (panels + 1) // 2, panels // 2
    h = features // 2
    one = pltpu.SemaphoreType.DMA
    arrays = [saved[k] for k in ("x", "ctx", "mid", "a", "df", "du", "dmid", "zh0", "qkv", "p", "y")]
    return pl.pallas_call(
        functools.partial(reduce_kernel, chain),
        out_shape=[S((features, width), bf16), S((16, PANEL), f32), S((2, tokens, features), bf16)],
        in_specs=[IN_SMEM] + [IN_VMEM] * 3 + [ANY] * 13,
        out_specs=[ANY, IN_VMEM, ANY],
        scratch_shapes=[
            vm(tokens, features), vm(4, features, tokens), vm(RING, tokens, PANEL), vm(RING, tokens, PANEL),
            vm(RING, features, PANEL), vm(panels, features, PANEL),
            vm(evens, h, PANEL), vm(evens, h, PANEL), vm(evens, h, PANEL),
            vm(odds, features, PANEL), vm(odds, h, PANEL), vm(odds, h, PANEL),
            vm(panels, features, PANEL), vm(2, tokens, features),
            vm(features, ff), vm(tokens, 3 * features), pltpu.VMEM(saved["p"].shape, bf16), vm(tokens, features),
            vm(tokens, features), pltpu.VMEM((tokens, features), f32), vm(tokens, features),
            pltpu.VMEM((4, features), f32), pltpu.VMEM((8, 16, PANEL), f32),
            one, dma(RING), dma(RING), dma(panels), dma(RING), dma(panels),
            dma(evens), dma(evens), dma(evens), dma(evens), dma(evens), dma(evens),
            dma(odds), dma(odds), dma(odds), dma(odds), dma(odds), dma(odds), dma(3, panels), dma(2, panels),
            one, one, one, dma(2), one, dma(ff // features), dma(5), dma(5), dma(5),
        ],
        compiler_params=params(3),
        name="reduce_gradients",
    )(lengths, saved["dnorm"], saved["norms"], saved["rstd0"], *arrays, first, saved["other_first"])


def finish_kernel(lengths, total, halves, norm_in, first_out, second_out, rows_out, gain_out, shift_out):
    step = pl.program_id(0)
    features = rows_out.shape[1]
    wide = first_out.shape[1]
    first_out[...] = total[:, pl.ds(0, wide)].astype(f32)
    second_out[...] = total[:, pl.ds(wide, second_out.shape[1])].astype(f32)
    size = rows_out.shape[0]
    row = step // (SEQ // size)
    _, _, first = span_scalars(lengths, row)
    at = lax.broadcasted_iota(jnp.int32, (size, BLOCK), 0) + step % (SEQ // size) * size
    out = None
    for side in range(2):
        hot = at == places(first, side, (size, BLOCK), 1)
        part = mm(hot.astype(f32).astype(bf16), halves[side])
        out = part if out is None else out + part
    rows_out[...] = out
    strips = features // PANEL
    for r, ref in enumerate((gain_out, shift_out)):
        ref[...] = jnp.concatenate([norm_in[r * strips + c : r * strips + c + 1, :] for c in range(strips)], axis=1)


def finish(lengths, total, halves, norm_in, ff):
    features, width = total.shape
    tokens = halves.shape[1]
    size = SEQ
    steps = 2 * tokens // size
    part = features // steps
    row_spec = pl.BlockSpec((1, features), lambda i: (0, 0))
    return pl.pallas_call(
        finish_kernel,
        grid=(steps,),
        out_shape=[
            S((features, ff), f32), S((features, width - ff), f32), S((2 * tokens, features), f32),
            S((1, features), f32), S((1, features), f32),
        ],
        in_specs=[
            IN_SMEM, pl.BlockSpec((part, width), lambda i: (i, 0)),
            pl.BlockSpec((2, BLOCK, features), lambda i: (0, i // (SEQ // size), 0)), IN_VMEM,
        ],
        out_specs=[
            pl.BlockSpec((part, ff), lambda i: (i, 0)), pl.BlockSpec((part, width - ff), lambda i: (i, 0)),
            pl.BlockSpec((size, features), lambda i: (i, 0)), row_spec, row_spec,
        ],
        compiler_params=params(None),
        name="finish",
    )(lengths, total, halves, norm_in)


def per_device(section_rows, span_lengths, first_weights, second_weights, norm_gain, norm_shift):
    first, second = first_weights[0], second_weights[0]
    saved = front(section_rows[0], span_lengths, first, second, norm_gain, norm_shift)
    total, norm_total, halves = reduce_gradients(span_lengths, first, saved, lax.axis_size("dp") // 2)
    d_first, d_second, rows, gain, shift = finish(span_lengths, total, halves, norm_total, first.shape[1])
    return rows[None], d_first[None], d_second[None], gain, shift


def solution(mesh):
    in_specs = (
        P("section", "dp", None),
        P("dp", None),
        P("section", None, None),
        P("section", None, None),
        P("section", None),
        P("section", None),
    )
    out_specs = (
        P("section", "dp", None),
        P("section", None, None),
        P("section", None, None),
        P("section", None),
        P("section", None),
    )
    return jax.shard_map(
        per_device, mesh=mesh, in_specs=in_specs, out_specs=out_specs, check_vma=False
    )
```

```python
import functools

import jax
import jax.numpy as jnp
from jax import lax
from jax.experimental import pallas as pl
from jax.experimental.pallas import tpu as pltpu
from jax.sharding import PartitionSpec as P

HEAD_DIM = 64
PAIR = 2 * HEAD_DIM
BLOCK = 256
SEQ = 512
LEADS = 16
VMEM_LIMIT = 60 << 20
MESH = pl.DeviceIdType.MESH
f32 = jnp.float32
bf16 = jnp.bfloat16
epsilon = 1e-12
NN = (((1,), (0,)), ((), ()))
NT = (((1,), (1,)), ((), ()))
TN = (((0,), (0,)), ((), ()))
LOG2E = 1.4426950408889634


def mm(a, b, dims=NN):
    return lax.dot_general(a, b, dims, preferred_element_type=f32)


def when(cond, step, *args):
    @pl.when(cond)
    def _():
        step(*args)


def remote(src, dst, ss, rs, target):
    return pltpu.make_async_remote_copy(
        src_ref=src, dst_ref=dst, send_sem=ss, recv_sem=rs, device_id=target, device_id_type=MESH
    )


def gelu_and_slope(u):
    bell = jnp.exp2(u * u * (-0.5 * LOG2E))
    t = 1.0 / (1.0 + (0.3275911 * 0.5**0.5) * jnp.abs(u))
    poly = t * (0.127414796 + t * (-0.142248368 + t * (0.7107068705 + t * (-0.7265760135 + t * 0.5307027145))))
    tail = poly * bell
    cdf = jnp.where(u < 0, tail, 1.0 - tail)
    return u * cdf, cdf + u * bell * 0.3989422804014327


def normalize(z):
    centered = z - jnp.mean(z, axis=-1, keepdims=True)
    rstd = lax.rsqrt(jnp.mean(centered * centered, axis=-1, keepdims=True) + epsilon)
    return centered * rstd, rstd


def normalize_back(zh, rstd, gain, dy):
    g = dy * gain
    mean_g = jnp.mean(g, axis=-1, keepdims=True)
    mean_gz = jnp.mean(g * zh, axis=-1, keepdims=True)
    dz = rstd * (g - mean_g - zh * mean_gz)
    return dz, jnp.sum(dy * zh, axis=0, keepdims=True), jnp.sum(dy, axis=0, keepdims=True)


def span_scalars(lengths, row):
    ends, starts, first, total = [], [], 0, 0
    for j in range(lengths.shape[1]):
        size = lengths[row, j]
        starts.append(total)
        first = first + jnp.where(size == BLOCK, total, 0)
        total = total + size
        ends.append(total)
    return ends, starts, first


def places(first, core, shape, axis):
    at = lax.broadcasted_iota(jnp.int32, shape, axis) + (first + core * BLOCK)
    return jnp.where(at >= SEQ, at - SEQ, at)


def mask_bias(lengths, row, core):
    ends, _, first = span_scalars(lengths, row)

    def segment(at):
        return sum((at >= end).astype(jnp.int32) for end in ends)

    rows = segment(places(first, core, (BLOCK, BLOCK), 0))
    cols = segment(places(first, core, (BLOCK, BLOCK), 1))
    return jnp.where(rows == cols, 0.0, -1e30)


def lead_picks(lengths, core, by_rows):
    parts = []
    per_row = lengths.shape[1] - 1
    shape = (BLOCK, LEADS) if by_rows else (LEADS, BLOCK)
    for row in range(lengths.shape[0]):
        _, starts, first = span_scalars(lengths, row)
        at = places(first, core, shape, 0 if by_rows else 1)
        slot = lax.broadcasted_iota(jnp.int32, shape, 1 if by_rows else 0)
        hit = sum(
            ((slot == row * per_row + j) & (at == starts[j])).astype(jnp.int32) for j in range(per_row)
        )
        parts.append(hit.astype(f32))
    return jnp.concatenate(parts, axis=0 if by_rows else 1)


def lane_masks():
    return lax.broadcasted_iota(jnp.int32, (BLOCK, PAIR), 1) < HEAD_DIM


def forward_pass(x, lengths, core, norms, wa, wu, wd, qkv, ctx, mid, acc, ready, arrive, save):
    tokens, features = x.shape
    pairs = features // PAIR
    first = lane_masks()
    zero = jnp.zeros((BLOCK, PAIR), bf16)

    def block_step(b, carry):
        rows = pl.ds(pl.multiple_of(b * BLOCK, BLOCK), BLOCK)
        arrive(b)
        for c in range(3):
            cols = pl.ds(c * features, features)
            qkv[rows, cols] = mm(x[rows, :], wa[:, cols]).astype(bf16)
        bias = mask_bias(lengths, b, core)
        for h in range(pairs):
            q = qkv[rows, pl.ds(h * PAIR, PAIR)]
            k = qkv[rows, pl.ds(features + h * PAIR, PAIR)]
            v = qkv[rows, pl.ds(2 * features + h * PAIR, PAIR)]
            total = None
            for side in range(2):
                own = first if side == 0 else ~first
                s = mm(q, jnp.where(own, k, zero), NT) * (HEAD_DIM**-0.5) + bias
                e = jnp.exp(s - jnp.max(s, axis=-1, keepdims=True))
                pr = (e * (1.0 / jnp.sum(e, axis=-1, keepdims=True))).astype(bf16)
                save["p"][b, h, :, pl.ds(side * BLOCK, BLOCK)] = pr
                part = mm(pr, jnp.where(own, v, zero))
                total = part if total is None else total + part
            ctx[rows, pl.ds(h * PAIR, PAIR)] = total.astype(bf16)
        return carry

    lax.fori_loop(0, tokens // BLOCK, block_step, 0)
    ready["a"](3)
    zn, r = normalize(x[...].astype(f32) + mm(ctx[...], wa[:, pl.ds(3 * features, features)]))
    save["keep"]("x", "qkv", "p", "ctx")
    save["rstd0"][...] = r
    save["zh0"][...] = zn.astype(bf16)
    mid[...] = (zn * norms[0, 0:1, :] + norms[0, 1:2, :]).astype(bf16)
    acc[...] = mid[...].astype(f32)
    save["keep"]("zh0", "mid")
    pieces = wu.shape[1] // features
    cols = [pl.ds(c * features, features) for c in range(pieces)]
    ready["u"](0)
    ahead = mm(mid[...], wu[:, cols[0]])
    for c in range(pieces):
        u = ahead
        if c + 1 < pieces:
            ready["u"](c + 1)
            ahead = mm(mid[...], wu[:, cols[c + 1]])
        act, slope = gelu_and_slope(u)
        act = act.astype(bf16)
        save["a"][:, cols[c]] = act
        save["slope"][:, cols[c]] = slope.astype(bf16)
        save["keep_cols"](c)
        ready["d"](c)
        acc[...] += mm(act, wd[:, cols[c]], NT)
    zn, r = normalize(acc[...])
    save["rstd1"][...] = r
    save["zh1"][...] = zn.astype(bf16)
    return (zn * norms[1, 0:1, :] + norms[1, 1:2, :]).astype(bf16)


def feed_forward_back(dy, norms, wu, wd, slope, zh1, rstd1, df, du, acc, dnorm, ready):
    features = wu.shape[0]
    dz, dgain, dshift = normalize_back(zh1[...].astype(f32), rstd1[...], norms[1, 0:1, :], dy.astype(f32))
    dnorm[2:3, :] = dgain
    dnorm[3:4, :] = dshift
    df[...] = dz.astype(bf16)
    acc[...] = dz
    for c in range(wu.shape[1] // features):
        cols = pl.ds(c * features, features)
        ready["d"](c)
        da = mm(df[...], wd[:, cols])
        ready["du"](c)
        g = (da * slope[:, cols].astype(f32)).astype(bf16)
        du[:, cols] = g
        ready["u"](c)
        acc[...] += mm(g, wu[:, cols], NT)


def attention_back_begin(d_mid, norms, wa, zh0, rstd0, do, dctx, acc, dnorm):
    tokens, features = acc.shape
    dgain = dshift = None
    for b in range(tokens // BLOCK):
        rows = pl.ds(b * BLOCK, BLOCK)
        dz, dg, ds = normalize_back(
            zh0[rows, :].astype(f32), rstd0[rows, :], norms[0, 0:1, :], d_mid[rows, :].astype(f32)
        )
        dgain, dshift = (dg, ds) if b == 0 else (dgain + dg, dshift + ds)
        acc[rows, :] = dz
        do[rows, :] = dz.astype(bf16)
        dctx[rows, :] = mm(dz.astype(bf16), wa[:, pl.ds(3 * features, features)], NT).astype(bf16)
    dnorm[0:1, :] = dgain
    dnorm[1:2, :] = dshift


def attention_back_item(b, h, qkv, p, dctx):
    features = dctx.shape[1]
    first = lane_masks()
    zero = jnp.zeros((BLOCK, PAIR), bf16)
    scale = HEAD_DIM**-0.5
    rows = pl.ds(pl.multiple_of(b * BLOCK, BLOCK), BLOCK)
    at = [pl.ds(pl.multiple_of(part * features + h * PAIR, PAIR), PAIR) for part in range(3)]
    q, k, v = (qkv[rows, cols] for cols in at)
    dc = dctx[rows, at[0]]
    dq = dk = dv = None
    for side in range(2):
        own = first if side == 0 else ~first
        pr = p[b, h, :, pl.ds(side * BLOCK, BLOCK)]
        prf = pr.astype(f32)
        dp = mm(dc, jnp.where(own, v, zero), NT)
        r = jnp.sum(dp * prf, axis=-1, keepdims=True)
        ds = (prf * (dp - r)).astype(bf16)
        parts = (
            mm(ds, jnp.where(own, k, zero)),
            mm(ds, jnp.where(own, q, zero), TN),
            mm(pr, jnp.where(own, dc, zero), TN),
        )
        if dq is None:
            dq, dk, dv = parts
        else:
            dq, dk, dv = dq + parts[0], dk + parts[1], dv + parts[2]
    qkv[rows, at[0]] = (dq * scale).astype(bf16)
    qkv[rows, at[1]] = (dk * scale).astype(bf16)
    qkv[rows, at[2]] = dv.astype(bf16)


def attention_back_end(part, wa, dqkv, acc):
    features = wa.shape[0]
    cols = pl.ds(part * features, features)
    for b in range(acc.shape[0] // BLOCK):
        rows = pl.ds(b * BLOCK, BLOCK)
        acc[rows, :] += mm(dqkv[rows, cols], wa[:, cols], NT)


def head_lanes(features):
    lane = lax.broadcasted_iota(jnp.int32, (LEADS, features), 1)
    return [(lane >= h * HEAD_DIM) & (lane < (h + 1) * HEAD_DIM) for h in range(features // HEAD_DIM)]


def spread_heads(rows):
    wide = rows.astype(f32)
    return jnp.concatenate([jnp.where(own, wide, 0.0) for own in head_lanes(rows.shape[1])], axis=0).astype(bf16)


def fold_heads(wide):
    total = None
    for h, own in enumerate(head_lanes(wide.shape[1])):
        part = jnp.where(own, wide[h * LEADS : (h + 1) * LEADS, :], 0.0)
        total = part if total is None else total + part
    return total


def lead_probs(queries, keys, lengths, core):
    tokens, features = keys.shape
    per_row = lengths.shape[1] - 1
    parts = []
    for row in range(tokens // BLOCK):
        ends, _, first = span_scalars(lengths, row)
        at = places(first, core, (LEADS, BLOCK), 1)
        segment = sum((at >= end).astype(jnp.int32) for end in ends)
        span = lax.broadcasted_iota(jnp.int32, (LEADS, BLOCK), 0) - row * per_row
        parts.append(jnp.where((span == segment) & (span < per_row), 0.0, -1e30))
    bias = jnp.concatenate([jnp.concatenate(parts, axis=1)] * (features // HEAD_DIM), axis=0)
    s = mm(spread_heads(queries), keys, NT) * (HEAD_DIM**-0.5) + bias
    e = jnp.exp(s - jnp.max(s, axis=-1, keepdims=True))
    return (e * (1.0 / jnp.sum(e, axis=-1, keepdims=True))).astype(bf16)


def lead_forward(x, lengths, core, norms, wa, wu, wd, qkv, ready):
    features = x.shape[1]
    pieces = wu.shape[1] // features
    cols = [pl.ds(c * features, features) for c in range(4)]
    own = mm(lead_picks(lengths, core, False).astype(bf16), x[...]).astype(bf16)
    for c in (1, 2):
        ready["a"](c)
        qkv[:, cols[c]] = mm(x[...], wa[:, cols[c]]).astype(bf16)
    ready["a"](0)
    probs = lead_probs(mm(own, wa[:, cols[0]]).astype(bf16), qkv[:, cols[1]], lengths, core)
    ctx = fold_heads(mm(probs, qkv[:, cols[2]])).astype(bf16)
    ready["a"](3)
    zn, _ = normalize(own.astype(f32) + mm(ctx, wa[:, cols[3]]))
    mid = (zn * norms[0, 0:1, :] + norms[0, 1:2, :]).astype(bf16)
    out = mid.astype(f32)
    for step in range(pieces):
        c = (step + core * (pieces // 2)) % pieces
        at = pl.ds(pl.multiple_of(c * features, features), features)
        ready["u"](c)
        act, _ = gelu_and_slope(mm(mid, wu[:, at]))
        if step % (pieces // 2) == 0:
            ready["half"](step)
        out = out + mm(act.astype(bf16), wd[:, at], NT)
    zn, _ = normalize(out)
    return (zn * norms[1, 0:1, :] + norms[1, 1:2, :]).astype(bf16)


def lead_back(pick, lengths, core, wa, qkv, p, ctx, dctx, dz):
    tokens, features = ctx.shape
    scale = HEAD_DIM**-0.5
    heads = features // HEAD_DIM
    cols = [pl.ds(c * features, features) for c in range(3)]
    q16, v16 = (mm(pick, qkv[:, cols[c]]).astype(bf16) for c in (0, 2))
    low = lead_probs(q16, qkv[:, cols[1]], lengths, core)
    probs = low.astype(f32)
    dp = mm(spread_heads(mm(pick, dctx[...]).astype(bf16)), qkv[:, cols[2]], NT)
    ds = (probs * (dp - jnp.sum(dp * probs, axis=-1, keepdims=True))).astype(bf16)
    dq = (fold_heads(mm(ds, qkv[:, cols[1]])) * scale).astype(bf16)
    seen = []
    for h in range(heads):
        keys = pl.ds(h % 2 * BLOCK, BLOCK)
        seen.append(
            jnp.concatenate(
                [mm(pick[:, b * BLOCK : (b + 1) * BLOCK], p[b, h // 2, :, keys], NT) for b in range(tokens // BLOCK)],
                axis=1,
            )
        )
    seen = jnp.concatenate(seen, axis=0)
    product = dctx[...].astype(f32) * ctx[...].astype(f32)
    high = product.astype(bf16)
    low = (product - high.astype(f32)).astype(bf16)
    lane = lax.broadcasted_iota(jnp.int32, (LEADS, features), 1)
    head = lax.broadcasted_iota(jnp.int32, (LEADS, features), 0) * HEAD_DIM
    select = ((lane >= head) & (lane < head + HEAD_DIM)).astype(f32).astype(bf16)
    sums = mm(select, high, NT) + mm(select, low, NT)
    sums = jnp.concatenate([jnp.broadcast_to(sums[h : h + 1, :], (LEADS, tokens)) for h in range(heads)], axis=0)
    ds = (seen * (mm(spread_heads(v16), dctx[...], NT) - sums)).astype(bf16)
    dk = (fold_heads(mm(ds, qkv[:, cols[0]])) * scale).astype(bf16)
    dv = fold_heads(mm(seen.astype(bf16), dctx[...])).astype(bf16)
    high = dz[...].astype(bf16)
    low = (dz[...] - high.astype(f32)).astype(bf16)
    out = mm(pick, high) + mm(pick, low)
    for c, part in enumerate((dq, dk, dv)):
        out = out + mm(part, wa[:, cols[c]], NT)
    return out


def front_kernel(
    rows_h, lengths, first_h, second_h, gain_in, shift_in,
    x_h, y_h, qkv_h, p_h, ctx_h, zh0_h, mid_h, a_h, df_h, du_h, dmid_h, other_first_h, rstd0, dnorm, norms, lead_du,
    wa, wu, wd, x, qkv, p, ctx, zh0, mid, a, slope, up, zh1, rstd1, do, dctx, acc, d_att,
    lead_slope, lead_zh, lead_rstd, hot_ref, grad_own, grad_in, row_own, row_in, norm_pair,
    row_sem, load, w_ss, w_rs, d_ss, d_rs, n_ss, n_rs, m_ss, m_rs, x_ss, x_rs, r_ss, r_rs, l_ss, l_rs, out_sem, col_sem, du_sem, other_sem,
):
    sec = lax.axis_index("section")
    core = sec % 2
    at_head = sec // 2
    tokens, features = x.shape
    blocks = tokens // BLOCK
    pieces = wu.shape[1] // features
    half = wd.shape[1] // 2
    even, odd = core == 0, core == 1
    head, backbone = at_head == 1, at_head == 0
    sibling = {"section": sec + 1 - 2 * core}
    peer = {"section": (sec + 2) % 4}
    halves = (do, dctx)
    y, df, dmid = mid, mid, x
    barrier = pltpu.get_barrier_semaphore()
    for step in range(1, 4):
        target = {"section": (sec + step) % 4}
        pl.semaphore_signal(barrier, inc=1, device_id=target, device_id_type=MESH)

    def cols(c):
        return pl.ds(c * features, features)

    def block(b):
        return pl.ds(b * BLOCK if isinstance(b, int) else pl.multiple_of(b * BLOCK, BLOCK), BLOCK)

    def piece(c):
        return pl.ds(c * features if isinstance(c, int) else pl.multiple_of(c * features, features), features)

    def local_first(c, dst):
        return pltpu.make_async_copy(first_h.at[:, piece(c)], dst.at[:, piece(c)], load.at[c])

    def sent_first(c, dst):
        return remote(first_h.at[:, piece(c)], dst.at[:, piece(c)], w_ss.at[c], w_rs.at[c], sibling)

    def local_second(side):
        return pltpu.make_async_copy(second_h, wd.at[:, pl.ds(side * half, half)], load.at[pieces])

    def sent_second(side):
        return remote(second_h, wd.at[:, pl.ds(side * half, half)], d_ss, d_rs, sibling)

    def row_load(row):
        return pltpu.make_async_copy(
            rows_h.at[pl.ds(row * SEQ, SEQ)], slope.at[pl.ds(0, SEQ), cols(row)], row_sem.at[row]
        )

    for row in range(blocks):
        row_load(row).start()
    turns = (1, 2, 0, *range(3, pieces))
    for c in range(pieces):
        when(even, lambda: local_first(turns[c], wa).start())
        when(odd, lambda: local_first(c, wu).start())
    when(even, lambda: local_second(0).start())
    when(odd, lambda: local_second(1).start())

    def inner_send(dst):
        return remote(halves[1] if dst is x else halves[0], dst, m_ss, m_rs, sibling)

    def cross_send(dst, side, b):
        target = {"section": 2 + side} if dst is x else {"section": side}
        return remote(halves[side].at[block(b)], dst.at[block(b)], x_ss.at[side, b], x_rs.at[b], target)

    def send_weights():
        for c in range(pieces):
            when(even, lambda: sent_first(turns[c], wa).start())
            when(odd, lambda: sent_first(c, wu).start())
        when(even, lambda: sent_second(0).start())
        when(odd, lambda: sent_second(1).start())

    for row in range(blocks):
        _, _, first = span_scalars(lengths, row)
        row_load(row).wait()
        packed = slope[0:SEQ, cols(row)]
        for side in range(2):
            at = places(first, side, (BLOCK, SEQ), 0)
            hot = at == lax.broadcasted_iota(jnp.int32, (BLOCK, SEQ), 1)
            halves[side][block(row), :] = mm(hot.astype(f32).astype(bf16), packed).astype(bf16)
        if row == 0:
            pl.semaphore_wait(barrier, 3)
        if row < blocks - 1:
            when(sec == 1, lambda: [cross_send(x, side, row).start() for side in range(2)])
        when(sec == 2, lambda: [cross_send(up, side, row).start() for side in range(2)])
        if row == 0:
            when(odd, send_weights)
    when(sec == 0, lambda: inner_send(x).start())
    norm_pair[core, 0:1, :] = gain_in[...]
    norm_pair[core, 1:2, :] = shift_in[...]
    sent_norm = remote(norm_pair.at[core], norm_pair.at[core], n_ss, n_rs, sibling)
    norm_from = remote(norm_pair.at[1 - core], norm_pair.at[1 - core], n_ss, n_rs, sibling)
    sent_norm.start()
    when(even, send_weights)
    when(sec == 3, lambda: inner_send(up).start())
    pairs_of = [(side, b) for b in range(blocks) for side in range(2)]

    @pl.when(sec == 0)
    def _():
        x[...] = halves[0][...]

    @pl.when(sec == 3)
    def _():
        up[...] = halves[1][...]

    norm_from.wait_recv()
    norms[...] = norm_pair[...]

    def ready_a(c):
        when(even, lambda: local_first(c, wa).wait())
        when(odd, lambda: sent_first(c, wa).wait_recv())

    def ready_u(c):
        when(odd, lambda: local_first(c, wu).wait())
        when(even, lambda: sent_first(c, wu).wait_recv())

    def ready_d(c):
        if c == 0:
            when(even, lambda: local_second(0).wait())
            when(odd, lambda: sent_second(0).wait_recv())
        if c == pieces // 2:
            when(odd, lambda: local_second(1).wait())
            when(even, lambda: sent_second(1).wait_recv())

    def ready_half(step):
        if step == 0:
            when(even, lambda: local_second(0).wait())
            when(odd, lambda: local_second(1).wait())
        else:
            when(even, lambda: sent_second(1).wait_recv())
            when(odd, lambda: sent_second(0).wait_recv())

    refs = dict(
        x=(x, x_h), y=(y, y_h), qkv=(qkv, qkv_h), p=(p, p_h), ctx=(ctx, ctx_h), zh0=(zh0, zh0_h), mid=(mid, mid_h),
        df=(df, df_h), dmid=(dmid, dmid_h),
    )
    order = list(refs)

    def store(name):
        return pltpu.make_async_copy(*refs[name], out_sem.at[order.index(name)])

    def store_cols(c):
        return pltpu.make_async_copy(a.at[:, cols(c)], a_h.at[:, cols(c)], col_sem.at[c])

    def store_du(c):
        return pltpu.make_async_copy(slope.at[:, cols(c)], du_h.at[:, cols(c)], du_sem.at[c])

    def keep(*names):
        for name in names:
            store(name).start()

    picks = lead_picks(lengths, core, True)
    leading = jnp.max(picks, axis=1, keepdims=True) > 0
    hot_leads = picks.astype(bf16)
    pick = lead_picks(lengths, core, False).astype(bf16)
    row_hop = remote(row_own, row_in, r_ss, r_rs, peer)

    @pl.when(backbone)
    def _():
        when(odd, lambda: inner_send(x).wait_recv())
        ready = dict(a=ready_a, u=ready_u, half=ready_half)
        row_own[...] = lead_forward(x, lengths, core, norms, wa, wu, wd, qkv, ready)
        row_hop.start()
        when(sec == 1, lambda: [cross_send(x, side, blocks - 1).start() for side in range(2)])

    @pl.when(head)
    def _():
        for c in range(3):
            ready_a(c)
        row_hop.wait_recv()

    hot_ref[...] = hot_leads

    def patched(b):
        cross_send(x, 0, b).wait_recv()
        hot = hot_ref[block(b), :]
        is_lead = jnp.max(hot.astype(f32), axis=1, keepdims=True) > 0
        x[block(b), :] = jnp.where(is_lead, mm(hot, row_in[...]).astype(bf16), x[block(b), :])

    def arrive(b):
        when(head, patched, b)

    at_first = {k: f for k, f in (("a", ready_a), ("u", ready_u), ("d", ready_d))}
    ready = {k: (lambda c, f=f: when(head, f, c)) for k, f in at_first.items()}
    save = dict(
        p=p, a=a, slope=slope, zh0=zh0, zh1=zh1, rstd0=rstd0, rstd1=rstd1, keep=keep,
        keep_cols=lambda c: store_cols(c).start(),
    )
    out = forward_pass(x, lengths, core, norms, wa, wu, wd, qkv, ctx, mid, acc, ready, arrive, save)
    for name in ("mid", "x"):
        store(name).wait()
    y[...] = out
    keep("y")
    other = pltpu.make_async_copy(wa, other_first_h, other_sem)
    when(odd, lambda: other.start())

    @pl.when(backbone)
    def _():
        lead_zh[...] = mm(pick, zh1[...])
        left = jnp.broadcast_to(rstd1[...], (tokens, PAIR))
        total = jnp.zeros((LEADS, PAIR), f32)
        for _ in range(3):
            high = left.astype(bf16)
            left = left - high.astype(f32)
            total = total + mm(pick, high)
        lead_rstd[...] = total[:, 0:1]
        for b in range(blocks):
            cross_send(up, 0, b).wait_recv()
        row_hop.wait_send()
        for c in range(pieces):
            lead_slope[:, cols(c)] = mm(pick, slope[:, cols(c)]).astype(bf16)

    when(sec == 2, lambda: inner_send(up).wait_recv())
    when(sec == 0, lambda: inner_send(x).wait_send())
    when(sec == 3, lambda: inner_send(up).wait_send())
    when((sec == 1) | (sec == 2), lambda: [cross_send(x, *at).wait_send() for at in pairs_of])
    sent_norm.wait_send()
    for c in range(pieces):
        sent_first(c, wa).wait_send()
    sent_second(0).wait_send()
    none = {k: (lambda *_: None) for k in ("u", "d", "du")}
    store("y").wait()
    feed_forward_back(up[...], norms, wu, wd, slope, zh1, rstd1, df, slope, acc, dnorm, none)
    for c in range(pieces):
        store_du(c).start()
    dmid[...] = acc[...].astype(bf16)
    dnorm[0:2, :] = jnp.zeros((2, features), f32)
    grad_hop = remote(grad_own, grad_in, l_ss, l_rs, peer)

    @pl.when(head)
    def _():
        keep("df", "dmid")
        lead_du[...] = jnp.zeros_like(lead_du)
        attention_back_begin(dmid, norms, wa, zh0, rstd0, do, dctx, acc, d_att)
        grad_own[...] = lead_back(pick, lengths, core, wa, qkv, p, ctx, dctx, acc)
        grad_hop.start()
        grad_hop.wait_send()

    @pl.when(backbone)
    def _():
        base = mm(pick, up[...])
        grad_hop.wait_recv()
        dy = (base + grad_in[...]).astype(bf16).astype(f32)
        extra = dy - base
        dnorm[2:3, :] += jnp.sum(extra * lead_zh[...], axis=0, keepdims=True)
        dnorm[3:4, :] += jnp.sum(extra, axis=0, keepdims=True)
        dz, _, _ = normalize_back(lead_zh[...], lead_rstd[...], norms[1, 0:1, :], dy)
        lead_df = dz.astype(bf16)
        df[...] = jnp.where(leading, mm(hot_leads, lead_df).astype(bf16), df[...])
        keep("df")
        g = (mm(lead_df, wd[...]) * lead_slope[...].astype(f32)).astype(bf16)
        lead_du[...] = g
        dz = dz + mm(g, wu[...], NT)
        dmid[...] = jnp.where(leading, mm(hot_leads, dz.astype(bf16)).astype(bf16), dmid[...])
        keep("dmid")

    for name in order:
        if name not in ("mid", "x", "y"):
            store(name).wait()
    for c in range(pieces):
        store_cols(c).wait()
        store_du(c).wait()
    when(odd, lambda: other.wait())


ANY = pl.BlockSpec(memory_space=pl.ANY)
IN_VMEM = pl.BlockSpec(memory_space=pltpu.VMEM)
IN_SMEM = pl.BlockSpec(memory_space=pltpu.SMEM)
S = jax.ShapeDtypeStruct


def vm(*shape):
    return pltpu.VMEM(shape, bf16)


def dma(*shape):
    return pltpu.SemaphoreType.DMA(shape)


def params(number):
    if number is None:
        return pltpu.CompilerParams(vmem_limit_bytes=VMEM_LIMIT)
    return pltpu.CompilerParams(vmem_limit_bytes=VMEM_LIMIT, collective_id=number, has_side_effects=True)


def front(rows_in, lengths, first, second, gain, shift):
    features, ff = first.shape
    tokens = rows_in.shape[0] // 2
    pieces = ff // features
    blocks, pairs = tokens // BLOCK, features // PAIR
    square = S((tokens, features), bf16)
    one = pltpu.SemaphoreType.DMA
    shapes = dict(
        x=square, y=square, qkv=S((tokens, 3 * features), bf16), p=S((blocks, pairs, BLOCK, 2 * BLOCK), bf16),
        ctx=square, zh0=square, mid=square, a=S((tokens, ff), bf16), df=square, du=S((tokens, ff), bf16), dmid=square,
        other_first=S(first.shape, bf16), rstd0=S((tokens, 1), f32), dnorm=S((4, features), f32),
        norms=S((2, 2, features), f32), lead_du=S((LEADS, ff), bf16),
    )
    small = ("rstd0", "dnorm", "norms", "lead_du")
    wide = vm(features, ff)
    outs = pl.pallas_call(
        front_kernel,
        out_shape=list(shapes.values()),
        in_specs=[ANY, IN_SMEM, ANY, ANY, IN_VMEM, IN_VMEM],
        out_specs=[IN_VMEM if k in small else ANY for k in shapes],
        scratch_shapes=[wide, wide, wide]
        + [pltpu.VMEM(shapes[k].shape, bf16) for k in ("x", "qkv", "p", "ctx", "zh0", "mid", "a", "du")]
        + [
            vm(tokens, features), vm(tokens, features), pltpu.VMEM((tokens, 1), f32), vm(tokens, features),
            vm(tokens, features), pltpu.VMEM((tokens, features), f32), pltpu.VMEM((2, features), f32), vm(LEADS, ff), pltpu.VMEM((LEADS, features), f32),
            pltpu.VMEM((LEADS, 1), f32), vm(tokens, LEADS),
            pltpu.VMEM((LEADS, features), f32), pltpu.VMEM((LEADS, features), f32), vm(LEADS, features), vm(LEADS, features),
            pltpu.VMEM((2, 2, features), f32),
            dma(blocks), dma(pieces + 1), dma(pieces), dma(pieces), one, one, one, one, one, one, dma(2, blocks), dma(blocks),
            one, one, one, one, dma(9), dma(pieces), dma(pieces), one,
        ],
        compiler_params=params(1),
        name="front",
    )(rows_in, lengths, first, second, gain, shift)
    return dict(zip(shapes, outs))


PANEL = 128
RING = 4


def reduce_kernel(
    chain, lengths, dnorm_in, norms, rstd0, lead_du, x_h, ctx_h, mid_h, a_h, df_h, du_h, dmid_h, zh0_h, qkv_h, p_h, y_h,
    first_h, other_first_h,
    out_h, norm_out, halves_h,
    left, left_t, own_ring, sib_ring, sib_send, part, y1, zin1, mid1, zin2, mid2, y2, final, halves,
    wa, qkv, p, do, dctx, acc, y_buf, dnorm, norm, hot_ref,
    left_sem, own_sem, ring_sem, out_sem, sib_ss, sib_rs, y1_ss, y1_rs, z1_ss, z1_rs, m1_ss, m1_rs,
    z2_ss, z2_rs, m2_ss, m2_rs, y2_ss, y2_rs, f_ss, f_rs, o_ss, o_rs, c_ss, c_rs, h_sem, a_sem, in_sem, n_ss, n_rs,
):
    sec = lax.axis_index("section")
    dp = lax.axis_index("dp")
    core = sec % 2
    panels, rows, _ = final.shape
    tokens = acc.shape[0]
    half = rows // 2
    features = rows
    last = panels
    spot = dp // 2
    side = spot // (chain // 2)
    depth = chain // 2 - 1
    dist = side * (spot - chain // 2) + (1 - side) * (chain // 2 - 1 - spot)
    inner = dist == 0
    y = dp % 2
    sibling = {"section": sec + 1 - 2 * core}
    across_y = {"dp": dp + 1 - 2 * y}
    inward = {"dp": dp + 2 - 4 * side}
    outward = {"dp": dp - 2 + 4 * side}
    has_out = dist < depth

    barrier = pltpu.get_barrier_semaphore()
    at_head = sec // 2
    dx_buf = dctx
    inside = (sec == 0) | (sec == 3)
    beyond = {"section": 2 - sec // 2}
    others = [{"section": (sec + step) % 4} for step in (1, 2, 3)]
    for target in (*others, across_y, inward):
        pl.semaphore_signal(barrier, inc=1, device_id=target, device_id_type=MESH)

    @pl.when(has_out)
    def _():
        pl.semaphore_signal(barrier, inc=1, device_id=outward, device_id_type=MESH)

    def rows_at(which):
        return pl.ds(pl.multiple_of(which * half, half), half)

    mine, theirs = rows_at(y), rows_at(1 - y)
    kept, rest = rows_at(side), rows_at(1 - side)

    def to_sibling(j):
        return remote(sib_send.at[j % RING], part.at[j], sib_ss.at[j % RING], sib_rs.at[j], sibling)

    def one_y(j):
        i = j // 2
        return remote(part.at[j, theirs], y1.at[i], y1_ss.at[i], y1_rs.at[i], across_y)

    def one_in(j):
        i = j // 2
        return remote(part.at[j, mine], zin1.at[i], z1_ss.at[i], z1_rs.at[i], inward)

    def one_mid(j):
        i = j // 2
        return remote(part.at[j, mine], mid1.at[i], m1_ss.at[i], m1_rs.at[i], inward)

    def one_out(j):
        return remote(final.at[j, mine], final.at[j, mine], f_ss.at[0, j], f_rs.at[0, j], outward)

    def one_back(j):
        return remote(final.at[j, mine], final.at[j, mine], f_ss.at[1, j], f_rs.at[1, j], across_y)

    def one_back_in(j):
        return remote(final.at[j, theirs], final.at[j, theirs], f_ss.at[1, j], f_rs.at[1, j], across_y)

    def two_in(j):
        i = j // 2
        return remote(part.at[j], zin2.at[i], z2_ss.at[i], z2_rs.at[i], inward)

    def two_mid(j):
        i = j // 2
        return remote(part.at[j, rest], mid2.at[i], m2_ss.at[i], m2_rs.at[i], inward)

    def two_y(j):
        i = j // 2
        return remote(part.at[j, kept], y2.at[i], y2_ss.at[i], y2_rs.at[i], across_y)

    def two_swap(j):
        return remote(final.at[j, kept], final.at[j, kept], f_ss.at[2, j], f_rs.at[1, j], inward)

    def two_swap_in(j):
        return remote(final.at[j, rest], final.at[j, rest], f_ss.at[2, j], f_rs.at[1, j], inward)

    def two_out_kept(j):
        return remote(final.at[j, kept], final.at[j, kept], f_ss.at[0, j], f_rs.at[0, j], outward)

    def two_out_rest(j):
        return remote(final.at[j, rest], final.at[j, rest], f_ss.at[1, j], f_rs.at[1, j], outward)

    down = a_h.shape[1] // (2 * PANEL)
    outer_cols = features // PANEL
    raw = dict(x=(x_h, 0), ctx=(ctx_h, 1), df=(df_h, 2), mid=(mid_h, 3))

    def left_of(who, j):
        late = jnp.minimum(j // down, 1)
        even = 2 * (1 - late) + late * (1 - jnp.minimum(j // (down + outer_cols), 1))
        odd = 2 * (1 - late) + 3 * late
        return who * odd + (1 - who) * even

    def columns(col):
        return pl.ds(pl.multiple_of(col * PANEL, PANEL), PANEL)

    def fetch_down(who, j, ring, sem):
        return pltpu.make_async_copy(a_h.at[:, columns(who * down + j)], ring.at[j % RING], sem.at[j % RING])

    def fetch_up(j, ring, sem):
        return pltpu.make_async_copy(du_h.at[:, columns(j - down)], ring.at[j % RING], sem.at[j % RING])

    def fetch(who, j, ring, sem):
        when(j < down, lambda: fetch_down(who, j, ring, sem).start())
        when((j >= down) & (j < last) & (who == 1), lambda: fetch_up(j, ring, sem).start())

    def right(who, j, ring, sem, use):
        def arrived():
            pltpu.make_async_copy(a_h.at[:, columns(0)], ring.at[j % RING], sem.at[j % RING]).wait()
            return ring[j % RING]

        def patched():
            block, hot = arrived(), hot_ref[...]
            is_lead = (jnp.max(hot.astype(f32), axis=1, keepdims=True) > 0) & (at_head == 0)
            use(jnp.where(is_lead, mm(hot, lead_du[:, columns(j - down)]).astype(bf16), block))

        when(j < down, lambda: use(arrived()))
        when((j >= down) & (j < last) & (who == 1), patched)
        when((j >= down) & (j < down + outer_cols) & (who == 0), lambda: use(do[:, columns(j - down)]))
        when(
            (j >= down + outer_cols) & (j < last) & (who == 0), lambda: use(qkv[:, columns(j - down - outer_cols)])
        )

    def to_out(j):
        late = jnp.minimum(j // down, 1)
        even = jnp.where(j < down + outer_cols, j - down + 3 * outer_cols, j - down - outer_cols)
        col = (1 - late) * (4 * outer_cols + j) + late * (core * (j - down) + (1 - core) * even)
        return pltpu.make_async_copy(final.at[j], out_h.at[:, columns(col)], out_sem.at[j])


    def own_send(src):
        return remote(src, halves.at[core], o_ss, o_rs, sibling)

    def own_from():
        return remote(dx_buf, halves.at[1 - core], o_ss, o_rs, sibling)

    def across_send(src):
        return remote(src, halves.at[core], c_ss, c_rs.at[core], beyond)

    def across_from(side):
        return remote(dx_buf, halves.at[side], c_ss, c_rs.at[side], beyond)

    def load_left(name):
        return pltpu.make_async_copy(raw[name][0], left, left_sem)

    loads = dict(dmid=(dmid_h, do), zh0=(zh0_h, dctx), qkv=(qkv_h, qkv), p=(p_h, p), y=(y_h, y_buf))
    names = list(loads)

    def load(name):
        return pltpu.make_async_copy(*loads[name], in_sem.at[names.index(name)])

    def load_wa(own, c):
        cols = pl.ds(c * features, features)
        return pltpu.make_async_copy((first_h if own else other_first_h).at[:, cols], wa.at[:, cols], a_sem.at[c])

    load_left("df").start()
    for j in range(RING):
        fetch_down(core, j, own_ring, own_sem).start()
        fetch_down(1 - core, j, sib_ring, ring_sem).start()
    load("dmid").start()
    load("zh0").start()
    for c in (3, 0, 1, 2):
        when(core == 0, lambda: load_wa(True, c).start())
        when(core == 1, lambda: load_wa(False, c).start())
    for name in ("qkv", "p", "y"):
        load(name).start()

    def turn(i):
        for b in range(features // BLOCK):
            grid = (BLOCK, features)
            eye = lax.broadcasted_iota(jnp.int32, grid, 0) + b * BLOCK == lax.broadcasted_iota(jnp.int32, grid, 1)
            left_t[i, pl.ds(b * BLOCK, BLOCK), :] = mm(eye.astype(f32).astype(bf16), left[...], NT).astype(bf16)

    def norm_panel(other):
        chosen = jnp.where(core == other, dnorm[2:4, :], dnorm[0:2, :])
        strips = [
            chosen[r : r + 1, c * PANEL : (c + 1) * PANEL]
            for r in range(2)
            for c in range(features // PANEL)
        ]
        return jnp.concatenate(strips + [jnp.zeros((16 - len(strips), PANEL), f32)], axis=0)

    pl.semaphore_wait(barrier, 5 + has_out.astype(jnp.int32))

    def stage_send(j):
        when(j >= RING, lambda: to_sibling(j - RING).wait_send())

        def use(block):
            sib_send[j % RING] = mm(left_t[left_of(1 - core, j)], block).astype(bf16)

        right(1 - core, j, sib_ring, ring_sem, use)
        to_sibling(j).start()
        fetch(1 - core, j + RING, sib_ring, ring_sem)

    def stage_part(j):
        to_sibling(j).wait_recv()

        def use(block):
            own = mm(left_t[left_of(core, j)], block)
            part[j] = (own + part[j].astype(f32)).astype(bf16)

        right(core, j, own_ring, own_sem, use)
        fetch(core, j + RING, own_ring, own_sem)
        when(j % 2 == 0, lambda: one_y(j).start())
        when((j % 2 == 1) & (dist == depth) & (depth > 0), lambda: two_in(j).start())
        when((j % 2 == 1) & (dist == depth) & (depth == 0), lambda: two_mid(j).start())

    def one_halves(j):
        one_y(j).wait_recv()
        part[j, mine, :] = (part[j, mine, :].astype(f32) + y1[j // 2].astype(f32)).astype(bf16)
        when((dist == depth) & (dist > 0), lambda: one_in(j).start())
        when((dist == depth) & inner, lambda: one_mid(j).start())

    def one_chain(j):
        one_in(j).wait_recv()
        part[j, mine, :] = (part[j, mine, :].astype(f32) + zin1[j // 2].astype(f32)).astype(bf16)
        when(dist > 0, lambda: one_in(j).start())
        when(inner, lambda: one_mid(j).start())

    def one_total(j):
        one_mid(j).wait_recv()
        final[j, mine, :] = (part[j, mine, :].astype(f32) + mid1[j // 2].astype(f32)).astype(bf16)
        when(has_out, lambda: one_out(j).start())
        one_back(j).start()

    def one_spread(j):
        one_out(j).wait_recv()
        when(has_out, lambda: one_out(j).start())
        one_back(j).start()

    def two_chain(j):
        two_in(j).wait_recv()
        part[j] = (part[j].astype(f32) + zin2[j // 2].astype(f32)).astype(bf16)
        when(dist > 0, lambda: two_in(j).start())
        when(inner, lambda: two_mid(j).start())

    def two_halves(j):
        two_mid(j).wait_recv()
        part[j, kept, :] = (part[j, kept, :].astype(f32) + mid2[j // 2].astype(f32)).astype(bf16)
        two_y(j).start()

    def two_total(j):
        two_y(j).wait_recv()
        final[j, kept, :] = (part[j, kept, :].astype(f32) + y2[j // 2].astype(f32)).astype(bf16)
        two_swap(j).start()
        when(has_out, lambda: two_out_kept(j).start())

    def two_swapped(j):
        two_swap_in(j).wait_recv()
        when(has_out, lambda: two_out_rest(j).start())

    def two_spread_kept(j):
        two_out_kept(j).wait_recv()
        when(has_out, lambda: two_out_kept(j).start())

    def two_spread_rest(j):
        two_out_rest(j).wait_recv()
        when(has_out, lambda: two_out_rest(j).start())

    def finish(j):
        when(j % 2 == 0, lambda: one_back_in(j).wait_recv())

        to_out(j).start()

    last_lag = 7 + 4 * depth

    pairs = features // PAIR
    items = tokens // BLOCK * pairs
    begin = 4

    def turn_next(name, following):
        load_left(name).wait()
        turn(raw[name][1])
        if following:
            load_left(following).start()

    def attention_begin():
        load("dmid").wait()
        load("zh0").wait()
        load_wa(True, 3).wait()
        attention_back_begin(do, norms, wa, dctx, rstd0, do, dctx, acc, dnorm)

    def send_rows():
        load("y").wait()

        @pl.when(at_head == 1)
        def _():
            leading = jnp.max(lead_picks(lengths, core, True), axis=1, keepdims=True) > 0
            dx_buf[...] = jnp.where(leading, 0.0, acc[...]).astype(bf16)

        @pl.when(at_head == 0)
        def _():
            dx_buf[...] = acc[...].astype(bf16)

        def go(own, across):
            across_send(across).start()
            when(~inside, lambda: own_send(own).start())

            @pl.when(inside)
            def _():
                halves[core] = own[...]

        when(at_head == 1, go, y_buf, dx_buf)
        when(at_head == 0, go, dx_buf, y_buf)

    def norm_hop(src, dst, i, target):
        return remote(norm.at[src], norm.at[dst], n_ss.at[i], n_rs.at[i], target)

    norm_sib = norm_hop(0, 1, 0, sibling)
    norm_y = norm_hop(2, 3, 1, across_y)
    norm_in_hop = norm_hop(7, 4, 2, inward)
    norm_mid = norm_hop(7, 5, 3, inward)
    norm_far = norm_hop(6, 6, 4, outward)

    def norm_steps(t):
        @pl.when(t == 0)
        def _():
            norm[0] = norm_panel(0)
            norm_sib.start()

        @pl.when(t == 2)
        def _():
            norm_sib.wait_recv()
            norm[2] = norm_panel(1) + norm[1]
            norm_y.start()

        @pl.when(t == 4)
        def _():
            norm_y.wait_recv()
            norm[7] = norm[2] + norm[3]

        @pl.when((t == 4 + 2 * (depth - dist)) & (dist < depth))
        def _():
            norm_in_hop.wait_recv()
            norm[7] = norm[7] + norm[4]

        @pl.when(t == 4 + 2 * (depth - dist))
        def _():
            when(dist > 0, lambda: norm_in_hop.start())
            when(inner, lambda: norm_mid.start())

        @pl.when((t == 6 + 2 * depth) & inner)
        def _():
            norm_mid.wait_recv()
            norm[6] = norm[7] + norm[5]
            when(has_out, lambda: norm_far.start())

        @pl.when((t == 6 + 2 * (depth + dist)) & (dist > 0))
        def _():
            norm_far.wait_recv()
            when(has_out, lambda: norm_far.start())

    dnorm[...] = dnorm_in[...]
    hot_ref[...] = lead_picks(lengths, core, True).astype(bf16)
    turn_next("df", "mid")

    def step(t, carry):
        def at(lag, kind, cond, run):
            j = t - lag
            ok = (j >= 0) & (j < panels)
            if kind is not None:
                ok = ok & (j % 2 == kind)
            if cond is not None:
                ok = ok & cond
            when(ok, run, j)

        at(7 + 2 * (depth + dist), 1, dist > 0, two_spread_rest)
        at(5 + 2 * (depth + dist), 1, dist > 0, two_spread_kept)
        at(5 + 2 * (depth + dist), 0, dist > 0, one_spread)
        at(7 + 2 * depth, 1, inner, two_swapped)
        at(5 + 2 * depth, 1, inner, two_total)
        at(5 + 2 * depth, 0, inner, one_total)
        at(3 + 2 * depth, 1, inner, two_halves)
        at(3 + 2 * (depth - dist), 0, dist < depth, one_chain)
        at(1 + 2 * (depth - dist), 1, dist < depth, two_chain)
        at(3, 0, None, one_halves)
        at(1, None, None, stage_part)
        at(0, None, None, stage_send)
        at(last_lag + 1, None, None, finish)
        when(t == begin, attention_begin)
        item = t - begin - 1
        when(t == begin + 1, lambda: [load("qkv").wait(), load("p").wait()])
        when((item >= 0) & (item < items), lambda: attention_back_item(item // pairs, item % pairs, qkv, p, dctx))
        when(t == 8, turn_next, "mid", "ctx")
        when(t == 9, turn_next, "ctx", "x")
        when(t == 10, turn_next, "x", None)
        for c in range(3):
            when(t == begin + items + 1 + c, lambda: [load_wa(True, c).wait(), attention_back_end(c, wa, qkv, acc)])
        when(t == begin + items + 4, send_rows)
        norm_steps(t - begin - 1)
        return carry

    lax.fori_loop(0, panels + last_lag + 1, step, 0)

    @pl.when(inside)
    def _():
        own_from().wait_recv()

    @pl.when(~inside)
    def _():
        own_send(dx_buf).wait_send()
        across_from(0).wait_recv()
        across_from(1).wait_recv()

    across_send(dx_buf).wait_send()
    norm_sib.wait_send()
    norm_y.wait_send()
    when(dist > 0, lambda: norm_in_hop.wait_send())
    when(inner, lambda: norm_mid.wait_send())
    when(has_out, lambda: norm_far.wait_send())
    norm_out[...] = norm[6]
    rows_done = pltpu.make_async_copy(halves, halves_h, h_sem)
    rows_done.start()

    def drain(j, carry):
        when(j >= panels - RING, lambda: to_sibling(j).wait_send())
        to_out(j).wait()

        @pl.when(j % 2 == 0)
        def _():
            one_y(j).wait_send()
            when(dist > 0, lambda: one_in(j).wait_send())
            when(inner, lambda: one_mid(j).wait_send())
            when(has_out, lambda: one_out(j).wait_send())
            one_back(j).wait_send()

        @pl.when(j % 2 == 1)
        def _():
            when(dist > 0, lambda: two_in(j).wait_send())

            @pl.when(inner)
            def _():
                two_mid(j).wait_send()
                two_y(j).wait_send()
                two_swap(j).wait_send()

            @pl.when(has_out)
            def _():
                two_out_kept(j).wait_send()
                two_out_rest(j).wait_send()

        return carry

    lax.fori_loop(0, panels, drain, 0)
    rows_done.wait()


def reduce_gradients(lengths, first, saved, chain):
    tokens, features = saved["x"].shape
    ff = saved["a"].shape[1]
    width = ff + ff // 2
    panels = width // PANEL
    evens, odds = (panels + 1) // 2, panels // 2
    h = features // 2
    one = pltpu.SemaphoreType.DMA
    arrays = [saved[k] for k in ("x", "ctx", "mid", "a", "df", "du", "dmid", "zh0", "qkv", "p", "y")]
    return pl.pallas_call(
        functools.partial(reduce_kernel, chain),
        out_shape=[S((features, width), bf16), S((16, PANEL), f32), S((2, tokens, features), bf16)],
        in_specs=[IN_SMEM] + [IN_VMEM] * 4 + [ANY] * 13,
        out_specs=[ANY, IN_VMEM, ANY],
        scratch_shapes=[
            vm(tokens, features), vm(4, features, tokens), vm(RING, tokens, PANEL), vm(RING, tokens, PANEL),
            vm(RING, features, PANEL), vm(panels, features, PANEL),
            vm(evens, h, PANEL), vm(evens, h, PANEL), vm(evens, h, PANEL),
            vm(odds, features, PANEL), vm(odds, h, PANEL), vm(odds, h, PANEL),
            vm(panels, features, PANEL), vm(2, tokens, features),
            vm(features, ff), vm(tokens, 3 * features), pltpu.VMEM(saved["p"].shape, bf16), vm(tokens, features),
            vm(tokens, features), pltpu.VMEM((tokens, features), f32), vm(tokens, features),
            pltpu.VMEM((4, features), f32), pltpu.VMEM((8, 16, PANEL), f32), vm(tokens, LEADS),
            one, dma(RING), dma(RING), dma(panels), dma(RING), dma(panels),
            dma(evens), dma(evens), dma(evens), dma(evens), dma(evens), dma(evens),
            dma(odds), dma(odds), dma(odds), dma(odds), dma(odds), dma(odds), dma(3, panels), dma(2, panels),
            one, one, one, dma(2), one, dma(ff // features), dma(5), dma(5), dma(5),
        ],
        compiler_params=params(3),
        name="reduce_gradients",
    )(lengths, saved["dnorm"], saved["norms"], saved["rstd0"], saved["lead_du"], *arrays, first, saved["other_first"])


def finish_kernel(lengths, total, halves, norm_in, first_out, second_out, rows_out, gain_out, shift_out):
    step = pl.program_id(0)
    features = rows_out.shape[1]
    wide = first_out.shape[1]
    first_out[...] = total[:, pl.ds(0, wide)].astype(f32)
    second_out[...] = total[:, pl.ds(wide, second_out.shape[1])].astype(f32)
    size = rows_out.shape[0]
    row = step // (SEQ // size)
    _, _, first = span_scalars(lengths, row)
    at = lax.broadcasted_iota(jnp.int32, (size, BLOCK), 0) + step % (SEQ // size) * size
    out = None
    for side in range(2):
        hot = at == places(first, side, (size, BLOCK), 1)
        part = mm(hot.astype(f32).astype(bf16), halves[side])
        out = part if out is None else out + part
    rows_out[...] = out
    strips = features // PANEL
    for r, ref in enumerate((gain_out, shift_out)):
        ref[...] = jnp.concatenate([norm_in[r * strips + c : r * strips + c + 1, :] for c in range(strips)], axis=1)


def finish(lengths, total, halves, norm_in, ff):
    features, width = total.shape
    tokens = halves.shape[1]
    size = SEQ
    steps = 2 * tokens // size
    part = features // steps
    row_spec = pl.BlockSpec((1, features), lambda i: (0, 0))
    return pl.pallas_call(
        finish_kernel,
        grid=(steps,),
        out_shape=[
            S((features, ff), f32), S((features, width - ff), f32), S((2 * tokens, features), f32),
            S((1, features), f32), S((1, features), f32),
        ],
        in_specs=[
            IN_SMEM, pl.BlockSpec((part, width), lambda i: (i, 0)),
            pl.BlockSpec((2, BLOCK, features), lambda i: (0, i // (SEQ // size), 0)), IN_VMEM,
        ],
        out_specs=[
            pl.BlockSpec((part, ff), lambda i: (i, 0)), pl.BlockSpec((part, width - ff), lambda i: (i, 0)),
            pl.BlockSpec((size, features), lambda i: (i, 0)), row_spec, row_spec,
        ],
        compiler_params=params(None),
        name="finish",
    )(lengths, total, halves, norm_in)


def per_device(section_rows, span_lengths, first_weights, second_weights, norm_gain, norm_shift):
    first, second = first_weights[0], second_weights[0]
    saved = front(section_rows[0], span_lengths, first, second, norm_gain, norm_shift)
    total, norm_total, halves = reduce_gradients(span_lengths, first, saved, lax.axis_size("dp") // 2)
    d_first, d_second, rows, gain, shift = finish(span_lengths, total, halves, norm_total, first.shape[1])
    return rows[None], d_first[None], d_second[None], gain, shift


def solution(mesh):
    in_specs = (
        P("section", "dp", None),
        P("dp", None),
        P("section", None, None),
        P("section", None, None),
        P("section", None),
        P("section", None),
    )
    out_specs = (
        P("section", "dp", None),
        P("section", None, None),
        P("section", None, None),
        P("section", None),
        P("section", None),
    )
    return jax.shard_map(
        per_device, mesh=mesh, in_specs=in_specs, out_specs=out_specs, check_vma=False
    )
```

```python
import functools

import jax
import jax.numpy as jnp
from jax import lax
from jax.experimental import pallas as pl
from jax.experimental.pallas import tpu as pltpu
from jax.sharding import PartitionSpec as P

HEAD_DIM = 64
PAIR = 2 * HEAD_DIM
BLOCK = 256
SEQ = 512
LEADS = 16
VMEM_LIMIT = 60 << 20
MESH = pl.DeviceIdType.MESH
f32 = jnp.float32
bf16 = jnp.bfloat16
epsilon = 1e-12
NN = (((1,), (0,)), ((), ()))
NT = (((1,), (1,)), ((), ()))
TN = (((0,), (0,)), ((), ()))
LOG2E = 1.4426950408889634


def mm(a, b, dims=NN):
    return lax.dot_general(a, b, dims, preferred_element_type=f32)


def when(cond, step, *args):
    @pl.when(cond)
    def _():
        step(*args)


def remote(src, dst, ss, rs, target):
    return pltpu.make_async_remote_copy(
        src_ref=src, dst_ref=dst, send_sem=ss, recv_sem=rs, device_id=target, device_id_type=MESH
    )


def gelu_and_slope(u):
    bell = jnp.exp2(u * u * (-0.5 * LOG2E))
    t = 1.0 / (1.0 + (0.3275911 * 0.5**0.5) * jnp.abs(u))
    poly = t * (0.127414796 + t * (-0.142248368 + t * (0.7107068705 + t * (-0.7265760135 + t * 0.5307027145))))
    tail = poly * bell
    cdf = jnp.where(u < 0, tail, 1.0 - tail)
    return u * cdf, cdf + u * bell * 0.3989422804014327


def normalize(z):
    centered = z - jnp.mean(z, axis=-1, keepdims=True)
    rstd = lax.rsqrt(jnp.mean(centered * centered, axis=-1, keepdims=True) + epsilon)
    return centered * rstd, rstd


def normalize_back(zh, rstd, gain, dy):
    g = dy * gain
    mean_g = jnp.mean(g, axis=-1, keepdims=True)
    mean_gz = jnp.mean(g * zh, axis=-1, keepdims=True)
    dz = rstd * (g - mean_g - zh * mean_gz)
    return dz, jnp.sum(dy * zh, axis=0, keepdims=True), jnp.sum(dy, axis=0, keepdims=True)


def span_scalars(lengths, row):
    ends, starts, first, total = [], [], 0, 0
    for j in range(lengths.shape[1]):
        size = lengths[row, j]
        starts.append(total)
        first = first + jnp.where(size == BLOCK, total, 0)
        total = total + size
        ends.append(total)
    return ends, starts, first


def places(first, core, shape, axis):
    at = lax.broadcasted_iota(jnp.int32, shape, axis) + (first + core * BLOCK)
    return jnp.where(at >= SEQ, at - SEQ, at)


def mask_bias(lengths, row, core):
    ends, _, first = span_scalars(lengths, row)

    def segment(at):
        return sum((at >= end).astype(jnp.int32) for end in ends)

    rows = segment(places(first, core, (BLOCK, BLOCK), 0))
    cols = segment(places(first, core, (BLOCK, BLOCK), 1))
    return jnp.where(rows == cols, 0.0, -1e30)


def lead_picks(lengths, core, by_rows):
    parts = []
    per_row = lengths.shape[1] - 1
    shape = (BLOCK, LEADS) if by_rows else (LEADS, BLOCK)
    for row in range(lengths.shape[0]):
        _, starts, first = span_scalars(lengths, row)
        at = places(first, core, shape, 0 if by_rows else 1)
        slot = lax.broadcasted_iota(jnp.int32, shape, 1 if by_rows else 0)
        hit = sum(
            ((slot == row * per_row + j) & (at == starts[j])).astype(jnp.int32) for j in range(per_row)
        )
        parts.append(hit.astype(f32))
    return jnp.concatenate(parts, axis=0 if by_rows else 1)


def lane_masks():
    return lax.broadcasted_iota(jnp.int32, (BLOCK, PAIR), 1) < HEAD_DIM


def forward_pass(x, lengths, core, norms, wa, wu, wd, qkv, ctx, mid, acc, ready, arrive, save):
    tokens, features = x.shape
    pairs = features // PAIR
    first = lane_masks()
    zero = jnp.zeros((BLOCK, PAIR), bf16)

    def block_step(b, carry):
        rows = pl.ds(pl.multiple_of(b * BLOCK, BLOCK), BLOCK)
        arrive(b)
        for c in range(3):
            cols = pl.ds(c * features, features)
            qkv[rows, cols] = mm(x[rows, :], wa[:, cols]).astype(bf16)
        bias = mask_bias(lengths, b, core)
        for h in range(pairs):
            q = qkv[rows, pl.ds(h * PAIR, PAIR)]
            k = qkv[rows, pl.ds(features + h * PAIR, PAIR)]
            v = qkv[rows, pl.ds(2 * features + h * PAIR, PAIR)]
            total = None
            for side in range(2):
                own = first if side == 0 else ~first
                s = mm(q, jnp.where(own, k, zero), NT) * (HEAD_DIM**-0.5) + bias
                e = jnp.exp(s - jnp.max(s, axis=-1, keepdims=True))
                pr = (e * (1.0 / jnp.sum(e, axis=-1, keepdims=True))).astype(bf16)
                save["p"][b, h, :, pl.ds(side * BLOCK, BLOCK)] = pr
                part = mm(pr, jnp.where(own, v, zero))
                total = part if total is None else total + part
            ctx[rows, pl.ds(h * PAIR, PAIR)] = total.astype(bf16)
        return carry

    lax.fori_loop(0, tokens // BLOCK, block_step, 0)
    ready["a"](3)
    zn, r = normalize(x[...].astype(f32) + mm(ctx[...], wa[:, pl.ds(3 * features, features)]))
    save["keep"]("x", "qkv", "p", "ctx")
    save["rstd0"][...] = r
    save["zh0"][...] = zn.astype(bf16)
    mid[...] = (zn * norms[0, 0:1, :] + norms[0, 1:2, :]).astype(bf16)
    acc[...] = mid[...].astype(f32)
    save["keep"]("zh0", "mid")
    pieces = wu.shape[1] // features
    cols = [pl.ds(c * features, features) for c in range(pieces)]
    ready["u"](0)
    ahead = mm(mid[...], wu[:, cols[0]])
    for c in range(pieces):
        u = ahead
        if c + 1 < pieces:
            ready["u"](c + 1)
            ahead = mm(mid[...], wu[:, cols[c + 1]])
        act, slope = gelu_and_slope(u)
        act = act.astype(bf16)
        save["a"][:, cols[c]] = act
        save["slope"][:, cols[c]] = slope.astype(bf16)
        save["keep_cols"](c)
        ready["d"](c)
        acc[...] += mm(act, wd[:, cols[c]], NT)
    zn, r = normalize(acc[...])
    save["rstd1"][...] = r
    save["zh1"][...] = zn.astype(bf16)
    return (zn * norms[1, 0:1, :] + norms[1, 1:2, :]).astype(bf16)


def feed_forward_back(dy, norms, wu, wd, slope, zh1, rstd1, df, du, acc, dnorm, ready):
    features = wu.shape[0]
    dz, dgain, dshift = normalize_back(zh1[...].astype(f32), rstd1[...], norms[1, 0:1, :], dy.astype(f32))
    dnorm[2:3, :] = dgain
    dnorm[3:4, :] = dshift
    df[...] = dz.astype(bf16)
    acc[...] = dz
    for c in range(wu.shape[1] // features):
        cols = pl.ds(c * features, features)
        ready["d"](c)
        da = mm(df[...], wd[:, cols])
        ready["du"](c)
        g = (da * slope[:, cols].astype(f32)).astype(bf16)
        du[:, cols] = g
        ready["u"](c)
        acc[...] += mm(g, wu[:, cols], NT)


def attention_back_begin(d_mid, norms, wa, zh0, rstd0, do, dctx, acc, dnorm):
    tokens, features = acc.shape
    dgain = dshift = None
    for b in range(tokens // BLOCK):
        rows = pl.ds(b * BLOCK, BLOCK)
        dz, dg, ds = normalize_back(
            zh0[rows, :].astype(f32), rstd0[rows, :], norms[0, 0:1, :], d_mid[rows, :].astype(f32)
        )
        dgain, dshift = (dg, ds) if b == 0 else (dgain + dg, dshift + ds)
        acc[rows, :] = dz
        do[rows, :] = dz.astype(bf16)
        dctx[rows, :] = mm(dz.astype(bf16), wa[:, pl.ds(3 * features, features)], NT).astype(bf16)
    dnorm[0:1, :] = dgain
    dnorm[1:2, :] = dshift


def attention_back_item(b, h, qkv, p, dctx):
    features = dctx.shape[1]
    first = lane_masks()
    zero = jnp.zeros((BLOCK, PAIR), bf16)
    scale = HEAD_DIM**-0.5
    rows = pl.ds(pl.multiple_of(b * BLOCK, BLOCK), BLOCK)
    at = [pl.ds(pl.multiple_of(part * features + h * PAIR, PAIR), PAIR) for part in range(3)]
    q, k, v = (qkv[rows, cols] for cols in at)
    dc = dctx[rows, at[0]]
    dq = dk = dv = None
    for side in range(2):
        own = first if side == 0 else ~first
        pr = p[b, h, :, pl.ds(side * BLOCK, BLOCK)]
        prf = pr.astype(f32)
        dp = mm(dc, jnp.where(own, v, zero), NT)
        r = jnp.sum(dp * prf, axis=-1, keepdims=True)
        ds = (prf * (dp - r)).astype(bf16)
        parts = (
            mm(ds, jnp.where(own, k, zero)),
            mm(ds, jnp.where(own, q, zero), TN),
            mm(pr, jnp.where(own, dc, zero), TN),
        )
        if dq is None:
            dq, dk, dv = parts
        else:
            dq, dk, dv = dq + parts[0], dk + parts[1], dv + parts[2]
    qkv[rows, at[0]] = (dq * scale).astype(bf16)
    qkv[rows, at[1]] = (dk * scale).astype(bf16)
    qkv[rows, at[2]] = dv.astype(bf16)


def attention_back_end(part, wa, dqkv, acc):
    features = wa.shape[0]
    cols = pl.ds(part * features, features)
    for b in range(acc.shape[0] // BLOCK):
        rows = pl.ds(b * BLOCK, BLOCK)
        acc[rows, :] += mm(dqkv[rows, cols], wa[:, cols], NT)


def head_lanes(features):
    lane = lax.broadcasted_iota(jnp.int32, (LEADS, features), 1)
    return [(lane >= h * HEAD_DIM) & (lane < (h + 1) * HEAD_DIM) for h in range(features // HEAD_DIM)]


def spread_heads(rows):
    wide = rows.astype(f32)
    return jnp.concatenate([jnp.where(own, wide, 0.0) for own in head_lanes(rows.shape[1])], axis=0).astype(bf16)


def fold_heads(wide):
    total = None
    for h, own in enumerate(head_lanes(wide.shape[1])):
        part = jnp.where(own, wide[h * LEADS : (h + 1) * LEADS, :], 0.0)
        total = part if total is None else total + part
    return total


def lead_probs(queries, keys, lengths, core):
    tokens, features = keys.shape
    per_row = lengths.shape[1] - 1
    parts = []
    for row in range(tokens // BLOCK):
        ends, _, first = span_scalars(lengths, row)
        at = places(first, core, (LEADS, BLOCK), 1)
        segment = sum((at >= end).astype(jnp.int32) for end in ends)
        span = lax.broadcasted_iota(jnp.int32, (LEADS, BLOCK), 0) - row * per_row
        parts.append(jnp.where((span == segment) & (span < per_row), 0.0, -1e30))
    bias = jnp.concatenate([jnp.concatenate(parts, axis=1)] * (features // HEAD_DIM), axis=0)
    s = mm(spread_heads(queries), keys, NT) * (HEAD_DIM**-0.5) + bias
    e = jnp.exp(s - jnp.max(s, axis=-1, keepdims=True))
    return (e * (1.0 / jnp.sum(e, axis=-1, keepdims=True))).astype(bf16)


def lead_forward(x, lengths, core, norms, wa, wu, wd, qkv, ready):
    features = x.shape[1]
    pieces = wu.shape[1] // features
    cols = [pl.ds(c * features, features) for c in range(4)]
    own = mm(lead_picks(lengths, core, False).astype(bf16), x[...]).astype(bf16)
    for c in (1, 2):
        ready["a"](c)
        qkv[:, cols[c]] = mm(x[...], wa[:, cols[c]]).astype(bf16)
    ready["a"](0)
    probs = lead_probs(mm(own, wa[:, cols[0]]).astype(bf16), qkv[:, cols[1]], lengths, core)
    ctx = fold_heads(mm(probs, qkv[:, cols[2]])).astype(bf16)
    ready["a"](3)
    zn, _ = normalize(own.astype(f32) + mm(ctx, wa[:, cols[3]]))
    mid = (zn * norms[0, 0:1, :] + norms[0, 1:2, :]).astype(bf16)
    out = mid.astype(f32)
    for step in range(pieces):
        c = (step + core * (pieces // 2)) % pieces
        at = pl.ds(pl.multiple_of(c * features, features), features)
        ready["u"](c)
        act, _ = gelu_and_slope(mm(mid, wu[:, at]))
        if step % (pieces // 2) == 0:
            ready["half"](step)
        out = out + mm(act.astype(bf16), wd[:, at], NT)
    zn, _ = normalize(out)
    return (zn * norms[1, 0:1, :] + norms[1, 1:2, :]).astype(bf16)


def lead_back(pick, lengths, core, wa, qkv, p, ctx, dctx, dz):
    tokens, features = ctx.shape
    scale = HEAD_DIM**-0.5
    heads = features // HEAD_DIM
    cols = [pl.ds(c * features, features) for c in range(3)]
    q16, v16 = (mm(pick, qkv[:, cols[c]]).astype(bf16) for c in (0, 2))
    low = lead_probs(q16, qkv[:, cols[1]], lengths, core)
    probs = low.astype(f32)
    dp = mm(spread_heads(mm(pick, dctx[...]).astype(bf16)), qkv[:, cols[2]], NT)
    ds = (probs * (dp - jnp.sum(dp * probs, axis=-1, keepdims=True))).astype(bf16)
    dq = (fold_heads(mm(ds, qkv[:, cols[1]])) * scale).astype(bf16)
    seen = []
    for h in range(heads):
        keys = pl.ds(h % 2 * BLOCK, BLOCK)
        seen.append(
            jnp.concatenate(
                [mm(pick[:, b * BLOCK : (b + 1) * BLOCK], p[b, h // 2, :, keys], NT) for b in range(tokens // BLOCK)],
                axis=1,
            )
        )
    seen = jnp.concatenate(seen, axis=0)
    product = dctx[...].astype(f32) * ctx[...].astype(f32)
    high = product.astype(bf16)
    low = (product - high.astype(f32)).astype(bf16)
    lane = lax.broadcasted_iota(jnp.int32, (LEADS, features), 1)
    head = lax.broadcasted_iota(jnp.int32, (LEADS, features), 0) * HEAD_DIM
    select = ((lane >= head) & (lane < head + HEAD_DIM)).astype(f32).astype(bf16)
    sums = mm(select, high, NT) + mm(select, low, NT)
    sums = jnp.concatenate([jnp.broadcast_to(sums[h : h + 1, :], (LEADS, tokens)) for h in range(heads)], axis=0)
    ds = (seen * (mm(spread_heads(v16), dctx[...], NT) - sums)).astype(bf16)
    dk = (fold_heads(mm(ds, qkv[:, cols[0]])) * scale).astype(bf16)
    dv = fold_heads(mm(seen.astype(bf16), dctx[...])).astype(bf16)
    high = dz[...].astype(bf16)
    low = (dz[...] - high.astype(f32)).astype(bf16)
    out = mm(pick, high) + mm(pick, low)
    for c, part in enumerate((dq, dk, dv)):
        out = out + mm(part, wa[:, cols[c]], NT)
    return out


def front_kernel(
    rows_h, lengths, first_h, second_h, gain_in, shift_in,
    x_h, y_h, qkv_h, p_h, ctx_h, zh0_h, mid_h, a_h, df_h, du_h, dmid_h, other_first_h, rstd0, dnorm, norms, lead_du,
    wa, wu, wd, x, qkv, p, ctx, zh0, mid, a, slope, up, zh1, rstd1, do, dctx, acc, d_att,
    lead_slope, lead_zh, lead_rstd, hot_ref, grad_own, grad_in, row_own, row_in, norm_pair,
    row_sem, load, w_ss, w_rs, d_ss, d_rs, n_ss, n_rs, m_ss, m_rs, x_ss, x_rs, r_ss, r_rs, l_ss, l_rs, out_sem, col_sem, du_sem, other_sem, b_ss, b_rs,
):
    sec = lax.axis_index("section")
    core = sec % 2
    at_head = sec // 2
    tokens, features = x.shape
    blocks = tokens // BLOCK
    pieces = wu.shape[1] // features
    half = wd.shape[1] // 2
    even, odd = core == 0, core == 1
    head, backbone = at_head == 1, at_head == 0
    sibling = {"section": sec + 1 - 2 * core}
    peer = {"section": (sec + 2) % 4}
    halves = (do, dctx)
    y, df, dmid = mid, mid, x
    barrier = pltpu.get_barrier_semaphore()
    for step in range(1, 4):
        target = {"section": (sec + step) % 4}
        pl.semaphore_signal(barrier, inc=1, device_id=target, device_id_type=MESH)

    def cols(c):
        return pl.ds(c * features, features)

    def block(b):
        return pl.ds(b * BLOCK if isinstance(b, int) else pl.multiple_of(b * BLOCK, BLOCK), BLOCK)

    def piece(c):
        return pl.ds(c * features if isinstance(c, int) else pl.multiple_of(c * features, features), features)

    def local_first(c, dst):
        return pltpu.make_async_copy(first_h.at[:, piece(c)], dst.at[:, piece(c)], load.at[c])

    def sent_first(c, dst):
        return remote(first_h.at[:, piece(c)], dst.at[:, piece(c)], w_ss.at[c], w_rs.at[c], sibling)

    def local_second(side):
        return pltpu.make_async_copy(second_h, wd.at[:, pl.ds(side * half, half)], load.at[pieces])

    def sent_second(side):
        return remote(second_h, wd.at[:, pl.ds(side * half, half)], d_ss, d_rs, sibling)

    def row_load(row):
        return pltpu.make_async_copy(
            rows_h.at[pl.ds(row * SEQ, SEQ)], slope.at[pl.ds(0, SEQ), cols(row)], row_sem.at[row]
        )

    for row in range(blocks):
        row_load(row).start()
    turns = (1, 2, 0, *range(3, pieces))
    for c in range(pieces):
        when(even, lambda: local_first(turns[c], wa).start())
        when(odd, lambda: local_first(c, wu).start())
    when(even, lambda: local_second(0).start())
    when(odd, lambda: local_second(1).start())

    def inner_send():
        return remote(halves[0], up, m_ss, m_rs, sibling)

    def inner_block(b):
        return remote(halves[1].at[block(b)], x.at[block(b)], b_ss.at[b], b_rs.at[b], sibling)

    def cross_send(dst, side, b):
        target = {"section": 2 + side} if dst is x else {"section": side}
        return remote(halves[side].at[block(b)], dst.at[block(b)], x_ss.at[side, b], x_rs.at[b], target)

    def send_weights():
        for c in range(pieces):
            when(even, lambda: sent_first(turns[c], wa).start())
            when(odd, lambda: sent_first(c, wu).start())
        when(even, lambda: sent_second(0).start())
        when(odd, lambda: sent_second(1).start())

    for row in range(blocks):
        _, _, first = span_scalars(lengths, row)
        row_load(row).wait()
        packed = slope[0:SEQ, cols(row)]
        for side in range(2):
            at = places(first, side, (BLOCK, SEQ), 0)
            hot = at == lax.broadcasted_iota(jnp.int32, (BLOCK, SEQ), 1)
            halves[side][block(row), :] = mm(hot.astype(f32).astype(bf16), packed).astype(bf16)
        if row == 0:
            pl.semaphore_wait(barrier, 3)
        if row < blocks - 1:
            when(sec == 1, lambda: [cross_send(x, side, row).start() for side in range(2)])
        when(sec == 2, lambda: [cross_send(up, side, row).start() for side in range(2)])
        when(sec == 0, lambda: inner_block(row).start())
        if row == 0:
            when(odd, send_weights)
    norm_pair[core, 0:1, :] = gain_in[...]
    norm_pair[core, 1:2, :] = shift_in[...]
    sent_norm = remote(norm_pair.at[core], norm_pair.at[core], n_ss, n_rs, sibling)
    norm_from = remote(norm_pair.at[1 - core], norm_pair.at[1 - core], n_ss, n_rs, sibling)
    sent_norm.start()
    when(even, send_weights)
    when(sec == 3, lambda: inner_send().start())
    pairs_of = [(side, b) for b in range(blocks) for side in range(2)]

    @pl.when(sec == 0)
    def _():
        x[...] = halves[0][...]

    @pl.when(sec == 3)
    def _():
        up[...] = halves[1][...]

    norm_from.wait_recv()
    norms[...] = norm_pair[...]

    def ready_a(c):
        when(even, lambda: local_first(c, wa).wait())
        when(odd, lambda: sent_first(c, wa).wait_recv())

    def ready_u(c):
        when(odd, lambda: local_first(c, wu).wait())
        when(even, lambda: sent_first(c, wu).wait_recv())

    def ready_d(c):
        if c == 0:
            when(even, lambda: local_second(0).wait())
            when(odd, lambda: sent_second(0).wait_recv())
        if c == pieces // 2:
            when(odd, lambda: local_second(1).wait())
            when(even, lambda: sent_second(1).wait_recv())

    def ready_half(step):
        if step == 0:
            when(even, lambda: local_second(0).wait())
            when(odd, lambda: local_second(1).wait())
        else:
            when(even, lambda: sent_second(1).wait_recv())
            when(odd, lambda: sent_second(0).wait_recv())

    refs = dict(
        x=(x, x_h), y=(y, y_h), qkv=(qkv, qkv_h), p=(p, p_h), ctx=(ctx, ctx_h), zh0=(zh0, zh0_h), mid=(mid, mid_h),
        df=(df, df_h), dmid=(dmid, dmid_h),
    )
    order = list(refs)

    def store(name):
        return pltpu.make_async_copy(*refs[name], out_sem.at[order.index(name)])

    def store_cols(c):
        return pltpu.make_async_copy(a.at[:, cols(c)], a_h.at[:, cols(c)], col_sem.at[c])

    def store_du(c):
        return pltpu.make_async_copy(slope.at[:, cols(c)], du_h.at[:, cols(c)], du_sem.at[c])

    def keep(*names):
        for name in names:
            store(name).start()

    picks = lead_picks(lengths, core, True)
    leading = jnp.max(picks, axis=1, keepdims=True) > 0
    hot_leads = picks.astype(bf16)
    pick = lead_picks(lengths, core, False).astype(bf16)
    row_hop = remote(row_own, row_in, r_ss, r_rs, peer)

    @pl.when(backbone)
    def _():
        when(odd, lambda: [inner_block(b).wait_recv() for b in range(blocks)])
        ready = dict(a=ready_a, u=ready_u, half=ready_half)
        row_own[...] = lead_forward(x, lengths, core, norms, wa, wu, wd, qkv, ready)
        row_hop.start()
        when(sec == 1, lambda: [cross_send(x, side, blocks - 1).start() for side in range(2)])

    @pl.when(head)
    def _():
        for c in range(3):
            ready_a(c)
        row_hop.wait_recv()

    hot_ref[...] = hot_leads

    def patched(b):
        cross_send(x, 0, b).wait_recv()
        hot = hot_ref[block(b), :]
        is_lead = jnp.max(hot.astype(f32), axis=1, keepdims=True) > 0
        x[block(b), :] = jnp.where(is_lead, mm(hot, row_in[...]).astype(bf16), x[block(b), :])

    def arrive(b):
        when(head, patched, b)

    at_first = {k: f for k, f in (("a", ready_a), ("u", ready_u), ("d", ready_d))}
    ready = {k: (lambda c, f=f: when(head, f, c)) for k, f in at_first.items()}
    save = dict(
        p=p, a=a, slope=slope, zh0=zh0, zh1=zh1, rstd0=rstd0, rstd1=rstd1, keep=keep,
        keep_cols=lambda c: store_cols(c).start(),
    )
    out = forward_pass(x, lengths, core, norms, wa, wu, wd, qkv, ctx, mid, acc, ready, arrive, save)
    for name in ("mid", "x"):
        store(name).wait()
    y[...] = out
    keep("y")
    other = pltpu.make_async_copy(wa, other_first_h, other_sem)
    when(odd, lambda: other.start())

    @pl.when(backbone)
    def _():
        lead_zh[...] = mm(pick, zh1[...])
        left = jnp.broadcast_to(rstd1[...], (tokens, PAIR))
        total = jnp.zeros((LEADS, PAIR), f32)
        for _ in range(3):
            high = left.astype(bf16)
            left = left - high.astype(f32)
            total = total + mm(pick, high)
        lead_rstd[...] = total[:, 0:1]
        for b in range(blocks):
            cross_send(up, 0, b).wait_recv()
        row_hop.wait_send()
        for c in range(pieces):
            lead_slope[:, cols(c)] = mm(pick, slope[:, cols(c)]).astype(bf16)

    when(sec == 2, lambda: inner_send().wait_recv())
    when(sec == 0, lambda: [inner_block(b).wait_send() for b in range(blocks)])
    when(sec == 3, lambda: inner_send().wait_send())
    when((sec == 1) | (sec == 2), lambda: [cross_send(x, *at).wait_send() for at in pairs_of])
    sent_norm.wait_send()
    for c in range(pieces):
        sent_first(c, wa).wait_send()
    sent_second(0).wait_send()
    none = {k: (lambda *_: None) for k in ("u", "d", "du")}
    store("y").wait()
    feed_forward_back(up[...], norms, wu, wd, slope, zh1, rstd1, df, slope, acc, dnorm, none)
    for c in range(pieces):
        store_du(c).start()
    dmid[...] = acc[...].astype(bf16)
    dnorm[0:2, :] = jnp.zeros((2, features), f32)
    grad_hop = remote(grad_own, grad_in, l_ss, l_rs, peer)

    @pl.when(head)
    def _():
        keep("df", "dmid")
        lead_du[...] = jnp.zeros_like(lead_du)
        attention_back_begin(dmid, norms, wa, zh0, rstd0, do, dctx, acc, d_att)
        grad_own[...] = lead_back(pick, lengths, core, wa, qkv, p, ctx, dctx, acc)
        grad_hop.start()
        grad_hop.wait_send()

    @pl.when(backbone)
    def _():
        base = mm(pick, up[...])
        grad_hop.wait_recv()
        dy = (base + grad_in[...]).astype(bf16).astype(f32)
        extra = dy - base
        dnorm[2:3, :] += jnp.sum(extra * lead_zh[...], axis=0, keepdims=True)
        dnorm[3:4, :] += jnp.sum(extra, axis=0, keepdims=True)
        dz, _, _ = normalize_back(lead_zh[...], lead_rstd[...], norms[1, 0:1, :], dy)
        lead_df = dz.astype(bf16)
        df[...] = jnp.where(leading, mm(hot_leads, lead_df).astype(bf16), df[...])
        keep("df")
        g = (mm(lead_df, wd[...]) * lead_slope[...].astype(f32)).astype(bf16)
        lead_du[...] = g
        dz = dz + mm(g, wu[...], NT)
        dmid[...] = jnp.where(leading, mm(hot_leads, dz.astype(bf16)).astype(bf16), dmid[...])
        keep("dmid")

    for name in order:
        if name not in ("mid", "x", "y"):
            store(name).wait()
    for c in range(pieces):
        store_cols(c).wait()
        store_du(c).wait()
    when(odd, lambda: other.wait())


ANY = pl.BlockSpec(memory_space=pl.ANY)
IN_VMEM = pl.BlockSpec(memory_space=pltpu.VMEM)
IN_SMEM = pl.BlockSpec(memory_space=pltpu.SMEM)
S = jax.ShapeDtypeStruct


def vm(*shape):
    return pltpu.VMEM(shape, bf16)


def dma(*shape):
    return pltpu.SemaphoreType.DMA(shape)


def params(number):
    if number is None:
        return pltpu.CompilerParams(vmem_limit_bytes=VMEM_LIMIT)
    return pltpu.CompilerParams(vmem_limit_bytes=VMEM_LIMIT, collective_id=number, has_side_effects=True)


def front(rows_in, lengths, first, second, gain, shift):
    features, ff = first.shape
    tokens = rows_in.shape[0] // 2
    pieces = ff // features
    blocks, pairs = tokens // BLOCK, features // PAIR
    square = S((tokens, features), bf16)
    one = pltpu.SemaphoreType.DMA
    shapes = dict(
        x=square, y=square, qkv=S((tokens, 3 * features), bf16), p=S((blocks, pairs, BLOCK, 2 * BLOCK), bf16),
        ctx=square, zh0=square, mid=square, a=S((tokens, ff), bf16), df=square, du=S((tokens, ff), bf16), dmid=square,
        other_first=S(first.shape, bf16), rstd0=S((tokens, 1), f32), dnorm=S((4, features), f32),
        norms=S((2, 2, features), f32), lead_du=S((LEADS, ff), bf16),
    )
    small = ("rstd0", "dnorm", "norms", "lead_du")
    wide = vm(features, ff)
    outs = pl.pallas_call(
        front_kernel,
        out_shape=list(shapes.values()),
        in_specs=[ANY, IN_SMEM, ANY, ANY, IN_VMEM, IN_VMEM],
        out_specs=[IN_VMEM if k in small else ANY for k in shapes],
        scratch_shapes=[wide, wide, wide]
        + [pltpu.VMEM(shapes[k].shape, bf16) for k in ("x", "qkv", "p", "ctx", "zh0", "mid", "a", "du")]
        + [
            vm(tokens, features), vm(tokens, features), pltpu.VMEM((tokens, 1), f32), vm(tokens, features),
            vm(tokens, features), pltpu.VMEM((tokens, features), f32), pltpu.VMEM((2, features), f32), vm(LEADS, ff), pltpu.VMEM((LEADS, features), f32),
            pltpu.VMEM((LEADS, 1), f32), vm(tokens, LEADS),
            pltpu.VMEM((LEADS, features), f32), pltpu.VMEM((LEADS, features), f32), vm(LEADS, features), vm(LEADS, features),
            pltpu.VMEM((2, 2, features), f32),
            dma(blocks), dma(pieces + 1), dma(pieces), dma(pieces), one, one, one, one, one, one, dma(2, blocks), dma(blocks),
            one, one, one, one, dma(9), dma(pieces), dma(pieces), one, dma(blocks), dma(blocks),
        ],
        compiler_params=params(1),
        name="front",
    )(rows_in, lengths, first, second, gain, shift)
    return dict(zip(shapes, outs))


PANEL = 128
RING = 4


def reduce_kernel(
    chain, lengths, dnorm_in, norms, rstd0, lead_du, x_h, ctx_h, mid_h, a_h, df_h, du_h, dmid_h, zh0_h, qkv_h, p_h, y_h,
    first_h, other_first_h,
    out_h, norm_out, halves_h,
    left, left_t, own_ring, sib_ring, sib_send, part, y1, zin1, mid1, zin2, mid2, y2, final, halves,
    wa, qkv, p, do, dctx, acc, y_buf, dnorm, norm, hot_ref,
    left_sem, own_sem, ring_sem, out_sem, sib_ss, sib_rs, y1_ss, y1_rs, z1_ss, z1_rs, m1_ss, m1_rs,
    z2_ss, z2_rs, m2_ss, m2_rs, y2_ss, y2_rs, f_ss, f_rs, o_ss, o_rs, c_ss, c_rs, h_sem, a_sem, in_sem, n_ss, n_rs,
):
    sec = lax.axis_index("section")
    dp = lax.axis_index("dp")
    core = sec % 2
    panels, rows, _ = final.shape
    tokens = acc.shape[0]
    half = rows // 2
    features = rows
    last = panels
    spot = dp // 2
    side = spot // (chain // 2)
    depth = chain // 2 - 1
    dist = side * (spot - chain // 2) + (1 - side) * (chain // 2 - 1 - spot)
    inner = dist == 0
    y = dp % 2
    sibling = {"section": sec + 1 - 2 * core}
    across_y = {"dp": dp + 1 - 2 * y}
    inward = {"dp": dp + 2 - 4 * side}
    outward = {"dp": dp - 2 + 4 * side}
    has_out = dist < depth

    barrier = pltpu.get_barrier_semaphore()
    at_head = sec // 2
    dx_buf = dctx
    inside = (sec == 0) | (sec == 3)
    beyond = {"section": 2 - sec // 2}
    others = [{"section": (sec + step) % 4} for step in (1, 2, 3)]
    for target in (*others, across_y, inward):
        pl.semaphore_signal(barrier, inc=1, device_id=target, device_id_type=MESH)

    @pl.when(has_out)
    def _():
        pl.semaphore_signal(barrier, inc=1, device_id=outward, device_id_type=MESH)

    def rows_at(which):
        return pl.ds(pl.multiple_of(which * half, half), half)

    mine, theirs = rows_at(y), rows_at(1 - y)
    kept, rest = rows_at(side), rows_at(1 - side)

    def to_sibling(j):
        return remote(sib_send.at[j % RING], part.at[j], sib_ss.at[j % RING], sib_rs.at[j], sibling)

    def one_y(j):
        i = j // 2
        return remote(part.at[j, theirs], y1.at[i], y1_ss.at[i], y1_rs.at[i], across_y)

    def one_in(j):
        i = j // 2
        return remote(part.at[j, mine], zin1.at[i], z1_ss.at[i], z1_rs.at[i], inward)

    def one_mid(j):
        i = j // 2
        return remote(part.at[j, mine], mid1.at[i], m1_ss.at[i], m1_rs.at[i], inward)

    def one_out(j):
        return remote(final.at[j, mine], final.at[j, mine], f_ss.at[0, j], f_rs.at[0, j], outward)

    def one_back(j):
        return remote(final.at[j, mine], final.at[j, mine], f_ss.at[1, j], f_rs.at[1, j], across_y)

    def one_back_in(j):
        return remote(final.at[j, theirs], final.at[j, theirs], f_ss.at[1, j], f_rs.at[1, j], across_y)

    def two_in(j):
        i = j // 2
        return remote(part.at[j], zin2.at[i], z2_ss.at[i], z2_rs.at[i], inward)

    def two_mid(j):
        i = j // 2
        return remote(part.at[j, rest], mid2.at[i], m2_ss.at[i], m2_rs.at[i], inward)

    def two_y(j):
        i = j // 2
        return remote(part.at[j, kept], y2.at[i], y2_ss.at[i], y2_rs.at[i], across_y)

    def two_swap(j):
        return remote(final.at[j, kept], final.at[j, kept], f_ss.at[2, j], f_rs.at[1, j], inward)

    def two_swap_in(j):
        return remote(final.at[j, rest], final.at[j, rest], f_ss.at[2, j], f_rs.at[1, j], inward)

    def two_out_kept(j):
        return remote(final.at[j, kept], final.at[j, kept], f_ss.at[0, j], f_rs.at[0, j], outward)

    def two_out_rest(j):
        return remote(final.at[j, rest], final.at[j, rest], f_ss.at[1, j], f_rs.at[1, j], outward)

    down = a_h.shape[1] // (2 * PANEL)
    outer_cols = features // PANEL
    raw = dict(x=(x_h, 0), ctx=(ctx_h, 1), df=(df_h, 2), mid=(mid_h, 3))

    def left_of(who, j):
        late = jnp.minimum(j // down, 1)
        even = 2 * (1 - late) + late * (1 - jnp.minimum(j // (down + outer_cols), 1))
        odd = 2 * (1 - late) + 3 * late
        return who * odd + (1 - who) * even

    def columns(col):
        return pl.ds(pl.multiple_of(col * PANEL, PANEL), PANEL)

    def fetch_down(who, j, ring, sem):
        return pltpu.make_async_copy(a_h.at[:, columns(who * down + j)], ring.at[j % RING], sem.at[j % RING])

    def fetch_up(j, ring, sem):
        return pltpu.make_async_copy(du_h.at[:, columns(j - down)], ring.at[j % RING], sem.at[j % RING])

    def fetch(who, j, ring, sem):
        when(j < down, lambda: fetch_down(who, j, ring, sem).start())
        when((j >= down) & (j < last) & (who == 1), lambda: fetch_up(j, ring, sem).start())

    def right(who, j, ring, sem, use):
        def arrived():
            pltpu.make_async_copy(a_h.at[:, columns(0)], ring.at[j % RING], sem.at[j % RING]).wait()
            return ring[j % RING]

        def patched():
            block, hot = arrived(), hot_ref[...]
            is_lead = (jnp.max(hot.astype(f32), axis=1, keepdims=True) > 0) & (at_head == 0)
            use(jnp.where(is_lead, mm(hot, lead_du[:, columns(j - down)]).astype(bf16), block))

        when(j < down, lambda: use(arrived()))
        when((j >= down) & (j < last) & (who == 1), patched)
        when((j >= down) & (j < down + outer_cols) & (who == 0), lambda: use(do[:, columns(j - down)]))
        when(
            (j >= down + outer_cols) & (j < last) & (who == 0), lambda: use(qkv[:, columns(j - down - outer_cols)])
        )

    def to_out(j):
        late = jnp.minimum(j // down, 1)
        even = jnp.where(j < down + outer_cols, j - down + 3 * outer_cols, j - down - outer_cols)
        col = (1 - late) * (4 * outer_cols + j) + late * (core * (j - down) + (1 - core) * even)
        return pltpu.make_async_copy(final.at[j], out_h.at[:, columns(col)], out_sem.at[j])


    def own_send(src):
        return remote(src, halves.at[core], o_ss, o_rs, sibling)

    def own_from():
        return remote(dx_buf, halves.at[1 - core], o_ss, o_rs, sibling)

    def across_send(src):
        return remote(src, halves.at[core], c_ss, c_rs.at[core], beyond)

    def across_from(side):
        return remote(dx_buf, halves.at[side], c_ss, c_rs.at[side], beyond)

    def load_left(name):
        return pltpu.make_async_copy(raw[name][0], left, left_sem)

    loads = dict(dmid=(dmid_h, do), zh0=(zh0_h, dctx), qkv=(qkv_h, qkv), p=(p_h, p), y=(y_h, y_buf))
    names = list(loads)

    def load(name):
        return pltpu.make_async_copy(*loads[name], in_sem.at[names.index(name)])

    def load_wa(own, c):
        cols = pl.ds(c * features, features)
        return pltpu.make_async_copy((first_h if own else other_first_h).at[:, cols], wa.at[:, cols], a_sem.at[c])

    load_left("df").start()
    for j in range(RING):
        fetch_down(core, j, own_ring, own_sem).start()
        fetch_down(1 - core, j, sib_ring, ring_sem).start()
    load("dmid").start()
    load("zh0").start()
    for c in (3, 0, 1, 2):
        when(core == 0, lambda: load_wa(True, c).start())
        when(core == 1, lambda: load_wa(False, c).start())
    for name in ("qkv", "p", "y"):
        load(name).start()

    def turn(i):
        for b in range(features // BLOCK):
            grid = (BLOCK, features)
            eye = lax.broadcasted_iota(jnp.int32, grid, 0) + b * BLOCK == lax.broadcasted_iota(jnp.int32, grid, 1)
            left_t[i, pl.ds(b * BLOCK, BLOCK), :] = mm(eye.astype(f32).astype(bf16), left[...], NT).astype(bf16)

    def norm_panel(other):
        chosen = jnp.where(core == other, dnorm[2:4, :], dnorm[0:2, :])
        strips = [
            chosen[r : r + 1, c * PANEL : (c + 1) * PANEL]
            for r in range(2)
            for c in range(features // PANEL)
        ]
        return jnp.concatenate(strips + [jnp.zeros((16 - len(strips), PANEL), f32)], axis=0)

    pl.semaphore_wait(barrier, 5 + has_out.astype(jnp.int32))

    def stage_send(j):
        when(j >= RING, lambda: to_sibling(j - RING).wait_send())

        def use(block):
            sib_send[j % RING] = mm(left_t[left_of(1 - core, j)], block).astype(bf16)

        right(1 - core, j, sib_ring, ring_sem, use)
        to_sibling(j).start()
        fetch(1 - core, j + RING, sib_ring, ring_sem)

    def stage_part(j):
        to_sibling(j).wait_recv()

        def use(block):
            own = mm(left_t[left_of(core, j)], block)
            part[j] = (own + part[j].astype(f32)).astype(bf16)

        right(core, j, own_ring, own_sem, use)
        fetch(core, j + RING, own_ring, own_sem)
        when(j % 2 == 0, lambda: one_y(j).start())
        when((j % 2 == 1) & (dist == depth) & (depth > 0), lambda: two_in(j).start())
        when((j % 2 == 1) & (dist == depth) & (depth == 0), lambda: two_mid(j).start())

    def one_halves(j):
        one_y(j).wait_recv()
        part[j, mine, :] = (part[j, mine, :].astype(f32) + y1[j // 2].astype(f32)).astype(bf16)
        when((dist == depth) & (dist > 0), lambda: one_in(j).start())
        when((dist == depth) & inner, lambda: one_mid(j).start())

    def one_chain(j):
        one_in(j).wait_recv()
        part[j, mine, :] = (part[j, mine, :].astype(f32) + zin1[j // 2].astype(f32)).astype(bf16)
        when(dist > 0, lambda: one_in(j).start())
        when(inner, lambda: one_mid(j).start())

    def one_total(j):
        one_mid(j).wait_recv()
        final[j, mine, :] = (part[j, mine, :].astype(f32) + mid1[j // 2].astype(f32)).astype(bf16)
        when(has_out, lambda: one_out(j).start())
        one_back(j).start()

    def one_spread(j):
        one_out(j).wait_recv()
        when(has_out, lambda: one_out(j).start())
        one_back(j).start()

    def two_chain(j):
        two_in(j).wait_recv()
        part[j] = (part[j].astype(f32) + zin2[j // 2].astype(f32)).astype(bf16)
        when(dist > 0, lambda: two_in(j).start())
        when(inner, lambda: two_mid(j).start())

    def two_halves(j):
        two_mid(j).wait_recv()
        part[j, kept, :] = (part[j, kept, :].astype(f32) + mid2[j // 2].astype(f32)).astype(bf16)
        two_y(j).start()

    def two_total(j):
        two_y(j).wait_recv()
        final[j, kept, :] = (part[j, kept, :].astype(f32) + y2[j // 2].astype(f32)).astype(bf16)
        two_swap(j).start()
        when(has_out, lambda: two_out_kept(j).start())

    def two_swapped(j):
        two_swap_in(j).wait_recv()
        when(has_out, lambda: two_out_rest(j).start())

    def two_spread_kept(j):
        two_out_kept(j).wait_recv()
        when(has_out, lambda: two_out_kept(j).start())

    def two_spread_rest(j):
        two_out_rest(j).wait_recv()
        when(has_out, lambda: two_out_rest(j).start())

    def finish(j):
        when(j % 2 == 0, lambda: one_back_in(j).wait_recv())

        to_out(j).start()

    last_lag = 7 + 4 * depth

    pairs = features // PAIR
    items = tokens // BLOCK * pairs
    begin = 4

    def turn_next(name, following):
        load_left(name).wait()
        turn(raw[name][1])
        if following:
            load_left(following).start()

    def attention_begin():
        load("dmid").wait()
        load("zh0").wait()
        load_wa(True, 3).wait()
        attention_back_begin(do, norms, wa, dctx, rstd0, do, dctx, acc, dnorm)

    def send_rows():
        load("y").wait()

        @pl.when(at_head == 1)
        def _():
            leading = jnp.max(lead_picks(lengths, core, True), axis=1, keepdims=True) > 0
            dx_buf[...] = jnp.where(leading, 0.0, acc[...]).astype(bf16)

        @pl.when(at_head == 0)
        def _():
            dx_buf[...] = acc[...].astype(bf16)

        def go(own, across):
            across_send(across).start()
            when(~inside, lambda: own_send(own).start())

            @pl.when(inside)
            def _():
                halves[core] = own[...]

        when(at_head == 1, go, y_buf, dx_buf)
        when(at_head == 0, go, dx_buf, y_buf)

    def norm_hop(src, dst, i, target):
        return remote(norm.at[src], norm.at[dst], n_ss.at[i], n_rs.at[i], target)

    norm_sib = norm_hop(0, 1, 0, sibling)
    norm_y = norm_hop(2, 3, 1, across_y)
    norm_in_hop = norm_hop(7, 4, 2, inward)
    norm_mid = norm_hop(7, 5, 3, inward)
    norm_far = norm_hop(6, 6, 4, outward)

    def norm_steps(t):
        @pl.when(t == 0)
        def _():
            norm[0] = norm_panel(0)
            norm_sib.start()

        @pl.when(t == 2)
        def _():
            norm_sib.wait_recv()
            norm[2] = norm_panel(1) + norm[1]
            norm_y.start()

        @pl.when(t == 4)
        def _():
            norm_y.wait_recv()
            norm[7] = norm[2] + norm[3]

        @pl.when((t == 4 + 2 * (depth - dist)) & (dist < depth))
        def _():
            norm_in_hop.wait_recv()
            norm[7] = norm[7] + norm[4]

        @pl.when(t == 4 + 2 * (depth - dist))
        def _():
            when(dist > 0, lambda: norm_in_hop.start())
            when(inner, lambda: norm_mid.start())

        @pl.when((t == 6 + 2 * depth) & inner)
        def _():
            norm_mid.wait_recv()
            norm[6] = norm[7] + norm[5]
            when(has_out, lambda: norm_far.start())

        @pl.when((t == 6 + 2 * (depth + dist)) & (dist > 0))
        def _():
            norm_far.wait_recv()
            when(has_out, lambda: norm_far.start())

    dnorm[...] = dnorm_in[...]
    hot_ref[...] = lead_picks(lengths, core, True).astype(bf16)
    turn_next("df", "mid")

    def step(t, carry):
        def at(lag, kind, cond, run):
            j = t - lag
            ok = (j >= 0) & (j < panels)
            if kind is not None:
                ok = ok & (j % 2 == kind)
            if cond is not None:
                ok = ok & cond
            when(ok, run, j)

        at(7 + 2 * (depth + dist), 1, dist > 0, two_spread_rest)
        at(5 + 2 * (depth + dist), 1, dist > 0, two_spread_kept)
        at(5 + 2 * (depth + dist), 0, dist > 0, one_spread)
        at(7 + 2 * depth, 1, inner, two_swapped)
        at(5 + 2 * depth, 1, inner, two_total)
        at(5 + 2 * depth, 0, inner, one_total)
        at(3 + 2 * depth, 1, inner, two_halves)
        at(3 + 2 * (depth - dist), 0, dist < depth, one_chain)
        at(1 + 2 * (depth - dist), 1, dist < depth, two_chain)
        at(3, 0, None, one_halves)
        at(1, None, None, stage_part)
        at(0, None, None, stage_send)
        at(last_lag + 1, None, None, finish)
        when(t == begin, attention_begin)
        item = t - begin - 1
        when(t == begin + 1, lambda: [load("qkv").wait(), load("p").wait()])
        when((item >= 0) & (item < items), lambda: attention_back_item(item // pairs, item % pairs, qkv, p, dctx))
        when(t == 8, turn_next, "mid", "ctx")
        when(t == 9, turn_next, "ctx", "x")
        when(t == 10, turn_next, "x", None)
        for c in range(3):
            when(t == begin + items + 1 + c, lambda: [load_wa(True, c).wait(), attention_back_end(c, wa, qkv, acc)])
        when(t == begin + items + 4, send_rows)
        norm_steps(t - begin - 1)
        return carry

    lax.fori_loop(0, panels + last_lag + 1, step, 0)

    @pl.when(inside)
    def _():
        own_from().wait_recv()

    @pl.when(~inside)
    def _():
        own_send(dx_buf).wait_send()
        across_from(0).wait_recv()
        across_from(1).wait_recv()

    across_send(dx_buf).wait_send()
    norm_sib.wait_send()
    norm_y.wait_send()
    when(dist > 0, lambda: norm_in_hop.wait_send())
    when(inner, lambda: norm_mid.wait_send())
    when(has_out, lambda: norm_far.wait_send())
    norm_out[...] = norm[6]
    rows_done = pltpu.make_async_copy(halves, halves_h, h_sem)
    rows_done.start()

    def drain(j, carry):
        when(j >= panels - RING, lambda: to_sibling(j).wait_send())
        to_out(j).wait()

        @pl.when(j % 2 == 0)
        def _():
            one_y(j).wait_send()
            when(dist > 0, lambda: one_in(j).wait_send())
            when(inner, lambda: one_mid(j).wait_send())
            when(has_out, lambda: one_out(j).wait_send())
            one_back(j).wait_send()

        @pl.when(j % 2 == 1)
        def _():
            when(dist > 0, lambda: two_in(j).wait_send())

            @pl.when(inner)
            def _():
                two_mid(j).wait_send()
                two_y(j).wait_send()
                two_swap(j).wait_send()

            @pl.when(has_out)
            def _():
                two_out_kept(j).wait_send()
                two_out_rest(j).wait_send()

        return carry

    lax.fori_loop(0, panels, drain, 0)
    rows_done.wait()


def reduce_gradients(lengths, first, saved, chain):
    tokens, features = saved["x"].shape
    ff = saved["a"].shape[1]
    width = ff + ff // 2
    panels = width // PANEL
    evens, odds = (panels + 1) // 2, panels // 2
    h = features // 2
    one = pltpu.SemaphoreType.DMA
    arrays = [saved[k] for k in ("x", "ctx", "mid", "a", "df", "du", "dmid", "zh0", "qkv", "p", "y")]
    return pl.pallas_call(
        functools.partial(reduce_kernel, chain),
        out_shape=[S((features, width), bf16), S((16, PANEL), f32), S((2, tokens, features), bf16)],
        in_specs=[IN_SMEM] + [IN_VMEM] * 4 + [ANY] * 13,
        out_specs=[ANY, IN_VMEM, ANY],
        scratch_shapes=[
            vm(tokens, features), vm(4, features, tokens), vm(RING, tokens, PANEL), vm(RING, tokens, PANEL),
            vm(RING, features, PANEL), vm(panels, features, PANEL),
            vm(evens, h, PANEL), vm(evens, h, PANEL), vm(evens, h, PANEL),
            vm(odds, features, PANEL), vm(odds, h, PANEL), vm(odds, h, PANEL),
            vm(panels, features, PANEL), vm(2, tokens, features),
            vm(features, ff), vm(tokens, 3 * features), pltpu.VMEM(saved["p"].shape, bf16), vm(tokens, features),
            vm(tokens, features), pltpu.VMEM((tokens, features), f32), vm(tokens, features),
            pltpu.VMEM((4, features), f32), pltpu.VMEM((8, 16, PANEL), f32), vm(tokens, LEADS),
            one, dma(RING), dma(RING), dma(panels), dma(RING), dma(panels),
            dma(evens), dma(evens), dma(evens), dma(evens), dma(evens), dma(evens),
            dma(odds), dma(odds), dma(odds), dma(odds), dma(odds), dma(odds), dma(3, panels), dma(2, panels),
            one, one, one, dma(2), one, dma(ff // features), dma(5), dma(5), dma(5),
        ],
        compiler_params=params(3),
        name="reduce_gradients",
    )(lengths, saved["dnorm"], saved["norms"], saved["rstd0"], saved["lead_du"], *arrays, first, saved["other_first"])


def finish_kernel(lengths, total, halves, norm_in, first_out, second_out, rows_out, gain_out, shift_out):
    step = pl.program_id(0)
    features = rows_out.shape[1]
    wide = first_out.shape[1]
    first_out[...] = total[:, pl.ds(0, wide)].astype(f32)
    second_out[...] = total[:, pl.ds(wide, second_out.shape[1])].astype(f32)
    size = rows_out.shape[0]
    row = step // (SEQ // size)
    _, _, first = span_scalars(lengths, row)
    at = lax.broadcasted_iota(jnp.int32, (size, BLOCK), 0) + step % (SEQ // size) * size
    out = None
    for side in range(2):
        hot = at == places(first, side, (size, BLOCK), 1)
        part = mm(hot.astype(f32).astype(bf16), halves[side])
        out = part if out is None else out + part
    rows_out[...] = out
    strips = features // PANEL
    for r, ref in enumerate((gain_out, shift_out)):
        ref[...] = jnp.concatenate([norm_in[r * strips + c : r * strips + c + 1, :] for c in range(strips)], axis=1)


def finish(lengths, total, halves, norm_in, ff):
    features, width = total.shape
    tokens = halves.shape[1]
    size = SEQ
    steps = 2 * tokens // size
    part = features // steps
    row_spec = pl.BlockSpec((1, features), lambda i: (0, 0))
    return pl.pallas_call(
        finish_kernel,
        grid=(steps,),
        out_shape=[
            S((features, ff), f32), S((features, width - ff), f32), S((2 * tokens, features), f32),
            S((1, features), f32), S((1, features), f32),
        ],
        in_specs=[
            IN_SMEM, pl.BlockSpec((part, width), lambda i: (i, 0)),
            pl.BlockSpec((2, BLOCK, features), lambda i: (0, i // (SEQ // size), 0)), IN_VMEM,
        ],
        out_specs=[
            pl.BlockSpec((part, ff), lambda i: (i, 0)), pl.BlockSpec((part, width - ff), lambda i: (i, 0)),
            pl.BlockSpec((size, features), lambda i: (i, 0)), row_spec, row_spec,
        ],
        compiler_params=params(None),
        name="finish",
    )(lengths, total, halves, norm_in)


def per_device(section_rows, span_lengths, first_weights, second_weights, norm_gain, norm_shift):
    first, second = first_weights[0], second_weights[0]
    saved = front(section_rows[0], span_lengths, first, second, norm_gain, norm_shift)
    total, norm_total, halves = reduce_gradients(span_lengths, first, saved, lax.axis_size("dp") // 2)
    d_first, d_second, rows, gain, shift = finish(span_lengths, total, halves, norm_total, first.shape[1])
    return rows[None], d_first[None], d_second[None], gain, shift


def solution(mesh):
    in_specs = (
        P("section", "dp", None),
        P("dp", None),
        P("section", None, None),
        P("section", None, None),
        P("section", None),
        P("section", None),
    )
    out_specs = (
        P("section", "dp", None),
        P("section", None, None),
        P("section", None, None),
        P("section", None),
        P("section", None),
    )
    return jax.shard_map(
        per_device, mesh=mesh, in_specs=in_specs, out_specs=out_specs, check_vma=False
    )
```

```python
import functools

import jax
import jax.numpy as jnp
from jax import lax
from jax.experimental import pallas as pl
from jax.experimental.pallas import tpu as pltpu
from jax.sharding import PartitionSpec as P

HEAD_DIM = 64
PAIR = 2 * HEAD_DIM
BLOCK = 256
SEQ = 512
LEADS = 16
VMEM_LIMIT = 60 << 20
MESH = pl.DeviceIdType.MESH
f32 = jnp.float32
bf16 = jnp.bfloat16
epsilon = 1e-12
NN = (((1,), (0,)), ((), ()))
NT = (((1,), (1,)), ((), ()))
TN = (((0,), (0,)), ((), ()))
LOG2E = 1.4426950408889634


def mm(a, b, dims=NN):
    return lax.dot_general(a, b, dims, preferred_element_type=f32)


def when(cond, step, *args):
    @pl.when(cond)
    def _():
        step(*args)


def remote(src, dst, ss, rs, target):
    return pltpu.make_async_remote_copy(
        src_ref=src, dst_ref=dst, send_sem=ss, recv_sem=rs, device_id=target, device_id_type=MESH
    )


def gelu_and_slope(u):
    bell = jnp.exp2(u * u * (-0.5 * LOG2E))
    t = 1.0 / (1.0 + (0.3275911 * 0.5**0.5) * jnp.abs(u))
    poly = t * (0.127414796 + t * (-0.142248368 + t * (0.7107068705 + t * (-0.7265760135 + t * 0.5307027145))))
    tail = poly * bell
    cdf = jnp.where(u < 0, tail, 1.0 - tail)
    return u * cdf, cdf + u * bell * 0.3989422804014327


def normalize(z):
    centered = z - jnp.mean(z, axis=-1, keepdims=True)
    rstd = lax.rsqrt(jnp.mean(centered * centered, axis=-1, keepdims=True) + epsilon)
    return centered * rstd, rstd


def normalize_back(zh, rstd, gain, dy):
    g = dy * gain
    mean_g = jnp.mean(g, axis=-1, keepdims=True)
    mean_gz = jnp.mean(g * zh, axis=-1, keepdims=True)
    dz = rstd * (g - mean_g - zh * mean_gz)
    return dz, jnp.sum(dy * zh, axis=0, keepdims=True), jnp.sum(dy, axis=0, keepdims=True)


def span_scalars(lengths, row):
    ends, starts, first, total = [], [], 0, 0
    for j in range(lengths.shape[1]):
        size = lengths[row, j]
        starts.append(total)
        first = first + jnp.where(size == BLOCK, total, 0)
        total = total + size
        ends.append(total)
    return ends, starts, first


def places(first, core, shape, axis):
    at = lax.broadcasted_iota(jnp.int32, shape, axis) + (first + core * BLOCK)
    return jnp.where(at >= SEQ, at - SEQ, at)


def mask_bias(lengths, row, core):
    ends, _, first = span_scalars(lengths, row)

    def segment(at):
        return sum((at >= end).astype(jnp.int32) for end in ends)

    rows = segment(places(first, core, (BLOCK, BLOCK), 0))
    cols = segment(places(first, core, (BLOCK, BLOCK), 1))
    return jnp.where(rows == cols, 0.0, -1e30)


def lead_picks(lengths, core, by_rows):
    parts = []
    per_row = lengths.shape[1] - 1
    shape = (BLOCK, LEADS) if by_rows else (LEADS, BLOCK)
    for row in range(lengths.shape[0]):
        _, starts, first = span_scalars(lengths, row)
        at = places(first, core, shape, 0 if by_rows else 1)
        slot = lax.broadcasted_iota(jnp.int32, shape, 1 if by_rows else 0)
        hit = sum(
            ((slot == row * per_row + j) & (at == starts[j])).astype(jnp.int32) for j in range(per_row)
        )
        parts.append(hit.astype(f32))
    return jnp.concatenate(parts, axis=0 if by_rows else 1)


def lane_masks():
    return lax.broadcasted_iota(jnp.int32, (BLOCK, PAIR), 1) < HEAD_DIM


def forward_pass(x, lengths, core, norms, wa, wu, wd, qkv, ctx, mid, acc, ready, arrive, save):
    tokens, features = x.shape
    pairs = features // PAIR
    first = lane_masks()
    zero = jnp.zeros((BLOCK, PAIR), bf16)

    def block_step(b, carry):
        rows = pl.ds(pl.multiple_of(b * BLOCK, BLOCK), BLOCK)
        arrive(b)
        for c in range(3):
            cols = pl.ds(c * features, features)
            qkv[rows, cols] = mm(x[rows, :], wa[:, cols]).astype(bf16)
        bias = mask_bias(lengths, b, core)
        for h in range(pairs):
            q = qkv[rows, pl.ds(h * PAIR, PAIR)]
            k = qkv[rows, pl.ds(features + h * PAIR, PAIR)]
            v = qkv[rows, pl.ds(2 * features + h * PAIR, PAIR)]
            total = None
            for side in range(2):
                own = first if side == 0 else ~first
                s = mm(q, jnp.where(own, k, zero), NT) * (HEAD_DIM**-0.5) + bias
                e = jnp.exp(s - jnp.max(s, axis=-1, keepdims=True))
                pr = (e * (1.0 / jnp.sum(e, axis=-1, keepdims=True))).astype(bf16)
                save["p"][b, h, :, pl.ds(side * BLOCK, BLOCK)] = pr
                part = mm(pr, jnp.where(own, v, zero))
                total = part if total is None else total + part
            ctx[rows, pl.ds(h * PAIR, PAIR)] = total.astype(bf16)
        return carry

    lax.fori_loop(0, tokens // BLOCK, block_step, 0)
    ready["a"](3)
    zn, r = normalize(x[...].astype(f32) + mm(ctx[...], wa[:, pl.ds(3 * features, features)]))
    save["keep"]("x", "qkv", "p", "ctx")
    save["rstd0"][...] = r
    save["zh0"][...] = zn.astype(bf16)
    mid[...] = (zn * norms[0, 0:1, :] + norms[0, 1:2, :]).astype(bf16)
    acc[...] = mid[...].astype(f32)
    save["keep"]("zh0", "mid")
    pieces = wu.shape[1] // features
    cols = [pl.ds(c * features, features) for c in range(pieces)]
    ready["u"](0)
    ahead = mm(mid[...], wu[:, cols[0]])
    for c in range(pieces):
        u = ahead
        if c + 1 < pieces:
            ready["u"](c + 1)
            ahead = mm(mid[...], wu[:, cols[c + 1]])
        act, slope = gelu_and_slope(u)
        act = act.astype(bf16)
        save["a"][:, cols[c]] = act
        save["slope"][:, cols[c]] = slope.astype(bf16)
        save["keep_cols"](c)
        ready["d"](c)
        acc[...] += mm(act, wd[:, cols[c]], NT)
    zn, r = normalize(acc[...])
    save["rstd1"][...] = r
    save["zh1"][...] = zn.astype(bf16)
    return (zn * norms[1, 0:1, :] + norms[1, 1:2, :]).astype(bf16)


def feed_forward_back(dy, norms, wu, wd, slope, zh1, rstd1, df, du, acc, dnorm):
    features = wu.shape[0]
    dz, dgain, dshift = normalize_back(zh1[...].astype(f32), rstd1[...], norms[1, 0:1, :], dy.astype(f32))
    dnorm[2:3, :] = dgain
    dnorm[3:4, :] = dshift
    df[...] = dz.astype(bf16)
    acc[...] = dz
    pieces = wu.shape[1] // features
    cols = [pl.ds(c * features, features) for c in range(pieces)]
    ahead = mm(df[...], wd[:, cols[0]])
    for c in range(pieces):
        da = ahead
        if c + 1 < pieces:
            ahead = mm(df[...], wd[:, cols[c + 1]])
        g = (da * slope[:, cols[c]].astype(f32)).astype(bf16)
        du[:, cols[c]] = g
        acc[...] += mm(g, wu[:, cols[c]], NT)


def attention_back_begin(d_mid, norms, wa, zh0, rstd0, do, dctx, acc, dnorm):
    tokens, features = acc.shape
    dgain = dshift = None
    for b in range(tokens // BLOCK):
        rows = pl.ds(b * BLOCK, BLOCK)
        dz, dg, ds = normalize_back(
            zh0[rows, :].astype(f32), rstd0[rows, :], norms[0, 0:1, :], d_mid[rows, :].astype(f32)
        )
        dgain, dshift = (dg, ds) if b == 0 else (dgain + dg, dshift + ds)
        acc[rows, :] = dz
        do[rows, :] = dz.astype(bf16)
        dctx[rows, :] = mm(dz.astype(bf16), wa[:, pl.ds(3 * features, features)], NT).astype(bf16)
    dnorm[0:1, :] = dgain
    dnorm[1:2, :] = dshift


def attention_back_item(b, h, qkv, p, dctx):
    features = dctx.shape[1]
    first = lane_masks()
    zero = jnp.zeros((BLOCK, PAIR), bf16)
    scale = HEAD_DIM**-0.5
    rows = pl.ds(pl.multiple_of(b * BLOCK, BLOCK), BLOCK)
    at = [pl.ds(pl.multiple_of(part * features + h * PAIR, PAIR), PAIR) for part in range(3)]
    q, k, v = (qkv[rows, cols] for cols in at)
    dc = dctx[rows, at[0]]
    dq = dk = dv = None
    for side in range(2):
        own = first if side == 0 else ~first
        pr = p[b, h, :, pl.ds(side * BLOCK, BLOCK)]
        prf = pr.astype(f32)
        dp = mm(dc, jnp.where(own, v, zero), NT)
        r = jnp.sum(dp * prf, axis=-1, keepdims=True)
        ds = (prf * (dp - r)).astype(bf16)
        parts = (
            mm(ds, jnp.where(own, k, zero)),
            mm(ds, jnp.where(own, q, zero), TN),
            mm(pr, jnp.where(own, dc, zero), TN),
        )
        if dq is None:
            dq, dk, dv = parts
        else:
            dq, dk, dv = dq + parts[0], dk + parts[1], dv + parts[2]
    qkv[rows, at[0]] = (dq * scale).astype(bf16)
    qkv[rows, at[1]] = (dk * scale).astype(bf16)
    qkv[rows, at[2]] = dv.astype(bf16)


def attention_back_end(part, wa, dqkv, acc):
    features = wa.shape[0]
    cols = pl.ds(part * features, features)
    for b in range(acc.shape[0] // BLOCK):
        rows = pl.ds(b * BLOCK, BLOCK)
        acc[rows, :] += mm(dqkv[rows, cols], wa[:, cols], NT)


def head_lanes(features):
    lane = lax.broadcasted_iota(jnp.int32, (LEADS, features), 1)
    return [(lane >= h * HEAD_DIM) & (lane < (h + 1) * HEAD_DIM) for h in range(features // HEAD_DIM)]


def spread_heads(rows):
    wide = rows.astype(f32)
    return jnp.concatenate([jnp.where(own, wide, 0.0) for own in head_lanes(rows.shape[1])], axis=0).astype(bf16)


def fold_heads(wide):
    total = None
    for h, own in enumerate(head_lanes(wide.shape[1])):
        part = jnp.where(own, wide[h * LEADS : (h + 1) * LEADS, :], 0.0)
        total = part if total is None else total + part
    return total


def lead_probs(queries, keys, lengths, core):
    tokens, features = keys.shape
    per_row = lengths.shape[1] - 1
    parts = []
    for row in range(tokens // BLOCK):
        ends, _, first = span_scalars(lengths, row)
        at = places(first, core, (LEADS, BLOCK), 1)
        segment = sum((at >= end).astype(jnp.int32) for end in ends)
        span = lax.broadcasted_iota(jnp.int32, (LEADS, BLOCK), 0) - row * per_row
        parts.append(jnp.where((span == segment) & (span < per_row), 0.0, -1e30))
    bias = jnp.concatenate([jnp.concatenate(parts, axis=1)] * (features // HEAD_DIM), axis=0)
    s = mm(spread_heads(queries), keys, NT) * (HEAD_DIM**-0.5) + bias
    e = jnp.exp(s - jnp.max(s, axis=-1, keepdims=True))
    return (e * (1.0 / jnp.sum(e, axis=-1, keepdims=True))).astype(bf16)


def lead_forward(x, lengths, core, norms, wa, wu, wd, qkv, ready):
    features = x.shape[1]
    pieces = wu.shape[1] // features
    cols = [pl.ds(c * features, features) for c in range(4)]
    own = mm(lead_picks(lengths, core, False).astype(bf16), x[...]).astype(bf16)
    for c in (1, 2):
        ready["a"](c)
        qkv[:, cols[c]] = mm(x[...], wa[:, cols[c]]).astype(bf16)
    ready["a"](0)
    probs = lead_probs(mm(own, wa[:, cols[0]]).astype(bf16), qkv[:, cols[1]], lengths, core)
    ctx = fold_heads(mm(probs, qkv[:, cols[2]])).astype(bf16)
    ready["a"](3)
    zn, _ = normalize(own.astype(f32) + mm(ctx, wa[:, cols[3]]))
    mid = (zn * norms[0, 0:1, :] + norms[0, 1:2, :]).astype(bf16)
    out = mid.astype(f32)
    for step in range(pieces):
        c = (step + core * (pieces // 2)) % pieces
        at = pl.ds(pl.multiple_of(c * features, features), features)
        ready["u"](c)
        act, _ = gelu_and_slope(mm(mid, wu[:, at]))
        if step % (pieces // 2) == 0:
            ready["half"](step)
        out = out + mm(act.astype(bf16), wd[:, at], NT)
    zn, _ = normalize(out)
    return (zn * norms[1, 0:1, :] + norms[1, 1:2, :]).astype(bf16)


def lead_back(pick, lengths, core, wa, qkv, p, ctx, dctx, dz):
    tokens, features = ctx.shape
    scale = HEAD_DIM**-0.5
    heads = features // HEAD_DIM
    cols = [pl.ds(c * features, features) for c in range(3)]
    q16, v16 = (mm(pick, qkv[:, cols[c]]).astype(bf16) for c in (0, 2))
    low = lead_probs(q16, qkv[:, cols[1]], lengths, core)
    probs = low.astype(f32)
    dp = mm(spread_heads(mm(pick, dctx[...]).astype(bf16)), qkv[:, cols[2]], NT)
    ds = (probs * (dp - jnp.sum(dp * probs, axis=-1, keepdims=True))).astype(bf16)
    dq = (fold_heads(mm(ds, qkv[:, cols[1]])) * scale).astype(bf16)
    seen = []
    for h in range(heads):
        keys = pl.ds(h % 2 * BLOCK, BLOCK)
        seen.append(
            jnp.concatenate(
                [mm(pick[:, b * BLOCK : (b + 1) * BLOCK], p[b, h // 2, :, keys], NT) for b in range(tokens // BLOCK)],
                axis=1,
            )
        )
    seen = jnp.concatenate(seen, axis=0)
    product = dctx[...].astype(f32) * ctx[...].astype(f32)
    high = product.astype(bf16)
    low = (product - high.astype(f32)).astype(bf16)
    lane = lax.broadcasted_iota(jnp.int32, (LEADS, features), 1)
    head = lax.broadcasted_iota(jnp.int32, (LEADS, features), 0) * HEAD_DIM
    select = ((lane >= head) & (lane < head + HEAD_DIM)).astype(f32).astype(bf16)
    sums = mm(select, high, NT) + mm(select, low, NT)
    sums = jnp.concatenate([jnp.broadcast_to(sums[h : h + 1, :], (LEADS, tokens)) for h in range(heads)], axis=0)
    ds = (seen * (mm(spread_heads(v16), dctx[...], NT) - sums)).astype(bf16)
    dk = (fold_heads(mm(ds, qkv[:, cols[0]])) * scale).astype(bf16)
    dv = fold_heads(mm(seen.astype(bf16), dctx[...])).astype(bf16)
    high = dz[...].astype(bf16)
    low = (dz[...] - high.astype(f32)).astype(bf16)
    out = mm(pick, high) + mm(pick, low)
    for c, part in enumerate((dq, dk, dv)):
        out = out + mm(part, wa[:, cols[c]], NT)
    return out


def front_kernel(
    rows_h, lengths, first_h, second_h, gain_in, shift_in,
    x_h, y_h, qkv_h, p_h, ctx_h, zh0_h, mid_h, a_h, df_h, du_h, dmid_h, other_first_h, rstd0, dnorm, norms, lead_du,
    wa, wu, wd, x, qkv, p, ctx, zh0, mid, a, slope, up, zh1, rstd1, do, dctx, acc, d_att,
    lead_slope, lead_zh, lead_rstd, hot_ref, grad_own, grad_in, row_own, row_in, norm_pair,
    row_sem, load, w_ss, w_rs, d_ss, d_rs, n_ss, n_rs, m_ss, m_rs, x_ss, x_rs, r_ss, r_rs, l_ss, l_rs, out_sem, col_sem, du_sem, other_sem,
):
    sec = lax.axis_index("section")
    core = sec % 2
    at_head = sec // 2
    tokens, features = x.shape
    blocks = tokens // BLOCK
    pieces = wu.shape[1] // features
    half = wd.shape[1] // 2
    even, odd = core == 0, core == 1
    head, backbone = at_head == 1, at_head == 0
    sibling = {"section": sec + 1 - 2 * core}
    peer = {"section": (sec + 2) % 4}
    halves = (do, dctx)
    y, df, dmid = mid, mid, x
    barrier = pltpu.get_barrier_semaphore()
    for step in range(1, 4):
        target = {"section": (sec + step) % 4}
        pl.semaphore_signal(barrier, inc=1, device_id=target, device_id_type=MESH)

    def cols(c):
        return pl.ds(c * features, features)

    def block(b):
        return pl.ds(b * BLOCK if isinstance(b, int) else pl.multiple_of(b * BLOCK, BLOCK), BLOCK)

    def piece(c):
        return pl.ds(c * features if isinstance(c, int) else pl.multiple_of(c * features, features), features)

    def local_first(c, dst):
        return pltpu.make_async_copy(first_h.at[:, piece(c)], dst.at[:, piece(c)], load.at[c])

    def sent_first(c, dst):
        return remote(first_h.at[:, piece(c)], dst.at[:, piece(c)], w_ss.at[c], w_rs.at[c], sibling)

    def local_second(side):
        return pltpu.make_async_copy(second_h, wd.at[:, pl.ds(side * half, half)], load.at[pieces])

    def sent_second(side):
        return remote(second_h, wd.at[:, pl.ds(side * half, half)], d_ss, d_rs, sibling)

    def row_load(row):
        return pltpu.make_async_copy(
            rows_h.at[pl.ds(row * SEQ, SEQ)], slope.at[pl.ds(0, SEQ), cols(row)], row_sem.at[row]
        )

    for row in range(blocks):
        row_load(row).start()
    turns = (1, 2, 0, *range(3, pieces))
    for c in range(pieces):
        when(even, lambda: local_first(turns[c], wa).start())
        when(odd, lambda: local_first(c, wu).start())
    when(even, lambda: local_second(0).start())
    when(odd, lambda: local_second(1).start())

    def inner_send(dst):
        return remote(halves[1] if dst is x else halves[0], dst, m_ss, m_rs, sibling)

    def cross_send(dst, side, b):
        target = {"section": 2 + side} if dst is x else {"section": side}
        return remote(halves[side].at[block(b)], dst.at[block(b)], x_ss.at[side, b], x_rs.at[b], target)

    def send_weights():
        for c in range(pieces):
            when(even, lambda: sent_first(turns[c], wa).start())
            when(odd, lambda: sent_first(c, wu).start())
        when(even, lambda: sent_second(0).start())
        when(odd, lambda: sent_second(1).start())

    for row in range(blocks):
        _, _, first = span_scalars(lengths, row)
        row_load(row).wait()
        packed = slope[0:SEQ, cols(row)]
        for side in range(2):
            at = places(first, side, (BLOCK, SEQ), 0)
            hot = at == lax.broadcasted_iota(jnp.int32, (BLOCK, SEQ), 1)
            halves[side][block(row), :] = mm(hot.astype(f32).astype(bf16), packed).astype(bf16)
        if row == 0:
            pl.semaphore_wait(barrier, 3)
        if row < blocks - 1:
            when(sec == 1, lambda: [cross_send(x, side, row).start() for side in range(2)])
        when(sec == 2, lambda: [cross_send(up, side, row).start() for side in range(2)])
        if row == 0:
            when(odd, send_weights)
    when(sec == 0, lambda: inner_send(x).start())
    norm_pair[core, 0:1, :] = gain_in[...]
    norm_pair[core, 1:2, :] = shift_in[...]
    sent_norm = remote(norm_pair.at[core], norm_pair.at[core], n_ss, n_rs, sibling)
    norm_from = remote(norm_pair.at[1 - core], norm_pair.at[1 - core], n_ss, n_rs, sibling)
    sent_norm.start()
    when(even, send_weights)
    when(sec == 3, lambda: inner_send(up).start())
    pairs_of = [(side, b) for b in range(blocks) for side in range(2)]

    @pl.when(sec == 0)
    def _():
        x[...] = halves[0][...]

    @pl.when(sec == 3)
    def _():
        up[...] = halves[1][...]

    norm_from.wait_recv()
    norms[...] = norm_pair[...]

    def ready_a(c):
        when(even, lambda: local_first(c, wa).wait())
        when(odd, lambda: sent_first(c, wa).wait_recv())

    def ready_u(c):
        when(odd, lambda: local_first(c, wu).wait())
        when(even, lambda: sent_first(c, wu).wait_recv())

    def ready_d(c):
        if c == 0:
            when(even, lambda: local_second(0).wait())
            when(odd, lambda: sent_second(0).wait_recv())
        if c == pieces // 2:
            when(odd, lambda: local_second(1).wait())
            when(even, lambda: sent_second(1).wait_recv())

    def ready_half(step):
        if step == 0:
            when(even, lambda: local_second(0).wait())
            when(odd, lambda: local_second(1).wait())
        else:
            when(even, lambda: sent_second(1).wait_recv())
            when(odd, lambda: sent_second(0).wait_recv())

    refs = dict(
        x=(x, x_h), y=(y, y_h), qkv=(qkv, qkv_h), p=(p, p_h), ctx=(ctx, ctx_h), zh0=(zh0, zh0_h), mid=(mid, mid_h),
        df=(df, df_h), dmid=(dmid, dmid_h),
    )
    order = list(refs)

    def store(name):
        return pltpu.make_async_copy(*refs[name], out_sem.at[order.index(name)])

    def store_cols(c):
        return pltpu.make_async_copy(a.at[:, cols(c)], a_h.at[:, cols(c)], col_sem.at[c])

    def store_du(c):
        return pltpu.make_async_copy(slope.at[:, cols(c)], du_h.at[:, cols(c)], du_sem.at[c])

    def keep(*names):
        for name in names:
            store(name).start()

    picks = lead_picks(lengths, core, True)
    leading = jnp.max(picks, axis=1, keepdims=True) > 0
    hot_leads = picks.astype(bf16)
    pick = lead_picks(lengths, core, False).astype(bf16)
    row_hop = remote(row_own, row_in, r_ss, r_rs, peer)

    @pl.when(backbone)
    def _():
        when(odd, lambda: inner_send(x).wait_recv())
        ready = dict(a=ready_a, u=ready_u, half=ready_half)
        row_own[...] = lead_forward(x, lengths, core, norms, wa, wu, wd, qkv, ready)
        row_hop.start()
        when(sec == 1, lambda: [cross_send(x, side, blocks - 1).start() for side in range(2)])

    @pl.when(head)
    def _():
        for c in range(3):
            ready_a(c)
        row_hop.wait_recv()

    hot_ref[...] = hot_leads

    def patched(b):
        cross_send(x, 0, b).wait_recv()
        hot = hot_ref[block(b), :]
        is_lead = jnp.max(hot.astype(f32), axis=1, keepdims=True) > 0
        x[block(b), :] = jnp.where(is_lead, mm(hot, row_in[...]).astype(bf16), x[block(b), :])

    def arrive(b):
        when(head, patched, b)

    at_first = {k: f for k, f in (("a", ready_a), ("u", ready_u), ("d", ready_d))}
    ready = {k: (lambda c, f=f: when(head, f, c)) for k, f in at_first.items()}
    save = dict(
        p=p, a=a, slope=slope, zh0=zh0, zh1=zh1, rstd0=rstd0, rstd1=rstd1, keep=keep,
        keep_cols=lambda c: store_cols(c).start(),
    )
    out = forward_pass(x, lengths, core, norms, wa, wu, wd, qkv, ctx, mid, acc, ready, arrive, save)
    for name in ("mid", "x"):
        store(name).wait()
    y[...] = out
    keep("y")
    other = pltpu.make_async_copy(wa, other_first_h, other_sem)
    when(odd, lambda: other.start())

    @pl.when(backbone)
    def _():
        lead_zh[...] = mm(pick, zh1[...])
        left = jnp.broadcast_to(rstd1[...], (tokens, PAIR))
        total = jnp.zeros((LEADS, PAIR), f32)
        for _ in range(3):
            high = left.astype(bf16)
            left = left - high.astype(f32)
            total = total + mm(pick, high)
        lead_rstd[...] = total[:, 0:1]
        for b in range(blocks):
            cross_send(up, 0, b).wait_recv()
        row_hop.wait_send()
        for c in range(pieces):
            lead_slope[:, cols(c)] = mm(pick, slope[:, cols(c)]).astype(bf16)

    when(sec == 2, lambda: inner_send(up).wait_recv())
    when(sec == 0, lambda: inner_send(x).wait_send())
    when(sec == 3, lambda: inner_send(up).wait_send())
    when((sec == 1) | (sec == 2), lambda: [cross_send(x, *at).wait_send() for at in pairs_of])
    sent_norm.wait_send()
    for c in range(pieces):
        sent_first(c, wa).wait_send()
    sent_second(0).wait_send()
    store("y").wait()
    feed_forward_back(up[...], norms, wu, wd, slope, zh1, rstd1, df, slope, acc, dnorm)
    for c in range(pieces):
        store_du(c).start()
    dmid[...] = acc[...].astype(bf16)
    dnorm[0:2, :] = jnp.zeros((2, features), f32)
    grad_hop = remote(grad_own, grad_in, l_ss, l_rs, peer)

    @pl.when(head)
    def _():
        keep("df", "dmid")
        lead_du[...] = jnp.zeros_like(lead_du)
        attention_back_begin(dmid, norms, wa, zh0, rstd0, do, dctx, acc, d_att)
        grad_own[...] = lead_back(pick, lengths, core, wa, qkv, p, ctx, dctx, acc)
        grad_hop.start()
        grad_hop.wait_send()

    @pl.when(backbone)
    def _():
        base = mm(pick, up[...])
        grad_hop.wait_recv()
        dy = (base + grad_in[...]).astype(bf16).astype(f32)
        extra = dy - base
        dnorm[2:3, :] += jnp.sum(extra * lead_zh[...], axis=0, keepdims=True)
        dnorm[3:4, :] += jnp.sum(extra, axis=0, keepdims=True)
        dz, _, _ = normalize_back(lead_zh[...], lead_rstd[...], norms[1, 0:1, :], dy)
        lead_df = dz.astype(bf16)
        df[...] = jnp.where(leading, mm(hot_leads, lead_df).astype(bf16), df[...])
        keep("df")
        g = (mm(lead_df, wd[...]) * lead_slope[...].astype(f32)).astype(bf16)
        lead_du[...] = g
        dz = dz + mm(g, wu[...], NT)
        dmid[...] = jnp.where(leading, mm(hot_leads, dz.astype(bf16)).astype(bf16), dmid[...])
        keep("dmid")

    for name in order:
        if name not in ("mid", "x", "y"):
            store(name).wait()
    for c in range(pieces):
        store_cols(c).wait()
        store_du(c).wait()
    when(odd, lambda: other.wait())


ANY = pl.BlockSpec(memory_space=pl.ANY)
IN_VMEM = pl.BlockSpec(memory_space=pltpu.VMEM)
IN_SMEM = pl.BlockSpec(memory_space=pltpu.SMEM)
S = jax.ShapeDtypeStruct


def vm(*shape):
    return pltpu.VMEM(shape, bf16)


def dma(*shape):
    return pltpu.SemaphoreType.DMA(shape)


def params(number):
    if number is None:
        return pltpu.CompilerParams(vmem_limit_bytes=VMEM_LIMIT)
    return pltpu.CompilerParams(vmem_limit_bytes=VMEM_LIMIT, collective_id=number, has_side_effects=True)


def front(rows_in, lengths, first, second, gain, shift):
    features, ff = first.shape
    tokens = rows_in.shape[0] // 2
    pieces = ff // features
    blocks, pairs = tokens // BLOCK, features // PAIR
    square = S((tokens, features), bf16)
    one = pltpu.SemaphoreType.DMA
    shapes = dict(
        x=square, y=square, qkv=S((tokens, 3 * features), bf16), p=S((blocks, pairs, BLOCK, 2 * BLOCK), bf16),
        ctx=square, zh0=square, mid=square, a=S((tokens, ff), bf16), df=square, du=S((tokens, ff), bf16), dmid=square,
        other_first=S(first.shape, bf16), rstd0=S((tokens, 1), f32), dnorm=S((4, features), f32),
        norms=S((2, 2, features), f32), lead_du=S((LEADS, ff), bf16),
    )
    small = ("rstd0", "dnorm", "norms", "lead_du")
    wide = vm(features, ff)
    outs = pl.pallas_call(
        front_kernel,
        out_shape=list(shapes.values()),
        in_specs=[ANY, IN_SMEM, ANY, ANY, IN_VMEM, IN_VMEM],
        out_specs=[IN_VMEM if k in small else ANY for k in shapes],
        scratch_shapes=[wide, wide, wide]
        + [pltpu.VMEM(shapes[k].shape, bf16) for k in ("x", "qkv", "p", "ctx", "zh0", "mid", "a", "du")]
        + [
            vm(tokens, features), vm(tokens, features), pltpu.VMEM((tokens, 1), f32), vm(tokens, features),
            vm(tokens, features), pltpu.VMEM((tokens, features), f32), pltpu.VMEM((2, features), f32), vm(LEADS, ff), pltpu.VMEM((LEADS, features), f32),
            pltpu.VMEM((LEADS, 1), f32), vm(tokens, LEADS),
            pltpu.VMEM((LEADS, features), f32), pltpu.VMEM((LEADS, features), f32), vm(LEADS, features), vm(LEADS, features),
            pltpu.VMEM((2, 2, features), f32),
            dma(blocks), dma(pieces + 1), dma(pieces), dma(pieces), one, one, one, one, one, one, dma(2, blocks), dma(blocks),
            one, one, one, one, dma(9), dma(pieces), dma(pieces), one,
        ],
        compiler_params=params(1),
        name="front",
    )(rows_in, lengths, first, second, gain, shift)
    return dict(zip(shapes, outs))


PANEL = 128
RING = 4


def reduce_kernel(
    chain, lengths, dnorm_in, norms, rstd0, lead_du, x_h, ctx_h, mid_h, a_h, df_h, du_h, dmid_h, zh0_h, qkv_h, p_h, y_h,
    first_h, other_first_h,
    out_h, norm_out, halves_h,
    left, left_t, own_ring, sib_ring, sib_send, part, y1, zin1, mid1, zin2, mid2, y2, final, halves,
    wa, qkv, p, do, dctx, acc, y_buf, dnorm, norm, hot_ref,
    left_sem, own_sem, ring_sem, out_sem, sib_ss, sib_rs, y1_ss, y1_rs, z1_ss, z1_rs, m1_ss, m1_rs,
    z2_ss, z2_rs, m2_ss, m2_rs, y2_ss, y2_rs, f_ss, f_rs, o_ss, o_rs, c_ss, c_rs, h_sem, a_sem, in_sem, n_ss, n_rs,
):
    sec = lax.axis_index("section")
    dp = lax.axis_index("dp")
    core = sec % 2
    panels, rows, _ = final.shape
    tokens = acc.shape[0]
    half = rows // 2
    features = rows
    last = panels
    spot = dp // 2
    side = spot // (chain // 2)
    depth = chain // 2 - 1
    dist = side * (spot - chain // 2) + (1 - side) * (chain // 2 - 1 - spot)
    inner = dist == 0
    y = dp % 2
    sibling = {"section": sec + 1 - 2 * core}
    across_y = {"dp": dp + 1 - 2 * y}
    inward = {"dp": dp + 2 - 4 * side}
    outward = {"dp": dp - 2 + 4 * side}
    has_out = dist < depth

    barrier = pltpu.get_barrier_semaphore()
    at_head = sec // 2
    dx_buf = dctx
    inside = (sec == 0) | (sec == 3)
    beyond = {"section": 2 - sec // 2}
    others = [{"section": (sec + step) % 4} for step in (1, 2, 3)]
    for target in (*others, across_y, inward):
        pl.semaphore_signal(barrier, inc=1, device_id=target, device_id_type=MESH)

    @pl.when(has_out)
    def _():
        pl.semaphore_signal(barrier, inc=1, device_id=outward, device_id_type=MESH)

    def rows_at(which):
        return pl.ds(pl.multiple_of(which * half, half), half)

    mine, theirs = rows_at(y), rows_at(1 - y)
    kept, rest = rows_at(side), rows_at(1 - side)

    def to_sibling(j):
        return remote(sib_send.at[j % RING], part.at[j], sib_ss.at[j % RING], sib_rs.at[j], sibling)

    def one_y(j):
        i = j // 2
        return remote(part.at[j, theirs], y1.at[i], y1_ss.at[i], y1_rs.at[i], across_y)

    def one_in(j):
        i = j // 2
        return remote(part.at[j, mine], zin1.at[i], z1_ss.at[i], z1_rs.at[i], inward)

    def one_mid(j):
        i = j // 2
        return remote(part.at[j, mine], mid1.at[i], m1_ss.at[i], m1_rs.at[i], inward)

    def one_out(j):
        return remote(final.at[j, mine], final.at[j, mine], f_ss.at[0, j], f_rs.at[0, j], outward)

    def one_back(j):
        return remote(final.at[j, mine], final.at[j, mine], f_ss.at[1, j], f_rs.at[1, j], across_y)

    def one_back_in(j):
        return remote(final.at[j, theirs], final.at[j, theirs], f_ss.at[1, j], f_rs.at[1, j], across_y)

    def two_in(j):
        i = j // 2
        return remote(part.at[j], zin2.at[i], z2_ss.at[i], z2_rs.at[i], inward)

    def two_mid(j):
        i = j // 2
        return remote(part.at[j, rest], mid2.at[i], m2_ss.at[i], m2_rs.at[i], inward)

    def two_y(j):
        i = j // 2
        return remote(part.at[j, kept], y2.at[i], y2_ss.at[i], y2_rs.at[i], across_y)

    def two_swap(j):
        return remote(final.at[j, kept], final.at[j, kept], f_ss.at[2, j], f_rs.at[1, j], inward)

    def two_swap_in(j):
        return remote(final.at[j, rest], final.at[j, rest], f_ss.at[2, j], f_rs.at[1, j], inward)

    def two_out_kept(j):
        return remote(final.at[j, kept], final.at[j, kept], f_ss.at[0, j], f_rs.at[0, j], outward)

    def two_out_rest(j):
        return remote(final.at[j, rest], final.at[j, rest], f_ss.at[1, j], f_rs.at[1, j], outward)

    down = a_h.shape[1] // (2 * PANEL)
    outer_cols = features // PANEL
    raw = dict(x=(x_h, 0), ctx=(ctx_h, 1), df=(df_h, 2), mid=(mid_h, 3))

    def left_of(who, j):
        late = jnp.minimum(j // down, 1)
        even = 2 * (1 - late) + late * (1 - jnp.minimum(j // (down + outer_cols), 1))
        odd = 2 * (1 - late) + 3 * late
        return who * odd + (1 - who) * even

    def columns(col):
        return pl.ds(pl.multiple_of(col * PANEL, PANEL), PANEL)

    def fetch_down(who, j, ring, sem):
        return pltpu.make_async_copy(a_h.at[:, columns(who * down + j)], ring.at[j % RING], sem.at[j % RING])

    def fetch_up(j, ring, sem):
        return pltpu.make_async_copy(du_h.at[:, columns(j - down)], ring.at[j % RING], sem.at[j % RING])

    def fetch(who, j, ring, sem):
        when(j < down, lambda: fetch_down(who, j, ring, sem).start())
        when((j >= down) & (j < last) & (who == 1), lambda: fetch_up(j, ring, sem).start())

    def right(who, j, ring, sem, use):
        def arrived():
            pltpu.make_async_copy(a_h.at[:, columns(0)], ring.at[j % RING], sem.at[j % RING]).wait()
            return ring[j % RING]

        def patched():
            block, hot = arrived(), hot_ref[...]
            is_lead = (jnp.max(hot.astype(f32), axis=1, keepdims=True) > 0) & (at_head == 0)
            use(jnp.where(is_lead, mm(hot, lead_du[:, columns(j - down)]).astype(bf16), block))

        when(j < down, lambda: use(arrived()))
        when((j >= down) & (j < last) & (who == 1), patched)
        when((j >= down) & (j < down + outer_cols) & (who == 0), lambda: use(do[:, columns(j - down)]))
        when(
            (j >= down + outer_cols) & (j < last) & (who == 0), lambda: use(qkv[:, columns(j - down - outer_cols)])
        )

    def to_out(j):
        late = jnp.minimum(j // down, 1)
        even = jnp.where(j < down + outer_cols, j - down + 3 * outer_cols, j - down - outer_cols)
        col = (1 - late) * (4 * outer_cols + j) + late * (core * (j - down) + (1 - core) * even)
        return pltpu.make_async_copy(final.at[j], out_h.at[:, columns(col)], out_sem.at[j])


    def own_send(src):
        return remote(src, halves.at[core], o_ss, o_rs, sibling)

    def own_from():
        return remote(dx_buf, halves.at[1 - core], o_ss, o_rs, sibling)

    def across_send(src):
        return remote(src, halves.at[core], c_ss, c_rs.at[core], beyond)

    def across_from(side):
        return remote(dx_buf, halves.at[side], c_ss, c_rs.at[side], beyond)

    def load_left(name):
        return pltpu.make_async_copy(raw[name][0], left, left_sem)

    loads = dict(dmid=(dmid_h, do), zh0=(zh0_h, dctx), qkv=(qkv_h, qkv), p=(p_h, p), y=(y_h, y_buf))
    names = list(loads)

    def load(name):
        return pltpu.make_async_copy(*loads[name], in_sem.at[names.index(name)])

    def load_wa(own, c):
        cols = pl.ds(c * features, features)
        return pltpu.make_async_copy((first_h if own else other_first_h).at[:, cols], wa.at[:, cols], a_sem.at[c])

    load_left("df").start()
    for j in range(RING):
        fetch_down(core, j, own_ring, own_sem).start()
        fetch_down(1 - core, j, sib_ring, ring_sem).start()
    load("dmid").start()
    load("zh0").start()
    for c in (3, 0, 1, 2):
        when(core == 0, lambda: load_wa(True, c).start())
        when(core == 1, lambda: load_wa(False, c).start())
    for name in ("qkv", "p", "y"):
        load(name).start()

    def turn(i):
        for b in range(features // BLOCK):
            grid = (BLOCK, features)
            eye = lax.broadcasted_iota(jnp.int32, grid, 0) + b * BLOCK == lax.broadcasted_iota(jnp.int32, grid, 1)
            left_t[i, pl.ds(b * BLOCK, BLOCK), :] = mm(eye.astype(f32).astype(bf16), left[...], NT).astype(bf16)

    def norm_panel(other):
        chosen = jnp.where(core == other, dnorm[2:4, :], dnorm[0:2, :])
        strips = [
            chosen[r : r + 1, c * PANEL : (c + 1) * PANEL]
            for r in range(2)
            for c in range(features // PANEL)
        ]
        return jnp.concatenate(strips + [jnp.zeros((16 - len(strips), PANEL), f32)], axis=0)

    pl.semaphore_wait(barrier, 5 + has_out.astype(jnp.int32))

    def stage_send(j):
        when(j >= RING, lambda: to_sibling(j - RING).wait_send())

        def use(block):
            sib_send[j % RING] = mm(left_t[left_of(1 - core, j)], block).astype(bf16)

        right(1 - core, j, sib_ring, ring_sem, use)
        to_sibling(j).start()
        fetch(1 - core, j + RING, sib_ring, ring_sem)

    def stage_part(j):
        to_sibling(j).wait_recv()

        def use(block):
            own = mm(left_t[left_of(core, j)], block)
            part[j] = (own + part[j].astype(f32)).astype(bf16)

        right(core, j, own_ring, own_sem, use)
        fetch(core, j + RING, own_ring, own_sem)
        when(j % 2 == 0, lambda: one_y(j).start())
        when((j % 2 == 1) & (dist == depth) & (depth > 0), lambda: two_in(j).start())
        when((j % 2 == 1) & (dist == depth) & (depth == 0), lambda: two_mid(j).start())

    def one_halves(j):
        one_y(j).wait_recv()
        part[j, mine, :] = (part[j, mine, :].astype(f32) + y1[j // 2].astype(f32)).astype(bf16)
        when((dist == depth) & (dist > 0), lambda: one_in(j).start())
        when((dist == depth) & inner, lambda: one_mid(j).start())

    def one_chain(j):
        one_in(j).wait_recv()
        part[j, mine, :] = (part[j, mine, :].astype(f32) + zin1[j // 2].astype(f32)).astype(bf16)
        when(dist > 0, lambda: one_in(j).start())
        when(inner, lambda: one_mid(j).start())

    def one_total(j):
        one_mid(j).wait_recv()
        final[j, mine, :] = (part[j, mine, :].astype(f32) + mid1[j // 2].astype(f32)).astype(bf16)
        when(has_out, lambda: one_out(j).start())
        one_back(j).start()

    def one_spread(j):
        one_out(j).wait_recv()
        when(has_out, lambda: one_out(j).start())
        one_back(j).start()

    def two_chain(j):
        two_in(j).wait_recv()
        part[j] = (part[j].astype(f32) + zin2[j // 2].astype(f32)).astype(bf16)
        when(dist > 0, lambda: two_in(j).start())
        when(inner, lambda: two_mid(j).start())

    def two_halves(j):
        two_mid(j).wait_recv()
        part[j, kept, :] = (part[j, kept, :].astype(f32) + mid2[j // 2].astype(f32)).astype(bf16)
        two_y(j).start()

    def two_total(j):
        two_y(j).wait_recv()
        final[j, kept, :] = (part[j, kept, :].astype(f32) + y2[j // 2].astype(f32)).astype(bf16)
        two_swap(j).start()
        when(has_out, lambda: two_out_kept(j).start())

    def two_swapped(j):
        two_swap_in(j).wait_recv()
        when(has_out, lambda: two_out_rest(j).start())

    def two_spread_kept(j):
        two_out_kept(j).wait_recv()
        when(has_out, lambda: two_out_kept(j).start())

    def two_spread_rest(j):
        two_out_rest(j).wait_recv()
        when(has_out, lambda: two_out_rest(j).start())

    def finish(j):
        when(j % 2 == 0, lambda: one_back_in(j).wait_recv())

        to_out(j).start()

    last_lag = 7 + 4 * depth

    pairs = features // PAIR
    items = tokens // BLOCK * pairs
    begin = 4

    def turn_next(name, following):
        load_left(name).wait()
        turn(raw[name][1])
        if following:
            load_left(following).start()

    def attention_begin():
        load("dmid").wait()
        load("zh0").wait()
        load_wa(True, 3).wait()
        attention_back_begin(do, norms, wa, dctx, rstd0, do, dctx, acc, dnorm)

    def send_rows():
        load("y").wait()

        @pl.when(at_head == 1)
        def _():
            leading = jnp.max(lead_picks(lengths, core, True), axis=1, keepdims=True) > 0
            dx_buf[...] = jnp.where(leading, 0.0, acc[...]).astype(bf16)

        @pl.when(at_head == 0)
        def _():
            dx_buf[...] = acc[...].astype(bf16)

        def go(own, across):
            across_send(across).start()
            when(~inside, lambda: own_send(own).start())

            @pl.when(inside)
            def _():
                halves[core] = own[...]

        when(at_head == 1, go, y_buf, dx_buf)
        when(at_head == 0, go, dx_buf, y_buf)

    def norm_hop(src, dst, i, target):
        return remote(norm.at[src], norm.at[dst], n_ss.at[i], n_rs.at[i], target)

    norm_sib = norm_hop(0, 1, 0, sibling)
    norm_y = norm_hop(2, 3, 1, across_y)
    norm_in_hop = norm_hop(7, 4, 2, inward)
    norm_mid = norm_hop(7, 5, 3, inward)
    norm_far = norm_hop(6, 6, 4, outward)

    def norm_steps(t):
        @pl.when(t == 0)
        def _():
            norm[0] = norm_panel(0)
            norm_sib.start()

        @pl.when(t == 2)
        def _():
            norm_sib.wait_recv()
            norm[2] = norm_panel(1) + norm[1]
            norm_y.start()

        @pl.when(t == 4)
        def _():
            norm_y.wait_recv()
            norm[7] = norm[2] + norm[3]

        @pl.when((t == 4 + 2 * (depth - dist)) & (dist < depth))
        def _():
            norm_in_hop.wait_recv()
            norm[7] = norm[7] + norm[4]

        @pl.when(t == 4 + 2 * (depth - dist))
        def _():
            when(dist > 0, lambda: norm_in_hop.start())
            when(inner, lambda: norm_mid.start())

        @pl.when((t == 6 + 2 * depth) & inner)
        def _():
            norm_mid.wait_recv()
            norm[6] = norm[7] + norm[5]
            when(has_out, lambda: norm_far.start())

        @pl.when((t == 6 + 2 * (depth + dist)) & (dist > 0))
        def _():
            norm_far.wait_recv()
            when(has_out, lambda: norm_far.start())

    dnorm[...] = dnorm_in[...]
    hot_ref[...] = lead_picks(lengths, core, True).astype(bf16)
    turn_next("df", "mid")

    def step(t, carry):
        def at(lag, kind, cond, run):
            j = t - lag
            ok = (j >= 0) & (j < panels)
            if kind is not None:
                ok = ok & (j % 2 == kind)
            if cond is not None:
                ok = ok & cond
            when(ok, run, j)

        at(7 + 2 * (depth + dist), 1, dist > 0, two_spread_rest)
        at(5 + 2 * (depth + dist), 1, dist > 0, two_spread_kept)
        at(5 + 2 * (depth + dist), 0, dist > 0, one_spread)
        at(7 + 2 * depth, 1, inner, two_swapped)
        at(5 + 2 * depth, 1, inner, two_total)
        at(5 + 2 * depth, 0, inner, one_total)
        at(3 + 2 * depth, 1, inner, two_halves)
        at(3 + 2 * (depth - dist), 0, dist < depth, one_chain)
        at(1 + 2 * (depth - dist), 1, dist < depth, two_chain)
        at(3, 0, None, one_halves)
        at(1, None, None, stage_part)
        at(0, None, None, stage_send)
        at(last_lag + 1, None, None, finish)
        when(t == begin, attention_begin)
        item = t - begin - 1
        when(t == begin + 1, lambda: [load("qkv").wait(), load("p").wait()])
        when((item >= 0) & (item < items), lambda: attention_back_item(item // pairs, item % pairs, qkv, p, dctx))
        when(t == 8, turn_next, "mid", "ctx")
        when(t == 9, turn_next, "ctx", "x")
        when(t == 10, turn_next, "x", None)
        for c in range(3):
            when(t == begin + items + 1 + c, lambda: [load_wa(True, c).wait(), attention_back_end(c, wa, qkv, acc)])
        when(t == begin + items + 4, send_rows)
        norm_steps(t - begin - 1)
        return carry

    lax.fori_loop(0, panels + last_lag + 1, step, 0)

    @pl.when(inside)
    def _():
        own_from().wait_recv()

    @pl.when(~inside)
    def _():
        own_send(dx_buf).wait_send()
        across_from(0).wait_recv()
        across_from(1).wait_recv()

    across_send(dx_buf).wait_send()
    norm_sib.wait_send()
    norm_y.wait_send()
    when(dist > 0, lambda: norm_in_hop.wait_send())
    when(inner, lambda: norm_mid.wait_send())
    when(has_out, lambda: norm_far.wait_send())
    norm_out[...] = norm[6]
    rows_done = pltpu.make_async_copy(halves, halves_h, h_sem)
    rows_done.start()

    def drain(j, carry):
        when(j >= panels - RING, lambda: to_sibling(j).wait_send())
        to_out(j).wait()

        @pl.when(j % 2 == 0)
        def _():
            one_y(j).wait_send()
            when(dist > 0, lambda: one_in(j).wait_send())
            when(inner, lambda: one_mid(j).wait_send())
            when(has_out, lambda: one_out(j).wait_send())
            one_back(j).wait_send()

        @pl.when(j % 2 == 1)
        def _():
            when(dist > 0, lambda: two_in(j).wait_send())

            @pl.when(inner)
            def _():
                two_mid(j).wait_send()
                two_y(j).wait_send()
                two_swap(j).wait_send()

            @pl.when(has_out)
            def _():
                two_out_kept(j).wait_send()
                two_out_rest(j).wait_send()

        return carry

    lax.fori_loop(0, panels, drain, 0)
    rows_done.wait()


def reduce_gradients(lengths, first, saved, chain):
    tokens, features = saved["x"].shape
    ff = saved["a"].shape[1]
    width = ff + ff // 2
    panels = width // PANEL
    evens, odds = (panels + 1) // 2, panels // 2
    h = features // 2
    one = pltpu.SemaphoreType.DMA
    arrays = [saved[k] for k in ("x", "ctx", "mid", "a", "df", "du", "dmid", "zh0", "qkv", "p", "y")]
    return pl.pallas_call(
        functools.partial(reduce_kernel, chain),
        out_shape=[S((features, width), bf16), S((16, PANEL), f32), S((2, tokens, features), bf16)],
        in_specs=[IN_SMEM] + [IN_VMEM] * 4 + [ANY] * 13,
        out_specs=[ANY, IN_VMEM, ANY],
        scratch_shapes=[
            vm(tokens, features), vm(4, features, tokens), vm(RING, tokens, PANEL), vm(RING, tokens, PANEL),
            vm(RING, features, PANEL), vm(panels, features, PANEL),
            vm(evens, h, PANEL), vm(evens, h, PANEL), vm(evens, h, PANEL),
            vm(odds, features, PANEL), vm(odds, h, PANEL), vm(odds, h, PANEL),
            vm(panels, features, PANEL), vm(2, tokens, features),
            vm(features, ff), vm(tokens, 3 * features), pltpu.VMEM(saved["p"].shape, bf16), vm(tokens, features),
            vm(tokens, features), pltpu.VMEM((tokens, features), f32), vm(tokens, features),
            pltpu.VMEM((4, features), f32), pltpu.VMEM((8, 16, PANEL), f32), vm(tokens, LEADS),
            one, dma(RING), dma(RING), dma(panels), dma(RING), dma(panels),
            dma(evens), dma(evens), dma(evens), dma(evens), dma(evens), dma(evens),
            dma(odds), dma(odds), dma(odds), dma(odds), dma(odds), dma(odds), dma(3, panels), dma(2, panels),
            one, one, one, dma(2), one, dma(ff // features), dma(5), dma(5), dma(5),
        ],
        compiler_params=params(3),
        name="reduce_gradients",
    )(lengths, saved["dnorm"], saved["norms"], saved["rstd0"], saved["lead_du"], *arrays, first, saved["other_first"])


def finish_kernel(lengths, total, halves, norm_in, first_out, second_out, rows_out, gain_out, shift_out):
    step = pl.program_id(0)
    features = rows_out.shape[1]
    wide = first_out.shape[1]
    first_out[...] = total[:, pl.ds(0, wide)].astype(f32)
    second_out[...] = total[:, pl.ds(wide, second_out.shape[1])].astype(f32)
    size = rows_out.shape[0]
    row = step // (SEQ // size)
    _, _, first = span_scalars(lengths, row)
    at = lax.broadcasted_iota(jnp.int32, (size, BLOCK), 0) + step % (SEQ // size) * size
    out = None
    for side in range(2):
        hot = at == places(first, side, (size, BLOCK), 1)
        part = mm(hot.astype(f32).astype(bf16), halves[side])
        out = part if out is None else out + part
    rows_out[...] = out
    strips = features // PANEL
    for r, ref in enumerate((gain_out, shift_out)):
        ref[...] = jnp.concatenate([norm_in[r * strips + c : r * strips + c + 1, :] for c in range(strips)], axis=1)


def finish(lengths, total, halves, norm_in, ff):
    features, width = total.shape
    tokens = halves.shape[1]
    size = SEQ
    steps = 2 * tokens // size
    part = features // steps
    row_spec = pl.BlockSpec((1, features), lambda i: (0, 0))
    return pl.pallas_call(
        finish_kernel,
        grid=(steps,),
        out_shape=[
            S((features, ff), f32), S((features, width - ff), f32), S((2 * tokens, features), f32),
            S((1, features), f32), S((1, features), f32),
        ],
        in_specs=[
            IN_SMEM, pl.BlockSpec((part, width), lambda i: (i, 0)),
            pl.BlockSpec((2, BLOCK, features), lambda i: (0, i // (SEQ // size), 0)), IN_VMEM,
        ],
        out_specs=[
            pl.BlockSpec((part, ff), lambda i: (i, 0)), pl.BlockSpec((part, width - ff), lambda i: (i, 0)),
            pl.BlockSpec((size, features), lambda i: (i, 0)), row_spec, row_spec,
        ],
        compiler_params=params(None),
        name="finish",
    )(lengths, total, halves, norm_in)


def per_device(section_rows, span_lengths, first_weights, second_weights, norm_gain, norm_shift):
    first, second = first_weights[0], second_weights[0]
    saved = front(section_rows[0], span_lengths, first, second, norm_gain, norm_shift)
    total, norm_total, halves = reduce_gradients(span_lengths, first, saved, lax.axis_size("dp") // 2)
    d_first, d_second, rows, gain, shift = finish(span_lengths, total, halves, norm_total, first.shape[1])
    return rows[None], d_first[None], d_second[None], gain, shift


def solution(mesh):
    in_specs = (
        P("section", "dp", None),
        P("dp", None),
        P("section", None, None),
        P("section", None, None),
        P("section", None),
        P("section", None),
    )
    out_specs = (
        P("section", "dp", None),
        P("section", None, None),
        P("section", None, None),
        P("section", None),
        P("section", None),
    )
    return jax.shard_map(
        per_device, mesh=mesh, in_specs=in_specs, out_specs=out_specs, check_vma=False
    )
```
